32 devices in a mesh: section: 2 (over core), dp: 16 (over z, y, x).
Axes of the slice: x: 2, y: 2, z: 4, core: 2. Of those that a mesh axis runs over, the one named last changes fastest.
Arguments:
- hidden_in: bfloat16 [2, 16, 512, 768], P(None, 'dp'), may hold values from -6 to 6
- segment_ids: int32 [2, 16, 512], P(None, 'dp'), may hold values from 0 to 31, never falling along the last dimension, each value on 1 to 64 neighbouring positions
- w_qkv: bfloat16 [2, 768, 2304], P('section'), may hold values from -0.21875 to 0.21875
- w_attn_out: bfloat16 [2, 768, 768], P('section'), may hold values from -0.625 to 0.625
- w_in: bfloat16 [2, 768, 6144], P('section'), may hold values from -0.21875 to 0.21875
- w_out: bfloat16 [2, 3072, 768], P('section'), may hold values from -0.109375 to 0.109375
- gains: float32 [2, 2, 768], P('section'), may hold values from 0.5 to 1.5
- biases: float32 [2, 6, 768], P('section'), may hold values from -4 to 4
- bias_in: float32 [2, 6144], P('section'), may hold values from -4 to 4
- cotangent: bfloat16 [2, 16, 512, 768], P(None, 'dp'), may hold values from -6 to 6
Outputs:
- activations: bfloat16 [2, 2, 16, 512, 768], P('section', None, 'dp')
- input_grads: bfloat16 [2, 2, 16, 512, 768], P('section', None, 'dp')
- grad_w_qkv: float32 [2, 768, 2304], P('section', 'dp')
- grad_w_attn_out: float32 [2, 768, 768], P('section', 'dp')
- grad_w_in: float32 [2, 768, 6144], P('section', 'dp')
- grad_w_out: float32 [2, 3072, 768], P('section', 'dp')
- grad_gains: float32 [2, 2, 768], P('section', None, 'dp')
- grad_biases: float32 [2, 6, 768], P('section', None, 'dp')
- grad_bias_in: float32 [2, 6144], P('section', 'dp')
The draws below stay inside these ranges and needn't reach their ends.
Inputs may be any that keep to these rules, and one draw needn't show every extreme that they name: `segment_ids`: within each row of 512 tokens the fragment numbers never fall; a fragment has at most 64 tokens.
All inputs are finite; a program needn't handle non-finite values.
Results may differ from the reference program's by a relative error of at most 0.02.
Values may be sent and summed in bfloat16 or wider, within the bound.
A program may use at most 320 MiB of HBM per device.

```python
import math
import jax
import jax.numpy as jnp
import numpy as np
from jax import lax

D = 768
HEADS = 12
HEAD = 64
FF = 3072
SEQ = 512
MICRO = 2
ROWS = 16


def spiked(values, rng, source, target, shards_of, factor):
    def block_of(dim):
        return (jnp.arange(values.shape[dim]) // (values.shape[dim] // shards_of)).reshape((-1,) + (1,) * (values.ndim - 1 - dim))

    first = jax.random.permutation(rng, shards_of)[block_of(target)]
    far = (block_of(target) + shards_of // 2) % shards_of
    return jnp.where((block_of(source) == first) | (block_of(source) == far), factor * values, values)


def levels(stream_key, extent, split, least, largest):
    factor_of, own = 1.0, jax.random.fold_in(stream_key, 6)
    for position, parts in split:
        heights = jnp.exp(jax.random.uniform(jax.random.fold_in(own, position), (parts,), jnp.float32, least / len(split), largest / len(split)))
        factor_of = factor_of * jnp.repeat(heights, extent[position] // parts).reshape([-1 if axis == position else 1 for axis in range(len(extent))])
    return factor_of


def profile(number_of, total, limit, slope):
    loads = [(1 << 20) // math.isqrt(standing ** slope) + 1 for standing in range(2, number_of + 1)]
    spare, given = total - limit - (number_of - 1), [1] * (number_of - 1)
    while spare > 0:
        movable = [i for i in range(number_of - 1) if given[i] < limit]
        whole, remaining = sum([loads[i] for i in movable]), spare
        for i in movable:
            extra = min(limit - given[i], max(1, remaining * loads[i] // whole), spare)
            given[i] = given[i] + extra
            spare = spare - extra
    return np.array([limit] + given)


def ragged(rng, number_of, total, bound, lean):
    if number_of == 2:
        one = jax.random.randint(rng, (), max(1, total - bound), min(bound, total - 1) + 1)
        return jnp.stack([one, total - one])
    tallies = jnp.asarray(profile(number_of, total, bound, lean), jnp.int32)
    twos = (number_of - 1) // 2
    donor, sink = tallies[1:1 + 2 * twos:2], tallies[2:2 + 2 * twos:2]
    room = jnp.minimum(donor - 1, bound - sink)
    passed = jax.random.randint(jax.random.fold_in(rng, 1), (twos,), 0, 1 << 20) % (room + 1)
    tallies = tallies.at[1:1 + 2 * twos:2].set(donor - passed).at[2:2 + 2 * twos:2].set(sink + passed)
    return tallies[jax.random.permutation(jax.random.fold_in(rng, 2), number_of)]


def gaussian(stream_key, extent, scale, limit, cuts=(), dtype=jnp.bfloat16):
    result = jax.random.normal(stream_key, extent, jnp.float32) * scale
    if len(cuts) > 0:
        result = levels(stream_key, extent, cuts, -0.22, 0.18) * result
    return jnp.clip(result, min=-limit, max=limit).astype(dtype)


def bell_draw_with(stream_key, dims, scale, limit, cuts, heavy, kind=jnp.bfloat16):
    drawn = scale * jax.random.normal(stream_key, dims, jnp.float32)
    if cuts:
        drawn = drawn * levels(stream_key, dims, cuts, -0.22, 0.18)
    return jnp.clip(spiked(drawn, jax.random.fold_in(stream_key, 3), *heavy), -limit, limit).astype(kind)


def setup_inputs(seed: int = 0) -> dict:
    seeds = jax.random.split(jax.random.key(seed), 11)
    return {
        "hidden_in": gaussian(seeds[0], (MICRO, ROWS, SEQ, D), 1.0, 6.0, ((1, 16),)),
        "segment_ids": jax.vmap(lambda own: jnp.searchsorted(jnp.cumsum(ragged(own, max(SEQ // 16, 4), SEQ, min(64, SEQ // 2), 1)), jnp.arange(SEQ), side="right"))(jax.random.split(seeds[1], MICRO * ROWS)).reshape((MICRO, ROWS, SEQ)).astype(jnp.int32),
        "w_qkv": gaussian(seeds[2], (2, D, 3 * D), D ** -0.5, 0.21875, ((0, 2),)),
        "w_attn_out": gaussian(seeds[3], (2, D, D), (D // 8) ** -0.5, 0.625, ((0, 2),)),
        "w_in": gaussian(seeds[4], (2, D, 2 * FF), D ** -0.5, 0.21875, ((0, 2),)),
        "w_out": gaussian(seeds[5], (2, FF, D), FF ** -0.5, 0.109375, ((0, 2),)),
        "gains": jnp.clip(1.0 + 0.1 * jax.random.normal(seeds[6], (2, 2, D), jnp.float32), 0.5, 1.5),
        "biases": gaussian(seeds[7], (2, 6, D), 0.3, 4.0, ((0, 2),), jnp.float32),
        "bias_in": gaussian(seeds[8], (2, 2 * FF), 0.3, 4.0, ((0, 2),), jnp.float32),
        "cotangent": bell_draw_with(seeds[9], (MICRO, ROWS, SEQ, D), 1.0, 6.0, ((1, 16),), (1, 3, 16, 2.0)),
    }


ln_eps = 1e-05
masked_score = -1000000000.0
highest = lax.Precision.HIGHEST

@jax.custom_vjp
def low(v):
    return lax.optimization_barrier(v.astype(jnp.bfloat16)).astype(jnp.float32)

@jax.custom_vjp
def low_back(v):
    return v

def low_keep(v):
    return (low(v), None)

def low_pass(kept, grad):
    return (grad,)

def back_keep(v):
    return (v, None)

def back_low(kept, grad):
    return (low(grad),)
low.defvjp(low_keep, low_pass)
low_back.defvjp(back_keep, back_low)

def alibi_slopes(head_count):
    base_count = 2 ** int(math.floor(math.log2(head_count)))
    leading = [2.0 ** (-8.0 * (number + 1) / base_count) for number in range(base_count)]
    trailing = [2.0 ** (-4.0 * (2 * number + 1) / base_count) for number in range(head_count - base_count)]
    return jnp.array(leading + trailing, jnp.float32)

def layer_norm(values, gain, offset_vec):
    center = values - lax.optimization_barrier(jnp.mean(values, axis=-1, keepdims=True))
    spread = lax.optimization_barrier(jnp.mean(center * center, axis=-1, keepdims=True))
    return center * lax.rsqrt(spread + ln_eps) * gain + offset_vec

def geglu_units(gate_up):
    half_width = gate_up.shape[-1] // 2
    return jax.nn.gelu(gate_up[..., :half_width], approximate=False) * gate_up[..., half_width:]

def attend_row(pieces):
    queries, keys_row, values_row, seg_row = pieces
    slopes = alibi_slopes(queries.shape[1])
    places = jnp.arange(queries.shape[0])
    distance = jnp.abs(places[:, None] - places[None, :]).astype(jnp.float32)
    same_frag = seg_row[:, None] == seg_row[None, :]
    raw_scores = jnp.einsum('qhe,khe->hqk', queries, keys_row, precision=highest) * queries.shape[-1] ** (-0.5)
    scores = low_back(jnp.where(same_frag[None], raw_scores - slopes[:, None, None] * distance[None], masked_score))
    probs = low(jax.nn.softmax(scores, axis=-1))
    return jnp.einsum('hqk,khe->qhe', probs, values_row, precision=highest)

def layer_forward(hidden, seg_rows, params):
    w_qkv, w_attn_out, w_in, w_out, gains, biases, bias_in = params
    projected = jnp.einsum('gsd,df->gsf', hidden, w_qkv, precision=highest)
    queries = low_back(low(projected[..., :D] + biases[0]))
    keys_all = low_back(low(projected[..., D:2 * D]))
    values_all = low_back(low(projected[..., 2 * D:] + biases[1]))
    split_shape = (hidden.shape[0], SEQ, HEADS, HEAD)
    attended = lax.map(jax.checkpoint(attend_row), (queries.reshape(split_shape), keys_all.reshape(split_shape), values_all.reshape(split_shape), seg_rows))
    attended = low_back(low(attended.reshape(hidden.shape)))
    branch = low_back(jnp.einsum('gsd,de->gse', attended, w_attn_out, precision=highest) + biases[2])
    normed_a = low(layer_norm(hidden + branch, gains[0], biases[3]))
    gate_up = low_back(jnp.einsum('gsd,df->gsf', normed_a, w_in, precision=highest) + bias_in)
    mixed = low(geglu_units(gate_up))
    ffn_out = low_back(jnp.einsum('gsf,fd->gsd', mixed, w_out, precision=highest) + biases[4])
    return layer_norm(normed_a + ffn_out, gains[1], biases[5])

def two_layers(hidden, probe, params_all, seg_rows):
    params_first = tuple((piece[0] for piece in params_all))
    params_second = tuple((piece[1] for piece in params_all))
    first_out = low_back(low(layer_forward(hidden, seg_rows, params_first)))
    second_out = low(layer_forward(first_out + probe, seg_rows, params_second))
    return (first_out, second_out)

def reference(hidden_in, segment_ids, w_qkv, w_attn_out, w_in, w_out, gains, biases, bias_in, cotangent):
    total_rows = MICRO * ROWS
    group_rows = math.gcd(total_rows, 8)
    group_count = total_rows // group_rows
    inputs = hidden_in.astype(jnp.float32).reshape(group_count, group_rows, SEQ, D)
    segs = segment_ids.reshape(group_count, group_rows, SEQ)
    cots = cotangent.astype(jnp.float32).reshape(group_count, group_rows, SEQ, D)
    params = tuple((piece.astype(jnp.float32) for piece in (w_qkv, w_attn_out, w_in, w_out, gains, biases, bias_in)))

    def one_group(carry, pieces):
        inputs_group, seg_group, cot_group = pieces

        def forward(hidden, probe, params_all):
            return two_layers(hidden, probe, params_all, seg_group)
        outs_pair, pullback = jax.vjp(forward, inputs_group, jnp.zeros_like(inputs_group), params)
        grad_hidden, grad_probe, grad_params = pullback((jnp.zeros_like(cot_group), cot_group))
        carry = tuple((total + piece for total, piece in zip(carry, grad_params)))
        return (carry, (outs_pair[0], outs_pair[1], grad_hidden, grad_probe))
    zero_sums = tuple((jnp.zeros_like(piece) for piece in params))
    sums, (first_out, second_out, grad_first, grad_second) = lax.scan(one_group, zero_sums, (inputs, segs, cots))
    full_shape = (MICRO, ROWS, SEQ, D)
    activations = jnp.stack([first_out.reshape(full_shape), second_out.reshape(full_shape)]).astype(jnp.bfloat16)
    input_grads = jnp.stack([grad_first.reshape(full_shape), grad_second.reshape(full_shape)]).astype(jnp.bfloat16)
    return (activations, input_grads, sums[0], sums[1], sums[2], sums[3], sums[4], sums[5], sums[6])
```

```python
import functools
import math

import jax
import jax.numpy as jnp
from jax import lax
from jax.experimental import pallas as pl
from jax.experimental.pallas import tpu as pltpu
from jax.sharding import PartitionSpec as P

HEADS = 12
HEAD = 64
GROUP = 4
QB = 128
HALO = 64
KW = QB + 2 * HALO
EPS = 1e-05
MASKED = -1.0e30
BF = jnp.bfloat16
F32 = jnp.float32
MESH = pl.DeviceIdType.MESH
Q_, K_, V_, O_, H_, NA_, NB_, X_ = range(8)
M_, P1_, P2_ = range(3)
NT = (((1,), (1,)), ((), ()))


def slope_list(head_count):
    base = 2 ** int(math.floor(math.log2(head_count)))
    leading = [2.0 ** (-8.0 * (k + 1) / base) for k in range(base)]
    trailing = [2.0 ** (-4.0 * (2 * k + 1) / base) for k in range(head_count - base)]
    return leading + trailing


def dot(a, b):
    return jnp.dot(a, b, preferred_element_type=F32)


def dot_nt(a, b):
    return lax.dot_general(a, b, NT, preferred_element_type=F32)


def normalize(v):
    c = v - jnp.mean(v, axis=-1, keepdims=True)
    rstd = lax.rsqrt(jnp.mean(c * c, axis=-1, keepdims=True) + EPS)
    return c * rstd, rstd


def stack_heads(v):
    head = lax.broadcasted_iota(jnp.int32, v.shape, 1) // HEAD
    zero = jnp.zeros_like(v)
    return jnp.concatenate([jnp.where(head == h, v, zero) for h in range(GROUP)], axis=0)


def merge_heads(r):
    rows = r.shape[0] // GROUP
    head = lax.broadcasted_iota(jnp.int32, (rows, r.shape[1]), 1) // HEAD
    out = r[:rows]
    for h in range(1, GROUP):
        out = jnp.where(head == h, r[h * rows : (h + 1) * rows], out)
    return out


def window_distance(ndist):
    r = lax.broadcasted_iota(jnp.int32, (QB, KW), 0)
    c = lax.broadcasted_iota(jnp.int32, (QB, KW), 1)
    ndist[...] = -jnp.abs(r + HALO - c).astype(F32)


def fwd_kernel(
    slopes, hid, segq, segk, wqkv_h, wo_h, win_h, wout_h, gains, biases, bin_,
    y_out, acts_out, big_out, stats_out,
    wqkv, wo, win, wout, xin, ybuf, sbuf, bigb, kpad, vpad, ndist, bacc, stats,
    wsem, xsem, send, recv, ysem, asem, bsem, ssem,
):
    dp = lax.axis_index("dp")
    sec = lax.axis_index("section")
    micro, seq, width = xin.shape
    ff = wout.shape[0]
    loads = [
        pltpu.make_async_copy(src, dst, wsem.at[i])
        for i, (src, dst) in enumerate(((wqkv_h, wqkv), (wo_h, wo), (win_h, win), (wout_h, wout)))
    ]

    def x_load(m):
        return pltpu.make_async_copy(hid.at[m], xin.at[m], xsem.at[m])

    @pl.when(sec == 0)
    def _():
        for m in range(micro):
            x_load(m).start()

    for c in loads:
        c.start()
    barrier = pltpu.get_barrier_semaphore()
    pl.semaphore_signal(barrier, inc=1, device_id=(1 - sec, dp), device_id_type=MESH)
    pl.semaphore_wait(barrier, 1)

    def hand(m):
        return pltpu.make_async_remote_copy(
            src_ref=ybuf.at[m], dst_ref=xin.at[m], send_sem=send.at[m], recv_sem=recv.at[m],
            device_id=(1, dp), device_id_type=MESH,
        )

    window_distance(ndist)
    for pad in (kpad, vpad):
        pad[0:HALO, :] = jnp.zeros((HALO, pad.shape[1]), BF)
        pad[HALO + seq :, :] = jnp.zeros((HALO, pad.shape[1]), BF)

    def save(kind, m):
        return pltpu.make_async_copy(
            xin.at[m] if kind == X_ else sbuf.at[kind], acts_out.at[kind, m], asem.at[kind]
        )

    def save_big(kind, m):
        return pltpu.make_async_copy(bigb.at[kind], big_out.at[kind, m], bsem.at[kind])

    def save_stats(m):
        return pltpu.make_async_copy(stats, stats_out.at[m], ssem)

    def save_y(m):
        return pltpu.make_async_copy(ybuf.at[m], y_out.at[m], ysem.at[m])

    def row(m, carry):
        @pl.when(sec == 0)
        def _():
            x_load(m).wait()

        @pl.when(sec == 1)
        def _():
            hand(m).wait_recv()

        @pl.when(m == 0)
        def _():
            loads[0].wait()

        @pl.when(m > 0)
        def _():
            for kind in range(8):
                save(kind, m - 1).wait()
            for kind in range(3):
                save_big(kind, m - 1).wait()
            save_stats(m - 1).wait()

        save(X_, m).start()

        def heads(g, carry):
            col = pl.multiple_of(g * 256, 256)
            x = xin[m]
            q = (dot(x, wqkv[:, pl.ds(col, 256)]) + biases[0:1, pl.ds(col, 256)]).astype(BF)
            k = dot(x, wqkv[:, pl.ds(width + col, 256)]).astype(BF)
            v = (dot(x, wqkv[:, pl.ds(2 * width + col, 256)]) + biases[1:2, pl.ds(col, 256)]).astype(BF)
            sbuf[Q_, :, pl.ds(col, 256)] = q
            sbuf[K_, :, pl.ds(col, 256)] = k
            sbuf[V_, :, pl.ds(col, 256)] = v
            kpad[HALO : HALO + seq, :] = k
            vpad[HALO : HALO + seq, :] = v
            lane = lax.broadcasted_iota(jnp.int32, (QB, 128), 1)
            for i in range(seq // QB):
                rows = slice(i * QB, (i + 1) * QB)
                same = segq[m, rows, :] == segk[m, i]
                away = jnp.where(same, ndist[...], MASKED)
                qs = stack_heads(sbuf[Q_, rows, pl.ds(col, 256)] * BF(HEAD**-0.5))
                s = dot_nt(qs, kpad[i * QB : i * QB + KW, :])
                probs = []
                kept = stats[rows, :]
                for h in range(GROUP):
                    sh = s[h * QB : (h + 1) * QB] + slopes[g * GROUP + h] * away
                    top = jnp.max(sh, axis=-1, keepdims=True)
                    e = jnp.exp(sh - top)
                    total = jnp.sum(e, axis=-1, keepdims=True)
                    probs.append((e * (1.0 / total)).astype(BF))
                    kept = jnp.where(lane == g * GROUP + h, top + jnp.log(total), kept)
                stats[rows, :] = kept
                r = dot(jnp.concatenate(probs, axis=0), vpad[i * QB : i * QB + KW, :])
                sbuf[O_, rows, pl.ds(col, 256)] = merge_heads(r).astype(BF)
            return carry

        lax.fori_loop(0, width // 256, heads, 0)
        for kind in (Q_, K_, V_, O_):
            save(kind, m).start()

        @pl.when(m == 0)
        def _():
            loads[1].wait()

        lane = lax.broadcasted_iota(jnp.int32, (256, 128), 1)

        def mix(t, carry):
            rows = pl.ds(pl.multiple_of(t * 256, 256), 256)
            a = xin[m, rows, :].astype(F32) + (dot(sbuf[O_, rows, :], wo[...]) + biases[2:3, :])
            n, rstd = normalize(a)
            sbuf[NA_, rows, :] = n.astype(BF)
            h = (n * gains[0:1, :] + biases[3:4, :]).astype(BF)
            sbuf[H_, rows, :] = h
            bacc[rows, :] = h.astype(F32) + biases[4:5, :]
            stats[rows, :] = jnp.where(lane == HEADS, rstd, stats[rows, :])
            return carry

        lax.fori_loop(0, seq // 256, mix, 0)
        save(H_, m).start()
        save(NA_, m).start()

        @pl.when(m == 0)
        def _():
            loads[2].wait()
            loads[3].wait()

        def chunk(c, carry):
            col = pl.multiple_of(c * 256, 256)
            h = sbuf[H_]
            gate = dot(h, win[:, pl.ds(col, 256)]) + bin_[0:1, pl.ds(col, 256)]
            up = dot(h, win[:, pl.ds(ff + col, 256)]) + bin_[0:1, pl.ds(ff + col, 256)]
            cdf = 0.5 + 0.5 * lax.erf(gate * (0.5**0.5))
            act = gate * cdf
            slope = cdf + gate * (jnp.exp(gate * gate * -0.5) * (2.0 * math.pi) ** -0.5)
            mixed = (act * up).astype(BF)
            bigb[M_, :, pl.ds(col, 256)] = mixed
            bigb[P1_, :, pl.ds(col, 256)] = act.astype(BF)
            bigb[P2_, :, pl.ds(col, 256)] = (up * slope).astype(BF)
            bacc[...] += dot(mixed, wout[pl.ds(col, 256), :])
            return carry

        lax.fori_loop(0, ff // 256, chunk, 0)
        for kind in range(3):
            save_big(kind, m).start()

        def finish(t, carry):
            rows = pl.ds(pl.multiple_of(t * 256, 256), 256)
            n, rstd = normalize(bacc[rows, :])
            sbuf[NB_, rows, :] = n.astype(BF)
            ybuf[m, rows, :] = (n * gains[1:2, :] + biases[5:6, :]).astype(BF)
            stats[rows, :] = jnp.where(lane == HEADS + 1, rstd, stats[rows, :])
            return carry

        lax.fori_loop(0, seq // 256, finish, 0)

        @pl.when(sec == 0)
        def _():
            hand(m).start()

        save_y(m).start()
        save(NB_, m).start()
        save_stats(m).start()
        return carry

    lax.fori_loop(0, micro, row, 0)
    last = micro - 1
    for kind in range(8):
        save(kind, last).wait()
    for kind in range(3):
        save_big(kind, last).wait()
    save_stats(last).wait()
    for m in range(micro):
        save_y(m).wait()

    @pl.when(sec == 0)
    def _():
        for m in range(micro):
            hand(m).wait_send()


def any_spec():
    return pl.BlockSpec(memory_space=pl.ANY)


def vmem_spec():
    return pl.BlockSpec(memory_space=pltpu.VMEM)


def smem_spec():
    return pl.BlockSpec(memory_space=pltpu.SMEM)


def run_forward(slopes, hid, segq, segk, w_qkv, w_o, w_in, w_out, gains, biases, b_in):
    micro, seq, width = hid.shape
    ff = w_out.shape[0]
    dma = pltpu.SemaphoreType.DMA
    return pl.pallas_call(
        fwd_kernel,
        out_shape=(
            jax.ShapeDtypeStruct((micro, seq, width), BF),
            jax.ShapeDtypeStruct((8, micro, seq, width), BF),
            jax.ShapeDtypeStruct((3, micro, seq, ff), BF),
            jax.ShapeDtypeStruct((micro, seq, 128), F32),
        ),
        in_specs=[smem_spec(), any_spec(), vmem_spec(), vmem_spec()]
        + [any_spec()] * 4
        + [vmem_spec()] * 3,
        out_specs=tuple([any_spec()] * 4),
        scratch_shapes=[
            pltpu.VMEM(w_qkv.shape, BF),
            pltpu.VMEM(w_o.shape, BF),
            pltpu.VMEM(w_in.shape, BF),
            pltpu.VMEM(w_out.shape, BF),
            pltpu.VMEM((micro, seq, width), BF),
            pltpu.VMEM((micro, seq, width), BF),
            pltpu.VMEM((7, seq, width), BF),
            pltpu.VMEM((3, seq, ff), BF),
            pltpu.VMEM((seq + 2 * HALO, 256), BF),
            pltpu.VMEM((seq + 2 * HALO, 256), BF),
            pltpu.VMEM((QB, KW), F32),
            pltpu.VMEM((seq, width), F32),
            pltpu.VMEM((seq, 128), F32),
            dma((4,)), dma((micro,)), dma((micro,)), dma((micro,)), dma((micro,)),
            dma((8,)), dma((3,)), dma,
        ],
        compiler_params=pltpu.CompilerParams(
            collective_id=1, has_side_effects=True, vmem_limit_bytes=60 << 20
        ),
        name="forward",
    )(slopes, hid, segq, segk, w_qkv, w_o, w_in, w_out, gains, biases, b_in)


def windows_of(segs):
    seq = segs.shape[-1]
    padded = jnp.pad(segs, ((0, 0), (HALO, HALO)), constant_values=-1)
    return jnp.stack([padded[:, i * QB : i * QB + KW] for i in range(seq // QB)], axis=1)[:, :, None, :]


TN = (((0,), (0,)), ((), ()))
TILE = 256
OUT_UNITS = 384
DG0, DG1, SQ, SV, SR, DB3, SF, DB5, BIN0 = range(9)


def dot_tn(a, b):
    return lax.dot_general(a, b, TN, preferred_element_type=F32)


def column_total(v):
    return jnp.sum(v.astype(F32), axis=0, keepdims=True)


def bwd_kernel(
    comm, slopes, cot, acts, big, stats_h, segq, segk, wqkv_h, wo_h, win_h, wout_h, gains,
    *refs,
):
    if comm:
        (dx_out, small_out, fq, fo, fi, fu, bu, bi, bo, bq,
         u1, i1, o1, q1, u2, i2, o2, q2, u3, i3, o3, q3, m1, m2, m3,
         *rest) = refs
        (s1, r1, s2, r2, s3, r3, ms, mr, *rest) = rest
    else:
        (dx_out, small_out, hu, hi, ho, hq, bu, bi, bo, bq, *rest) = refs
        (gsem, *rest) = rest
    (acc, df, dy, tr, nat, small, stats, pool, wpool, wslot, gbuf, kpad, vpad, dkacc, dvacc, ndist,
     psem, wsem, osem, nsem, ssem, ysem, xsem, send, recv) = rest
    dp = lax.axis_index("dp")
    sec = lax.axis_index("section")
    tokens, width = acc.shape
    rows_n, seq = segq.shape[0], segq.shape[1]
    ff = wout_h.shape[0]
    units = 256
    ntile = tokens // TILE

    def tile(t):
        return pl.ds(pl.multiple_of(t * TILE, TILE), TILE)

    if comm:
        bx, by, bz = dp % 2, (dp // 2) % 2, dp // 4
        xp = dp + 1 - 2 * bx
        yp = dp + 2 - 4 * by
        zp = [((bz + d) % 4) * 4 + dp % 4 for d in range(1, 4)]
        peers = [(sec, xp), (sec, yp)] + [(sec, z) for z in zp]
    else:
        peers = []

    def pool_load(slot, lanes, src, first):
        return pltpu.make_async_copy(
            src.at[:, pl.ds(first, lanes)], pool.at[slot, :, 0:lanes], psem.at[slot]
        )

    def weight_load(slot, part, src, first):
        return pltpu.make_async_copy(
            src.at[:, pl.ds(first, units)], wpool.at[slot, part], wsem.at[slot, part]
        )

    def wout_load(slot, c):
        return pltpu.make_async_copy(
            wout_h.at[pl.ds(pl.multiple_of(c * units, units), units), :], wslot.at[slot], osem.at[slot]
        )

    def nat_load(kind):
        return pltpu.make_async_copy(acts.at[kind], nat, nsem)

    stats_load = pltpu.make_async_copy(stats_h, stats, ssem)
    cot_load = pltpu.make_async_copy(cot, dy, ysem)

    def m_load(i):
        return pool_load(i % 2, OUT_UNITS, big.at[M_], pl.multiple_of(i * OUT_UNITS, OUT_UNITS))

    stats_load.start()
    nat_load(NB_).start()

    @pl.when(sec == 1)
    def _():
        cot_load.start()

    for j in range(3):
        pool_load(2 + j, 256, acts.at[H_], j * 256).start()
    m_load(0).start()

    def chunk_loads(slot, c):
        first = pl.multiple_of(c * units, units)
        return [
            weight_load(slot, 0, win_h, first),
            weight_load(slot, 1, win_h, ff + first),
            wout_load(slot, c),
            pool_load(2 + 2 * slot, units, big.at[P1_], first),
            pool_load(3 + 2 * slot, units, big.at[P2_], first),
        ]

    barrier = pltpu.get_barrier_semaphore()
    for peer in [(1 - sec, dp)] + peers:
        pl.semaphore_signal(barrier, inc=1, device_id=peer, device_id_type=MESH)
    pl.semaphore_wait(barrier, 1 + len(peers))

    def hand():
        return pltpu.make_async_remote_copy(
            src_ref=df, dst_ref=dy, send_sem=send, recv_sem=recv, device_id=(0, dp), device_id_type=MESH
        )

    def put(buf, lead, kind, lane, value):
        lanes = pl.ds(lane, value.shape[1])
        if not comm:
            buf[(*lead, slice(None), lanes)] = value
            return
        share = value.shape[0] // 16
        for o in range(16):
            x, y, z = o % 2, (o // 2) % 2, o // 4
            f, s = (x, y) if kind == 0 else (y, x)
            buf[(*lead, f, s, z, slice(None), lanes)] = value[o * share : (o + 1) * share]

    if comm:
        firsts = (bx, by)
        seconds = (by, bx)
        near = (xp, yp)
        far = (yp, xp)
        pieces = {}
        number = 0

        def piece(buf, a, b, c, lead, kind, out, lane):
            return dict(buf=buf, a=a, b=b, c=c, lead=lead, kind=kind, out=out, lane=lane)

        def remote(src, dst, ss, rs, to):
            return pltpu.make_async_remote_copy(
                src_ref=src, dst_ref=dst, send_sem=ss, recv_sem=rs, device_id=(sec, to), device_id_type=MESH
            )

        def first_stage(p, n):
            k = p["kind"]
            return remote(
                p["buf"].at[(*p["lead"], 1 - firsts[k])], p["a"].at[p["lead"]], s1.at[n], r1.at[n], near[k]
            )

        def second_stage(p, n):
            k = p["kind"]
            return remote(
                p["buf"].at[(*p["lead"], firsts[k], 1 - seconds[k])], p["b"].at[p["lead"]], s2.at[n], r2.at[n], far[k]
            )

        def third_stage(p, n, d):
            k = p["kind"]
            return remote(
                p["buf"].at[(*p["lead"], firsts[k], seconds[k], (bz + d) % 4)],
                p["c"].at[(*p["lead"], d - 1)], s3.at[n, d - 1], r3.at[n, d - 1], zp[d - 1],
            )

        def add_first(p, second):
            k = p["kind"]

            def one(z, carry):
                at = (*p["lead"], firsts[k], second, z)
                p["buf"][at] = (p["buf"][at].astype(F32) + p["a"][(*p["lead"], second, z)].astype(F32)).astype(BF)
                return carry

            lax.fori_loop(0, 4, one, 0)

        def after_first(p, n):
            k = p["kind"]
            first_stage(p, n).wait()
            add_first(p, 1 - seconds[k])
            second_stage(p, n).start()
            add_first(p, seconds[k])

        def after_second(p, n):
            k = p["kind"]
            second_stage(p, n).wait()

            def one(z, carry):
                at = (*p["lead"], firsts[k], seconds[k], z)
                p["buf"][at] = (p["buf"][at].astype(F32) + p["b"][(*p["lead"], z)].astype(F32)).astype(BF)
                return carry

            lax.fori_loop(0, 4, one, 0)
            for d in (1, 2, 3):
                third_stage(p, n, d).start()

        def after_third(p, n):
            k = p["kind"]
            for d in (1, 2, 3):
                third_stage(p, n, d).wait()
            total = p["buf"][(*p["lead"], firsts[k], seconds[k], bz)].astype(F32)
            for d in (0, 1, 2):
                total = total + p["c"][(*p["lead"], d)].astype(F32)
            for out, lane, begin, count in p["out"]:
                out[:, pl.ds(lane, count)] = total[:, begin : begin + count]

        def pieces_u():
            return [
                (piece(bu, u1, u2, u3, (k,), k, [(fu, k * 384, 0, 384)], 0), k) for k in (0, 1)
            ]

        def pieces_i(j):
            first = pl.multiple_of(j * 512, 512)
            return [
                (piece(bi, i1, i2, i3, (j, k), k, [(fi, k * ff + first, 0, 512)], 0), 2 + 2 * j + k)
                for k in (0, 1)
            ]

        def pieces_o():
            return [
                (piece(bo, o1, o2, o3, (k,), k, [(fo, k * 384, 0, 384)], 0), 14 + k) for k in (0, 1)
            ]

        def pieces_q(g):
            first = pl.multiple_of(g * 256, 256)
            outs = (
                [(fq, first, 0, 256), (fq, width + first, 256, 128)],
                [(fq, width + 128 + first, 0, 128), (fq, 2 * width + first, 128, 256)],
            )
            return [
                (piece(bq, q1, q2, q3, (g, k), k, outs[k], 0), 16 + 2 * g + k) for k in (0, 1)
            ]

        def launch(pairs):
            for p, n in pairs:
                first_stage(p, n).start()

    def transpose_in(slots, kind_ready=None):
        for j, slot in enumerate(slots):
            pool_load(slot, 256, acts.at[H_], 0).wait()
            tr[j * 256 : (j + 1) * 256, :] = pool[slot, :, 0:256].T

    transpose_in((2, 3, 4))
    for load in chunk_loads(0, 0):
        load.start()
    small[...] = jnp.zeros_like(small)
    window_distance(ndist)
    for pad in (kpad, vpad):
        pad[0:HALO, :] = jnp.zeros((HALO, pad.shape[1]), BF)
        pad[HALO + seq :, :] = jnp.zeros((HALO, pad.shape[1]), BF)
    stats_load.wait()
    nat_load(NB_).wait()

    @pl.when(sec == 1)
    def _():
        cot_load.wait()

    @pl.when(sec == 0)
    def _():
        hand().wait_recv()

    def norm_back(dv, rows, which, gain_row, gain_sum, offset_sum, round_sum):
        n = nat[rows, :].astype(F32)
        rstd = stats[rows, HEADS + which : HEADS + which + 1]
        dn = dv * gains[gain_row : gain_row + 1, :]
        d = rstd * (
            dn - jnp.mean(dn, axis=-1, keepdims=True) - n * jnp.mean(dn * n, axis=-1, keepdims=True)
        )
        low = d.astype(BF)
        acc[rows, :] = d
        df[rows, :] = low
        small[gain_sum : gain_sum + 1, :] += column_total(dv * n)
        small[offset_sum : offset_sum + 1, :] += column_total(dv)
        small[round_sum : round_sum + 1, :] += column_total(low)

    def out_norm(t, carry):
        rows = tile(t)
        norm_back(dy[rows, :].astype(F32), rows, 1, 1, DG1, DB5, SF)
        return carry

    lax.fori_loop(0, ntile, out_norm, 0)
    nat_load(NA_).start()

    def out_grad(i, carry):
        m_load(i).wait()

        @pl.when(i + 1 < ff // OUT_UNITS)
        def _():
            m_load(i + 1).start()

        g = dot(pool[i % 2].T, df[...]).astype(BF)
        if comm:
            y, z = i % 2, i // 2
            for x in range(2):
                part = g[x * 192 : (x + 1) * 192]
                bu[0, x, y, z] = part[:, :384]
                bu[1, y, x, z] = part[:, 384:]
        else:
            rows = pl.ds(pl.multiple_of(i * OUT_UNITS, OUT_UNITS), OUT_UNITS)
            bu[0, rows, :] = g[:, :384]
            bu[1, rows, :] = g[:, 384:]
        return carry

    lax.fori_loop(0, ff // OUT_UNITS, out_grad, 0)
    if comm:
        launch(pieces_u())

    def feed(j, carry):
        for half in range(2):
            c = 2 * j + half
            for load in chunk_loads(half, c):
                load.wait()

            @pl.when(c + 1 < ff // units)
            def _():
                for load in chunk_loads(1 - half, c + 1):
                    load.start()

            def gate(t, carry):
                rows = tile(t)
                dm = dot_nt(df[rows, :], wslot[half])
                gbuf[0, rows, :] = (dm * pool[3 + 2 * half, rows, 0:units].astype(F32)).astype(BF)
                gbuf[1, rows, :] = (dm * pool[2 + 2 * half, rows, 0:units].astype(F32)).astype(BF)
                return carry

            lax.fori_loop(0, ntile, gate, 0)
            lane = pl.multiple_of((c % 3) * units, units)
            for k in range(2):
                small[pl.ds(BIN0 + 4 * k + c // 3, 1), pl.ds(lane, units)] = column_total(gbuf[k])
                put(bi, (j, k), k, half * units, dot(tr[...], gbuf[k]).astype(BF))

            def back(t, carry):
                rows = tile(t)
                acc[rows, :] += dot_nt(gbuf[0, rows, :], wpool[half, 0]) + dot_nt(
                    gbuf[1, rows, :], wpool[half, 1]
                )
                return carry

            lax.fori_loop(0, ntile, back, 0)
        if comm:
            launch(pieces_i(j))
        return carry

    for j in range(3):
        pass
    lax.fori_loop(0, ff // (2 * units), feed, 0)

    o_loads = [pool_load(j, 256, acts.at[O_], j * 256) for j in range(3)]
    wo_loads = [weight_load(0, j, wo_h, j * 256) for j in range(3)]
    for load in o_loads + wo_loads:
        load.start()
    nat_load(NA_).wait()

    def attn_norm(t, carry):
        rows = tile(t)
        norm_back(acc[rows, :], rows, 0, 0, DG0, DB3, SR)
        return carry

    lax.fori_loop(0, ntile, attn_norm, 0)

    def head_loads(slot, g):
        first = pl.multiple_of(g * 256, 256)
        return [weight_load(slot, j, wqkv_h, j * width + first) for j in range(3)] + [
            pool_load(3 * slot + j, 256, acts.at[kind], first) for j, kind in enumerate((Q_, K_, V_))
        ]

    for j in range(3):
        o_loads[j].wait()
        tr[j * 256 : (j + 1) * 256, :] = pool[j, :, 0:256].T
    for load in wo_loads:
        load.wait()
    for load in head_loads(1, 0):
        load.start()
    x_loads = [pool_load(j, 256, acts.at[X_], j * 256) for j in range(3)]
    for load in x_loads:
        load.start()

    def project(t, carry):
        rows = tile(t)
        total = dot_nt(df[rows, 0:256], wpool[0, 0])
        for j in (1, 2):
            total += dot_nt(df[rows, j * 256 : (j + 1) * 256], wpool[0, j])
        dy[rows, :] = total.astype(BF)
        return carry

    lax.fori_loop(0, ntile, project, 0)
    for k in range(2):
        put(bo, (k,), k, 0, dot(tr[...], df[:, k * 384 : (k + 1) * 384]).astype(BF))
    if comm:
        launch(pieces_o())
    for j in range(3):
        x_loads[j].wait()
        tr[j * 256 : (j + 1) * 256, :] = pool[j, :, 0:256].T

    def heads(g, carry):
        slot = (g + 1) % 2
        col = pl.multiple_of(g * 256, 256)
        for load in head_loads(slot, g):
            load.wait()

        @pl.when(g + 1 < width // 256)
        def _():
            for load in head_loads(1 - slot, g + 1):
                load.start()

        def row(r, carry):
            base = pl.multiple_of(r * seq, seq)
            kpad[HALO : HALO + seq, :] = pool[3 * slot + 1, pl.ds(base, seq), 0:256]
            vpad[HALO : HALO + seq, :] = pool[3 * slot + 2, pl.ds(base, seq), 0:256]
            dkacc[...] = jnp.zeros_like(dkacc)
            dvacc[...] = jnp.zeros_like(dvacc)
            lane = lax.broadcasted_iota(jnp.int32, (QB, 128), 1)
            for i in range(seq // QB):
                rows = pl.ds(pl.multiple_of(base + i * QB, QB), QB)
                same = segq[r, i * QB : (i + 1) * QB, :] == segk[r, i]
                away = jnp.where(same, ndist[...], MASKED)
                kw = kpad[i * QB : i * QB + KW, :]
                vw = vpad[i * QB : i * QB + KW, :]
                qs = stack_heads(pool[3 * slot, rows, 0:256] * BF(HEAD**-0.5))
                os = stack_heads(dy[rows, pl.ds(col, 256)])
                s = dot_nt(qs, kw)
                d = dot_nt(os, vw)
                kept = stats[rows, :]
                ps, ds = [], []
                for h in range(GROUP):
                    part = slice(h * QB, (h + 1) * QB)
                    lse = jnp.sum(jnp.where(lane == g * GROUP + h, kept, 0.0), axis=-1, keepdims=True)
                    p = jnp.exp(s[part] + slopes[g * GROUP + h] * away - lse)
                    pd = p * d[part]
                    ds.append((pd - p * jnp.sum(pd, axis=-1, keepdims=True)).astype(BF))
                    ps.append(p.astype(BF))
                ds = jnp.concatenate(ds, axis=0)
                ps = jnp.concatenate(ps, axis=0)
                gbuf[0, rows, :] = (merge_heads(dot(ds, kw)) * HEAD**-0.5).astype(BF)
                dkacc[i * QB : i * QB + KW, :] += dot_tn(ds, qs)
                dvacc[i * QB : i * QB + KW, :] += dot_tn(ps, os)
            gbuf[1, pl.ds(base, seq), :] = dkacc[HALO : HALO + seq, :].astype(BF)
            gbuf[2, pl.ds(base, seq), :] = dvacc[HALO : HALO + seq, :].astype(BF)
            return carry

        lax.fori_loop(0, rows_n, row, 0)
        small[SQ : SQ + 1, pl.ds(col, 256)] = column_total(gbuf[0])
        small[SV : SV + 1, pl.ds(col, 256)] = column_total(gbuf[2])

        def back(t, carry):
            rows = tile(t)
            total = acc[rows, :]
            for j in range(3):
                total += dot_nt(gbuf[j, rows, :], wpool[slot, j])
            acc[rows, :] = total
            return carry

        lax.fori_loop(0, ntile, back, 0)
        put(bq, (g, 0), 0, 0, dot(tr[...], gbuf[0]).astype(BF))
        dk = dot(tr[...], gbuf[1]).astype(BF)
        put(bq, (g, 0), 0, 256, dk[:, :128])
        put(bq, (g, 1), 1, 0, dk[:, 128:])
        put(bq, (g, 1), 1, 128, dot(tr[...], gbuf[2]).astype(BF))
        if comm:
            launch(pieces_q(g))
        return carry

    lax.fori_loop(0, width // 256, heads, 0)

    def result(t, carry):
        rows = tile(t)
        df[rows, :] = acc[rows, :].astype(BF)
        return carry

    lax.fori_loop(0, ntile, result, 0)

    @pl.when(sec == 1)
    def _():
        hand().start()

    x_store = pltpu.make_async_copy(df, dx_out, xsem)
    x_store.start()

    if comm:
        def small_copies(stage):
            if stage == 0:
                return [remote(small, m1, ms.at[0], mr.at[0], xp)]
            if stage == 1:
                return [remote(m1, m2, ms.at[1], mr.at[1], yp)]
            return [remote(m2, m3.at[d], ms.at[2 + d], mr.at[2 + d], zp[d]) for d in range(3)]

        def each(fn):
            for p, n in pieces_u():
                fn(p, n)

            def loop_i(j, carry):
                for p, n in pieces_i(j):
                    fn(p, n)
                return carry

            lax.fori_loop(0, ff // (2 * units), loop_i, 0)
            for p, n in pieces_o():
                fn(p, n)

            def loop_q(g, carry):
                for p, n in pieces_q(g):
                    fn(p, n)
                return carry

            lax.fori_loop(0, width // 256, loop_q, 0)

        for c in small_copies(0):
            c.start()
        each(after_first)
        for c in small_copies(0):
            c.wait()
        m1[...] += small[...]
        for c in small_copies(1):
            c.start()
        each(after_second)
        for c in small_copies(1):
            c.wait()
        m2[...] += m1[...]
        for c in small_copies(2):
            c.start()
        each(after_third)
        for c in small_copies(2):
            c.wait()
        small_out[...] = m2[...] + m3[0] + m3[1] + m3[2]
    else:
        stores = [
            pltpu.make_async_copy(src, dst, gsem.at[i])
            for i, (src, dst) in enumerate(((bu, hu), (bi, hi), (bo, ho), (bq, hq)))
        ]
        for c in stores:
            c.start()
        small_out[...] = small[...]
        for c in stores:
            c.wait()
    x_store.wait()

    @pl.when(sec == 1)
    def _():
        hand().wait_send()


def run_backward(comm, slopes, cot, acts, big, stats, segq, segk, w_qkv, w_o, w_in, w_out, gains):
    tokens, width = cot.shape
    ff = w_out.shape[0]
    dma = pltpu.SemaphoreType.DMA
    groups, chunks = width // 256, ff // 512

    def vm(*shape, dtype=BF):
        return pltpu.VMEM(shape, dtype)

    small = jax.ShapeDtypeStruct((16, width), F32)
    dx = jax.ShapeDtypeStruct((tokens, width), BF)
    if comm:
        ru, ri = ff // 16, width // 16
        kinds = (((2,), ru, 384), ((chunks, 2), ri, 512), ((2,), ri, 384), ((groups, 2), ri, 384))
        bufs = [vm(*lead, 2, 2, 4, r, c) for lead, r, c in kinds]
        lands = (
            [vm(*lead, 2, 4, r, c) for lead, r, c in kinds]
            + [vm(*lead, 4, r, c) for lead, r, c in kinds]
            + [vm(*lead, 3, r, c) for lead, r, c in kinds]
            + [vm(16, width, dtype=F32), vm(16, width, dtype=F32), vm(3, 16, width, dtype=F32)]
        )
        n = 4 + 2 * chunks + 2 * groups
        sems = [dma((n,)), dma((n,)), dma((n,)), dma((n,)), dma((n, 3)), dma((n, 3)), dma((5,)), dma((5,))]
        outs = [
            jax.ShapeDtypeStruct((ri, 3 * width), F32),
            jax.ShapeDtypeStruct((ri, width), F32),
            jax.ShapeDtypeStruct((ri, 2 * ff), F32),
            jax.ShapeDtypeStruct((ru, width), F32),
        ]
        out_specs = [vmem_spec()] * 4
        special = bufs + lands + sems
    else:
        shapes = ((2, ff, 384), (chunks, 2, width, 512), (2, width, 384), (groups, 2, width, 384))
        outs = [jax.ShapeDtypeStruct(s, BF) for s in shapes]
        out_specs = [any_spec()] * 4
        special = [vm(*s) for s in shapes] + [dma((4,))]
    seq = segq.shape[1]
    scratch = special + [
        vm(tokens, width, dtype=F32),
        vm(tokens, width),
        vm(tokens, width),
        vm(width, tokens),
        vm(tokens, width),
        vm(16, width, dtype=F32),
        vm(tokens, 128, dtype=F32),
        vm(6, tokens, OUT_UNITS),
        vm(2, 3, width, 256),
        vm(2, 256, width),
        vm(3, tokens, 256),
        vm(seq + 2 * HALO, 256),
        vm(seq + 2 * HALO, 256),
        vm(seq + 2 * HALO, 256, dtype=F32),
        vm(seq + 2 * HALO, 256, dtype=F32),
        vm(QB, KW, dtype=F32),
        dma((6,)), dma((2, 3)), dma((2,)), dma, dma, dma, dma, dma, dma,
    ]
    return pl.pallas_call(
        functools.partial(bwd_kernel, comm),
        out_shape=tuple([dx, small] + outs),
        in_specs=[smem_spec()] + [any_spec()] * 4 + [vmem_spec()] * 2 + [any_spec()] * 4 + [vmem_spec()],
        out_specs=tuple([any_spec(), vmem_spec()] + out_specs),
        scratch_shapes=scratch,
        compiler_params=pltpu.CompilerParams(
            collective_id=2, has_side_effects=True, vmem_limit_bytes=64 << 20
        ),
        name="backward",
    )(slopes, cot, acts, big, stats, segq, segk, w_qkv, w_o, w_in, w_out, gains)


def shards(comm, hidden, segs, w_qkv, w_o, w_in, w_out, gains, biases, b_in, cot):
    w_qkv, w_o, w_in, w_out, gains, biases = (v[0] for v in (w_qkv, w_o, w_in, w_out, gains, biases))
    micro, _, seq, width = hidden.shape
    ff = w_out.shape[0]
    tokens = micro * seq
    segs = segs.reshape(micro, seq)
    segq, segk = segs[:, :, None], windows_of(segs)
    slopes = jnp.array(slope_list(HEADS), F32)
    y, acts, big, stats = run_forward(
        slopes, hidden.reshape(micro, seq, width), segq, segk, w_qkv, w_o, w_in, w_out, gains, biases, b_in
    )
    dx, small, *grads = run_backward(
        comm, slopes, cot.reshape(tokens, width), acts.reshape(8, tokens, width), big.reshape(3, tokens, ff),
        stats.reshape(tokens, 128), segq, segk, w_qkv, w_o, w_in, w_out, gains,
    )
    owners, me = lax.axis_size("dp"), lax.axis_index("dp")
    if comm:
        gq, go, gi, gu = grads
    else:
        hu, hi, ho, hq = grads
        gu = jnp.concatenate([hu[0], hu[1]], axis=1)
        gi = jnp.transpose(hi, (2, 1, 0, 3)).reshape(width, 2 * ff)
        go = jnp.concatenate([ho[0], ho[1]], axis=1)
        flat = jnp.concatenate([hq[:, 0], hq[:, 1]], axis=-1).reshape(width // 256, width, 3, 256)
        gq = jnp.transpose(flat, (1, 2, 0, 3)).reshape(width, 3 * width)

        def share(v):
            parts = v.reshape(owners, v.shape[0] // owners, v.shape[1])
            got = lax.all_to_all(parts, "dp", split_axis=0, concat_axis=0, tiled=True)
            return jnp.sum(got.astype(F32), axis=0)

        gq, go, gi, gu = (share(v) for v in (gq, go, gi, gu))
        small = lax.psum(small, "dp")
    part = width // owners
    mine = lax.dynamic_slice_in_dim(small[:8], me * part, part, axis=1)
    inner = lax.dynamic_slice_in_dim(small[8:].reshape(1, 2 * ff), me * (2 * ff // owners), 2 * ff // owners, axis=1)
    return (
        y.reshape(1, *hidden.shape), dx.reshape(1, *hidden.shape), gq[None], go[None], gi[None], gu[None],
        mine[None, :2], mine[None, 2:], inner,
    )


def solution(mesh):
    rows = P(None, "dp", None, None)
    layer = P("section", None, None)
    comm = mesh.shape["dp"] == 16
    return jax.shard_map(
        functools.partial(shards, comm),
        mesh=mesh,
        in_specs=(rows, P(None, "dp", None)) + (layer,) * 6 + (P("section", None), rows),
        out_specs=(
            P("section", None, "dp", None, None),
            P("section", None, "dp", None, None),
            P("section", "dp", None),
            P("section", "dp", None),
            P("section", "dp", None),
            P("section", "dp", None),
            P("section", None, "dp"),
            P("section", None, "dp"),
            P("section", "dp"),
        ),
        check_vma=False,
    )
```

```python
import functools
import math

import jax
import jax.numpy as jnp
from jax import lax
from jax.experimental import pallas as pl
from jax.experimental.pallas import tpu as pltpu
from jax.sharding import PartitionSpec as P

HEADS = 12
HEAD = 64
GROUP = 2
LANES = GROUP * HEAD
QB = 128
HALO = 64
KW = QB + 2 * HALO
EPS = 1e-05
MASKED = -1.0e30
TILE = 256
UNITS = 256
PIECE = 384
BF = jnp.bfloat16
F32 = jnp.float32
MESH = pl.DeviceIdType.MESH
NT = (((1,), (1,)), ((), ()))
TN = (((0,), (0,)), ((), ()))
H_, NA_, NB_, X_ = range(4)
M_, P1_, P2_ = range(3)
GAIN0, GAIN1, BIAS_Q, BIAS_V, BIAS_O, BIAS_A, BIAS_F, BIAS_B, BIAS_IN = range(9)
VECTORS = 16
RSTD_A, RSTD_B = HEADS, HEADS + 1


def slope_list(head_count):
    base = 2 ** int(math.floor(math.log2(head_count)))
    leading = [2.0 ** (-8.0 * (k + 1) / base) for k in range(base)]
    trailing = [2.0 ** (-4.0 * (2 * k + 1) / base) for k in range(head_count - base)]
    return leading + trailing


def dot(a, b):
    return jnp.dot(a, b, preferred_element_type=F32)


def dot_nt(a, b):
    return lax.dot_general(a, b, NT, preferred_element_type=F32)


def dot_tn(a, b):
    return lax.dot_general(a, b, TN, preferred_element_type=F32)


def normalize(v):
    c = v - jnp.mean(v, axis=-1, keepdims=True)
    rstd = lax.rsqrt(jnp.mean(c * c, axis=-1, keepdims=True) + EPS)
    return c * rstd, rstd


def stack_heads(v):
    head = lax.broadcasted_iota(jnp.int32, v.shape, 1) // HEAD
    zero = jnp.zeros_like(v)
    return jnp.concatenate([jnp.where(head == h, v, zero) for h in range(GROUP)], axis=0)


def merge_heads(r):
    rows = r.shape[0] // GROUP
    head = lax.broadcasted_iota(jnp.int32, (rows, r.shape[1]), 1) // HEAD
    out = r[:rows]
    for h in range(1, GROUP):
        out = jnp.where(head == h, r[h * rows : (h + 1) * rows], out)
    return out


def window_distance(ndist):
    r = lax.broadcasted_iota(jnp.int32, (QB, KW), 0)
    c = lax.broadcasted_iota(jnp.int32, (QB, KW), 1)
    ndist[...] = -jnp.abs(r + HALO - c).astype(F32)


def tile_rows(t):
    return pl.ds(pl.multiple_of(t * TILE, TILE), TILE)


def lanes_at(start, count):
    return pl.ds(pl.multiple_of(start, 128), count)


def fwd_kernel(
    slopes, hid, segq, segk, wqkv_h, wo_h, win_h, wout_h, par_in,
    y_out, acts_out, o_out, m_out, qkv_out, p_out, stats_out,
    wqkv_out, wo_out, win_out, wout_out, par_out,
    wqkv, wo, win, wout, par, xy, qkvs, os_, hs, big, psend, precv, acc, kpad, vpad, ndist, stats,
    lsem, rsend, rrecv, wsave, hsem, ysem, asem, qsem, osem, osend, orecv, bsem, msend, mrecv, tsem, ssend, srecv,
    parsem,
):
    dp = lax.axis_index("dp")
    sec = lax.axis_index("section")
    _, micro, seq, width = xy.shape
    half, ffh, ff = wo.shape[1], wout.shape[1], wout_h.shape[0]
    sib = (1 - sec, dp)

    parts = []
    for j in range(3):
        parts.append((wqkv_h, wqkv, lambda c, j=j: (slice(None), lanes_at(j * width + c * half, half)),
                      (slice(None), slice(j * half, (j + 1) * half))))
    parts.append((wo_h, wo, lambda c: (pl.ds(pl.multiple_of(c * half, 128), half), slice(None)), (slice(None), slice(None))))
    for j in range(2):
        parts.append((win_h, win, lambda c, j=j: (slice(None), lanes_at(j * ff + c * ffh, ffh)),
                      (slice(None), slice(j * ffh, (j + 1) * ffh))))
    parts.append((wout_h, wout, lambda c: (pl.ds(pl.multiple_of(c * ffh, 128), ffh), slice(None)), (slice(None), slice(None))))

    def own_part(i):
        src, dst, pick, place = parts[i]
        return pltpu.make_async_copy(src.at[pick(sec)], dst.at[(sec, *place)], lsem.at[i])

    def other_part(i):
        src, dst, pick, place = parts[i]
        return pltpu.make_async_remote_copy(
            src_ref=src.at[pick(1 - sec)], dst_ref=dst.at[(sec, *place)],
            send_sem=rsend.at[i], recv_sem=rrecv.at[i], device_id=sib, device_id_type=MESH,
        )

    def other_par():
        return pltpu.make_async_remote_copy(
            src_ref=par_in, dst_ref=par.at[sec], send_sem=rsend.at[7], recv_sem=rrecv.at[7],
            device_id=sib, device_id_type=MESH,
        )

    def x_load(m):
        return pltpu.make_async_copy(hid.at[m], xy.at[0, m], hsem.at[m])

    for m in range(micro):
        x_load(m).start()
    for i in range(7):
        own_part(i).start()
    barrier = pltpu.get_barrier_semaphore()
    pl.semaphore_signal(barrier, inc=1, device_id=sib, device_id_type=MESH)
    pl.semaphore_wait(barrier, 1)
    other_par().start()
    for i in range(7):
        other_part(i).start()
    par[sec] = par_in[...]
    window_distance(ndist)
    for pad in (kpad, vpad):
        pad[0:HALO, :] = jnp.zeros((HALO, half), BF)
        pad[HALO + seq :, :] = jnp.zeros((HALO, half), BF)
    for m in range(micro):
        x_load(m).wait()

    def need(l, which):
        @pl.when(l == sec)
        def _():
            for i in which:
                own_part(i).wait()

        @pl.when(l != sec)
        def _():
            for i in which:
                other_part(i).wait_recv()

    def save(kind, l, m):
        src = xy.at[l, m] if kind == X_ else hs.at[kind, m]
        return pltpu.make_async_copy(src, acts_out.at[l, kind, m], asem.at[kind, l, m])

    def save_qkv(kind, l, m):
        return pltpu.make_async_copy(qkvs.at[m, kind], qkv_out.at[l, kind, m], qsem.at[kind, l, m])

    def save_o(l, m):
        return pltpu.make_async_copy(os_.at[m], o_out.at[l, m, :, lanes_at(sec * half, half)], osem.at[l, m])

    def share_o(l, m):
        return pltpu.make_async_remote_copy(
            src_ref=os_.at[m], dst_ref=o_out.at[l, m, :, lanes_at(sec * half, half)],
            send_sem=osend.at[l, m], recv_sem=orecv.at[l, m], device_id=sib, device_id_type=MESH,
        )

    def save_big(kind, l, m):
        if kind == M_:
            dst = m_out.at[l, m, :, lanes_at(sec * ffh, ffh)]
        else:
            dst = p_out.at[l, kind - 1, m]
        return pltpu.make_async_copy(big.at[m, kind], dst, bsem.at[kind, l, m])

    def share_m(l, m):
        return pltpu.make_async_remote_copy(
            src_ref=big.at[m, M_], dst_ref=m_out.at[l, m, :, lanes_at(sec * ffh, ffh)],
            send_sem=msend.at[l, m], recv_sem=mrecv.at[l, m], device_id=sib, device_id_type=MESH,
        )

    def save_stats(l, m):
        return pltpu.make_async_copy(stats.at[l, m], stats_out.at[l, m], tsem.at[l, m])

    def save_y(m):
        return pltpu.make_async_copy(xy.at[sec + 1, m], y_out.at[m], ysem.at[m])

    def partial(phase, l, m):
        return pltpu.make_async_remote_copy(
            src_ref=psend.at[phase, m], dst_ref=precv.at[phase, l, m],
            send_sem=ssend.at[phase, l, m], recv_sem=srecv.at[phase, l, m], device_id=sib, device_id_type=MESH,
        )

    def weight_saves(l):
        pairs = ((wqkv, wqkv_out), (wo, wo_out), (win, win_out), (wout, wout_out))
        return [pltpu.make_async_copy(s.at[l], d.at[l], wsave.at[i, l]) for i, (s, d) in enumerate(pairs)]

    par_save = pltpu.make_async_copy(par, par_out, parsem)

    def attend(l, m):
        @pl.when(m == 0)
        def _():
            need(l, (0, 1, 2))

            @pl.when(l != sec)
            def _():
                other_par().wait_recv()

        @pl.when(l > 0)
        def _():
            for kind in range(3):
                save_qkv(kind, l - 1, m).wait()
            save_o(l - 1, m).wait()
            share_o(l - 1, m).wait_send()
            partial(0, l - 1, m).wait_send()

        save(X_, l, m).start()
        bias_q = par[l, BIAS_Q : BIAS_Q + 1, lanes_at(sec * half, half)]
        bias_v = par[l, BIAS_V : BIAS_V + 1, lanes_at(sec * half, half)]

        def project(t, carry):
            rows = tile_rows(t)
            r = dot(xy[l, m, rows, :], wqkv[l])
            q = (r[:, :half] + bias_q).astype(BF)
            k = r[:, half : 2 * half].astype(BF)
            v = (r[:, 2 * half :] + bias_v).astype(BF)
            qkvs[m, 0, rows, :] = q
            qkvs[m, 1, rows, :] = k
            qkvs[m, 2, rows, :] = v
            below = pl.ds(pl.multiple_of(HALO + t * TILE, HALO), TILE)
            kpad[below, :] = k
            vpad[below, :] = v
            return carry

        lax.fori_loop(0, seq // TILE, project, 0)
        for kind in range(3):
            save_qkv(kind, l, m).start()

        def heads(g, carry):
            cols = lanes_at(g * LANES, LANES)
            lane = lax.broadcasted_iota(jnp.int32, (QB, 128), 1)
            for i in range(seq // QB):
                rows = slice(i * QB, (i + 1) * QB)
                same = segq[m, rows, :] == segk[m, i]
                away = jnp.where(same, ndist[...], MASKED)
                qs = stack_heads(qkvs[m, 0, rows, cols] * BF(HEAD**-0.5))
                s = dot_nt(qs, kpad[i * QB : i * QB + KW, cols])
                probs = []
                kept = stats[l, m, rows, :]
                for h in range(GROUP):
                    sh = s[h * QB : (h + 1) * QB] + slopes[sec * (HEADS // 2) + g * GROUP + h] * away
                    top = jnp.max(sh, axis=-1, keepdims=True)
                    e = jnp.exp(sh - top)
                    total = jnp.sum(e, axis=-1, keepdims=True)
                    probs.append((e * (1.0 / total)).astype(BF))
                    kept = jnp.where(lane == g * GROUP + h, top + jnp.log(total), kept)
                stats[l, m, rows, :] = kept
                r = dot(jnp.concatenate(probs, axis=0), vpad[i * QB : i * QB + KW, cols])
                os_[m, rows, cols] = merge_heads(r).astype(BF)
            return carry

        lax.fori_loop(0, half // LANES, heads, 0)
        save_o(l, m).start()
        share_o(l, m).start()

        @pl.when(m == 0)
        def _():
            need(l, (3,))

        def mix(t, carry):
            rows = tile_rows(t)
            psend[0, m, rows, :] = dot(os_[m, rows, :], wo[l]).astype(BF)
            return carry

        lax.fori_loop(0, seq // TILE, mix, 0)
        partial(0, l, m).start()

    def feed(l, m):
        @pl.when(m == 0)
        def _():
            need(l, (4, 5, 6))
            for c in weight_saves(l):
                c.start()

        @pl.when(l > 0)
        def _():
            save(H_, l - 1, m).wait()
            save(NA_, l - 1, m).wait()
            for kind in range(3):
                save_big(kind, l - 1, m).wait()
            share_m(l - 1, m).wait_send()
            partial(1, l - 1, m).wait_send()

        partial(0, l, m).wait_recv()
        lane = lax.broadcasted_iota(jnp.int32, (TILE, 128), 1)

        def norm(t, carry):
            rows = tile_rows(t)
            a = xy[l, m, rows, :].astype(F32) + (
                psend[0, m, rows, :].astype(F32) + precv[0, l, m, rows, :].astype(F32) + par[l, BIAS_O : BIAS_O + 1, :]
            )
            n, rstd = normalize(a)
            hs[NA_, m, rows, :] = n.astype(BF)
            hs[H_, m, rows, :] = (n * par[l, GAIN0 : GAIN0 + 1, :] + par[l, BIAS_A : BIAS_A + 1, :]).astype(BF)
            stats[l, m, rows, :] = jnp.where(lane == RSTD_A, rstd, stats[l, m, rows, :])
            return carry

        lax.fori_loop(0, seq // TILE, norm, 0)
        save(H_, l, m).start()
        save(NA_, l, m).start()
        acc[...] = jnp.zeros_like(acc)

        def chunk(c, carry):
            cols = lanes_at(c * UNITS, UNITS)
            unit = sec * ffh + c * UNITS
            spot = lanes_at(unit % width, UNITS)
            h = hs[H_, m]
            gate = dot(h, win[l, :, cols]) + par[l, pl.ds(BIAS_IN + unit // width, 1), spot]
            up = dot(h, win[l, :, lanes_at(ffh + c * UNITS, UNITS)]) + par[
                l, pl.ds(BIAS_IN + ff // width + unit // width, 1), spot
            ]
            cdf = 0.5 + 0.5 * lax.erf(gate * (0.5**0.5))
            act = gate * cdf
            slope = cdf + gate * (jnp.exp(gate * gate * -0.5) * (2.0 * math.pi) ** -0.5)
            mixed = (act * up).astype(BF)
            big[m, M_, :, cols] = mixed
            big[m, P1_, :, cols] = act.astype(BF)
            big[m, P2_, :, cols] = (up * slope).astype(BF)
            acc[...] += dot(mixed, wout[l, pl.ds(pl.multiple_of(c * UNITS, UNITS), UNITS), :])
            return carry

        lax.fori_loop(0, ffh // UNITS, chunk, 0)
        psend[1, m] = acc[...].astype(BF)
        partial(1, l, m).start()
        for kind in range(3):
            save_big(kind, l, m).start()
        share_m(l, m).start()

    def finish(l, m):
        @pl.when(l > 0)
        def _():
            save(NB_, l - 1, m).wait()

        partial(1, l, m).wait_recv()
        lane = lax.broadcasted_iota(jnp.int32, (TILE, 128), 1)

        def norm(t, carry):
            rows = tile_rows(t)
            b = hs[H_, m, rows, :].astype(F32) + (
                psend[1, m, rows, :].astype(F32) + precv[1, l, m, rows, :].astype(F32) + par[l, BIAS_F : BIAS_F + 1, :]
            )
            n, rstd = normalize(b)
            hs[NB_, m, rows, :] = n.astype(BF)
            xy[l + 1, m, rows, :] = (n * par[l, GAIN1 : GAIN1 + 1, :] + par[l, BIAS_B : BIAS_B + 1, :]).astype(BF)
            stats[l, m, rows, :] = jnp.where(lane == RSTD_B, rstd, stats[l, m, rows, :])
            return carry

        lax.fori_loop(0, seq // TILE, norm, 0)
        save(NB_, l, m).start()
        save_stats(l, m).start()

        @pl.when(l == sec)
        def _():
            save_y(m).start()

    def layer(l, carry):
        def first(m, carry):
            @pl.when(l > 0)
            def _():
                finish(l - 1, m)

            attend(l, m)
            return carry

        lax.fori_loop(0, micro, first, 0)

        def second(m, carry):
            feed(l, m)
            return carry

        lax.fori_loop(0, micro, second, 0)
        return carry

    lax.fori_loop(0, 2, layer, 0)
    par_save.start()

    def last(m, carry):
        finish(1, m)
        return carry

    lax.fori_loop(0, micro, last, 0)

    def drain(m, carry):
        for kind in range(3):
            save_qkv(kind, 1, m).wait()
            save_big(kind, 1, m).wait()
        for kind in (H_, NA_, NB_):
            save(kind, 1, m).wait()
        save_o(1, m).wait()
        share_o(1, m).wait_send()
        share_m(1, m).wait_send()
        for phase in range(2):
            partial(phase, 1, m).wait_send()
        for l in range(2):
            save(X_, l, m).wait()
            save_stats(l, m).wait()
            share_o(l, m).wait_recv()
            share_m(l, m).wait_recv()
        save_y(m).wait()
        return carry

    lax.fori_loop(0, micro, drain, 0)
    for l in range(2):
        for c in weight_saves(l):
            c.wait()
    for i in range(7):
        other_part(i).wait_send()
    other_par().wait_send()
    par_save.wait()


def any_spec():
    return pl.BlockSpec(memory_space=pl.ANY)


def vmem_spec():
    return pl.BlockSpec(memory_space=pltpu.VMEM)


def smem_spec():
    return pl.BlockSpec(memory_space=pltpu.SMEM)


def vm(*shape, dtype=BF):
    return pltpu.VMEM(shape, dtype)


def run_forward(slopes, hid, segq, segk, w_qkv, w_o, w_in, w_out, par):
    micro, seq, width = hid.shape
    ff = w_out.shape[0]
    half, ffh = width // 2, ff // 2
    dma = pltpu.SemaphoreType.DMA

    def out(*shape, dtype=BF):
        return jax.ShapeDtypeStruct(shape, dtype)

    shapes = (
        out(micro, seq, width),
        out(2, 4, micro, seq, width),
        out(2, micro, seq, width),
        out(2, micro, seq, ff),
        out(2, 3, micro, seq, half),
        out(2, 2, micro, seq, ffh),
        out(2, micro, seq, 128, dtype=F32),
        out(2, width, 3 * half),
        out(2, half, width),
        out(2, width, 2 * ffh),
        out(2, ffh, width),
        out(2, VECTORS, width, dtype=F32),
    )
    return pl.pallas_call(
        fwd_kernel,
        out_shape=shapes,
        in_specs=[smem_spec(), any_spec(), vmem_spec(), vmem_spec()] + [any_spec()] * 4 + [vmem_spec()],
        out_specs=tuple([any_spec()] * len(shapes)),
        scratch_shapes=[
            vm(2, width, 3 * half),
            vm(2, half, width),
            vm(2, width, 2 * ffh),
            vm(2, ffh, width),
            vm(2, VECTORS, width, dtype=F32),
            vm(3, micro, seq, width),
            vm(micro, 3, seq, half),
            vm(micro, seq, half),
            vm(3, micro, seq, width),
            vm(micro, 3, seq, ffh),
            vm(2, micro, seq, width),
            vm(2, 2, micro, seq, width),
            vm(seq, width, dtype=F32),
            vm(seq + 2 * HALO, half),
            vm(seq + 2 * HALO, half),
            vm(QB, KW, dtype=F32),
            vm(2, micro, seq, 128, dtype=F32),
            dma((7,)), dma((8,)), dma((8,)), dma((4, 2)), dma((micro,)), dma((micro,)), dma((4, 2, micro)),
            dma((3, 2, micro)), dma((2, micro)), dma((2, micro)), dma((2, micro)), dma((3, 2, micro)),
            dma((2, micro)), dma((2, micro)), dma((2, micro)), dma((2, 2, micro)), dma((2, 2, micro)), dma,
        ],
        compiler_params=pltpu.CompilerParams(
            collective_id=1, has_side_effects=True, vmem_limit_bytes=62 << 20
        ),
        name="forward",
    )(slopes, hid, segq, segk, w_qkv, w_o, w_in, w_out, par)


def windows_of(segs):
    seq = segs.shape[-1]
    padded = jnp.pad(segs, ((0, 0), (HALO, HALO)), constant_values=-1)
    return jnp.stack([padded[:, i * QB : i * QB + KW] for i in range(seq // QB)], axis=1)[:, :, None, :]


def column_total(v):
    return jnp.sum(v.astype(F32), axis=0, keepdims=True)


def bwd_kernel(
    comm, slopes, cot, acts, o_full, m_full, qkv, pp, stats_h, segq, segk, wqkv, wo, win, wout, par, *refs
):
    if comm:
        (dx_out, small_out, fq, fo, fi, fu, *rest) = refs
        (buf, l1, l2, l3, v1, v2, v3, v4, s1, r1, s2, r2, s3, r3, vs, vr, fsem, *rest) = rest
        share_rows = fq.shape[0]
    else:
        (dx_out, small_out, grads_out, *rest) = refs
        (buf, gsem, *rest) = rest
    (acc, df, dy, tr, dft, nat, small, stats, pool, wpool, wslot, gbuf, kpad, vpad, dkacc, dvacc, ndist, psend, precv,
     poolsem, wsem, usem, nsem, ssem, ysem, xsem, esend, erecv) = rest
    dp = lax.axis_index("dp")
    sec = lax.axis_index("section")
    sib = (1 - sec, dp)
    tokens, width = df.shape
    rows_n, seq = segq.shape[0], segq.shape[1]
    ff = m_full.shape[2]
    half, ffh = width // 2, ff // 2
    ntile = tokens // TILE
    own = lanes_at(sec * half, half)

    if comm:
        bx, by, bz = dp % 2, (dp // 2) % 2, dp // 4
        xp = dp + 1 - 2 * bx
        yp = dp + 2 - 4 * by
        zp = [dp] + [((bz + d) % 4) * 4 + dp % 4 for d in range(1, 4)]
        near = xp * (1 - sec) + yp * sec
        far = yp * (1 - sec) + xp * sec
        b1 = bx * (1 - sec) + by * sec
        b2 = by * (1 - sec) + bx * sec
        greet = [(sec, xp), (sec, yp)] + [(sec, z) for z in zp[1:]] + [(1 - sec, z) for z in zp[1:]]
    else:
        greet = []

    def pool_load(slot, count, src, first):
        return pltpu.make_async_copy(src.at[:, lanes_at(first, count)], pool.at[slot, :, 0:count], poolsem.at[slot])

    def weight_load(slot, count, src, first):
        return pltpu.make_async_copy(src.at[:, lanes_at(first, count)], wpool.at[slot, :, 0:count], wsem.at[slot])

    def rows_load(slot, count, src, first):
        return pltpu.make_async_copy(
            src.at[pl.ds(pl.multiple_of(first, 128), count), :], wslot.at[slot, 0:count], usem.at[slot]
        )

    def nat_load(l, kind):
        return pltpu.make_async_copy(acts.at[l, kind], nat, nsem)

    def stats_load(l):
        return pltpu.make_async_copy(stats_h.at[l], stats, ssem)

    def m_load(l, i):
        return pool_load(2 + i % 2, PIECE, m_full.at[l], i * PIECE)

    def h_loads(l):
        return [pool_load(j, half, acts.at[l, H_], j * half) for j in range(2)]

    def chunk_loads(l, slot, c):
        first = c * UNITS
        return [
            weight_load(2 * slot, UNITS, win.at[l], first),
            weight_load(2 * slot + 1, UNITS, win.at[l], ffh + first),
            rows_load(slot, UNITS, wout.at[l], first),
            pool_load(2 * slot, UNITS, pp.at[l, 0], first),
            pool_load(2 * slot + 1, UNITS, pp.at[l, 1], first),
        ]

    def exchange(e):
        return pltpu.make_async_remote_copy(
            src_ref=psend, dst_ref=precv.at[e % 2], send_sem=esend.at[e], recv_sem=erecv.at[e],
            device_id=sib, device_id_type=MESH,
        )

    x_store = pltpu.make_async_copy(dy, dx_out, xsem)
    cot_load = pltpu.make_async_copy(cot, dy, ysem)
    cot_load.start()

    def first_loads(l):
        for load in h_loads(l):
            load.start()
        stats_load(l).start()
        nat_load(l, NB_).start()
        m_load(l, 0).start()

    first_loads(1)
    barrier = pltpu.get_barrier_semaphore()
    for peer in [sib] + greet:
        pl.semaphore_signal(barrier, inc=1, device_id=peer, device_id_type=MESH)
    pl.semaphore_wait(barrier, 1 + len(greet))

    def put(t, n, lane, value):
        lanes = slice(lane, lane + value.shape[1])
        if not comm:
            buf[t, n, :, lanes] = value
            return
        share = value.shape[0] // 16
        for o in range(16):
            x, y, z = o % 2, (o // 2) % 2, o // 4
            f = x * (1 - sec) + y * sec
            s = y * (1 - sec) + x * sec
            buf[t, n, f, s, z, :, lanes] = value[o * share : (o + 1) * share]

    if comm:

        def remote(src, dst, ss, rs, to):
            return pltpu.make_async_remote_copy(
                src_ref=src, dst_ref=dst, send_sem=ss, recv_sem=rs, device_id=to, device_id_type=MESH
            )

        def stage1(t, n):
            return remote(buf.at[t, n, 1 - b1], l1.at[t, n], s1.at[t, n], r1.at[t, n], (sec, near))

        def stage2(t, n):
            return remote(buf.at[t, n, b1, 1 - b2], l2.at[t, n], s2.at[t, n], r2.at[t, n], (sec, far))

        def stage3(t, n, d):
            return remote(
                buf.at[t, n, b1, b2, (bz + d) % 4], l3.at[n, sec, d], s3.at[t, n, d], r3.at[n, sec, d], (1 - t, zp[d])
            )

        def landed(n, k, d):
            return remote(l3.at[n, k, d], l3.at[n, k, d], s3.at[0, n, d], r3.at[n, k, d], (1 - sec, dp))

        def join(t, n, second):
            for z in range(4):
                at = (t, n, b1, second, z)
                buf[at] = (buf[at].astype(F32) + l1[t, n, second, z].astype(F32)).astype(BF)

        def after1(t, n):
            stage1(t, n).wait()
            join(t, n, 1 - b2)
            stage2(t, n).start()
            join(t, n, b2)

        def after2(t, n):
            stage2(t, n).wait()
            for z in range(4):
                at = (t, n, b1, b2, z)
                buf[at] = (buf[at].astype(F32) + l2[t, n, z].astype(F32)).astype(BF)
            for d in (1, 2, 3):
                stage3(t, n, d).start()

            @pl.when(sec != 1 - t)
            def _():
                stage3(t, n, 0).start()

        def sent3(t, n):
            for d in (1, 2, 3):
                stage3(t, n, d).wait_send()

            @pl.when(sec != 1 - t)
            def _():
                stage3(t, n, 0).wait_send()

        def total(n, k):
            for d in (1, 2, 3):
                landed(n, k, d).wait_recv()
            mine = l3[n, k, 1].astype(F32) + l3[n, k, 2].astype(F32) + l3[n, k, 3].astype(F32)
            return mine

        def collect(t, n, store):
            for k in range(2):
                value = total(n, k)

                @pl.when(sec == k)
                def _():
                    store(k, value + buf[t, n, b1, b2, bz].astype(F32))

                @pl.when(sec != k)
                def _():
                    landed(n, k, 0).wait_recv()
                    store(k, value + l3[n, k, 0].astype(F32))

        def span(lo, hi, fn):
            def one(n, carry):
                fn(n)
                return carry

            lax.fori_loop(lo, hi, one, 0)

        def run1(t, lo, hi):
            span(lo, hi, lambda n: after1(t, n))

        def run2(t, lo, hi):
            span(lo, hi, lambda n: after2(t, n))

        def out_copies(n, k, dst):
            src = acc.at[pl.ds(pl.multiple_of(n * share_rows, 16), share_rows), k * half : (k + 1) * half]
            return pltpu.make_async_copy(src, dst, fsem.at[n, k])

        def each_output(fn):
            def u_rows(n, k):
                return fu.at[pl.ds(pl.multiple_of(n * share_rows, 16), share_rows), k * half : (k + 1) * half]

            span(0, 4, lambda n: fn(n, lambda k: u_rows(n, k)))
            for jj in range(2):
                for g in range(2):
                    for i in range(2):
                        start = g * ff + (2 * jj + i) * PIECE
                        fn(4 + 4 * jj + 2 * g + i, lambda k, start=start: fi.at[:, pl.ds(start + k * ffh, PIECE)])
            fn(12, lambda k: fo.at[:, k * half : (k + 1) * half])
            for j in range(3):
                fn(13 + j, lambda k, j=j: fq.at[:, j * width + k * half : j * width + (k + 1) * half])

        def run3(t):
            def one(n, dst):
                def store(k, v):
                    acc[pl.ds(pl.multiple_of(n * share_rows, 16), share_rows), k * half : (k + 1) * half] = v

                collect(t, n, store)
                for k in range(2):
                    out_copies(n, k, dst(k)).start()

            each_output(one)

        def stored():
            def one(n, dst):
                for k in range(2):
                    out_copies(n, k, dst(k)).wait()

            each_output(one)

        def launch(t, lo, hi):
            span(lo, hi, lambda n: stage1(t, n).start())

    small[...] = jnp.zeros_like(small)
    window_distance(ndist)
    for pad in (kpad, vpad):
        pad[0:HALO, :] = jnp.zeros((HALO, half), BF)
        pad[HALO + seq :, :] = jnp.zeros((HALO, half), BF)
    cot_load.wait()

    def layer(t, carry):
        l = 1 - t

        def transpose_pool(slots):
            for j, slot in enumerate(slots):
                tr[j * half : (j + 1) * half, :] = pool[slot].T

        for load in h_loads(l):
            load.wait()
        transpose_pool((0, 1))
        for load in chunk_loads(l, 0, 0):
            load.start()
        stats_load(l).wait()
        nat_load(l, NB_).wait()

        def norm_back(dv, rows, rstd_lane, gain, gain_sum, offset_sum, round_sum):
            n = nat[rows, :].astype(F32)
            rstd = stats[rows, rstd_lane : rstd_lane + 1]
            dn = dv * par[l, gain : gain + 1, :]
            d = rstd * (
                dn - jnp.mean(dn, axis=-1, keepdims=True) - n * jnp.mean(dn * n, axis=-1, keepdims=True)
            )
            low = d.astype(BF)
            df[rows, :] = low
            small[t, gain_sum : gain_sum + 1, :] += column_total(dv * n)
            small[t, offset_sum : offset_sum + 1, :] += column_total(dv)
            small[t, round_sum : round_sum + 1, :] += column_total(low)

        def out_norm(i, carry):
            rows = tile_rows(i)
            norm_back(dy[rows, :].astype(F32), rows, RSTD_B, GAIN1, GAIN1, BIAS_B, BIAS_F)
            acc[rows, :] = jnp.zeros((TILE, width), F32)
            return carry

        lax.fori_loop(0, ntile, out_norm, 0)
        nat_load(l, NA_).start()

        dft[...] = df[:, own].T

        def out_grad(i, carry):
            m_load(l, i).wait()

            @pl.when(i + 1 < ff // PIECE)
            def _():
                m_load(l, i + 1).start()

            g = dot(dft[...], pool[2 + i % 2]).T.astype(BF)
            if comm:
                y, z = i % 2, i // 2
                for x in range(2):
                    f = x * (1 - sec) + y * sec
                    s = y * (1 - sec) + x * sec
                    for q in range(4):
                        buf[t, q, f, s, z] = g[x * 192 + q * 48 : x * 192 + (q + 1) * 48]
            else:
                buf[t, i // 2, pl.ds(pl.multiple_of(i % 2 * PIECE, 128), PIECE), :] = g
            return carry

        lax.fori_loop(0, ff // PIECE, out_grad, 0)
        if comm:
            launch(t, 0, 4)

            @pl.when(t == 1)
            def _():
                run1(0, 12, 16)
                run2(0, 0, 4)

        def feed(jj, carry):
            for part in range(3):
                c = 3 * jj + part
                slot = c % 2
                for load in chunk_loads(l, slot, c):
                    load.wait()

                @pl.when(c + 1 < ffh // UNITS)
                def _():
                    for load in chunk_loads(l, 1 - slot, c + 1):
                        load.start()

                def gate(i, carry):
                    rows = tile_rows(i)
                    dm = dot_nt(df[rows, :], wslot[slot, 0:UNITS])
                    gbuf[0, rows, 0:UNITS] = (dm * pool[2 * slot + 1, rows, 0:UNITS].astype(F32)).astype(BF)
                    gbuf[1, rows, 0:UNITS] = (dm * pool[2 * slot, rows, 0:UNITS].astype(F32)).astype(BF)
                    return carry

                lax.fori_loop(0, ntile, gate, 0)

                def back(i, carry):
                    rows = tile_rows(i)
                    acc[rows, :] += dot_nt(gbuf[0, rows, 0:UNITS], wpool[2 * slot, :, 0:UNITS]) + dot_nt(
                        gbuf[1, rows, 0:UNITS], wpool[2 * slot + 1, :, 0:UNITS]
                    )
                    return carry

                lax.fori_loop(0, ntile, back, 0)

                @pl.when(c == ffh // UNITS - 1)
                def _():
                    @pl.when(t > 0)
                    def _():
                        exchange(1).wait_send()

                    psend[...] = acc[...].astype(BF)
                    exchange(2 * t).start()

                unit = sec * ffh + c * UNITS
                spot = lanes_at(unit % width, UNITS)
                for k in range(2):
                    small[t, pl.ds(BIAS_IN + k * (ff // width) + unit // width, 1), spot] = column_total(
                        gbuf[k, :, 0:UNITS]
                    )
                    g = dot(tr[...], gbuf[k, :, 0:UNITS]).astype(BF)
                    n = 4 + 4 * jj + 2 * k
                    if part == 0:
                        put(t, n, 0, g)
                    elif part == 1:
                        put(t, n, 256, g[:, :128])
                        put(t, n + 1, 0, g[:, 128:])
                    else:
                        put(t, n + 1, 128, g)
            if comm:
                launch(t, 4 + 4 * jj, 8 + 4 * jj)
            return carry

        lax.fori_loop(0, ffh // (3 * UNITS), feed, 0)
        for j in range(2):
            pool_load(j, half, o_full.at[l], j * half).start()
        wo_load = rows_load(0, half, wo.at[l], 0)
        wo_load.start()
        head_weights = [weight_load(j, half, wqkv.at[l], j * half) for j in range(3)]
        for load in head_weights:
            load.start()
        if comm:
            run1(t, 0, 4)

            @pl.when(t == 1)
            def _():
                run2(0, 4, 16)

        nat_load(l, NA_).wait()
        for j in range(2):
            pool_load(j, half, o_full.at[l], j * half).wait()
        transpose_pool((0, 1))
        head_rows = [pool_load(j, half, qkv.at[l, j], 0) for j in range(3)]
        for load in head_rows:
            load.start()
        pool_load(3, half, acts.at[l, X_], 0).start()
        exchange(2 * t).wait_recv()

        def attn_norm(i, carry):
            rows = tile_rows(i)
            dh = df[rows, :].astype(F32) + (psend[rows, :].astype(F32) + precv[0, rows, :].astype(F32))
            norm_back(dh, rows, RSTD_A, GAIN0, GAIN0, BIAS_A, BIAS_O)
            return carry

        lax.fori_loop(0, ntile, attn_norm, 0)

        wo_load.wait()

        @pl.when((t == 1) & (sec == 1))
        def _():
            x_store.wait()

        def project(i, carry):
            rows = tile_rows(i)
            dy[rows, 0:half] = dot_nt(df[rows, :], wslot[0]).astype(BF)
            return carry

        lax.fori_loop(0, ntile, project, 0)
        put(t, 12, 0, dot(tr[...], df[:, own]).astype(BF))
        if comm:
            launch(t, 12, 13)
            run1(t, 4, 8)

        for load in head_rows:
            load.wait()

        def row(r, carry):
            base = pl.multiple_of(r * seq, seq)
            kpad[HALO : HALO + seq, :] = pool[1, pl.ds(base, seq), :]
            vpad[HALO : HALO + seq, :] = pool[2, pl.ds(base, seq), :]
            lane = lax.broadcasted_iota(jnp.int32, (QB, 128), 1)

            def heads(g, carry):
                cols = lanes_at(g * LANES, LANES)
                dkacc[...] = jnp.zeros_like(dkacc)
                dvacc[...] = jnp.zeros_like(dvacc)
                for i in range(seq // QB):
                    rows = pl.ds(pl.multiple_of(base + i * QB, QB), QB)
                    same = segq[r, i * QB : (i + 1) * QB, :] == segk[r, i]
                    away = jnp.where(same, ndist[...], MASKED)
                    kw = kpad[i * QB : i * QB + KW, cols]
                    vw = vpad[i * QB : i * QB + KW, cols]
                    qs = stack_heads(pool[0, rows, cols] * BF(HEAD**-0.5))
                    os = stack_heads(dy[rows, cols])
                    s = dot_nt(qs, kw)
                    d = dot_nt(os, vw)
                    kept = stats[rows, :]
                    ps, ds = [], []
                    for h in range(GROUP):
                        part = slice(h * QB, (h + 1) * QB)
                        lse = jnp.sum(jnp.where(lane == g * GROUP + h, kept, 0.0), axis=-1, keepdims=True)
                        p = jnp.exp(s[part] + slopes[sec * (HEADS // 2) + g * GROUP + h] * away - lse)
                        pd = p * d[part]
                        ds.append((pd - p * jnp.sum(pd, axis=-1, keepdims=True)).astype(BF))
                        ps.append(p.astype(BF))
                    ds = jnp.concatenate(ds, axis=0)
                    ps = jnp.concatenate(ps, axis=0)
                    gbuf[0, rows, cols] = (merge_heads(dot(ds, kw)) * HEAD**-0.5).astype(BF)
                    dkacc[i * QB : i * QB + KW, :] += dot_tn(ds, qs)
                    dvacc[i * QB : i * QB + KW, :] += dot_tn(ps, os)
                gbuf[1, pl.ds(base, seq), cols] = dkacc[HALO : HALO + seq, :].astype(BF)
                gbuf[2, pl.ds(base, seq), cols] = dvacc[HALO : HALO + seq, :].astype(BF)
                return carry

            lax.fori_loop(0, half // LANES, heads, 0)
            return carry

        lax.fori_loop(0, rows_n, row, 0)
        pool_load(0, half, acts.at[l, X_], half).start()
        for load in head_weights:
            load.wait()
        exchange(2 * t).wait_send()

        def back(i, carry):
            rows = tile_rows(i)
            total = dot_nt(gbuf[0, rows, :], wpool[0])
            for j in (1, 2):
                total += dot_nt(gbuf[j, rows, :], wpool[j])
            psend[rows, :] = total.astype(BF)
            return carry

        lax.fori_loop(0, ntile, back, 0)
        exchange(2 * t + 1).start()
        small[t, BIAS_Q : BIAS_Q + 1, own] = column_total(gbuf[0])
        small[t, BIAS_V : BIAS_V + 1, own] = column_total(gbuf[2])
        pool_load(3, half, acts.at[l, X_], 0).wait()
        pool_load(0, half, acts.at[l, X_], half).wait()
        transpose_pool((3, 0))

        @pl.when(t == 0)
        def _():
            first_loads(0)

        for j in range(3):
            put(t, 13 + j, 0, dot(tr[...], gbuf[j]).astype(BF))
        if comm:
            launch(t, 13, 16)
        exchange(2 * t + 1).wait_recv()

        def result(i, carry):
            rows = tile_rows(i)
            dx = df[rows, :].astype(F32) + (psend[rows, :].astype(F32) + precv[1, rows, :].astype(F32))
            dy[rows, :] = dx.astype(BF)
            return carry

        lax.fori_loop(0, ntile, result, 0)

        @pl.when(sec == l)
        def _():
            x_store.start()

        @pl.when(sec != l)
        def _():
            small[t, 0:2, :] = jnp.zeros((2, width), F32)
            small[t, BIAS_O:BIAS_IN, :] = jnp.zeros((BIAS_IN - BIAS_O, width), F32)

        if comm:
            run1(t, 8, 12)
        return carry

    lax.fori_loop(0, 2, layer, 0)
    exchange(3).wait_send()

    @pl.when(sec == 0)
    def _():
        x_store.wait()

    if comm:
        mine = 1 - sec

        def vectors(stage):
            if stage == 0:
                return [remote(small.at[sec], v1, vs.at[0], vr.at[0], sib)]
            if stage == 1:
                return [remote(v1, v2, vs.at[1], vr.at[1], (sec, xp))]
            if stage == 2:
                return [remote(v2, v3, vs.at[2], vr.at[2], (sec, yp))]
            return [remote(v3, v4.at[d - 1], vs.at[2 + d], vr.at[2 + d], (sec, zp[d])) for d in (1, 2, 3)]

        def go(stage):
            for c in vectors(stage):
                c.start()

        def done(stage):
            for c in vectors(stage):
                c.wait()

        go(0)
        run1(1, 12, 16)
        done(0)
        v1[...] += small[mine]
        go(1)
        run2(1, 0, 12)
        done(1)
        v2[...] += v1[...]
        go(2)
        run2(1, 12, 16)
        done(2)
        v3[...] += v2[...]
        go(3)
        run3(mine)
        done(3)
        small_out[...] = v3[...] + v4[0] + v4[1] + v4[2]
        for t in range(2):
            span(0, 16, lambda n, t=t: sent3(t, n))
        stored()
    else:
        store = pltpu.make_async_copy(buf, grads_out, gsem)
        store.start()
        small_out[...] = small[...]
        store.wait()


def run_backward(comm, slopes, cot, acts, o_full, m_full, qkv, pp, stats, segq, segk, wqkv, wo, win, wout, par):
    tokens, width = cot.shape
    ff = m_full.shape[2]
    half = width // 2
    dma = pltpu.SemaphoreType.DMA
    dx = jax.ShapeDtypeStruct((tokens, width), BF)
    if comm:
        r = width // 16
        small = jax.ShapeDtypeStruct((VECTORS, width), F32)
        outs = [
            jax.ShapeDtypeStruct((r, 3 * width), F32),
            jax.ShapeDtypeStruct((r, width), F32),
            jax.ShapeDtypeStruct((r, 2 * ff), F32),
            jax.ShapeDtypeStruct((ff // 16, width), F32),
        ]
        out_specs = [any_spec()] * 4
        special = [
            vm(2, 16, 2, 2, 4, r, PIECE),
            vm(2, 16, 2, 4, r, PIECE),
            vm(2, 16, 4, r, PIECE),
            vm(16, 2, 4, r, PIECE),
            vm(VECTORS, width, dtype=F32),
            vm(VECTORS, width, dtype=F32),
            vm(VECTORS, width, dtype=F32),
            vm(3, VECTORS, width, dtype=F32),
            dma((2, 16)), dma((2, 16)), dma((2, 16)), dma((2, 16)), dma((2, 16, 4)), dma((16, 2, 4)), dma((6,)), dma((6,)), dma((16, 2)),
        ]
    else:
        small = jax.ShapeDtypeStruct((2, VECTORS, width), F32)
        outs = [jax.ShapeDtypeStruct((2, 16, width, PIECE), BF)]
        out_specs = [any_spec()]
        special = [vm(2, 16, width, PIECE), dma]
    seq = segq.shape[1]
    scratch = special + [
        vm(tokens, width, dtype=F32),
        vm(tokens, width),
        vm(tokens, width),
        vm(width, tokens),
        vm(half, tokens),
        vm(tokens, width),
        vm(2, VECTORS, width, dtype=F32),
        vm(tokens, 128, dtype=F32),
        vm(4, tokens, PIECE),
        vm(4, width, PIECE),
        vm(2, half, width),
        vm(3, tokens, half),
        vm(seq + 2 * HALO, half),
        vm(seq + 2 * HALO, half),
        vm(seq + 2 * HALO, LANES, dtype=F32),
        vm(seq + 2 * HALO, LANES, dtype=F32),
        vm(QB, KW, dtype=F32),
        vm(tokens, width),
        vm(2, tokens, width),
        dma((4,)), dma((4,)), dma((2,)), dma, dma, dma, dma, dma((4,)), dma((4,)),
    ]
    return pl.pallas_call(
        functools.partial(bwd_kernel, comm),
        out_shape=tuple([dx, small] + outs),
        in_specs=[smem_spec()] + [any_spec()] * 7 + [vmem_spec()] * 2 + [any_spec()] * 4 + [vmem_spec()],
        out_specs=tuple([any_spec(), vmem_spec()] + out_specs),
        scratch_shapes=scratch,
        compiler_params=pltpu.CompilerParams(
            collective_id=2, has_side_effects=True, vmem_limit_bytes=64 << 20
        ),
        name="backward",
    )(slopes, cot, acts, o_full, m_full, qkv, pp, stats, segq, segk, wqkv, wo, win, wout, par)


def assemble(halves, width, ff):
    def columns(v):
        return jnp.concatenate(v, axis=1)

    gu = columns([h[:4].reshape(ff, PIECE) for h in halves])
    inner = [
        columns([h[4 + 4 * jj + 2 * k + i] for jj in range(2) for i in range(2)]) for k in range(2) for h in halves
    ]
    gi = columns(inner)
    go = columns([h[12] for h in halves])
    gq = columns([h[13 + j] for j in range(3) for h in halves])
    return gq, go, gi, gu


def shards(comm, hidden, segs, w_qkv, w_o, w_in, w_out, gains, biases, b_in, cot):
    w_qkv, w_o, w_in, w_out, gains, biases = (v[0] for v in (w_qkv, w_o, w_in, w_out, gains, biases))
    micro, _, seq, width = hidden.shape
    ff = w_out.shape[0]
    tokens = micro * seq
    segs = segs.reshape(micro, seq)
    segq, segk = segs[:, :, None], windows_of(segs)
    slopes = jnp.array(slope_list(HEADS), F32)
    par = jnp.concatenate([gains, biases, b_in.reshape(2 * ff // width, width)], axis=0)
    y, acts, o_full, m_full, qkv, pp, stats, wqkv2, wo2, win2, wout2, par2 = run_forward(
        slopes, hidden.reshape(micro, seq, width), segq, segk, w_qkv, w_o, w_in, w_out, par
    )
    dx, small, *grads = run_backward(
        comm, slopes, cot.reshape(tokens, width), acts.reshape(2, 4, tokens, width), o_full.reshape(2, tokens, width),
        m_full.reshape(2, tokens, ff), qkv.reshape(2, 3, tokens, width // 2), pp.reshape(2, 2, tokens, ff // 2),
        stats.reshape(2, tokens, 128), segq, segk, wqkv2, wo2, win2, wout2, par2,
    )
    owners, me = lax.axis_size("dp"), lax.axis_index("dp")
    if comm:
        gq, go, gi, gu = grads
    else:
        first = lax.axis_index("section") == 0
        swap = [(0, 1), (1, 0)]

        def pick(v):
            own = jnp.where(first, v[1], v[0])
            return own, lax.ppermute(jnp.where(first, v[0], v[1]), "section", swap)

        own, other = pick(grads[0])
        halves = [jnp.where(first, own, other), jnp.where(first, other, own)]

        def share(v):
            parts = v.reshape(owners, v.shape[0] // owners, v.shape[1])
            got = lax.all_to_all(parts, "dp", split_axis=0, concat_axis=0, tiled=True)
            return jnp.sum(got.astype(F32), axis=0)

        gq, go, gi, gu = (share(v) for v in assemble(halves, width, ff))
        own, other = pick(small)
        small = lax.psum(own + other, "dp")
    part = width // owners
    mine = lax.dynamic_slice_in_dim(small[:8], me * part, part, axis=1)
    inner = lax.dynamic_slice_in_dim(small[8:].reshape(1, 2 * ff), me * (2 * ff // owners), 2 * ff // owners, axis=1)
    return (
        y.reshape(1, *hidden.shape), dx.reshape(1, *hidden.shape), gq[None], go[None], gi[None], gu[None],
        mine[None, :2], mine[None, 2:], inner,
    )


def solution(mesh):
    rows = P(None, "dp", None, None)
    layer = P("section", None, None)
    comm = mesh.shape["dp"] == 16
    return jax.shard_map(
        functools.partial(shards, comm),
        mesh=mesh,
        in_specs=(rows, P(None, "dp", None)) + (layer,) * 6 + (P("section", None), rows),
        out_specs=(
            P("section", None, "dp", None, None),
            P("section", None, "dp", None, None),
            P("section", "dp", None),
            P("section", "dp", None),
            P("section", "dp", None),
            P("section", "dp", None),
            P("section", None, "dp"),
            P("section", None, "dp"),
            P("section", "dp"),
        ),
        check_vma=False,
    )
```

```python
import functools
import math

import jax
import jax.numpy as jnp
from jax import lax
from jax.experimental import pallas as pl
from jax.experimental.pallas import tpu as pltpu
from jax.sharding import PartitionSpec as P

HEADS = 12
HEAD = 64
GROUP = 2
LANES = GROUP * HEAD
QB = 128
HALO = 64
KW = QB + 2 * HALO
EPS = 1e-05
MASKED = -1.0e30
TILE = 256
UNITS = 256
PIECE = 384
BF = jnp.bfloat16
F32 = jnp.float32
MESH = pl.DeviceIdType.MESH
NT = (((1,), (1,)), ((), ()))
TN = (((0,), (0,)), ((), ()))
H_, NA_, NB_, X_ = range(4)
M_, P1_, P2_ = range(3)
GAIN0, GAIN1, BIAS_Q, BIAS_V, BIAS_O, BIAS_A, BIAS_F, BIAS_B, BIAS_IN = range(9)
VECTORS = 16
FEED = 512
AHEAD1, AHEAD2 = 3, 3
RSTD_A, RSTD_B = HEADS, HEADS + 1


def slope_list(head_count):
    base = 2 ** int(math.floor(math.log2(head_count)))
    leading = [2.0 ** (-8.0 * (k + 1) / base) for k in range(base)]
    trailing = [2.0 ** (-4.0 * (2 * k + 1) / base) for k in range(head_count - base)]
    return leading + trailing


def dot(a, b):
    return jnp.dot(a, b, preferred_element_type=F32)


def dot_nt(a, b):
    return lax.dot_general(a, b, NT, preferred_element_type=F32)


def dot_tn(a, b):
    return lax.dot_general(a, b, TN, preferred_element_type=F32)


def normalize(v):
    c = v - jnp.mean(v, axis=-1, keepdims=True)
    rstd = lax.rsqrt(jnp.mean(c * c, axis=-1, keepdims=True) + EPS)
    return c * rstd, rstd


def stack_heads(v):
    head = lax.broadcasted_iota(jnp.int32, v.shape, 1) // HEAD
    zero = jnp.zeros_like(v)
    return jnp.concatenate([jnp.where(head == h, v, zero) for h in range(GROUP)], axis=0)


def merge_heads(r):
    rows = r.shape[0] // GROUP
    head = lax.broadcasted_iota(jnp.int32, (rows, r.shape[1]), 1) // HEAD
    out = r[:rows]
    for h in range(1, GROUP):
        out = jnp.where(head == h, r[h * rows : (h + 1) * rows], out)
    return out


def fill_away(away, segs):
    micro, _, seq = segs.shape
    r = lax.broadcasted_iota(jnp.int32, (QB, KW), 0)
    c = lax.broadcasted_iota(jnp.int32, (QB, KW), 1)
    apart = -jnp.abs(r + HALO - c).astype(F32)
    outside = jnp.full((QB, 128), -1.0, F32)
    for m in range(micro):
        seg = jnp.broadcast_to(segs[m].astype(F32), (QB, seq))
        keys = pltpu.roll(jnp.concatenate([outside, seg, outside], axis=1), seq + 256 - HALO, axis=1)
        for i in range(seq // QB):
            own = seg[:, i * QB : (i + 1) * QB].T
            own = jnp.concatenate([own, own], axis=1)
            same = own == keys[:, i * QB : i * QB + KW]
            away[m, i] = jnp.where(same, apart, MASKED).astype(BF)


def slope_of(sec, g, h):
    table = slope_list(HEADS)
    return jnp.where(sec == 0, table[g * GROUP + h], table[HEADS // 2 + g * GROUP + h]).astype(F32)


def tile_rows(t):
    return pl.ds(pl.multiple_of(t * TILE, TILE), TILE)


def lanes_at(start, count):
    return pl.ds(pl.multiple_of(start, 128), count)


def fwd_kernel(
    hid, segs, wqkv_h, wo_h, win_h, wout_h, gains_in, biases_in, bin_in,
    y_out, acts_out, o_out, m_out, qkv_out, p_out, stats_out,
    wqkv_out, wo_out, win_out, wout_out, par_out, away_out,
    wqkv, wo, win, wout, par, bin_, xy, qkvs, os_, hs, big, psend, precv, acc, kpad, vpad, away, stats,
    lsem, rsend, rrecv, wsave, hsem, ysem, asem, qsem, osem, osend, orecv, bsem, msend, mrecv, tsem, ssend, srecv,
    parsem, awaysem,
):
    dp = lax.axis_index("dp")
    sec = lax.axis_index("section")
    _, micro, seq, width = xy.shape
    half, ffh, ff = wo.shape[1], wout.shape[1], wout_h.shape[0]
    sib = (1 - sec, dp)

    parts = []
    for j in range(3):
        parts.append((wqkv_h, wqkv, lambda c, j=j: (slice(None), lanes_at(j * width + c * half, half)),
                      (slice(None), slice(j * half, (j + 1) * half))))
    parts.append((wo_h, wo, lambda c: (pl.ds(pl.multiple_of(c * half, 128), half), slice(None)), (slice(None), slice(None))))
    for j in range(2):
        parts.append((win_h, win, lambda c, j=j: (slice(None), lanes_at(j * ff + c * ffh, ffh)),
                      (slice(None), slice(j * ffh, (j + 1) * ffh))))
    parts.append((wout_h, wout, lambda c: (pl.ds(pl.multiple_of(c * ffh, 128), ffh), slice(None)), (slice(None), slice(None))))

    def own_part(i):
        src, dst, pick, place = parts[i]
        return pltpu.make_async_copy(src.at[pick(sec)], dst.at[(sec, *place)], lsem.at[i])

    def other_part(i):
        src, dst, pick, place = parts[i]
        return pltpu.make_async_remote_copy(
            src_ref=src.at[pick(1 - sec)], dst_ref=dst.at[(sec, *place)],
            send_sem=rsend.at[i], recv_sem=rrecv.at[i], device_id=sib, device_id_type=MESH,
        )

    def other_vectors():
        return [
            pltpu.make_async_remote_copy(
                src_ref=v.at[sec], dst_ref=v.at[sec], send_sem=rsend.at[7 + i], recv_sem=rrecv.at[7 + i],
                device_id=sib, device_id_type=MESH,
            )
            for i, v in enumerate((par, bin_))
        ]

    def x_load(m):
        return pltpu.make_async_copy(hid.at[m], xy.at[0, m], hsem.at[m])

    for m in range(micro):
        x_load(m).start()
    for i in range(7):
        own_part(i).start()
    par[sec, 0:2] = gains_in[...]
    for j in range(6):
        par[sec, 2 + j : 3 + j] = biases_in[j]
    bin_[sec] = bin_in[...]
    barrier = pltpu.get_barrier_semaphore()
    pl.semaphore_signal(barrier, inc=1, device_id=sib, device_id_type=MESH)
    pl.semaphore_wait(barrier, 1)
    for c in other_vectors():
        c.start()
    for i in range(7):
        other_part(i).start()
    fill_away(away, segs)
    away_save = pltpu.make_async_copy(away, away_out, awaysem)
    away_save.start()
    for pad in (kpad, vpad):
        pad[0:HALO, :] = jnp.zeros((HALO, half), BF)
        pad[HALO + seq :, :] = jnp.zeros((HALO, half), BF)
    for m in range(micro):
        x_load(m).wait()

    def need(l, which):
        @pl.when(l == sec)
        def _():
            for i in which:
                own_part(i).wait()

        @pl.when(l != sec)
        def _():
            for i in which:
                other_part(i).wait_recv()

    def save(kind, l, m):
        src = xy.at[l, m] if kind == X_ else hs.at[kind, m]
        return pltpu.make_async_copy(src, acts_out.at[l, kind, m], asem.at[kind, l, m])

    def save_qkv(kind, l, m):
        return pltpu.make_async_copy(qkvs.at[m, kind], qkv_out.at[l, kind, m], qsem.at[kind, l, m])

    def save_o(l, m):
        return pltpu.make_async_copy(os_.at[m], o_out.at[l, m, :, lanes_at(sec * half, half)], osem.at[l, m])

    def share_o(l, m):
        return pltpu.make_async_remote_copy(
            src_ref=os_.at[m], dst_ref=o_out.at[l, m, :, lanes_at(sec * half, half)],
            send_sem=osend.at[l, m], recv_sem=orecv.at[l, m], device_id=sib, device_id_type=MESH,
        )

    def save_big(kind, l, m):
        if kind == M_:
            dst = m_out.at[l, m, :, lanes_at(sec * ffh, ffh)]
        else:
            dst = p_out.at[l, kind - 1, m]
        return pltpu.make_async_copy(big.at[m, kind], dst, bsem.at[kind, l, m])

    def share_m(l, m):
        return pltpu.make_async_remote_copy(
            src_ref=big.at[m, M_], dst_ref=m_out.at[l, m, :, lanes_at(sec * ffh, ffh)],
            send_sem=msend.at[l, m], recv_sem=mrecv.at[l, m], device_id=sib, device_id_type=MESH,
        )

    def save_stats(l, m):
        return pltpu.make_async_copy(stats.at[l, m], stats_out.at[l, m], tsem.at[l, m])

    def save_y(m):
        return pltpu.make_async_copy(xy.at[sec + 1, m], y_out.at[m], ysem.at[m])

    def partial(phase, l, m):
        return pltpu.make_async_remote_copy(
            src_ref=psend.at[phase, m], dst_ref=precv.at[phase, l, m],
            send_sem=ssend.at[phase, l, m], recv_sem=srecv.at[phase, l, m], device_id=sib, device_id_type=MESH,
        )

    def weight_saves(l):
        pairs = ((wqkv, wqkv_out), (wo, wo_out), (win, win_out), (wout, wout_out))
        return [pltpu.make_async_copy(s.at[l], d.at[l], wsave.at[i, l]) for i, (s, d) in enumerate(pairs)]

    par_save = pltpu.make_async_copy(par, par_out, parsem)

    def attend(l, m):
        @pl.when(m == 0)
        def _():
            need(l, (0, 1, 2))

            @pl.when(l != sec)
            def _():
                for c in other_vectors():
                    c.wait_recv()

        @pl.when(l > 0)
        def _():
            for kind in range(3):
                save_qkv(kind, l - 1, m).wait()
            save_o(l - 1, m).wait()
            share_o(l - 1, m).wait_send()
            partial(0, l - 1, m).wait_send()

        save(X_, l, m).start()
        bias_q = par[l, BIAS_Q : BIAS_Q + 1, lanes_at(sec * half, half)]
        bias_v = par[l, BIAS_V : BIAS_V + 1, lanes_at(sec * half, half)]

        r = dot(xy[l, m], wqkv[l])
        q = (r[:, :half] + bias_q).astype(BF)
        k = r[:, half : 2 * half].astype(BF)
        v = (r[:, 2 * half :] + bias_v).astype(BF)
        for j, w in enumerate((q, k, v)):
            qkvs[m, j] = w
        kpad[HALO : HALO + seq, :] = k
        vpad[HALO : HALO + seq, :] = v
        for kind in range(3):
            save_qkv(kind, l, m).start()

        lane = lax.broadcasted_iota(jnp.int32, (QB, 128), 1)
        for g in range(half // LANES):
            cols = slice(g * LANES, (g + 1) * LANES)
            for i in range(seq // QB):
                rows = slice(i * QB, (i + 1) * QB)
                far = away[m, i].astype(F32)
                qs = stack_heads(qkvs[m, 0, rows, cols] * BF(HEAD**-0.5))
                s = dot_nt(qs, kpad[i * QB : i * QB + KW, cols])
                probs = []
                kept = stats[l, m, rows, :]
                for h in range(GROUP):
                    sh = s[h * QB : (h + 1) * QB] + slope_of(sec, g, h) * far
                    top = jnp.max(sh, axis=-1, keepdims=True)
                    e = jnp.exp(sh - top)
                    total = jnp.sum(e, axis=-1, keepdims=True)
                    probs.append((e * (1.0 / total)).astype(BF))
                    kept = jnp.where(lane == g * GROUP + h, top + jnp.log(total), kept)
                stats[l, m, rows, :] = kept
                r = dot(jnp.concatenate(probs, axis=0), vpad[i * QB : i * QB + KW, cols])
                os_[m, rows, cols] = merge_heads(r).astype(BF)

        save_o(l, m).start()
        share_o(l, m).start()

        @pl.when(m == 0)
        def _():
            need(l, (3,))

        psend[0, m] = dot(os_[m], wo[l]).astype(BF)
        partial(0, l, m).start()

    def feed(l, m):
        @pl.when(m == 0)
        def _():
            need(l, (4, 5, 6))
            for c in weight_saves(l):
                c.start()

        @pl.when(l > 0)
        def _():
            save(H_, l - 1, m).wait()
            save(NA_, l - 1, m).wait()
            for kind in range(3):
                save_big(kind, l - 1, m).wait()
            share_m(l - 1, m).wait_send()
            partial(1, l - 1, m).wait_send()

        partial(0, l, m).wait_recv()
        lane = lax.broadcasted_iota(jnp.int32, (TILE, 128), 1)

        def norm(t, carry):
            rows = tile_rows(t)
            a = xy[l, m, rows, :].astype(F32) + (
                psend[0, m, rows, :].astype(F32) + precv[0, l, m, rows, :].astype(F32) + par[l, BIAS_O : BIAS_O + 1, :]
            )
            n, rstd = normalize(a)
            hs[NA_, m, rows, :] = n.astype(BF)
            hs[H_, m, rows, :] = (n * par[l, GAIN0 : GAIN0 + 1, :] + par[l, BIAS_A : BIAS_A + 1, :]).astype(BF)
            stats[l, m, rows, :] = jnp.where(lane == RSTD_A, rstd, stats[l, m, rows, :])
            return carry

        lax.fori_loop(0, seq // TILE, norm, 0)
        save(H_, l, m).start()
        save(NA_, l, m).start()
        h = hs[H_, m]
        for c in range(ffh // FEED):
            cols = slice(c * FEED, (c + 1) * FEED)
            unit = sec * ffh + c * FEED
            gate = dot(h, win[l, :, cols]) + bin_[l, :, lanes_at(unit, FEED)]
            up = dot(h, win[l, :, ffh + c * FEED : ffh + (c + 1) * FEED]) + bin_[l, :, lanes_at(ff + unit, FEED)]
            cdf = 0.5 + 0.5 * lax.erf(gate * (0.5**0.5))
            act = gate * cdf
            slope = cdf + gate * (jnp.exp(gate * gate * -0.5) * (2.0 * math.pi) ** -0.5)
            mixed = (act * up).astype(BF)
            big[m, M_, :, cols] = mixed
            big[m, P1_, :, cols] = act.astype(BF)
            big[m, P2_, :, cols] = (up * slope).astype(BF)
            down = dot(mixed, wout[l, cols, :])
            acc[...] = down if c == 0 else acc[...] + down

        psend[1, m] = acc[...].astype(BF)
        partial(1, l, m).start()
        for kind in range(3):
            save_big(kind, l, m).start()
        share_m(l, m).start()

    def finish(l, m):
        @pl.when(l > 0)
        def _():
            save(NB_, l - 1, m).wait()

        partial(1, l, m).wait_recv()
        lane = lax.broadcasted_iota(jnp.int32, (TILE, 128), 1)

        def norm(t, carry):
            rows = tile_rows(t)
            b = hs[H_, m, rows, :].astype(F32) + (
                psend[1, m, rows, :].astype(F32) + precv[1, l, m, rows, :].astype(F32) + par[l, BIAS_F : BIAS_F + 1, :]
            )
            n, rstd = normalize(b)
            hs[NB_, m, rows, :] = n.astype(BF)
            xy[l + 1, m, rows, :] = (n * par[l, GAIN1 : GAIN1 + 1, :] + par[l, BIAS_B : BIAS_B + 1, :]).astype(BF)
            stats[l, m, rows, :] = jnp.where(lane == RSTD_B, rstd, stats[l, m, rows, :])
            return carry

        lax.fori_loop(0, seq // TILE, norm, 0)
        save(NB_, l, m).start()
        save_stats(l, m).start()

        @pl.when(l == sec)
        def _():
            save_y(m).start()

    def layer(l, carry):
        def first(m, carry):
            @pl.when(l > 0)
            def _():
                finish(l - 1, m)

            attend(l, m)
            return carry

        lax.fori_loop(0, micro, first, 0)

        def second(m, carry):
            feed(l, m)
            return carry

        lax.fori_loop(0, micro, second, 0)
        return carry

    lax.fori_loop(0, 2, layer, 0)
    par_save.start()

    def last(m, carry):
        finish(1, m)
        return carry

    lax.fori_loop(0, micro, last, 0)

    def drain(m, carry):
        for kind in range(3):
            save_qkv(kind, 1, m).wait()
            save_big(kind, 1, m).wait()
        for kind in (H_, NA_, NB_):
            save(kind, 1, m).wait()
        save_o(1, m).wait()
        share_o(1, m).wait_send()
        share_m(1, m).wait_send()
        for phase in range(2):
            partial(phase, 1, m).wait_send()
        for l in range(2):
            save(X_, l, m).wait()
            save_stats(l, m).wait()
            share_o(l, m).wait_recv()
            share_m(l, m).wait_recv()
        save_y(m).wait()
        return carry

    lax.fori_loop(0, micro, drain, 0)
    for l in range(2):
        for c in weight_saves(l):
            c.wait()
    for i in range(7):
        other_part(i).wait_send()
    for c in other_vectors():
        c.wait_send()
    par_save.wait()
    away_save.wait()


def any_spec():
    return pl.BlockSpec(memory_space=pl.ANY)


def vmem_spec():
    return pl.BlockSpec(memory_space=pltpu.VMEM)


def smem_spec():
    return pl.BlockSpec(memory_space=pltpu.SMEM)


def vm(*shape, dtype=BF):
    return pltpu.VMEM(shape, dtype)


def run_forward(hid, segs, w_qkv, w_o, w_in, w_out, gains, biases, b_in):
    micro, seq, width = hid.shape
    ff = w_out.shape[0]
    half, ffh = width // 2, ff // 2
    dma = pltpu.SemaphoreType.DMA

    def out(*shape, dtype=BF):
        return jax.ShapeDtypeStruct(shape, dtype)

    shapes = (
        out(micro, seq, width),
        out(2, 4, micro, seq, width),
        out(2, micro, seq, width),
        out(2, micro, seq, ff),
        out(2, 3, micro, seq, half),
        out(2, 2, micro, seq, ffh),
        out(2, micro, seq, 128, dtype=F32),
        out(2, width, 3 * half),
        out(2, half, width),
        out(2, width, 2 * ffh),
        out(2, ffh, width),
        out(2, 8, width, dtype=F32),
        out(micro, seq // QB, QB, KW),
    )
    return pl.pallas_call(
        fwd_kernel,
        out_shape=shapes,
        in_specs=[any_spec(), vmem_spec()] + [any_spec()] * 4 + [vmem_spec()] * 3,
        out_specs=tuple([any_spec()] * len(shapes)),
        scratch_shapes=[
            vm(2, width, 3 * half),
            vm(2, half, width),
            vm(2, width, 2 * ffh),
            vm(2, ffh, width),
            vm(2, 8, width, dtype=F32),
            vm(2, 1, 2 * ff, dtype=F32),
            vm(3, micro, seq, width),
            vm(micro, 3, seq, half),
            vm(micro, seq, half),
            vm(3, micro, seq, width),
            vm(micro, 3, seq, ffh),
            vm(2, micro, seq, width),
            vm(2, 2, micro, seq, width),
            vm(seq, width, dtype=F32),
            vm(seq + 2 * HALO, half),
            vm(seq + 2 * HALO, half),
            vm(micro, seq // QB, QB, KW),
            vm(2, micro, seq, 128, dtype=F32),
            dma((7,)), dma((9,)), dma((9,)), dma((4, 2)), dma((micro,)), dma((micro,)), dma((4, 2, micro)),
            dma((3, 2, micro)), dma((2, micro)), dma((2, micro)), dma((2, micro)), dma((3, 2, micro)),
            dma((2, micro)), dma((2, micro)), dma((2, micro)), dma((2, 2, micro)), dma((2, 2, micro)), dma, dma,
        ],
        compiler_params=pltpu.CompilerParams(
            collective_id=1, has_side_effects=True, vmem_limit_bytes=62 << 20
        ),
        name="forward",
    )(hid, segs, w_qkv, w_o, w_in, w_out, gains, biases, b_in)


def column_total(v):
    return jnp.sum(v.astype(F32), axis=0, keepdims=True)


def bwd_kernel(
    comm, cot, acts, o_full, m_full, qkv, pp, stats_h, away, wqkv, wo, win, wout, par, *refs
):
    if comm:
        (dx_out, small_out, shares, *rest) = refs
        (buf, l1, l2, v1, v2, v3, v4, s1, r1, s2, r2, s3, r3, ksem, vs, vr, *rest) = rest
    else:
        (dx_out, small_out, grads_out, *rest) = refs
        (buf, gsem, *rest) = rest
    (acc, df, dy, tr, mt, small, stats, pool, wpool, wslot, gbuf, kpad, vpad, psend, precv,
     poolsem, wsem, usem, nsem, ssem, ysem, xsem, esend, erecv) = rest
    dp = lax.axis_index("dp")
    sec = lax.axis_index("section")
    sib = (1 - sec, dp)
    tokens, width = df.shape
    rows_n, seq = away.shape[0], away.shape[1] * QB
    ff = m_full.shape[2]
    half, ffh = width // 2, ff // 2
    ntile = tokens // TILE
    own = lanes_at(sec * half, half)

    if comm:
        bx, by, bz = dp % 2, (dp // 2) % 2, dp // 4
        xp = dp + 1 - 2 * bx
        yp = dp + 2 - 4 * by
        zp = [dp] + [((bz + d) % 4) * 4 + dp % 4 for d in range(1, 4)]
        near = xp * (1 - sec) + yp * sec
        far = yp * (1 - sec) + xp * sec
        b1 = bx * (1 - sec) + by * sec
        b2 = by * (1 - sec) + bx * sec
        greet = [(sec, xp), (sec, yp)] + [(sec, z) for z in zp[1:]] + [(1 - sec, z) for z in zp[1:]]
    else:
        greet = []

    def pool_load(slot, count, src, first):
        return pltpu.make_async_copy(src.at[:, lanes_at(first, count)], pool.at[slot, :, 0:count], poolsem.at[slot])

    def weight_load(slot, count, src, first):
        return pltpu.make_async_copy(src.at[:, lanes_at(first, count)], wpool.at[slot, :, 0:count], wsem.at[slot])

    def rows_load(slot, count, src, first):
        return pltpu.make_async_copy(
            src.at[pl.ds(pl.multiple_of(first, 128), count), :], wslot.at[slot, 0:count], usem.at[slot]
        )

    def norm_loads(l, kind):
        return [
            pltpu.make_async_copy(acts.at[l, kind, :, j * half : (j + 1) * half], gbuf.at[j], nsem.at[j]) for j in range(2)
        ]

    def stats_load(l):
        return pltpu.make_async_copy(stats_h.at[l], stats, ssem)

    def m_loads(l, i):
        return [pool_load(2 + j, PIECE, m_full.at[l], (2 * i + j) * PIECE) for j in range(2)]

    def h_loads(l):
        return [pool_load(j, half, acts.at[l, H_], j * half) for j in range(2)]

    def chunk_loads(l, slot, c):
        first = c * UNITS
        return [
            weight_load(2 * slot, UNITS, win.at[l], first),
            weight_load(2 * slot + 1, UNITS, win.at[l], ffh + first),
            rows_load(slot, UNITS, wout.at[l], first),
            pool_load(2 * slot, UNITS, pp.at[l, 0], first),
            pool_load(2 * slot + 1, UNITS, pp.at[l, 1], first),
        ]

    def exchange(e):
        return pltpu.make_async_remote_copy(
            src_ref=psend, dst_ref=precv.at[e % 2], send_sem=esend.at[e], recv_sem=erecv.at[e],
            device_id=sib, device_id_type=MESH,
        )

    x_store = pltpu.make_async_copy(dy, dx_out, xsem)
    cot_load = pltpu.make_async_copy(cot, dy, ysem)
    cot_load.start()

    def first_loads(l):
        for load in h_loads(l):
            load.start()
        stats_load(l).start()
        for load in m_loads(l, 0):
            load.start()

    first_loads(1)
    barrier = pltpu.get_barrier_semaphore()
    for peer in [sib] + greet:
        pl.semaphore_signal(barrier, inc=1, device_id=peer, device_id_type=MESH)
    pl.semaphore_wait(barrier, 1 + len(greet))

    def put(t, n, lane, value):
        lanes = slice(lane, lane + value.shape[1])
        if not comm:
            buf[t, n, :, lanes] = value
            return
        share = value.shape[0] // 16
        for o in range(16):
            x, y, z = o % 2, (o // 2) % 2, o // 4
            f = x * (1 - sec) + y * sec
            s = y * (1 - sec) + x * sec
            buf[t, n, f, s, z, :, lanes] = value[o * share : (o + 1) * share]

    if comm:

        def remote(src, dst, ss, rs, to):
            return pltpu.make_async_remote_copy(
                src_ref=src, dst_ref=dst, send_sem=ss, recv_sem=rs, device_id=to, device_id_type=MESH
            )

        def stage1(t, n):
            return remote(buf.at[t, n, 1 - b1], l1.at[t, n], s1.at[t, n], r1.at[t, n], (sec, near))

        def stage2(t, n):
            return remote(buf.at[t, n, b1, 1 - b2], l2.at[t, n], s2.at[t, n], r2.at[t, n], (sec, far))

        def stage3(t, n, d):
            return remote(
                buf.at[t, n, b1, b2, (bz + d) % 4], shares.at[n, sec, d], s3.at[t, n, d], r3.at[n, sec, d], (1 - t, zp[d])
            )

        def keep(t, n):
            return pltpu.make_async_copy(buf.at[t, n, b1, b2, bz], shares.at[n, sec, 0], ksem.at[n])

        def landed(n, k, d):
            return remote(shares.at[n, k, d], shares.at[n, k, d], s3.at[0, n, d], r3.at[n, k, d], (1 - sec, dp))

        def join(t, n, second):
            for z in range(4):
                at = (t, n, b1, second, z)
                buf[at] = (buf[at].astype(F32) + l1[t, n, second, z].astype(F32)).astype(BF)

        def after1(t, n):
            stage1(t, n).wait()
            join(t, n, 1 - b2)
            stage2(t, n).start()
            join(t, n, b2)

        def after2(t, n):
            stage2(t, n).wait()
            for z in range(4):
                at = (t, n, b1, b2, z)
                buf[at] = (buf[at].astype(F32) + l2[t, n, z].astype(F32)).astype(BF)
            for d in (1, 2, 3):
                stage3(t, n, d).start()

            @pl.when(sec != 1 - t)
            def _():
                stage3(t, n, 0).start()

            @pl.when(sec == 1 - t)
            def _():
                keep(t, n).start()

        def sent3(t, n):
            for d in (1, 2, 3):
                stage3(t, n, d).wait_send()

            @pl.when(sec != 1 - t)
            def _():
                stage3(t, n, 0).wait_send()

        def arrived(t, n):
            for k in range(2):
                for d in (1, 2, 3):
                    landed(n, k, d).wait_recv()

                @pl.when(sec != k)
                def _():
                    landed(n, k, 0).wait_recv()

            keep(t, n).wait()

        def span(lo, hi, fn):
            def one(n, carry):
                fn(n)
                return carry

            lax.fori_loop(lo, hi, one, 0)

        def step(i, fresh=True):
            if fresh:
                stage1(i // 16, i % 16).start()
            for back, fn in ((AHEAD1, after1), (AHEAD1 + AHEAD2, after2)):
                j = i - back

                @pl.when((j >= 0) & (j < 32))
                def _():
                    fn(j // 16, j % 16)

    small[...] = jnp.zeros_like(small)
    for pad in (kpad, vpad):
        pad[0:HALO, :] = jnp.zeros((HALO, half), BF)
        pad[HALO + seq :, :] = jnp.zeros((HALO, half), BF)
    cot_load.wait()

    def layer(t, carry):
        l = 1 - t

        def transpose_pool(slots):
            for j, slot in enumerate(slots):
                tr[j * half : (j + 1) * half, :] = pool[slot].T

        for load in norm_loads(l, NB_):
            load.start()
        for load in h_loads(l):
            load.wait()
        transpose_pool((0, 1))
        for load in chunk_loads(l, 0, 0):
            load.start()
        stats_load(l).wait()
        for load in norm_loads(l, NB_):
            load.wait()

        def norm_back(dv, rows, rstd_lane, gain, gain_sum, offset_sum, round_sum):
            n = jnp.concatenate([gbuf[0, rows, :], gbuf[1, rows, :]], axis=1).astype(F32)
            rstd = stats[rows, rstd_lane : rstd_lane + 1]
            dn = dv * par[l, gain : gain + 1, :]
            d = rstd * (
                dn - jnp.mean(dn, axis=-1, keepdims=True) - n * jnp.mean(dn * n, axis=-1, keepdims=True)
            )
            low = d.astype(BF)
            df[rows, :] = low
            small[t, gain_sum : gain_sum + 1, :] += column_total(dv * n)
            small[t, offset_sum : offset_sum + 1, :] += column_total(dv)
            small[t, round_sum : round_sum + 1, :] += column_total(low)

        def out_norm(i, carry):
            rows = tile_rows(i)
            norm_back(dy[rows, :].astype(F32), rows, RSTD_B, GAIN1, GAIN1, BIAS_B, BIAS_F)
            acc[rows, :] = jnp.zeros((TILE, width), F32)
            return carry

        lax.fori_loop(0, ntile, out_norm, 0)

        def out_grad(i, carry):
            for load in m_loads(l, i):
                load.wait()
            for j in range(2):
                mt[j * PIECE : (j + 1) * PIECE, :] = pool[2 + j].T

            @pl.when(i + 1 < ff // width)
            def _():
                for load in m_loads(l, i + 1):
                    load.start()

            g = dot(mt[...], df[:, own]).astype(BF)
            if comm:
                for o in range(4):
                    x, y = o % 2, o // 2
                    f = x * (1 - sec) + y * sec
                    s = y * (1 - sec) + x * sec
                    for q in range(4):
                        buf[t, q, f, s, i] = g[o * 192 + q * 48 : o * 192 + (q + 1) * 48]
            else:
                buf[t, i] = g
            return carry

        lax.fori_loop(0, ff // width, out_grad, 0)
        if comm:
            step(16 * t)
            step(16 * t + 1)

        def feed(jj, carry):
            for part in range(3):
                c = 3 * jj + part
                slot = c % 2
                for load in chunk_loads(l, slot, c):
                    load.wait()

                @pl.when(c + 1 < ffh // UNITS)
                def _():
                    for load in chunk_loads(l, 1 - slot, c + 1):
                        load.start()

                dm = dot_nt(df[...], wslot[slot, 0:UNITS])
                gbuf[0, :, 0:UNITS] = (dm * pool[2 * slot + 1, :, 0:UNITS].astype(F32)).astype(BF)
                gbuf[1, :, 0:UNITS] = (dm * pool[2 * slot, :, 0:UNITS].astype(F32)).astype(BF)
                acc[...] += dot_nt(gbuf[0, :, 0:UNITS], wpool[2 * slot, :, 0:UNITS]) + dot_nt(
                    gbuf[1, :, 0:UNITS], wpool[2 * slot + 1, :, 0:UNITS]
                )

                @pl.when(c == ffh // UNITS - 1)
                def _():
                    @pl.when(t > 0)
                    def _():
                        exchange(1).wait_send()

                    psend[...] = acc[...].astype(BF)
                    exchange(2 * t).start()

                unit = sec * ffh + c * UNITS
                spot = lanes_at(unit % width, UNITS)
                for k in range(2):
                    small[t, pl.ds(BIAS_IN + k * (ff // width) + unit // width, 1), spot] = column_total(
                        gbuf[k, :, 0:UNITS]
                    )
                    g = dot(tr[...], gbuf[k, :, 0:UNITS]).astype(BF)
                    n = 4 + 4 * jj + 2 * k
                    if part == 0:
                        put(t, n, 0, g)
                    elif part == 1:
                        put(t, n, 256, g[:, :128])
                        put(t, n + 1, 0, g[:, 128:])
                    else:
                        put(t, n + 1, 128, g)
                if comm:
                    step(16 * t + 2 + c)
            return carry

        lax.fori_loop(0, ffh // (3 * UNITS), feed, 0)
        for load in norm_loads(l, NA_):
            load.start()
        for j in range(2):
            pool_load(j, half, o_full.at[l], j * half).start()
        wo_load = rows_load(0, half, wo.at[l], 0)
        wo_load.start()
        head_weights = [weight_load(j, half, wqkv.at[l], j * half) for j in range(3)]
        for load in head_weights:
            load.start()
        for load in norm_loads(l, NA_):
            load.wait()
        for j in range(2):
            pool_load(j, half, o_full.at[l], j * half).wait()
        transpose_pool((0, 1))
        head_rows = [pool_load(j, half, qkv.at[l, j], 0) for j in range(3)]
        for load in head_rows:
            load.start()
        pool_load(3, half, acts.at[l, X_], 0).start()
        exchange(2 * t).wait_recv()

        def attn_norm(i, carry):
            rows = tile_rows(i)
            dh = df[rows, :].astype(F32) + (psend[rows, :].astype(F32) + precv[0, rows, :].astype(F32))
            norm_back(dh, rows, RSTD_A, GAIN0, GAIN0, BIAS_A, BIAS_O)
            return carry

        lax.fori_loop(0, ntile, attn_norm, 0)

        wo_load.wait()

        @pl.when((t == 1) & (sec == 1))
        def _():
            x_store.wait()

        dy[:, 0:half] = dot_nt(df[...], wslot[0]).astype(BF)
        put(t, 12, 0, dot(tr[...], df[:, own]).astype(BF))
        if comm:
            step(16 * t + 8)
            step(16 * t + 9)

        for load in head_rows:
            load.wait()

        def row(r, carry):
            base = pl.multiple_of(r * seq, seq)
            kpad[HALO : HALO + seq, :] = pool[1, pl.ds(base, seq), :]
            vpad[HALO : HALO + seq, :] = pool[2, pl.ds(base, seq), :]
            lane = lax.broadcasted_iota(jnp.int32, (QB, 128), 1)

            for g in range(half // LANES):
                cols = slice(g * LANES, (g + 1) * LANES)
                for i in range(seq // QB):
                    rows = pl.ds(pl.multiple_of(base + i * QB, QB), QB)
                    far = away[r, i].astype(F32)
                    kw = kpad[i * QB : i * QB + KW, cols]
                    vw = vpad[i * QB : i * QB + KW, cols]
                    qs = stack_heads(pool[0, rows, cols] * BF(HEAD**-0.5))
                    os = stack_heads(dy[rows, cols])
                    s = dot_nt(qs, kw)
                    d = dot_nt(os, vw)
                    kept = stats[rows, :]
                    ps, ds = [], []
                    for h in range(GROUP):
                        part = slice(h * QB, (h + 1) * QB)
                        lse = jnp.sum(jnp.where(lane == g * GROUP + h, kept, 0.0), axis=-1, keepdims=True)
                        p = jnp.exp(s[part] + slope_of(sec, g, h) * far - lse)
                        pd = p * d[part]
                        ds.append((pd - p * jnp.sum(pd, axis=-1, keepdims=True)).astype(BF))
                        ps.append(p.astype(BF))
                    ds = jnp.concatenate(ds, axis=0)
                    ps = jnp.concatenate(ps, axis=0)
                    gbuf[0, rows, cols] = (merge_heads(dot(ds, kw)) * HEAD**-0.5).astype(BF)
                    dk, dv = dot_tn(ds, qs), dot_tn(ps, os)
                    if i == 0:
                        at, skip = pl.ds(base, HALO), HALO
                    else:
                        at, skip = pl.ds(pl.multiple_of(base + i * QB - HALO, HALO), QB), 0
                        dk = jnp.concatenate([dk[:QB] + left_k, dk[QB:]], axis=0)
                        dv = jnp.concatenate([dv[:QB] + left_v, dv[QB:]], axis=0)
                    gbuf[1, at, cols] = dk[skip:QB].astype(BF)
                    gbuf[2, at, cols] = dv[skip:QB].astype(BF)
                    left_k, left_v = dk[QB:], dv[QB:]
                at = pl.ds(pl.multiple_of(base + seq - HALO, HALO), HALO)
                gbuf[1, at, cols] = left_k[:HALO].astype(BF)
                gbuf[2, at, cols] = left_v[:HALO].astype(BF)
            if comm:
                step(16 * t + 10 + r)
            return carry

        lax.fori_loop(0, rows_n, row, 0)
        pool_load(0, half, acts.at[l, X_], half).start()
        for load in head_weights:
            load.wait()
        exchange(2 * t).wait_send()

        total = dot_nt(gbuf[0], wpool[0])
        for j in (1, 2):
            total += dot_nt(gbuf[j], wpool[j])
        psend[...] = total.astype(BF)
        exchange(2 * t + 1).start()
        small[t, BIAS_Q : BIAS_Q + 1, own] = column_total(gbuf[0])
        small[t, BIAS_V : BIAS_V + 1, own] = column_total(gbuf[2])
        pool_load(3, half, acts.at[l, X_], 0).wait()
        pool_load(0, half, acts.at[l, X_], half).wait()
        transpose_pool((3, 0))

        @pl.when(t == 0)
        def _():
            first_loads(0)

        if comm:
            step(16 * t + 12)
        for j in range(3):
            put(t, 13 + j, 0, dot(tr[...], gbuf[j]).astype(BF))
            if comm and j == 0:
                step(16 * t + 13)
        exchange(2 * t + 1).wait_recv()

        def result(i, carry):
            rows = tile_rows(i)
            dx = df[rows, :].astype(F32) + (psend[rows, :].astype(F32) + precv[1, rows, :].astype(F32))
            dy[rows, :] = dx.astype(BF)
            return carry

        lax.fori_loop(0, ntile, result, 0)

        @pl.when(sec == l)
        def _():
            x_store.start()

        @pl.when(sec != l)
        def _():
            small[t, 0:2, :] = jnp.zeros((2, width), F32)
            small[t, BIAS_O:BIAS_IN, :] = jnp.zeros((BIAS_IN - BIAS_O, width), F32)

        if comm:
            step(16 * t + 14)
            step(16 * t + 15)
        return carry

    lax.fori_loop(0, 2, layer, 0)
    exchange(3).wait_send()

    @pl.when(sec == 0)
    def _():
        x_store.wait()

    if comm:
        mine = 1 - sec

        def vectors(stage):
            if stage == 0:
                return [remote(small.at[sec], v1, vs.at[0], vr.at[0], sib)]
            if stage == 1:
                return [remote(v1, v2, vs.at[1], vr.at[1], (sec, xp))]
            if stage == 2:
                return [remote(v2, v3, vs.at[2], vr.at[2], (sec, yp))]
            return [remote(v3, v4.at[d - 1], vs.at[2 + d], vr.at[2 + d], (sec, zp[d])) for d in (1, 2, 3)]

        def go(stage):
            for c in vectors(stage):
                c.start()

        def done(stage):
            for c in vectors(stage):
                c.wait()

        def rest(lo, hi):
            span(lo, hi, lambda i: step(i, False))

        go(0)
        rest(32, 33)
        done(0)
        v1[...] += small[mine]
        go(1)
        rest(33, 34)
        done(1)
        v2[...] += v1[...]
        go(2)
        rest(34, 35)
        done(2)
        v3[...] += v2[...]
        go(3)
        rest(35, 32 + AHEAD1 + AHEAD2)
        done(3)
        small_out[...] = v3[...] + v4[0] + v4[1] + v4[2]
        for t in range(2):
            span(0, 16, lambda n, t=t: sent3(t, n))
        span(0, 16, lambda n: arrived(mine, n))
    else:
        store = pltpu.make_async_copy(buf, grads_out, gsem)
        store.start()
        small_out[...] = small[...]
        store.wait()


def run_backward(comm, cot, acts, o_full, m_full, qkv, pp, stats, away, wqkv, wo, win, wout, par):
    tokens, width = cot.shape
    ff = m_full.shape[2]
    half = width // 2
    dma = pltpu.SemaphoreType.DMA
    dx = jax.ShapeDtypeStruct((tokens, width), BF)
    if comm:
        r = width // 16
        small = jax.ShapeDtypeStruct((VECTORS, width), F32)
        grads = jax.ShapeDtypeStruct((16, 2, 4, r, PIECE), BF)
        special = [
            vm(2, 16, 2, 2, 4, r, PIECE),
            vm(2, 16, 2, 4, r, PIECE),
            vm(2, 16, 4, r, PIECE),
            vm(VECTORS, width, dtype=F32),
            vm(VECTORS, width, dtype=F32),
            vm(VECTORS, width, dtype=F32),
            vm(3, VECTORS, width, dtype=F32),
            dma((2, 16)), dma((2, 16)), dma((2, 16)), dma((2, 16)), dma((2, 16, 4)), dma((16, 2, 4)), dma((16,)),
            dma((6,)), dma((6,)),
        ]
    else:
        small = jax.ShapeDtypeStruct((2, VECTORS, width), F32)
        grads = jax.ShapeDtypeStruct((2, 16, width, PIECE), BF)
        special = [vm(2, 16, width, PIECE), dma]
    seq = away.shape[1] * QB
    scratch = special + [
        vm(tokens, width, dtype=F32),
        vm(tokens, width),
        vm(tokens, width),
        vm(width, tokens),
        vm(width, tokens),
        vm(2, VECTORS, width, dtype=F32),
        vm(tokens, 128, dtype=F32),
        vm(4, tokens, PIECE),
        vm(4, width, PIECE),
        vm(2, half, width),
        vm(3, tokens, half),
        vm(seq + 2 * HALO, half),
        vm(seq + 2 * HALO, half),
        vm(tokens, width),
        vm(2, tokens, width),
        dma((4,)), dma((4,)), dma((2,)), dma((2,)), dma, dma, dma, dma((4,)), dma((4,)),
    ]
    return pl.pallas_call(
        functools.partial(bwd_kernel, comm),
        out_shape=(dx, small, grads),
        in_specs=[any_spec()] * 7 + [vmem_spec()] + [any_spec()] * 4 + [vmem_spec()],
        out_specs=(any_spec(), vmem_spec(), any_spec()),
        scratch_shapes=scratch,
        compiler_params=pltpu.CompilerParams(
            collective_id=2, has_side_effects=True, vmem_limit_bytes=64 << 20
        ),
        name="backward",
    )(cot, acts, o_full, m_full, qkv, pp, stats, away, wqkv, wo, win, wout, par)


def results_kernel(shares, vectors, y, dx, y_out, dx_out, fq, fo, fi, fu, gain_out, bias_out, inner_out, land, stage, lsem, fsem, csem):
    me = lax.axis_index("dp")
    rows, width = fo.shape
    half, ff = width // 2, fi.shape[1] // 2
    ffh = ff // 2
    copies = [pltpu.make_async_copy(y, y_out, csem.at[0]), pltpu.make_async_copy(dx, dx_out, csem.at[1])]
    loads = [pltpu.make_async_copy(shares.at[n], land.at[n], lsem.at[n]) for n in range(16)]
    for c in loads + copies:
        c.start()

    def place(n, k):
        if n < 4:
            return fu.at[n * rows : (n + 1) * rows, k * half : (k + 1) * half]
        if n < 12:
            jj, g, i = (n - 4) // 4, (n - 4) // 2 % 2, n % 2
            start = g * ff + k * ffh + (2 * jj + i) * PIECE
            return fi.at[:, start : start + PIECE]
        if n == 12:
            return fo.at[:, k * half : (k + 1) * half]
        start = (n - 13) * width + k * half
        return fq.at[:, start : start + half]

    stores = []
    for n in range(16):
        loads[n].wait()
        for k in range(2):
            parts = [land[n, k, d].astype(F32) for d in range(4)]
            stage[n, k] = (parts[0] + parts[1]) + (parts[2] + parts[3])
            stores.append(pltpu.make_async_copy(stage.at[n, k], place(n, k), fsem.at[n, k]))
            stores[-1].start()
    turned = pltpu.roll(vectors[0:8, :], (width - me * rows) % width, axis=1)
    gain_out[...] = turned[0:2, 0:rows]
    for j in range(6):
        bias_out[j] = turned[2 + j : 3 + j, 0:rows]
    line = vectors[pl.ds(8 + me // 2, 1), :]
    inner_out[...] = jnp.where(me % 2 == 0, line[:, :half], line[:, half:])
    for c in stores + copies:
        c.wait()


def run_results(shares, vectors, y, dx, ff):
    _, _, _, rows, half = shares.shape
    width = 2 * half
    dma = pltpu.SemaphoreType.DMA

    def out(*shape):
        return jax.ShapeDtypeStruct(shape, F32)

    return pl.pallas_call(
        results_kernel,
        out_shape=(
            jax.ShapeDtypeStruct(y.shape, BF), jax.ShapeDtypeStruct(dx.shape, BF),
            out(rows, 3 * width), out(rows, width), out(rows, 2 * ff), out(ff // 16, width),
            out(2, rows), out(6, 1, rows), out(1, 2 * ff // 16),
        ),
        in_specs=[any_spec(), vmem_spec(), any_spec(), any_spec()],
        out_specs=tuple([any_spec()] * 6 + [vmem_spec()] * 3),
        scratch_shapes=[
            vm(*shares.shape), vm(16, 2, rows, half, dtype=F32), dma((16,)), dma((16, 2)), dma((2,)),
        ],
        compiler_params=pltpu.CompilerParams(vmem_limit_bytes=60 << 20),
        name="results",
    )(shares, vectors, y, dx)


def assemble(halves, width, ff):
    def columns(v):
        return jnp.concatenate(v, axis=1)

    gu = columns([h[:4].reshape(ff, PIECE) for h in halves])
    inner = [
        columns([h[4 + 4 * jj + 2 * k + i] for jj in range(2) for i in range(2)]) for k in range(2) for h in halves
    ]
    gi = columns(inner)
    go = columns([h[12] for h in halves])
    gq = columns([h[13 + j] for j in range(3) for h in halves])
    return gq, go, gi, gu


def shards(comm, hidden, segs, w_qkv, w_o, w_in, w_out, gains, biases, b_in, cot):
    w_qkv, w_o, w_in, w_out, gains = (v[0] for v in (w_qkv, w_o, w_in, w_out, gains))
    biases = jnp.transpose(biases, (1, 0, 2))
    micro, _, seq, width = hidden.shape
    ff = w_out.shape[0]
    tokens = micro * seq
    y, acts, o_full, m_full, qkv, pp, stats, wqkv2, wo2, win2, wout2, par2, away = run_forward(
        hidden.reshape(micro, seq, width), segs, w_qkv, w_o, w_in, w_out, gains, biases, b_in
    )
    dx, small, grads = run_backward(
        comm, cot.reshape(tokens, width), acts.reshape(2, 4, tokens, width), o_full.reshape(2, tokens, width),
        m_full.reshape(2, tokens, ff), qkv.reshape(2, 3, tokens, width // 2), pp.reshape(2, 2, tokens, ff // 2),
        stats.reshape(2, tokens, 128), away, wqkv2, wo2, win2, wout2, par2,
    )
    if comm:
        y, dx, gq, go, gi, gu, gain, bias, inner = run_results(grads, small, y, dx, ff)
        return (
            y.reshape(1, *hidden.shape), dx.reshape(1, *hidden.shape), gq[None], go[None], gi[None], gu[None],
            gain[None], jnp.transpose(bias, (1, 0, 2)), inner,
        )
    owners, me = lax.axis_size("dp"), lax.axis_index("dp")
    first = lax.axis_index("section") == 0
    swap = [(0, 1), (1, 0)]

    def pick(v):
        own = jnp.where(first, v[1], v[0])
        return own, lax.ppermute(jnp.where(first, v[0], v[1]), "section", swap)

    own, other = pick(grads)
    halves = [jnp.where(first, own, other), jnp.where(first, other, own)]

    def share(v):
        parts = v.reshape(owners, v.shape[0] // owners, v.shape[1])
        got = lax.all_to_all(parts, "dp", split_axis=0, concat_axis=0, tiled=True)
        return jnp.sum(got.astype(F32), axis=0)

    gq, go, gi, gu = (share(v) for v in assemble(halves, width, ff))
    own, other = pick(small)
    small = lax.psum(own + other, "dp")
    part = width // owners
    mine = lax.dynamic_slice_in_dim(small[:8], me * part, part, axis=1)
    inner = lax.dynamic_slice_in_dim(small[8:].reshape(1, 2 * ff), me * (2 * ff // owners), 2 * ff // owners, axis=1)
    return (
        y.reshape(1, *hidden.shape), dx.reshape(1, *hidden.shape), gq[None], go[None], gi[None], gu[None],
        mine[None, :2], mine[None, 2:], inner,
    )


def solution(mesh):
    rows = P(None, "dp", None, None)
    layer = P("section", None, None)
    comm = mesh.shape["dp"] == 16
    return jax.shard_map(
        functools.partial(shards, comm),
        mesh=mesh,
        in_specs=(rows, P(None, "dp", None)) + (layer,) * 6 + (P("section", None), rows),
        out_specs=(
            P("section", None, "dp", None, None),
            P("section", None, "dp", None, None),
            P("section", "dp", None),
            P("section", "dp", None),
            P("section", "dp", None),
            P("section", "dp", None),
            P("section", None, "dp"),
            P("section", None, "dp"),
            P("section", "dp"),
        ),
        check_vma=False,
    )
```

```python
import functools
import math

import jax
import jax.numpy as jnp
from jax import lax
from jax.experimental import pallas as pl
from jax.experimental.pallas import tpu as pltpu
from jax.sharding import PartitionSpec as P

HEADS = 12
HEAD = 64
GROUP = 2
LANES = GROUP * HEAD
QB = 128
HALO = 64
KW = QB + 2 * HALO
EPS = 1e-05
MASKED = -1.0e30
TILE = 256
UNITS = 256
PIECE = 384
BF = jnp.bfloat16
F32 = jnp.float32
MESH = pl.DeviceIdType.MESH
NT = (((1,), (1,)), ((), ()))
TN = (((0,), (0,)), ((), ()))
H_, NA_, NB_, X_ = range(4)
M_, P1_, P2_ = range(3)
GAIN0, GAIN1, BIAS_Q, BIAS_V, BIAS_O, BIAS_A, BIAS_F, BIAS_B, BIAS_IN = range(9)
VECTORS = 16
FEED = 512
AHEAD1, AHEAD2 = 3, 3
EARLY = 3
RSTD_A, RSTD_B = HEADS, HEADS + 1


def slope_list(head_count):
    base = 2 ** int(math.floor(math.log2(head_count)))
    leading = [2.0 ** (-8.0 * (k + 1) / base) for k in range(base)]
    trailing = [2.0 ** (-4.0 * (2 * k + 1) / base) for k in range(head_count - base)]
    return leading + trailing


def dot(a, b):
    return jnp.dot(a, b, preferred_element_type=F32)


def dot_nt(a, b):
    return lax.dot_general(a, b, NT, preferred_element_type=F32)


def dot_tn(a, b):
    return lax.dot_general(a, b, TN, preferred_element_type=F32)


def normalize(v):
    c = v - jnp.mean(v, axis=-1, keepdims=True)
    rstd = lax.rsqrt(jnp.mean(c * c, axis=-1, keepdims=True) + EPS)
    return c * rstd, rstd


def stack_heads(v):
    head = lax.broadcasted_iota(jnp.int32, v.shape, 1) // HEAD
    zero = jnp.zeros_like(v)
    return jnp.concatenate([jnp.where(head == h, v, zero) for h in range(GROUP)], axis=0)


def merge_heads(r):
    rows = r.shape[0] // GROUP
    head = lax.broadcasted_iota(jnp.int32, (rows, r.shape[1]), 1) // HEAD
    out = r[:rows]
    for h in range(1, GROUP):
        out = jnp.where(head == h, r[h * rows : (h + 1) * rows], out)
    return out


def fill_away(away, segs):
    micro, _, seq = segs.shape
    r = lax.broadcasted_iota(jnp.int32, (QB, KW), 0)
    c = lax.broadcasted_iota(jnp.int32, (QB, KW), 1)
    apart = -jnp.abs(r + HALO - c).astype(F32)
    outside = jnp.full((QB, 128), -1.0, F32)
    for m in range(micro):
        seg = jnp.broadcast_to(segs[m].astype(F32), (QB, seq))
        keys = pltpu.roll(jnp.concatenate([outside, seg, outside], axis=1), seq + 256 - HALO, axis=1)
        for i in range(seq // QB):
            own = seg[:, i * QB : (i + 1) * QB].T
            own = jnp.concatenate([own, own], axis=1)
            same = own == keys[:, i * QB : i * QB + KW]
            away[m, i] = jnp.where(same, apart, MASKED).astype(BF)


def slope_of(sec, g, h):
    table = slope_list(HEADS)
    return jnp.where(sec == 0, table[g * GROUP + h], table[HEADS // 2 + g * GROUP + h]).astype(F32)


def tile_rows(t):
    return pl.ds(pl.multiple_of(t * TILE, TILE), TILE)


def lanes_at(start, count):
    return pl.ds(pl.multiple_of(start, 128), count)


def fwd_kernel(
    hid, segs, wqkv_h, wo_h, win_h, wout_h, gains_in, biases_in, bin_in,
    y_out, acts_out, o_out, m_out, qkv_out, p_out, stats_out,
    wqkv_out, wo_out, win_out, wout_out, par_out, away_out,
    wqkv, wo, win, wout, par, bin_, xy, qkvs, os_, hs, big, psend, precv, acc, kpad, vpad, away, stats,
    lsem, rsend, rrecv, wsave, hsem, ysem, asem, qsem, osem, osend, orecv, bsem, msend, mrecv, tsem, ssend, srecv,
    parsem, awaysem,
):
    dp = lax.axis_index("dp")
    sec = lax.axis_index("section")
    _, micro, seq, width = xy.shape
    half, ffh, ff = wo.shape[1], wout.shape[1], wout_h.shape[0]
    sib = (1 - sec, dp)

    parts = []
    for j in range(3):
        parts.append((wqkv_h, wqkv, lambda c, j=j: (slice(None), lanes_at(j * width + c * half, half)),
                      (slice(None), slice(j * half, (j + 1) * half))))
    parts.append((wo_h, wo, lambda c: (pl.ds(pl.multiple_of(c * half, 128), half), slice(None)), (slice(None), slice(None))))
    for j in range(2):
        parts.append((win_h, win, lambda c, j=j: (slice(None), lanes_at(j * ff + c * ffh, ffh)),
                      (slice(None), slice(j * ffh, (j + 1) * ffh))))
    parts.append((wout_h, wout, lambda c: (pl.ds(pl.multiple_of(c * ffh, 128), ffh), slice(None)), (slice(None), slice(None))))

    def own_part(i):
        src, dst, pick, place = parts[i]
        return pltpu.make_async_copy(src.at[pick(sec)], dst.at[(sec, *place)], lsem.at[i])

    def other_part(i):
        src, dst, pick, place = parts[i]
        return pltpu.make_async_remote_copy(
            src_ref=src.at[pick(1 - sec)], dst_ref=dst.at[(sec, *place)],
            send_sem=rsend.at[i], recv_sem=rrecv.at[i], device_id=sib, device_id_type=MESH,
        )

    def other_vectors():
        return [
            pltpu.make_async_remote_copy(
                src_ref=v.at[sec], dst_ref=v.at[sec], send_sem=rsend.at[7 + i], recv_sem=rrecv.at[7 + i],
                device_id=sib, device_id_type=MESH,
            )
            for i, v in enumerate((par, bin_))
        ]

    def x_load(m):
        return pltpu.make_async_copy(hid.at[m], xy.at[0, m], hsem.at[m])

    for m in range(micro):
        x_load(m).start()
    for i in range(7):
        own_part(i).start()
    par[sec, 0:2] = gains_in[...]
    for j in range(6):
        par[sec, 2 + j : 3 + j] = biases_in[j]
    bin_[sec] = bin_in[...]
    barrier = pltpu.get_barrier_semaphore()
    pl.semaphore_signal(barrier, inc=1, device_id=sib, device_id_type=MESH)
    pl.semaphore_wait(barrier, 1)
    for c in other_vectors():
        c.start()
    for i in range(7):
        other_part(i).start()
    fill_away(away, segs)
    away_save = pltpu.make_async_copy(away, away_out, awaysem)
    away_save.start()
    for pad in (kpad, vpad):
        pad[0:HALO, :] = jnp.zeros((HALO, half), BF)
        pad[HALO + seq :, :] = jnp.zeros((HALO, half), BF)
    for m in range(micro):
        x_load(m).wait()

    def need(l, which):
        @pl.when(l == sec)
        def _():
            for i in which:
                own_part(i).wait()

        @pl.when(l != sec)
        def _():
            for i in which:
                other_part(i).wait_recv()

    def save(kind, l, m):
        src = xy.at[l, m] if kind == X_ else hs.at[kind, m]
        return pltpu.make_async_copy(src, acts_out.at[l, kind, m], asem.at[kind, l, m])

    def save_qkv(kind, l, m):
        return pltpu.make_async_copy(qkvs.at[m, kind], qkv_out.at[l, kind, m], qsem.at[kind, l, m])

    def save_o(l, m):
        return pltpu.make_async_copy(os_.at[m], o_out.at[l, m, :, lanes_at(sec * half, half)], osem.at[l, m])

    def share_o(l, m):
        return pltpu.make_async_remote_copy(
            src_ref=os_.at[m], dst_ref=o_out.at[l, m, :, lanes_at(sec * half, half)],
            send_sem=osend.at[l, m], recv_sem=orecv.at[l, m], device_id=sib, device_id_type=MESH,
        )

    def save_big(kind, l, m):
        if kind == M_:
            dst = m_out.at[l, m, :, lanes_at(sec * ffh, ffh)]
        else:
            dst = p_out.at[l, kind - 1, m]
        return pltpu.make_async_copy(big.at[m, kind], dst, bsem.at[kind, l, m])

    def share_m(l, m):
        return pltpu.make_async_remote_copy(
            src_ref=big.at[m, M_], dst_ref=m_out.at[l, m, :, lanes_at(sec * ffh, ffh)],
            send_sem=msend.at[l, m], recv_sem=mrecv.at[l, m], device_id=sib, device_id_type=MESH,
        )

    def save_stats(l, m):
        return pltpu.make_async_copy(stats.at[l, m], stats_out.at[l, m], tsem.at[l, m])

    def save_y(m):
        return pltpu.make_async_copy(xy.at[sec + 1, m], y_out.at[m], ysem.at[m])

    def partial(phase, l, m):
        return pltpu.make_async_remote_copy(
            src_ref=psend.at[phase, m], dst_ref=precv.at[phase, l, m],
            send_sem=ssend.at[phase, l, m], recv_sem=srecv.at[phase, l, m], device_id=sib, device_id_type=MESH,
        )

    def weight_saves(l):
        pairs = ((wqkv, wqkv_out), (wo, wo_out), (win, win_out), (wout, wout_out))
        return [pltpu.make_async_copy(s.at[l], d.at[l], wsave.at[i, l]) for i, (s, d) in enumerate(pairs)]

    par_save = pltpu.make_async_copy(par, par_out, parsem)

    def attend(l, m):
        @pl.when(m == 0)
        def _():
            need(l, (0, 1, 2))

            @pl.when(l != sec)
            def _():
                for c in other_vectors():
                    c.wait_recv()

        @pl.when(l > 0)
        def _():
            for kind in range(3):
                save_qkv(kind, l - 1, m).wait()
            save_o(l - 1, m).wait()
            share_o(l - 1, m).wait_send()
            partial(0, l - 1, m).wait_send()

        save(X_, l, m).start()
        bias_q = par[l, BIAS_Q : BIAS_Q + 1, lanes_at(sec * half, half)]
        bias_v = par[l, BIAS_V : BIAS_V + 1, lanes_at(sec * half, half)]

        r = dot(xy[l, m], wqkv[l])
        q = (r[:, :half] + bias_q).astype(BF)
        k = r[:, half : 2 * half].astype(BF)
        v = (r[:, 2 * half :] + bias_v).astype(BF)
        for j, w in enumerate((q, k, v)):
            qkvs[m, j] = w
        kpad[HALO : HALO + seq, :] = k
        vpad[HALO : HALO + seq, :] = v
        for kind in range(3):
            save_qkv(kind, l, m).start()

        lane = lax.broadcasted_iota(jnp.int32, (QB, 128), 1)
        for g in range(half // LANES):
            cols = slice(g * LANES, (g + 1) * LANES)
            for i in range(seq // QB):
                rows = slice(i * QB, (i + 1) * QB)
                far = away[m, i].astype(F32)
                qs = stack_heads(qkvs[m, 0, rows, cols] * BF(HEAD**-0.5))
                s = dot_nt(qs, kpad[i * QB : i * QB + KW, cols])
                probs = []
                kept = stats[l, m, rows, :]
                for h in range(GROUP):
                    sh = s[h * QB : (h + 1) * QB] + slope_of(sec, g, h) * far
                    top = jnp.max(sh, axis=-1, keepdims=True)
                    e = jnp.exp(sh - top)
                    total = jnp.sum(e, axis=-1, keepdims=True)
                    probs.append((e * (1.0 / total)).astype(BF))
                    kept = jnp.where(lane == g * GROUP + h, top + jnp.log(total), kept)
                stats[l, m, rows, :] = kept
                r = dot(jnp.concatenate(probs, axis=0), vpad[i * QB : i * QB + KW, cols])
                os_[m, rows, cols] = merge_heads(r).astype(BF)

        save_o(l, m).start()
        share_o(l, m).start()

        @pl.when(m == 0)
        def _():
            need(l, (3,))

        psend[0, m] = dot(os_[m], wo[l]).astype(BF)
        partial(0, l, m).start()

    def feed(l, m):
        @pl.when(m == 0)
        def _():
            need(l, (4, 5, 6))
            for c in weight_saves(l):
                c.start()

        @pl.when(l > 0)
        def _():
            save(H_, l - 1, m).wait()
            save(NA_, l - 1, m).wait()
            for kind in range(3):
                save_big(kind, l - 1, m).wait()
            share_m(l - 1, m).wait_send()
            partial(1, l - 1, m).wait_send()

        partial(0, l, m).wait_recv()
        lane = lax.broadcasted_iota(jnp.int32, (TILE, 128), 1)

        def norm(t, carry):
            rows = tile_rows(t)
            a = xy[l, m, rows, :].astype(F32) + (
                psend[0, m, rows, :].astype(F32) + precv[0, l, m, rows, :].astype(F32) + par[l, BIAS_O : BIAS_O + 1, :]
            )
            n, rstd = normalize(a)
            hs[NA_, m, rows, :] = n.astype(BF)
            hs[H_, m, rows, :] = (n * par[l, GAIN0 : GAIN0 + 1, :] + par[l, BIAS_A : BIAS_A + 1, :]).astype(BF)
            stats[l, m, rows, :] = jnp.where(lane == RSTD_A, rstd, stats[l, m, rows, :])
            return carry

        lax.fori_loop(0, seq // TILE, norm, 0)
        save(H_, l, m).start()
        save(NA_, l, m).start()
        h = hs[H_, m]
        for c in range(ffh // FEED):
            cols = slice(c * FEED, (c + 1) * FEED)
            unit = sec * ffh + c * FEED
            gate = dot(h, win[l, :, cols]) + bin_[l, :, lanes_at(unit, FEED)]
            up = dot(h, win[l, :, ffh + c * FEED : ffh + (c + 1) * FEED]) + bin_[l, :, lanes_at(ff + unit, FEED)]
            cdf = 0.5 + 0.5 * lax.erf(gate * (0.5**0.5))
            act = gate * cdf
            slope = cdf + gate * (jnp.exp(gate * gate * -0.5) * (2.0 * math.pi) ** -0.5)
            mixed = (act * up).astype(BF)
            big[m, M_, :, cols] = mixed
            big[m, P1_, :, cols] = act.astype(BF)
            big[m, P2_, :, cols] = (up * slope).astype(BF)
            down = dot(mixed, wout[l, cols, :])
            acc[...] = down if c == 0 else acc[...] + down

        psend[1, m] = acc[...].astype(BF)
        partial(1, l, m).start()
        for kind in range(3):
            save_big(kind, l, m).start()
        share_m(l, m).start()

    def finish(l, m):
        @pl.when(l > 0)
        def _():
            save(NB_, l - 1, m).wait()

        partial(1, l, m).wait_recv()
        lane = lax.broadcasted_iota(jnp.int32, (TILE, 128), 1)

        def norm(t, carry):
            rows = tile_rows(t)
            b = hs[H_, m, rows, :].astype(F32) + (
                psend[1, m, rows, :].astype(F32) + precv[1, l, m, rows, :].astype(F32) + par[l, BIAS_F : BIAS_F + 1, :]
            )
            n, rstd = normalize(b)
            hs[NB_, m, rows, :] = n.astype(BF)
            xy[l + 1, m, rows, :] = (n * par[l, GAIN1 : GAIN1 + 1, :] + par[l, BIAS_B : BIAS_B + 1, :]).astype(BF)
            stats[l, m, rows, :] = jnp.where(lane == RSTD_B, rstd, stats[l, m, rows, :])
            return carry

        lax.fori_loop(0, seq // TILE, norm, 0)
        save(NB_, l, m).start()
        save_stats(l, m).start()

        @pl.when(l == sec)
        def _():
            save_y(m).start()

    def layer(l, carry):
        def first(m, carry):
            @pl.when(l > 0)
            def _():
                finish(l - 1, m)

            attend(l, m)
            return carry

        lax.fori_loop(0, micro, first, 0)

        def second(m, carry):
            feed(l, m)
            return carry

        lax.fori_loop(0, micro, second, 0)
        return carry

    lax.fori_loop(0, 2, layer, 0)
    par_save.start()

    def last(m, carry):
        finish(1, m)
        return carry

    lax.fori_loop(0, micro, last, 0)

    def drain(m, carry):
        for kind in range(3):
            save_qkv(kind, 1, m).wait()
            save_big(kind, 1, m).wait()
        for kind in (H_, NA_, NB_):
            save(kind, 1, m).wait()
        save_o(1, m).wait()
        share_o(1, m).wait_send()
        share_m(1, m).wait_send()
        for phase in range(2):
            partial(phase, 1, m).wait_send()
        for l in range(2):
            save(X_, l, m).wait()
            save_stats(l, m).wait()
            share_o(l, m).wait_recv()
            share_m(l, m).wait_recv()
        save_y(m).wait()
        return carry

    lax.fori_loop(0, micro, drain, 0)
    for l in range(2):
        for c in weight_saves(l):
            c.wait()
    for i in range(7):
        other_part(i).wait_send()
    for c in other_vectors():
        c.wait_send()
    par_save.wait()
    away_save.wait()


def any_spec():
    return pl.BlockSpec(memory_space=pl.ANY)


def vmem_spec():
    return pl.BlockSpec(memory_space=pltpu.VMEM)


def smem_spec():
    return pl.BlockSpec(memory_space=pltpu.SMEM)


def vm(*shape, dtype=BF):
    return pltpu.VMEM(shape, dtype)


def run_forward(hid, segs, w_qkv, w_o, w_in, w_out, gains, biases, b_in):
    micro, seq, width = hid.shape
    ff = w_out.shape[0]
    half, ffh = width // 2, ff // 2
    dma = pltpu.SemaphoreType.DMA

    def out(*shape, dtype=BF):
        return jax.ShapeDtypeStruct(shape, dtype)

    shapes = (
        out(micro, seq, width),
        out(2, 4, micro, seq, width),
        out(2, micro, seq, width),
        out(2, micro, seq, ff),
        out(2, 3, micro, seq, half),
        out(2, 2, micro, seq, ffh),
        out(2, micro, seq, 128, dtype=F32),
        out(2, width, 3 * half),
        out(2, half, width),
        out(2, width, 2 * ffh),
        out(2, ffh, width),
        out(2, 8, width, dtype=F32),
        out(micro, seq // QB, QB, KW),
    )
    return pl.pallas_call(
        fwd_kernel,
        out_shape=shapes,
        in_specs=[any_spec(), vmem_spec()] + [any_spec()] * 4 + [vmem_spec()] * 3,
        out_specs=tuple([any_spec()] * len(shapes)),
        scratch_shapes=[
            vm(2, width, 3 * half),
            vm(2, half, width),
            vm(2, width, 2 * ffh),
            vm(2, ffh, width),
            vm(2, 8, width, dtype=F32),
            vm(2, 1, 2 * ff, dtype=F32),
            vm(3, micro, seq, width),
            vm(micro, 3, seq, half),
            vm(micro, seq, half),
            vm(3, micro, seq, width),
            vm(micro, 3, seq, ffh),
            vm(2, micro, seq, width),
            vm(2, 2, micro, seq, width),
            vm(seq, width, dtype=F32),
            vm(seq + 2 * HALO, half),
            vm(seq + 2 * HALO, half),
            vm(micro, seq // QB, QB, KW),
            vm(2, micro, seq, 128, dtype=F32),
            dma((7,)), dma((9,)), dma((9,)), dma((4, 2)), dma((micro,)), dma((micro,)), dma((4, 2, micro)),
            dma((3, 2, micro)), dma((2, micro)), dma((2, micro)), dma((2, micro)), dma((3, 2, micro)),
            dma((2, micro)), dma((2, micro)), dma((2, micro)), dma((2, 2, micro)), dma((2, 2, micro)), dma, dma,
        ],
        compiler_params=pltpu.CompilerParams(
            collective_id=1, has_side_effects=True, vmem_limit_bytes=62 << 20
        ),
        name="forward",
    )(hid, segs, w_qkv, w_o, w_in, w_out, gains, biases, b_in)


def column_total(v):
    return jnp.sum(v.astype(F32), axis=0, keepdims=True)


def bwd_kernel(
    comm, cot, acts, o_full, m_full, qkv, pp, stats_h, away, wqkv, wo, win, wout, par, *refs
):
    if comm:
        (dx_out, small_out, shares, *rest) = refs
        (buf, l1, l2, lz, v1, v2, v3, v4, s1, r1, s2, r2, sz, rz, s3, r3, ksem, vs, vr, *rest) = rest
    else:
        (dx_out, small_out, grads_out, *rest) = refs
        (buf, gsem, *rest) = rest
    (acc, df, dy, tr, mt, small, stats, pool, wpool, wslot, gbuf, kpad, vpad, psend, precv,
     poolsem, wsem, usem, nsem, ssem, ysem, xsem, esend, erecv) = rest
    dp = lax.axis_index("dp")
    sec = lax.axis_index("section")
    sib = (1 - sec, dp)
    tokens, width = df.shape
    rows_n, seq = away.shape[0], away.shape[1] * QB
    ff = m_full.shape[2]
    half, ffh = width // 2, ff // 2
    ntile = tokens // TILE
    own = lanes_at(sec * half, half)

    if comm:
        bx, by, bz = dp % 2, (dp // 2) % 2, dp // 4
        xp = dp + 1 - 2 * bx
        yp = dp + 2 - 4 * by
        zp = [dp] + [((bz + d) % 4) * 4 + dp % 4 for d in range(1, 4)]
        near = xp * (1 - sec) + yp * sec
        far = yp * (1 - sec) + xp * sec
        b1 = bx * (1 - sec) + by * sec
        b2 = by * (1 - sec) + bx * sec
        greet = [(sec, xp), (sec, yp)] + [(sec, z) for z in zp[1:]] + [(1 - sec, z) for z in zp[1:] + [xp, yp]]
    else:
        greet = []

    def pool_load(slot, count, src, first):
        return pltpu.make_async_copy(src.at[:, lanes_at(first, count)], pool.at[slot, :, 0:count], poolsem.at[slot])

    def weight_load(slot, count, src, first):
        return pltpu.make_async_copy(src.at[:, lanes_at(first, count)], wpool.at[slot, :, 0:count], wsem.at[slot])

    def rows_load(slot, count, src, first):
        return pltpu.make_async_copy(
            src.at[pl.ds(pl.multiple_of(first, 128), count), :], wslot.at[slot, 0:count], usem.at[slot]
        )

    def norm_loads(l, kind):
        return [
            pltpu.make_async_copy(acts.at[l, kind, :, j * half : (j + 1) * half], gbuf.at[j], nsem.at[j]) for j in range(2)
        ]

    def stats_load(l):
        return pltpu.make_async_copy(stats_h.at[l], stats, ssem)

    def m_loads(l, i):
        return [pool_load(2 + j, PIECE, m_full.at[l], (2 * i + j) * PIECE) for j in range(2)]

    def h_loads(l):
        return [pool_load(j, half, acts.at[l, H_], j * half) for j in range(2)]

    def chunk_loads(l, slot, c):
        first = c * UNITS
        return [
            weight_load(2 * slot, UNITS, win.at[l], first),
            weight_load(2 * slot + 1, UNITS, win.at[l], ffh + first),
            rows_load(slot, UNITS, wout.at[l], first),
            pool_load(2 * slot, UNITS, pp.at[l, 0], first),
            pool_load(2 * slot + 1, UNITS, pp.at[l, 1], first),
        ]

    def exchange(e):
        return pltpu.make_async_remote_copy(
            src_ref=psend, dst_ref=precv.at[e % 2], send_sem=esend.at[e], recv_sem=erecv.at[e],
            device_id=sib, device_id_type=MESH,
        )

    x_store = pltpu.make_async_copy(dy, dx_out, xsem)
    cot_load = pltpu.make_async_copy(cot, dy, ysem)
    cot_load.start()

    def first_loads(l):
        for load in h_loads(l):
            load.start()
        stats_load(l).start()
        for load in m_loads(l, 0):
            load.start()

    first_loads(1)
    barrier = pltpu.get_barrier_semaphore()
    for peer in [sib] + greet:
        pl.semaphore_signal(barrier, inc=1, device_id=peer, device_id_type=MESH)
    pl.semaphore_wait(barrier, 1 + len(greet))

    def put(t, n, lane, value):
        lanes = slice(lane, lane + value.shape[1])
        if not comm:
            buf[t, n, :, lanes] = value
            return
        share = value.shape[0] // 16
        for o in range(16):
            x, y, z = o % 2, (o // 2) % 2, o // 4
            f = x * (1 - sec) + y * sec
            s = y * (1 - sec) + x * sec
            buf[t, n, f, s, z, :, lanes] = value[o * share : (o + 1) * share]

    if comm:

        def remote(src, dst, ss, rs, to):
            return pltpu.make_async_remote_copy(
                src_ref=src, dst_ref=dst, send_sem=ss, recv_sem=rs, device_id=to, device_id_type=MESH
            )

        def stage1(t, n):
            return remote(buf.at[t, n, 1 - b1], l1.at[t, n], s1.at[t, n], r1.at[t, n], (sec, near))

        def stage2(t, n):
            return remote(buf.at[t, n, b1, 1 - b2], l2.at[t, n], s2.at[t, n], r2.at[t, n], (sec, far))

        def early(n):
            return n % EARLY == 1

        def stagez(t, n, d):
            dst = l2.at[t, n, pl.ds(2 * (d - 1), 2)] if d < 3 else lz.at[t, n // EARLY]
            return remote(
                buf.at[t, n, b1, :, (bz + d) % 4], dst, sz.at[t, n // EARLY, d - 1], rz.at[t, n // EARLY, d - 1], (sec, zp[d])
            )

        def stage3(t, n, d):
            return remote(
                buf.at[t, n, b1, b2, (bz + d) % 4], shares.at[n, sec, d], s3.at[t, n, d], r3.at[n, sec, d], (1 - t, zp[d])
            )

        def stage3_far(t, n):
            return remote(
                buf.at[t, n, b1, 1 - b2, bz], shares.at[n, sec, 1], s3.at[t, n, 1], r3.at[n, sec, 1], (1 - t, far)
            )

        def keep(t, n):
            return pltpu.make_async_copy(buf.at[t, n, b1, b2, bz], shares.at[n, sec, 0], ksem.at[n])

        def landed(n, k, d):
            return remote(shares.at[n, k, d], shares.at[n, k, d], s3.at[0, n, d], r3.at[n, k, d], (1 - sec, dp))

        def join(t, n, second):
            for z in range(4):
                at = (t, n, b1, second, z)
                buf[at] = (buf[at].astype(F32) + l1[t, n, second, z].astype(F32)).astype(BF)

        def after1(t, n):
            stage1(t, n).wait()
            join(t, n, 1 - b2)

            @pl.when(early(n))
            def _():
                join(t, n, b2)
                for d in (1, 2, 3):
                    stagez(t, n, d).start()

            @pl.when(~early(n))
            def _():
                stage2(t, n).start()
                join(t, n, b2)

        def own_share(t, n):
            @pl.when(sec != 1 - t)
            def _():
                stage3(t, n, 0).start()

            @pl.when(sec == 1 - t)
            def _():
                keep(t, n).start()

        def after2(t, n):
            @pl.when(early(n))
            def _():
                for d in (1, 2, 3):
                    stagez(t, n, d).wait()
                for order in (0, 1):
                    second = (1 - b2) if order == 0 else b2
                    at = (t, n, b1, second, bz)
                    total = buf[at].astype(F32) + l2[t, n, second].astype(F32)
                    total = total + (l2[t, n, 2 + second].astype(F32) + lz[t, n // EARLY, second].astype(F32))
                    buf[at] = total.astype(BF)
                    if order == 0:
                        stage3_far(t, n).start()
                own_share(t, n)

            @pl.when(~early(n))
            def _():
                stage2(t, n).wait()
                for z in range(4):
                    at = (t, n, b1, b2, z)
                    buf[at] = (buf[at].astype(F32) + l2[t, n, z].astype(F32)).astype(BF)
                for d in (1, 2, 3):
                    stage3(t, n, d).start()
                own_share(t, n)

        def sent3(t, n):
            @pl.when(early(n))
            def _():
                stage3_far(t, n).wait_send()

            @pl.when(~early(n))
            def _():
                for d in (1, 2, 3):
                    stage3(t, n, d).wait_send()

            @pl.when(sec != 1 - t)
            def _():
                stage3(t, n, 0).wait_send()

        def arrived(t, n):
            for k in range(2):
                landed(n, k, 1).wait_recv()

                @pl.when(~early(n))
                def _():
                    for d in (2, 3):
                        landed(n, k, d).wait_recv()

                @pl.when(sec != k)
                def _():
                    landed(n, k, 0).wait_recv()

            keep(t, n).wait()

        def span(lo, hi, fn):
            def one(n, carry):
                fn(n)
                return carry

            lax.fori_loop(lo, hi, one, 0)

        def step(i, fresh=True):
            if fresh:
                stage1(i // 16, i % 16).start()
            for back, fn in ((AHEAD1, after1), (AHEAD1 + AHEAD2, after2)):
                j = i - back

                @pl.when((j >= 0) & (j < 32))
                def _():
                    fn(j // 16, j % 16)

    small[...] = jnp.zeros_like(small)
    for pad in (kpad, vpad):
        pad[0:HALO, :] = jnp.zeros((HALO, half), BF)
        pad[HALO + seq :, :] = jnp.zeros((HALO, half), BF)
    cot_load.wait()

    def layer(t, carry):
        l = 1 - t

        def transpose_pool(slots):
            for j, slot in enumerate(slots):
                tr[j * half : (j + 1) * half, :] = pool[slot].T

        for load in norm_loads(l, NB_):
            load.start()
        for load in h_loads(l):
            load.wait()
        transpose_pool((0, 1))
        for load in chunk_loads(l, 0, 0):
            load.start()
        stats_load(l).wait()
        for load in norm_loads(l, NB_):
            load.wait()

        def norm_back(dv, rows, rstd_lane, gain, gain_sum, offset_sum, round_sum):
            n = jnp.concatenate([gbuf[0, rows, :], gbuf[1, rows, :]], axis=1).astype(F32)
            rstd = stats[rows, rstd_lane : rstd_lane + 1]
            dn = dv * par[l, gain : gain + 1, :]
            d = rstd * (
                dn - jnp.mean(dn, axis=-1, keepdims=True) - n * jnp.mean(dn * n, axis=-1, keepdims=True)
            )
            low = d.astype(BF)
            df[rows, :] = low
            small[t, gain_sum : gain_sum + 1, :] += column_total(dv * n)
            small[t, offset_sum : offset_sum + 1, :] += column_total(dv)
            small[t, round_sum : round_sum + 1, :] += column_total(low)

        def out_norm(i, carry):
            rows = tile_rows(i)
            norm_back(dy[rows, :].astype(F32), rows, RSTD_B, GAIN1, GAIN1, BIAS_B, BIAS_F)
            acc[rows, :] = jnp.zeros((TILE, width), F32)
            return carry

        lax.fori_loop(0, ntile, out_norm, 0)

        def out_grad(i, carry):
            for load in m_loads(l, i):
                load.wait()
            for j in range(2):
                mt[j * PIECE : (j + 1) * PIECE, :] = pool[2 + j].T

            @pl.when(i + 1 < ff // width)
            def _():
                for load in m_loads(l, i + 1):
                    load.start()

            g = dot(mt[...], df[:, own]).astype(BF)
            if comm:
                for o in range(4):
                    x, y = o % 2, o // 2
                    f = x * (1 - sec) + y * sec
                    s = y * (1 - sec) + x * sec
                    for q in range(4):
                        buf[t, q, f, s, i] = g[o * 192 + q * 48 : o * 192 + (q + 1) * 48]
            else:
                buf[t, i] = g
            return carry

        lax.fori_loop(0, ff // width, out_grad, 0)
        if comm:
            step(16 * t)
            step(16 * t + 1)

        def feed(jj, carry):
            for part in range(3):
                c = 3 * jj + part
                slot = c % 2
                for load in chunk_loads(l, slot, c):
                    load.wait()

                @pl.when(c + 1 < ffh // UNITS)
                def _():
                    for load in chunk_loads(l, 1 - slot, c + 1):
                        load.start()

                dm = dot_nt(df[...], wslot[slot, 0:UNITS])
                gbuf[0, :, 0:UNITS] = (dm * pool[2 * slot + 1, :, 0:UNITS].astype(F32)).astype(BF)
                gbuf[1, :, 0:UNITS] = (dm * pool[2 * slot, :, 0:UNITS].astype(F32)).astype(BF)
                acc[...] += dot_nt(gbuf[0, :, 0:UNITS], wpool[2 * slot, :, 0:UNITS]) + dot_nt(
                    gbuf[1, :, 0:UNITS], wpool[2 * slot + 1, :, 0:UNITS]
                )

                @pl.when(c == ffh // UNITS - 1)
                def _():
                    @pl.when(t > 0)
                    def _():
                        exchange(1).wait_send()

                    psend[...] = acc[...].astype(BF)
                    exchange(2 * t).start()

                unit = sec * ffh + c * UNITS
                spot = lanes_at(unit % width, UNITS)
                for k in range(2):
                    small[t, pl.ds(BIAS_IN + k * (ff // width) + unit // width, 1), spot] = column_total(
                        gbuf[k, :, 0:UNITS]
                    )
                    g = dot(tr[...], gbuf[k, :, 0:UNITS]).astype(BF)
                    n = 4 + 4 * jj + 2 * k
                    if part == 0:
                        put(t, n, 0, g)
                    elif part == 1:
                        put(t, n, 256, g[:, :128])
                        put(t, n + 1, 0, g[:, 128:])
                    else:
                        put(t, n + 1, 128, g)
                if comm:
                    step(16 * t + 2 + c)
            return carry

        lax.fori_loop(0, ffh // (3 * UNITS), feed, 0)
        for load in norm_loads(l, NA_):
            load.start()
        for j in range(2):
            pool_load(j, half, o_full.at[l], j * half).start()
        wo_load = rows_load(0, half, wo.at[l], 0)
        wo_load.start()
        head_weights = [weight_load(j, half, wqkv.at[l], j * half) for j in range(3)]
        for load in head_weights:
            load.start()
        for load in norm_loads(l, NA_):
            load.wait()
        for j in range(2):
            pool_load(j, half, o_full.at[l], j * half).wait()
        transpose_pool((0, 1))
        head_rows = [pool_load(j, half, qkv.at[l, j], 0) for j in range(3)]
        for load in head_rows:
            load.start()
        pool_load(3, half, acts.at[l, X_], 0).start()
        exchange(2 * t).wait_recv()

        def attn_norm(i, carry):
            rows = tile_rows(i)
            dh = df[rows, :].astype(F32) + (psend[rows, :].astype(F32) + precv[0, rows, :].astype(F32))
            norm_back(dh, rows, RSTD_A, GAIN0, GAIN0, BIAS_A, BIAS_O)
            return carry

        lax.fori_loop(0, ntile, attn_norm, 0)

        wo_load.wait()

        @pl.when((t == 1) & (sec == 1))
        def _():
            x_store.wait()

        dy[:, 0:half] = dot_nt(df[...], wslot[0]).astype(BF)
        put(t, 12, 0, dot(tr[...], df[:, own]).astype(BF))
        if comm:
            step(16 * t + 8)
            step(16 * t + 9)

        for load in head_rows:
            load.wait()

        def row(r, carry):
            base = pl.multiple_of(r * seq, seq)
            kpad[HALO : HALO + seq, :] = pool[1, pl.ds(base, seq), :]
            vpad[HALO : HALO + seq, :] = pool[2, pl.ds(base, seq), :]
            lane = lax.broadcasted_iota(jnp.int32, (QB, 128), 1)

            for g in range(half // LANES):
                cols = slice(g * LANES, (g + 1) * LANES)
                for i in range(seq // QB):
                    rows = pl.ds(pl.multiple_of(base + i * QB, QB), QB)
                    far = away[r, i].astype(F32)
                    kw = kpad[i * QB : i * QB + KW, cols]
                    vw = vpad[i * QB : i * QB + KW, cols]
                    qs = stack_heads(pool[0, rows, cols] * BF(HEAD**-0.5))
                    os = stack_heads(dy[rows, cols])
                    s = dot_nt(qs, kw)
                    d = dot_nt(os, vw)
                    kept = stats[rows, :]
                    ps, ds = [], []
                    for h in range(GROUP):
                        part = slice(h * QB, (h + 1) * QB)
                        lse = jnp.sum(jnp.where(lane == g * GROUP + h, kept, 0.0), axis=-1, keepdims=True)
                        p = jnp.exp(s[part] + slope_of(sec, g, h) * far - lse)
                        pd = p * d[part]
                        ds.append((pd - p * jnp.sum(pd, axis=-1, keepdims=True)).astype(BF))
                        ps.append(p.astype(BF))
                    ds = jnp.concatenate(ds, axis=0)
                    ps = jnp.concatenate(ps, axis=0)
                    gbuf[0, rows, cols] = (merge_heads(dot(ds, kw)) * HEAD**-0.5).astype(BF)
                    dk, dv = dot_tn(ds, qs), dot_tn(ps, os)
                    if i == 0:
                        at, skip = pl.ds(base, HALO), HALO
                    else:
                        at, skip = pl.ds(pl.multiple_of(base + i * QB - HALO, HALO), QB), 0
                        dk = jnp.concatenate([dk[:QB] + left_k, dk[QB:]], axis=0)
                        dv = jnp.concatenate([dv[:QB] + left_v, dv[QB:]], axis=0)
                    gbuf[1, at, cols] = dk[skip:QB].astype(BF)
                    gbuf[2, at, cols] = dv[skip:QB].astype(BF)
                    left_k, left_v = dk[QB:], dv[QB:]
                at = pl.ds(pl.multiple_of(base + seq - HALO, HALO), HALO)
                gbuf[1, at, cols] = left_k[:HALO].astype(BF)
                gbuf[2, at, cols] = left_v[:HALO].astype(BF)
            if comm:
                step(16 * t + 10 + r)
            return carry

        lax.fori_loop(0, rows_n, row, 0)
        pool_load(0, half, acts.at[l, X_], half).start()
        for load in head_weights:
            load.wait()
        exchange(2 * t).wait_send()

        total = dot_nt(gbuf[0], wpool[0])
        for j in (1, 2):
            total += dot_nt(gbuf[j], wpool[j])
        psend[...] = total.astype(BF)
        exchange(2 * t + 1).start()
        small[t, BIAS_Q : BIAS_Q + 1, own] = column_total(gbuf[0])
        small[t, BIAS_V : BIAS_V + 1, own] = column_total(gbuf[2])
        pool_load(3, half, acts.at[l, X_], 0).wait()
        pool_load(0, half, acts.at[l, X_], half).wait()
        transpose_pool((3, 0))

        @pl.when(t == 0)
        def _():
            first_loads(0)

        if comm:
            step(16 * t + 12)
        for j in range(3):
            put(t, 13 + j, 0, dot(tr[...], gbuf[j]).astype(BF))
            if comm and j == 0:
                step(16 * t + 13)
        exchange(2 * t + 1).wait_recv()

        def result(i, carry):
            rows = tile_rows(i)
            dx = df[rows, :].astype(F32) + (psend[rows, :].astype(F32) + precv[1, rows, :].astype(F32))
            dy[rows, :] = dx.astype(BF)
            return carry

        lax.fori_loop(0, ntile, result, 0)

        @pl.when(sec == l)
        def _():
            x_store.start()

        @pl.when(sec != l)
        def _():
            small[t, 0:2, :] = jnp.zeros((2, width), F32)
            small[t, BIAS_O:BIAS_IN, :] = jnp.zeros((BIAS_IN - BIAS_O, width), F32)

        if comm:
            step(16 * t + 14)
            step(16 * t + 15)
        return carry

    lax.fori_loop(0, 2, layer, 0)
    exchange(3).wait_send()

    @pl.when(sec == 0)
    def _():
        x_store.wait()

    if comm:
        mine = 1 - sec

        def vectors(stage):
            if stage == 0:
                return [remote(small.at[sec], v1, vs.at[0], vr.at[0], sib)]
            if stage == 1:
                return [remote(v1, v2, vs.at[1], vr.at[1], (sec, xp))]
            if stage == 2:
                return [remote(v2, v3, vs.at[2], vr.at[2], (sec, yp))]
            return [remote(v3, v4.at[d - 1], vs.at[2 + d], vr.at[2 + d], (sec, zp[d])) for d in (1, 2, 3)]

        def go(stage):
            for c in vectors(stage):
                c.start()

        def done(stage):
            for c in vectors(stage):
                c.wait()

        def rest(lo, hi):
            span(lo, hi, lambda i: step(i, False))

        go(0)
        rest(32, 33)
        done(0)
        v1[...] += small[mine]
        go(1)
        rest(33, 34)
        done(1)
        v2[...] += v1[...]
        go(2)
        rest(34, 35)
        done(2)
        v3[...] += v2[...]
        go(3)
        rest(35, 32 + AHEAD1 + AHEAD2)
        done(3)
        small_out[...] = v3[...] + v4[0] + v4[1] + v4[2]
        for t in range(2):
            span(0, 16, lambda n, t=t: sent3(t, n))
        span(0, 16, lambda n: arrived(mine, n))
    else:
        store = pltpu.make_async_copy(buf, grads_out, gsem)
        store.start()
        small_out[...] = small[...]
        store.wait()


def run_backward(comm, cot, acts, o_full, m_full, qkv, pp, stats, away, wqkv, wo, win, wout, par):
    tokens, width = cot.shape
    ff = m_full.shape[2]
    half = width // 2
    dma = pltpu.SemaphoreType.DMA
    dx = jax.ShapeDtypeStruct((tokens, width), BF)
    if comm:
        r = width // 16
        small = jax.ShapeDtypeStruct((VECTORS, width), F32)
        grads = jax.ShapeDtypeStruct((16, 2, 4, r, PIECE), BF)
        special = [
            vm(2, 16, 2, 2, 4, r, PIECE),
            vm(2, 16, 2, 4, r, PIECE),
            vm(2, 16, 4, r, PIECE),
            vm(2, 5, 2, r, PIECE),
            vm(VECTORS, width, dtype=F32),
            vm(VECTORS, width, dtype=F32),
            vm(VECTORS, width, dtype=F32),
            vm(3, VECTORS, width, dtype=F32),
            dma((2, 16)), dma((2, 16)), dma((2, 16)), dma((2, 16)), dma((2, 5, 3)), dma((2, 5, 3)),
            dma((2, 16, 4)), dma((16, 2, 4)), dma((16,)),
            dma((6,)), dma((6,)),
        ]
    else:
        small = jax.ShapeDtypeStruct((2, VECTORS, width), F32)
        grads = jax.ShapeDtypeStruct((2, 16, width, PIECE), BF)
        special = [vm(2, 16, width, PIECE), dma]
    seq = away.shape[1] * QB
    scratch = special + [
        vm(tokens, width, dtype=F32),
        vm(tokens, width),
        vm(tokens, width),
        vm(width, tokens),
        vm(width, tokens),
        vm(2, VECTORS, width, dtype=F32),
        vm(tokens, 128, dtype=F32),
        vm(4, tokens, PIECE),
        vm(4, width, PIECE),
        vm(2, half, width),
        vm(3, tokens, half),
        vm(seq + 2 * HALO, half),
        vm(seq + 2 * HALO, half),
        vm(tokens, width),
        vm(2, tokens, width),
        dma((4,)), dma((4,)), dma((2,)), dma((2,)), dma, dma, dma, dma((4,)), dma((4,)),
    ]
    return pl.pallas_call(
        functools.partial(bwd_kernel, comm),
        out_shape=(dx, small, grads),
        in_specs=[any_spec()] * 7 + [vmem_spec()] + [any_spec()] * 4 + [vmem_spec()],
        out_specs=(any_spec(), vmem_spec(), any_spec()),
        scratch_shapes=scratch,
        compiler_params=pltpu.CompilerParams(
            collective_id=2, has_side_effects=True, vmem_limit_bytes=64 << 20
        ),
        name="backward",
    )(cot, acts, o_full, m_full, qkv, pp, stats, away, wqkv, wo, win, wout, par)


def results_kernel(shares, vectors, y, dx, y_out, dx_out, fq, fo, fi, fu, gain_out, bias_out, inner_out, land, stage, rows_in, lsem, fsem, csem):
    me = lax.axis_index("dp")
    rows, width = fo.shape
    half, ff = width // 2, fi.shape[1] // 2
    ffh = ff // 2
    arrivals = [pltpu.make_async_copy(v, rows_in.at[i], csem.at[i]) for i, v in enumerate((y, dx))]
    copies = [pltpu.make_async_copy(rows_in.at[i], v, csem.at[2 + i]) for i, v in enumerate((y_out, dx_out))]
    loads = [pltpu.make_async_copy(shares.at[n], land.at[n], lsem.at[n]) for n in range(16)]
    for c in arrivals + loads:
        c.start()
    for i in range(2):
        arrivals[i].wait()
        copies[i].start()

    def place(n, k):
        if n < 4:
            return fu.at[n * rows : (n + 1) * rows, k * half : (k + 1) * half]
        if n < 12:
            jj, g, i = (n - 4) // 4, (n - 4) // 2 % 2, n % 2
            start = g * ff + k * ffh + (2 * jj + i) * PIECE
            return fi.at[:, start : start + PIECE]
        if n == 12:
            return fo.at[:, k * half : (k + 1) * half]
        start = (n - 13) * width + k * half
        return fq.at[:, start : start + half]

    stores = []
    for n in range(16):
        loads[n].wait()
        for k in range(2):
            total = land[n, k, 0].astype(F32) + land[n, k, 1].astype(F32)
            if n % EARLY != 1:
                total = total + (land[n, k, 2].astype(F32) + land[n, k, 3].astype(F32))
            stage[n, k] = total
            stores.append(pltpu.make_async_copy(stage.at[n, k], place(n, k), fsem.at[n, k]))
            stores[-1].start()
    turned = pltpu.roll(vectors[0:8, :], (width - me * rows) % width, axis=1)
    gain_out[...] = turned[0:2, 0:rows]
    for j in range(6):
        bias_out[j] = turned[2 + j : 3 + j, 0:rows]
    line = vectors[pl.ds(8 + me // 2, 1), :]
    inner_out[...] = jnp.where(me % 2 == 0, line[:, :half], line[:, half:])
    for c in stores + copies:
        c.wait()


def run_results(shares, vectors, y, dx, ff):
    _, _, _, rows, half = shares.shape
    width = 2 * half
    dma = pltpu.SemaphoreType.DMA

    def out(*shape):
        return jax.ShapeDtypeStruct(shape, F32)

    return pl.pallas_call(
        results_kernel,
        out_shape=(
            jax.ShapeDtypeStruct(y.shape, BF), jax.ShapeDtypeStruct(dx.shape, BF),
            out(rows, 3 * width), out(rows, width), out(rows, 2 * ff), out(ff // 16, width),
            out(2, rows), out(6, 1, rows), out(1, 2 * ff // 16),
        ),
        in_specs=[any_spec(), vmem_spec(), any_spec(), any_spec()],
        out_specs=tuple([any_spec()] * 6 + [vmem_spec()] * 3),
        scratch_shapes=[
            vm(*shares.shape), vm(16, 2, rows, half, dtype=F32), vm(2, *y.shape), dma((16,)), dma((16, 2)), dma((4,)),
        ],
        compiler_params=pltpu.CompilerParams(vmem_limit_bytes=60 << 20),
        name="results",
    )(shares, vectors, y, dx)


def assemble(halves, width, ff):
    def columns(v):
        return jnp.concatenate(v, axis=1)

    gu = columns([h[:4].reshape(ff, PIECE) for h in halves])
    inner = [
        columns([h[4 + 4 * jj + 2 * k + i] for jj in range(2) for i in range(2)]) for k in range(2) for h in halves
    ]
    gi = columns(inner)
    go = columns([h[12] for h in halves])
    gq = columns([h[13 + j] for j in range(3) for h in halves])
    return gq, go, gi, gu


def shards(comm, hidden, segs, w_qkv, w_o, w_in, w_out, gains, biases, b_in, cot):
    w_qkv, w_o, w_in, w_out, gains = (v[0] for v in (w_qkv, w_o, w_in, w_out, gains))
    biases = jnp.transpose(biases, (1, 0, 2))
    micro, _, seq, width = hidden.shape
    ff = w_out.shape[0]
    tokens = micro * seq
    y, acts, o_full, m_full, qkv, pp, stats, wqkv2, wo2, win2, wout2, par2, away = run_forward(
        hidden.reshape(micro, seq, width), segs, w_qkv, w_o, w_in, w_out, gains, biases, b_in
    )
    dx, small, grads = run_backward(
        comm, cot.reshape(tokens, width), acts.reshape(2, 4, tokens, width), o_full.reshape(2, tokens, width),
        m_full.reshape(2, tokens, ff), qkv.reshape(2, 3, tokens, width // 2), pp.reshape(2, 2, tokens, ff // 2),
        stats.reshape(2, tokens, 128), away, wqkv2, wo2, win2, wout2, par2,
    )
    if comm:
        y, dx, gq, go, gi, gu, gain, bias, inner = run_results(grads, small, y.reshape(tokens, width), dx, ff)
        return (
            y.reshape(1, *hidden.shape), dx.reshape(1, *hidden.shape), gq[None], go[None], gi[None], gu[None],
            gain[None], jnp.transpose(bias, (1, 0, 2)), inner,
        )
    owners, me = lax.axis_size("dp"), lax.axis_index("dp")
    first = lax.axis_index("section") == 0
    swap = [(0, 1), (1, 0)]

    def pick(v):
        own = jnp.where(first, v[1], v[0])
        return own, lax.ppermute(jnp.where(first, v[0], v[1]), "section", swap)

    own, other = pick(grads)
    halves = [jnp.where(first, own, other), jnp.where(first, other, own)]

    def share(v):
        parts = v.reshape(owners, v.shape[0] // owners, v.shape[1])
        got = lax.all_to_all(parts, "dp", split_axis=0, concat_axis=0, tiled=True)
        return jnp.sum(got.astype(F32), axis=0)

    gq, go, gi, gu = (share(v) for v in assemble(halves, width, ff))
    own, other = pick(small)
    small = lax.psum(own + other, "dp")
    part = width // owners
    mine = lax.dynamic_slice_in_dim(small[:8], me * part, part, axis=1)
    inner = lax.dynamic_slice_in_dim(small[8:].reshape(1, 2 * ff), me * (2 * ff // owners), 2 * ff // owners, axis=1)
    return (
        y.reshape(1, *hidden.shape), dx.reshape(1, *hidden.shape), gq[None], go[None], gi[None], gu[None],
        mine[None, :2], mine[None, 2:], inner,
    )


def solution(mesh):
    rows = P(None, "dp", None, None)
    layer = P("section", None, None)
    comm = mesh.shape["dp"] == 16
    return jax.shard_map(
        functools.partial(shards, comm),
        mesh=mesh,
        in_specs=(rows, P(None, "dp", None)) + (layer,) * 6 + (P("section", None), rows),
        out_specs=(
            P("section", None, "dp", None, None),
            P("section", None, "dp", None, None),
            P("section", "dp", None),
            P("section", "dp", None),
            P("section", "dp", None),
            P("section", "dp", None),
            P("section", None, "dp"),
            P("section", None, "dp"),
            P("section", "dp"),
        ),
        check_vma=False,
    )
```

```python
import functools
import math

import jax
import jax.numpy as jnp
from jax import lax
from jax.experimental import pallas as pl
from jax.experimental.pallas import tpu as pltpu
from jax.sharding import PartitionSpec as P

HEADS = 12
HEAD = 64
GROUP = 2
LANES = GROUP * HEAD
QB = 128
HALO = 64
KW = QB + 2 * HALO
EPS = 1e-05
MASKED = -1.0e30
TILE = 256
UNITS = 256
PIECE = 384
BF = jnp.bfloat16
F32 = jnp.float32
MESH = pl.DeviceIdType.MESH
NT = (((1,), (1,)), ((), ()))
TN = (((0,), (0,)), ((), ()))
H_, NA_, NB_, X_ = range(4)
M_, P1_, P2_ = range(3)
GAIN0, GAIN1, BIAS_Q, BIAS_V, BIAS_O, BIAS_A, BIAS_F, BIAS_B, BIAS_IN = range(9)
VECTORS = 16
FEED = 512
AHEAD1, AHEAD2 = 3, 3
EARLY = 3
RSTD_A, RSTD_B = HEADS, HEADS + 1


def slope_list(head_count):
    base = 2 ** int(math.floor(math.log2(head_count)))
    leading = [2.0 ** (-8.0 * (k + 1) / base) for k in range(base)]
    trailing = [2.0 ** (-4.0 * (2 * k + 1) / base) for k in range(head_count - base)]
    return leading + trailing


def dot(a, b):
    return jnp.dot(a, b, preferred_element_type=F32)


def dot_nt(a, b):
    return lax.dot_general(a, b, NT, preferred_element_type=F32)


def dot_tn(a, b):
    return lax.dot_general(a, b, TN, preferred_element_type=F32)


def normalize(v):
    c = v - jnp.mean(v, axis=-1, keepdims=True)
    rstd = lax.rsqrt(jnp.mean(c * c, axis=-1, keepdims=True) + EPS)
    return c * rstd, rstd


def stack_heads(v):
    head = lax.broadcasted_iota(jnp.int32, v.shape, 1) // HEAD
    zero = jnp.zeros_like(v)
    return jnp.concatenate([jnp.where(head == h, v, zero) for h in range(GROUP)], axis=0)


def merge_heads(r):
    rows = r.shape[0] // GROUP
    head = lax.broadcasted_iota(jnp.int32, (rows, r.shape[1]), 1) // HEAD
    out = r[:rows]
    for h in range(1, GROUP):
        out = jnp.where(head == h, r[h * rows : (h + 1) * rows], out)
    return out


def fill_away(away, segs):
    micro, _, seq = segs.shape
    r = lax.broadcasted_iota(jnp.int32, (QB, KW), 0)
    c = lax.broadcasted_iota(jnp.int32, (QB, KW), 1)
    apart = -jnp.abs(r + HALO - c).astype(F32)
    outside = jnp.full((QB, 128), -1.0, F32)
    for m in range(micro):
        seg = jnp.broadcast_to(segs[m].astype(F32), (QB, seq))
        keys = pltpu.roll(jnp.concatenate([outside, seg, outside], axis=1), seq + 256 - HALO, axis=1)
        for i in range(seq // QB):
            own = seg[:, i * QB : (i + 1) * QB].T
            own = jnp.concatenate([own, own], axis=1)
            same = own == keys[:, i * QB : i * QB + KW]
            away[m, i] = jnp.where(same, apart, MASKED).astype(BF)


def slope_of(sec, g, h):
    table = slope_list(HEADS)
    return jnp.where(sec == 0, table[g * GROUP + h], table[HEADS // 2 + g * GROUP + h]).astype(F32)


def tile_rows(t):
    return pl.ds(pl.multiple_of(t * TILE, TILE), TILE)


def lanes_at(start, count):
    return pl.ds(pl.multiple_of(start, 128), count)


def fwd_kernel(
    hid, segs, wqkv_h, wo_h, win_h, wout_h, gains_in, biases_in, bin_in,
    y_out, acts_out, o_out, m_out, qkv_out, p_out, stats_out,
    wqkv_out, wo_out, win_out, wout_out, par_out, away_out,
    wqkv, wo, win, wout, par, bin_, xy, qkvs, os_, hs, big, psend, precv, acc, kpad, vpad, away, stats,
    lsem, rsend, rrecv, wsave, hsem, ysem, asem, qsem, osem, osend, orecv, bsem, msend, mrecv, tsem, ssend, srecv,
    parsem, awaysem,
):
    dp = lax.axis_index("dp")
    sec = lax.axis_index("section")
    _, micro, seq, width = xy.shape
    half, ffh, ff = wo.shape[1], wout.shape[1], wout_h.shape[0]
    sib = (1 - sec, dp)

    parts = []
    for j in range(3):
        parts.append((wqkv_h, wqkv, lambda c, j=j: (slice(None), lanes_at(j * width + c * half, half)),
                      (slice(None), slice(j * half, (j + 1) * half))))
    parts.append((wo_h, wo, lambda c: (pl.ds(pl.multiple_of(c * half, 128), half), slice(None)), (slice(None), slice(None))))
    for j in range(2):
        parts.append((win_h, win, lambda c, j=j: (slice(None), lanes_at(j * ff + c * ffh, ffh)),
                      (slice(None), slice(j * ffh, (j + 1) * ffh))))
    parts.append((wout_h, wout, lambda c: (pl.ds(pl.multiple_of(c * ffh, 128), ffh), slice(None)), (slice(None), slice(None))))

    def own_part(i):
        src, dst, pick, place = parts[i]
        return pltpu.make_async_copy(src.at[pick(sec)], dst.at[(sec, *place)], lsem.at[i])

    def other_part(i):
        src, dst, pick, place = parts[i]
        return pltpu.make_async_remote_copy(
            src_ref=src.at[pick(1 - sec)], dst_ref=dst.at[(sec, *place)],
            send_sem=rsend.at[i], recv_sem=rrecv.at[i], device_id=sib, device_id_type=MESH,
        )

    def other_vectors():
        return [
            pltpu.make_async_remote_copy(
                src_ref=v.at[sec], dst_ref=v.at[sec], send_sem=rsend.at[7 + i], recv_sem=rrecv.at[7 + i],
                device_id=sib, device_id_type=MESH,
            )
            for i, v in enumerate((par, bin_))
        ]

    def x_load(m):
        return pltpu.make_async_copy(hid.at[m], xy.at[0, m], hsem.at[m])

    for m in range(micro):
        x_load(m).start()
    for i in range(7):
        own_part(i).start()
    par[sec, 0:2] = gains_in[...]
    for j in range(6):
        par[sec, 2 + j : 3 + j] = biases_in[j]
    bin_[sec] = bin_in[...]
    barrier = pltpu.get_barrier_semaphore()
    pl.semaphore_signal(barrier, inc=1, device_id=sib, device_id_type=MESH)
    pl.semaphore_wait(barrier, 1)
    for c in other_vectors():
        c.start()
    for i in range(7):
        other_part(i).start()
    fill_away(away, segs)
    away_save = pltpu.make_async_copy(away, away_out, awaysem)
    away_save.start()
    for pad in (kpad, vpad):
        pad[0:HALO, :] = jnp.zeros((HALO, half), BF)
        pad[HALO + seq :, :] = jnp.zeros((HALO, half), BF)
    for m in range(micro):
        x_load(m).wait()

    def need(l, which):
        @pl.when(l == sec)
        def _():
            for i in which:
                own_part(i).wait()

        @pl.when(l != sec)
        def _():
            for i in which:
                other_part(i).wait_recv()

    def save(kind, l, m):
        src = xy.at[l, m] if kind == X_ else hs.at[kind, m]
        return pltpu.make_async_copy(src, acts_out.at[l, kind, m], asem.at[kind, l, m])

    def save_qkv(kind, l, m):
        return pltpu.make_async_copy(qkvs.at[m, kind], qkv_out.at[l, kind, m], qsem.at[kind, l, m])

    def save_o(l, m):
        return pltpu.make_async_copy(os_.at[m], o_out.at[l, m, :, lanes_at(sec * half, half)], osem.at[l, m])

    def share_o(l, m):
        return pltpu.make_async_remote_copy(
            src_ref=os_.at[m], dst_ref=o_out.at[l, m, :, lanes_at(sec * half, half)],
            send_sem=osend.at[l, m], recv_sem=orecv.at[l, m], device_id=sib, device_id_type=MESH,
        )

    def save_big(kind, l, m):
        if kind == M_:
            dst = m_out.at[l, m, :, lanes_at(sec * ffh, ffh)]
        else:
            dst = p_out.at[l, kind - 1, m]
        return pltpu.make_async_copy(big.at[m, kind], dst, bsem.at[kind, l, m])

    def share_m(l, m):
        return pltpu.make_async_remote_copy(
            src_ref=big.at[m, M_], dst_ref=m_out.at[l, m, :, lanes_at(sec * ffh, ffh)],
            send_sem=msend.at[l, m], recv_sem=mrecv.at[l, m], device_id=sib, device_id_type=MESH,
        )

    def save_stats(l, m):
        return pltpu.make_async_copy(stats.at[l, m], stats_out.at[l, m], tsem.at[l, m])

    def save_y(m):
        return pltpu.make_async_copy(xy.at[sec + 1, m], y_out.at[m], ysem.at[m])

    def partial(phase, l, m):
        return pltpu.make_async_remote_copy(
            src_ref=psend.at[phase, m], dst_ref=precv.at[phase, l, m],
            send_sem=ssend.at[phase, l, m], recv_sem=srecv.at[phase, l, m], device_id=sib, device_id_type=MESH,
        )

    def weight_saves(l):
        pairs = ((wqkv, wqkv_out), (wo, wo_out), (win, win_out), (wout, wout_out))
        return [pltpu.make_async_copy(s.at[l], d.at[l], wsave.at[i, l]) for i, (s, d) in enumerate(pairs)]

    par_save = pltpu.make_async_copy(par, par_out, parsem)

    def attend(l, m):
        @pl.when(m == 0)
        def _():
            need(l, (0, 1, 2))

            @pl.when(l != sec)
            def _():
                for c in other_vectors():
                    c.wait_recv()

        @pl.when(l > 0)
        def _():
            for kind in range(3):
                save_qkv(kind, l - 1, m).wait()
            save_o(l - 1, m).wait()
            share_o(l - 1, m).wait_send()
            partial(0, l - 1, m).wait_send()

        save(X_, l, m).start()
        bias_q = par[l, BIAS_Q : BIAS_Q + 1, lanes_at(sec * half, half)]
        bias_v = par[l, BIAS_V : BIAS_V + 1, lanes_at(sec * half, half)]

        r = dot(xy[l, m], wqkv[l])
        q = (r[:, :half] + bias_q).astype(BF)
        k = r[:, half : 2 * half].astype(BF)
        v = (r[:, 2 * half :] + bias_v).astype(BF)
        for j, w in enumerate((q, k, v)):
            qkvs[m, j] = w
        kpad[HALO : HALO + seq, :] = k
        vpad[HALO : HALO + seq, :] = v
        for kind in range(3):
            save_qkv(kind, l, m).start()

        lane = lax.broadcasted_iota(jnp.int32, (QB, 128), 1)
        for g in range(half // LANES):
            cols = slice(g * LANES, (g + 1) * LANES)
            for i in range(seq // QB):
                rows = slice(i * QB, (i + 1) * QB)
                far = away[m, i].astype(F32)
                qs = stack_heads(qkvs[m, 0, rows, cols] * BF(HEAD**-0.5))
                s = dot_nt(qs, kpad[i * QB : i * QB + KW, cols])
                probs = []
                kept = stats[l, m, rows, :]
                for h in range(GROUP):
                    sh = s[h * QB : (h + 1) * QB] + slope_of(sec, g, h) * far
                    top = jnp.max(sh, axis=-1, keepdims=True)
                    e = jnp.exp(sh - top)
                    total = jnp.sum(e, axis=-1, keepdims=True)
                    probs.append((e * (1.0 / total)).astype(BF))
                    kept = jnp.where(lane == g * GROUP + h, top + jnp.log(total), kept)
                stats[l, m, rows, :] = kept
                r = dot(jnp.concatenate(probs, axis=0), vpad[i * QB : i * QB + KW, cols])
                os_[m, rows, cols] = merge_heads(r).astype(BF)

        save_o(l, m).start()
        share_o(l, m).start()

        @pl.when(m == 0)
        def _():
            need(l, (3,))

        psend[0, m] = dot(os_[m], wo[l]).astype(BF)
        partial(0, l, m).start()

    def feed(l, m):
        @pl.when(m == 0)
        def _():
            need(l, (4, 5, 6))
            for c in weight_saves(l):
                c.start()

        @pl.when(l > 0)
        def _():
            save(H_, l - 1, m).wait()
            save(NA_, l - 1, m).wait()
            for kind in range(3):
                save_big(kind, l - 1, m).wait()
            share_m(l - 1, m).wait_send()
            partial(1, l - 1, m).wait_send()

        partial(0, l, m).wait_recv()
        lane = lax.broadcasted_iota(jnp.int32, (TILE, 128), 1)

        def norm(t, carry):
            rows = tile_rows(t)
            a = xy[l, m, rows, :].astype(F32) + (
                psend[0, m, rows, :].astype(F32) + precv[0, l, m, rows, :].astype(F32) + par[l, BIAS_O : BIAS_O + 1, :]
            )
            n, rstd = normalize(a)
            hs[NA_, m, rows, :] = n.astype(BF)
            hs[H_, m, rows, :] = (n * par[l, GAIN0 : GAIN0 + 1, :] + par[l, BIAS_A : BIAS_A + 1, :]).astype(BF)
            stats[l, m, rows, :] = jnp.where(lane == RSTD_A, rstd, stats[l, m, rows, :])
            return carry

        lax.fori_loop(0, seq // TILE, norm, 0)
        save(H_, l, m).start()
        save(NA_, l, m).start()
        h = hs[H_, m]
        for c in range(ffh // FEED):
            cols = slice(c * FEED, (c + 1) * FEED)
            unit = sec * ffh + c * FEED
            gate = dot(h, win[l, :, cols]) + bin_[l, :, lanes_at(unit, FEED)]
            up = dot(h, win[l, :, ffh + c * FEED : ffh + (c + 1) * FEED]) + bin_[l, :, lanes_at(ff + unit, FEED)]
            cdf = 0.5 + 0.5 * lax.erf(gate * (0.5**0.5))
            act = gate * cdf
            slope = cdf + gate * (jnp.exp(gate * gate * -0.5) * (2.0 * math.pi) ** -0.5)
            mixed = (act * up).astype(BF)
            big[m, M_, :, cols] = mixed
            big[m, P1_, :, cols] = act.astype(BF)
            big[m, P2_, :, cols] = (up * slope).astype(BF)
            down = dot(mixed, wout[l, cols, :])
            acc[...] = down if c == 0 else acc[...] + down

        psend[1, m] = acc[...].astype(BF)
        partial(1, l, m).start()
        for kind in range(3):
            save_big(kind, l, m).start()
        share_m(l, m).start()

    def finish(l, m):
        @pl.when(l > 0)
        def _():
            save(NB_, l - 1, m).wait()

        partial(1, l, m).wait_recv()
        lane = lax.broadcasted_iota(jnp.int32, (TILE, 128), 1)

        def norm(t, carry):
            rows = tile_rows(t)
            b = hs[H_, m, rows, :].astype(F32) + (
                psend[1, m, rows, :].astype(F32) + precv[1, l, m, rows, :].astype(F32) + par[l, BIAS_F : BIAS_F + 1, :]
            )
            n, rstd = normalize(b)
            hs[NB_, m, rows, :] = n.astype(BF)
            xy[l + 1, m, rows, :] = (n * par[l, GAIN1 : GAIN1 + 1, :] + par[l, BIAS_B : BIAS_B + 1, :]).astype(BF)
            stats[l, m, rows, :] = jnp.where(lane == RSTD_B, rstd, stats[l, m, rows, :])
            return carry

        lax.fori_loop(0, seq // TILE, norm, 0)
        save(NB_, l, m).start()
        save_stats(l, m).start()

        @pl.when(l == sec)
        def _():
            save_y(m).start()

    def layer(l, carry):
        def first(m, carry):
            @pl.when(l > 0)
            def _():
                finish(l - 1, m)

            attend(l, m)
            return carry

        lax.fori_loop(0, micro, first, 0)

        def second(m, carry):
            feed(l, m)
            return carry

        lax.fori_loop(0, micro, second, 0)
        return carry

    lax.fori_loop(0, 2, layer, 0)
    par_save.start()

    def last(m, carry):
        finish(1, m)
        return carry

    lax.fori_loop(0, micro, last, 0)

    def drain(m, carry):
        for kind in range(3):
            save_qkv(kind, 1, m).wait()
            save_big(kind, 1, m).wait()
        for kind in (H_, NA_, NB_):
            save(kind, 1, m).wait()
        save_o(1, m).wait()
        share_o(1, m).wait_send()
        share_m(1, m).wait_send()
        for phase in range(2):
            partial(phase, 1, m).wait_send()
        for l in range(2):
            save(X_, l, m).wait()
            save_stats(l, m).wait()
            share_o(l, m).wait_recv()
            share_m(l, m).wait_recv()
        save_y(m).wait()
        return carry

    lax.fori_loop(0, micro, drain, 0)
    for l in range(2):
        for c in weight_saves(l):
            c.wait()
    for i in range(7):
        other_part(i).wait_send()
    for c in other_vectors():
        c.wait_send()
    par_save.wait()
    away_save.wait()


def any_spec():
    return pl.BlockSpec(memory_space=pl.ANY)


def vmem_spec():
    return pl.BlockSpec(memory_space=pltpu.VMEM)


def smem_spec():
    return pl.BlockSpec(memory_space=pltpu.SMEM)


def vm(*shape, dtype=BF):
    return pltpu.VMEM(shape, dtype)


def run_forward(hid, segs, w_qkv, w_o, w_in, w_out, gains, biases, b_in):
    micro, seq, width = hid.shape
    ff = w_out.shape[0]
    half, ffh = width // 2, ff // 2
    dma = pltpu.SemaphoreType.DMA

    def out(*shape, dtype=BF):
        return jax.ShapeDtypeStruct(shape, dtype)

    shapes = (
        out(micro, seq, width),
        out(2, 4, micro, seq, width),
        out(2, micro, seq, width),
        out(2, micro, seq, ff),
        out(2, 3, micro, seq, half),
        out(2, 2, micro, seq, ffh),
        out(2, micro, seq, 128, dtype=F32),
        out(2, width, 3 * half),
        out(2, half, width),
        out(2, width, 2 * ffh),
        out(2, ffh, width),
        out(2, 8, width, dtype=F32),
        out(micro, seq // QB, QB, KW),
    )
    return pl.pallas_call(
        fwd_kernel,
        out_shape=shapes,
        in_specs=[any_spec(), vmem_spec()] + [any_spec()] * 4 + [vmem_spec()] * 3,
        out_specs=tuple([any_spec()] * len(shapes)),
        scratch_shapes=[
            vm(2, width, 3 * half),
            vm(2, half, width),
            vm(2, width, 2 * ffh),
            vm(2, ffh, width),
            vm(2, 8, width, dtype=F32),
            vm(2, 1, 2 * ff, dtype=F32),
            vm(3, micro, seq, width),
            vm(micro, 3, seq, half),
            vm(micro, seq, half),
            vm(3, micro, seq, width),
            vm(micro, 3, seq, ffh),
            vm(2, micro, seq, width),
            vm(2, 2, micro, seq, width),
            vm(seq, width, dtype=F32),
            vm(seq + 2 * HALO, half),
            vm(seq + 2 * HALO, half),
            vm(micro, seq // QB, QB, KW),
            vm(2, micro, seq, 128, dtype=F32),
            dma((7,)), dma((9,)), dma((9,)), dma((4, 2)), dma((micro,)), dma((micro,)), dma((4, 2, micro)),
            dma((3, 2, micro)), dma((2, micro)), dma((2, micro)), dma((2, micro)), dma((3, 2, micro)),
            dma((2, micro)), dma((2, micro)), dma((2, micro)), dma((2, 2, micro)), dma((2, 2, micro)), dma, dma,
        ],
        compiler_params=pltpu.CompilerParams(
            collective_id=1, has_side_effects=True, vmem_limit_bytes=62 << 20
        ),
        name="forward",
    )(hid, segs, w_qkv, w_o, w_in, w_out, gains, biases, b_in)


def column_total(v):
    return jnp.sum(v.astype(F32), axis=0, keepdims=True)


def bwd_kernel(
    comm, cot, acts, o_full, m_full, qkv, pp, stats_h, away, wqkv, wo, win, wout, par, *refs
):
    if comm:
        (dx_out, small_out, shares, *rest) = refs
        (buf, l1, l2, lz, v1, v2, v3, v4, s1, r1, s2, r2, sz, rz, s3, r3, ksem, vs, vr, *rest) = rest
    else:
        (dx_out, small_out, grads_out, *rest) = refs
        (buf, gsem, *rest) = rest
    (acc, df, dy, tr, mt, small, stats, pool, wpool, wslot, gbuf, kpad, vpad, psend, precv,
     poolsem, wsem, usem, nsem, ssem, ysem, xsem, esend, erecv) = rest
    dp = lax.axis_index("dp")
    sec = lax.axis_index("section")
    sib = (1 - sec, dp)
    tokens, width = df.shape
    rows_n, seq = away.shape[0], away.shape[1] * QB
    ff = m_full.shape[2]
    half, ffh = width // 2, ff // 2
    ntile = tokens // TILE
    own = lanes_at(sec * half, half)

    if comm:
        bx, by, bz = dp % 2, (dp // 2) % 2, dp // 4
        xp = dp + 1 - 2 * bx
        yp = dp + 2 - 4 * by
        zp = [dp] + [((bz + d) % 4) * 4 + dp % 4 for d in range(1, 4)]
        near = xp * (1 - sec) + yp * sec
        far = yp * (1 - sec) + xp * sec
        b1 = bx * (1 - sec) + by * sec
        b2 = by * (1 - sec) + bx * sec
        greet = [(sec, xp), (sec, yp)] + [(sec, z) for z in zp[1:]] + [(1 - sec, z) for z in zp[1:] + [xp, yp]]
    else:
        greet = []

    def pool_load(slot, count, src, first):
        return pltpu.make_async_copy(src.at[:, lanes_at(first, count)], pool.at[slot, :, 0:count], poolsem.at[slot])

    def weight_load(slot, count, src, first):
        return pltpu.make_async_copy(src.at[:, lanes_at(first, count)], wpool.at[slot, :, 0:count], wsem.at[slot])

    def rows_load(slot, count, src, first):
        return pltpu.make_async_copy(
            src.at[pl.ds(pl.multiple_of(first, 128), count), :], wslot.at[slot, 0:count], usem.at[slot]
        )

    def norm_load(l, kind, j, slot):
        return pltpu.make_async_copy(acts.at[l, kind, :, j * half : (j + 1) * half], gbuf.at[slot], nsem.at[slot])

    def stats_load(l):
        return pltpu.make_async_copy(stats_h.at[l], stats, ssem)

    def m_loads(l, i, odd):
        return [
            pltpu.make_async_copy(
                m_full.at[l, :, lanes_at((2 * i + j) * PIECE, PIECE)],
                gbuf.at[j] if odd else pool.at[2 + j],
                nsem.at[j] if odd else poolsem.at[2 + j],
            )
            for j in range(2)
        ]

    def h_loads(l):
        return [pool_load(j, half, acts.at[l, H_], j * half) for j in range(2)]

    def chunk_loads(l, slot, c):
        first = c * UNITS
        return [
            weight_load(2 * slot, UNITS, win.at[l], first),
            weight_load(2 * slot + 1, UNITS, win.at[l], ffh + first),
            rows_load(slot, UNITS, wout.at[l], first),
            pool_load(2 * slot, UNITS, pp.at[l, 0], first),
            pool_load(2 * slot + 1, UNITS, pp.at[l, 1], first),
        ]

    def exchange(e):
        return pltpu.make_async_remote_copy(
            src_ref=psend, dst_ref=precv.at[e % 2], send_sem=esend.at[e], recv_sem=erecv.at[e],
            device_id=sib, device_id_type=MESH,
        )

    x_store = pltpu.make_async_copy(dy, dx_out, xsem)
    cot_load = pltpu.make_async_copy(cot, dy, ysem)
    cot_load.start()

    def first_loads(l):
        stats_load(l).start()
        for load in m_loads(l, 0, False) + h_loads(l):
            load.start()

    for j in range(2):
        norm_load(1, NB_, j, j).start()
    first_loads(1)
    barrier = pltpu.get_barrier_semaphore()
    for peer in [sib] + greet:
        pl.semaphore_signal(barrier, inc=1, device_id=peer, device_id_type=MESH)
    pl.semaphore_wait(barrier, 1 + len(greet))

    def put(t, n, lane, value):
        lanes = slice(lane, lane + value.shape[1])
        if not comm:
            buf[t, n, :, lanes] = value
            return
        share = value.shape[0] // 16
        for o in range(16):
            x, y, z = o % 2, (o // 2) % 2, o // 4
            f = x * (1 - sec) + y * sec
            s = y * (1 - sec) + x * sec
            buf[t, n, f, s, z, :, lanes] = value[o * share : (o + 1) * share]

    if comm:

        def remote(src, dst, ss, rs, to):
            return pltpu.make_async_remote_copy(
                src_ref=src, dst_ref=dst, send_sem=ss, recv_sem=rs, device_id=to, device_id_type=MESH
            )

        def stage1(t, n):
            return remote(buf.at[t, n, 1 - b1], l1.at[t, n], s1.at[t, n], r1.at[t, n], (sec, near))

        def stage2(t, n):
            return remote(buf.at[t, n, b1, 1 - b2], l2.at[t, n], s2.at[t, n], r2.at[t, n], (sec, far))

        def early(n):
            return n % EARLY == 1

        def stagez(t, n, d):
            dst = l2.at[t, n, pl.ds(2 * (d - 1), 2)] if d < 3 else lz.at[t, n // EARLY]
            return remote(
                buf.at[t, n, b1, :, (bz + d) % 4], dst, sz.at[t, n // EARLY, d - 1], rz.at[t, n // EARLY, d - 1], (sec, zp[d])
            )

        def stage3(t, n, d):
            return remote(
                buf.at[t, n, b1, b2, (bz + d) % 4], shares.at[n, sec, d], s3.at[t, n, d], r3.at[n, sec, d], (1 - t, zp[d])
            )

        def stage3_far(t, n):
            return remote(
                buf.at[t, n, b1, 1 - b2, bz], shares.at[n, sec, 1], s3.at[t, n, 1], r3.at[n, sec, 1], (1 - t, far)
            )

        def keep(t, n):
            return pltpu.make_async_copy(buf.at[t, n, b1, b2, bz], shares.at[n, sec, 0], ksem.at[n])

        def landed(n, k, d):
            return remote(shares.at[n, k, d], shares.at[n, k, d], s3.at[0, n, d], r3.at[n, k, d], (1 - sec, dp))

        def join(t, n, second):
            for z in range(4):
                at = (t, n, b1, second, z)
                buf[at] = (buf[at].astype(F32) + l1[t, n, second, z].astype(F32)).astype(BF)

        def after1(t, n):
            stage1(t, n).wait()
            join(t, n, 1 - b2)

            @pl.when(early(n))
            def _():
                join(t, n, b2)
                for d in (1, 2, 3):
                    stagez(t, n, d).start()

            @pl.when(~early(n))
            def _():
                stage2(t, n).start()
                join(t, n, b2)

        def own_share(t, n):
            @pl.when(sec != 1 - t)
            def _():
                stage3(t, n, 0).start()

            @pl.when(sec == 1 - t)
            def _():
                keep(t, n).start()

        def after2(t, n):
            @pl.when(early(n))
            def _():
                for d in (1, 2, 3):
                    stagez(t, n, d).wait()
                for order in (0, 1):
                    second = (1 - b2) if order == 0 else b2
                    at = (t, n, b1, second, bz)
                    total = buf[at].astype(F32) + l2[t, n, second].astype(F32)
                    total = total + (l2[t, n, 2 + second].astype(F32) + lz[t, n // EARLY, second].astype(F32))
                    buf[at] = total.astype(BF)
                    if order == 0:
                        stage3_far(t, n).start()
                own_share(t, n)

            @pl.when(~early(n))
            def _():
                stage2(t, n).wait()
                for z in range(4):
                    at = (t, n, b1, b2, z)
                    buf[at] = (buf[at].astype(F32) + l2[t, n, z].astype(F32)).astype(BF)
                for d in (1, 2, 3):
                    stage3(t, n, d).start()
                own_share(t, n)

        def sent3(t, n):
            @pl.when(early(n))
            def _():
                stage3_far(t, n).wait_send()

            @pl.when(~early(n))
            def _():
                for d in (1, 2, 3):
                    stage3(t, n, d).wait_send()

            @pl.when(sec != 1 - t)
            def _():
                stage3(t, n, 0).wait_send()

        def arrived(t, n):
            for k in range(2):
                landed(n, k, 1).wait_recv()

                @pl.when(~early(n))
                def _():
                    for d in (2, 3):
                        landed(n, k, d).wait_recv()

                @pl.when(sec != k)
                def _():
                    landed(n, k, 0).wait_recv()

            keep(t, n).wait()

        def span(lo, hi, fn):
            def one(n, carry):
                fn(n)
                return carry

            lax.fori_loop(lo, hi, one, 0)

        def step(i, fresh=True):
            if fresh:
                stage1(i // 16, i % 16).start()
            for back, fn in ((AHEAD1, after1), (AHEAD1 + AHEAD2, after2)):
                j = i - back

                @pl.when((j >= 0) & (j < 32))
                def _():
                    fn(j // 16, j % 16)

    small[...] = jnp.zeros_like(small)
    for pad in (kpad, vpad):
        pad[0:HALO, :] = jnp.zeros((HALO, half), BF)
        pad[HALO + seq :, :] = jnp.zeros((HALO, half), BF)
    cot_load.wait()

    def layer(t, carry):
        l = 1 - t

        def transpose_pool(slots):
            for j, slot in enumerate(slots):
                tr[j * half : (j + 1) * half, :] = pool[slot].T

        stats_load(l).wait()
        for j in range(2):
            norm_load(l, NB_, j, j).wait()

        def norm_back(slots, counted, dv, rows, rstd_lane, gain, gain_sum, offset_sum, round_sum):
            n = jnp.concatenate([gbuf[j, rows, :] for j in slots], axis=1).astype(F32)
            rstd = stats[rows, rstd_lane : rstd_lane + 1]
            dn = dv * par[l, gain : gain + 1, :]
            d = rstd * (
                dn - jnp.mean(dn, axis=-1, keepdims=True) - n * jnp.mean(dn * n, axis=-1, keepdims=True)
            )
            low = d.astype(BF)
            df[rows, :] = low

            @pl.when(counted)
            def _():
                small[t, gain_sum : gain_sum + 1, :] += column_total(dv * n)
                small[t, offset_sum : offset_sum + 1, :] += column_total(dv)
                small[t, round_sum : round_sum + 1, :] += column_total(low)

        def out_norm(i, carry):
            rows = tile_rows(i)
            norm_back((0, 1), i // (ntile // 2) == sec, dy[rows, :].astype(F32), rows, RSTD_B, GAIN1, GAIN1, BIAS_B, BIAS_F)
            acc[rows, :] = jnp.zeros((TILE, width), F32)
            return carry

        lax.fori_loop(0, ntile, out_norm, 0)

        for load in m_loads(l, 1, True):
            load.start()
        for load in h_loads(l):
            load.wait()
        transpose_pool((0, 1))
        for load in chunk_loads(l, 0, 0):
            load.start()

        def out_grad(ii, carry):
            for odd in range(2):
                i = 2 * ii + odd
                for load in m_loads(l, i, odd):
                    load.wait()
                for j in range(2):
                    mt[j * PIECE : (j + 1) * PIECE, :] = (gbuf[j] if odd else pool[2 + j]).T

                @pl.when(i + 2 < ff // width)
                def _():
                    for load in m_loads(l, i + 2, odd):
                        load.start()

                g = dot(mt[...], df[:, own]).astype(BF)
                if comm:
                    for o in range(4):
                        x, y = o % 2, o // 2
                        f = x * (1 - sec) + y * sec
                        s = y * (1 - sec) + x * sec
                        for q in range(4):
                            buf[t, q, f, s, i] = g[o * 192 + q * 48 : o * 192 + (q + 1) * 48]
                else:
                    buf[t, i] = g
            return carry

        lax.fori_loop(0, ff // width // 2, out_grad, 0)
        if comm:
            step(16 * t)
            step(16 * t + 1)

        o_loads = [pool_load(j, half, o_full.at[l], j * half) for j in range(2)]
        wo_load = rows_load(0, half, wo.at[l], 0)
        head_weights = [weight_load(j, half, wqkv.at[l], j * half) for j in range(3)]
        late_loads = [norm_load(l, NA_, 0, 2)] + o_loads + [wo_load] + head_weights[:2]

        def feed(jj, carry):
            for part in range(3):
                c = 3 * jj + part
                slot = c % 2
                for load in chunk_loads(l, slot, c):
                    load.wait()

                @pl.when(c + 1 < ffh // UNITS)
                def _():
                    for load in chunk_loads(l, 1 - slot, c + 1):
                        load.start()

                @pl.when(c + 1 == ffh // UNITS)
                def _():
                    for load in late_loads:
                        load.start()

                dm = dot_nt(df[...], wslot[slot, 0:UNITS])
                gbuf[0, :, 0:UNITS] = (dm * pool[2 * slot + 1, :, 0:UNITS].astype(F32)).astype(BF)
                gbuf[1, :, 0:UNITS] = (dm * pool[2 * slot, :, 0:UNITS].astype(F32)).astype(BF)
                acc[...] += dot_nt(gbuf[0, :, 0:UNITS], wpool[2 * slot, :, 0:UNITS]) + dot_nt(
                    gbuf[1, :, 0:UNITS], wpool[2 * slot + 1, :, 0:UNITS]
                )

                @pl.when(c == ffh // UNITS - 1)
                def _():
                    @pl.when(t > 0)
                    def _():
                        exchange(1).wait_send()

                    psend[...] = acc[...].astype(BF)
                    exchange(2 * t).start()

                unit = sec * ffh + c * UNITS
                spot = lanes_at(unit % width, UNITS)
                for k in range(2):
                    small[t, pl.ds(BIAS_IN + k * (ff // width) + unit // width, 1), spot] = column_total(
                        gbuf[k, :, 0:UNITS]
                    )
                    g = dot(tr[...], gbuf[k, :, 0:UNITS]).astype(BF)
                    n = 4 + 4 * jj + 2 * k
                    if part == 0:
                        put(t, n, 0, g)
                    elif part == 1:
                        put(t, n, 256, g[:, :128])
                        put(t, n + 1, 0, g[:, 128:])
                    else:
                        put(t, n + 1, 128, g)
                if comm:
                    step(16 * t + 2 + c)
            return carry

        lax.fori_loop(0, ffh // (3 * UNITS), feed, 0)
        norm_load(l, NA_, 1, 0).start()
        head_weights[2].start()

        for load in o_loads:
            load.wait()
        transpose_pool((0, 1))
        head_rows = [pool_load(j, half, qkv.at[l, j], 0) for j in range(3)]
        for load in head_rows:
            load.start()
        pool_load(3, half, acts.at[l, X_], 0).start()
        norm_load(l, NA_, 0, 2).wait()
        norm_load(l, NA_, 1, 0).wait()
        exchange(2 * t).wait_recv()

        def attn_norm(i, carry):
            rows = tile_rows(i)
            dh = df[rows, :].astype(F32) + (psend[rows, :].astype(F32) + precv[0, rows, :].astype(F32))
            norm_back((2, 0), i // (ntile // 2) == sec, dh, rows, RSTD_A, GAIN0, GAIN0, BIAS_A, BIAS_O)
            return carry

        lax.fori_loop(0, ntile, attn_norm, 0)

        wo_load.wait()

        @pl.when((t == 1) & (sec == 1))
        def _():
            x_store.wait()

        dy[:, 0:half] = dot_nt(df[...], wslot[0]).astype(BF)
        put(t, 12, 0, dot(tr[...], df[:, own]).astype(BF))
        if comm:
            step(16 * t + 8)
            step(16 * t + 9)

        for load in head_rows:
            load.wait()

        def row(r, carry):
            base = pl.multiple_of(r * seq, seq)
            kpad[HALO : HALO + seq, :] = pool[1, pl.ds(base, seq), :]
            vpad[HALO : HALO + seq, :] = pool[2, pl.ds(base, seq), :]
            lane = lax.broadcasted_iota(jnp.int32, (QB, 128), 1)

            for g in range(half // LANES):
                cols = slice(g * LANES, (g + 1) * LANES)
                for i in range(seq // QB):
                    rows = pl.ds(pl.multiple_of(base + i * QB, QB), QB)
                    far = away[r, i].astype(F32)
                    kw = kpad[i * QB : i * QB + KW, cols]
                    vw = vpad[i * QB : i * QB + KW, cols]
                    qs = stack_heads(pool[0, rows, cols] * BF(HEAD**-0.5))
                    os = stack_heads(dy[rows, cols])
                    s = dot_nt(qs, kw)
                    d = dot_nt(os, vw)
                    kept = stats[rows, :]
                    ps, ds = [], []
                    for h in range(GROUP):
                        part = slice(h * QB, (h + 1) * QB)
                        lse = jnp.sum(jnp.where(lane == g * GROUP + h, kept, 0.0), axis=-1, keepdims=True)
                        p = jnp.exp(s[part] + slope_of(sec, g, h) * far - lse)
                        pd = p * d[part]
                        ds.append((pd - p * jnp.sum(pd, axis=-1, keepdims=True)).astype(BF))
                        ps.append(p.astype(BF))
                    ds = jnp.concatenate(ds, axis=0)
                    ps = jnp.concatenate(ps, axis=0)
                    gbuf[0, rows, cols] = (merge_heads(dot(ds, kw)) * HEAD**-0.5).astype(BF)
                    dk, dv = dot_tn(ds, qs), dot_tn(ps, os)
                    if i == 0:
                        at, skip = pl.ds(base, HALO), HALO
                    else:
                        at, skip = pl.ds(pl.multiple_of(base + i * QB - HALO, HALO), QB), 0
                        dk = jnp.concatenate([dk[:QB] + left_k, dk[QB:]], axis=0)
                        dv = jnp.concatenate([dv[:QB] + left_v, dv[QB:]], axis=0)
                    gbuf[1, at, cols] = dk[skip:QB].astype(BF)
                    gbuf[2, at, cols] = dv[skip:QB].astype(BF)
                    left_k, left_v = dk[QB:], dv[QB:]
                at = pl.ds(pl.multiple_of(base + seq - HALO, HALO), HALO)
                gbuf[1, at, cols] = left_k[:HALO].astype(BF)
                gbuf[2, at, cols] = left_v[:HALO].astype(BF)
            if comm:
                step(16 * t + 10 + r)
            return carry

        lax.fori_loop(0, rows_n, row, 0)
        pool_load(0, half, acts.at[l, X_], half).start()
        for load in head_weights:
            load.wait()
        exchange(2 * t).wait_send()

        total = dot_nt(gbuf[0], wpool[0])
        for j in (1, 2):
            total += dot_nt(gbuf[j], wpool[j])
        psend[...] = total.astype(BF)
        exchange(2 * t + 1).start()
        small[t, BIAS_Q : BIAS_Q + 1, own] = column_total(gbuf[0])
        small[t, BIAS_V : BIAS_V + 1, own] = column_total(gbuf[2])
        pool_load(3, half, acts.at[l, X_], 0).wait()
        pool_load(0, half, acts.at[l, X_], half).wait()
        transpose_pool((3, 0))

        @pl.when(t == 0)
        def _():
            first_loads(0)

        if comm:
            step(16 * t + 12)
        for j in range(3):
            put(t, 13 + j, 0, dot(tr[...], gbuf[j]).astype(BF))
            if j < 2:

                @pl.when(t == 0)
                def _():
                    norm_load(0, NB_, j, j).start()

            if comm and j == 0:
                step(16 * t + 13)
        exchange(2 * t + 1).wait_recv()

        def result(i, carry):
            rows = tile_rows(i)
            dx = df[rows, :].astype(F32) + (psend[rows, :].astype(F32) + precv[1, rows, :].astype(F32))
            dy[rows, :] = dx.astype(BF)
            return carry

        lax.fori_loop(0, ntile, result, 0)

        @pl.when(sec == l)
        def _():
            x_store.start()

        if comm:
            step(16 * t + 14)
            step(16 * t + 15)
        return carry

    lax.fori_loop(0, 2, layer, 0)
    exchange(3).wait_send()

    @pl.when(sec == 0)
    def _():
        x_store.wait()

    if comm:
        mine = 1 - sec

        def vectors(stage):
            if stage == 0:
                return [remote(small.at[sec], v1, vs.at[0], vr.at[0], sib)]
            if stage == 1:
                return [remote(v1, v2, vs.at[1], vr.at[1], (sec, xp))]
            if stage == 2:
                return [remote(v2, v3, vs.at[2], vr.at[2], (sec, yp))]
            return [remote(v3, v4.at[d - 1], vs.at[2 + d], vr.at[2 + d], (sec, zp[d])) for d in (1, 2, 3)]

        def go(stage):
            for c in vectors(stage):
                c.start()

        def done(stage):
            for c in vectors(stage):
                c.wait()

        def rest(lo, hi):
            span(lo, hi, lambda i: step(i, False))

        def combine(stage, there, here):
            done(stage)
            there[...] += here
            go(stage + 1)

        last = 32 + AHEAD1 + AHEAD2
        go(0)
        rest(32, 34)
        combine(0, v1, small[mine])
        rest(34, 36)
        combine(1, v2, v1[...])
        rest(36, last)
        combine(2, v3, v2[...])
        for t in range(2):
            span(0, 16, lambda n, t=t: sent3(t, n))
        span(0, 16, lambda n: arrived(mine, n))
        done(3)
        small_out[...] = v3[...] + v4[0] + v4[1] + v4[2]
    else:
        store = pltpu.make_async_copy(buf, grads_out, gsem)
        store.start()
        small_out[...] = small[...]
        store.wait()


def run_backward(comm, cot, acts, o_full, m_full, qkv, pp, stats, away, wqkv, wo, win, wout, par):
    tokens, width = cot.shape
    ff = m_full.shape[2]
    half = width // 2
    dma = pltpu.SemaphoreType.DMA
    dx = jax.ShapeDtypeStruct((tokens, width), BF)
    if comm:
        r = width // 16
        small = jax.ShapeDtypeStruct((VECTORS, width), F32)
        grads = jax.ShapeDtypeStruct((16, 2, 4, r, PIECE), BF)
        special = [
            vm(2, 16, 2, 2, 4, r, PIECE),
            vm(2, 16, 2, 4, r, PIECE),
            vm(2, 16, 4, r, PIECE),
            vm(2, 5, 2, r, PIECE),
            vm(VECTORS, width, dtype=F32),
            vm(VECTORS, width, dtype=F32),
            vm(VECTORS, width, dtype=F32),
            vm(3, VECTORS, width, dtype=F32),
            dma((2, 16)), dma((2, 16)), dma((2, 16)), dma((2, 16)), dma((2, 5, 3)), dma((2, 5, 3)),
            dma((2, 16, 4)), dma((16, 2, 4)), dma((16,)),
            dma((6,)), dma((6,)),
        ]
    else:
        small = jax.ShapeDtypeStruct((2, VECTORS, width), F32)
        grads = jax.ShapeDtypeStruct((2, 16, width, PIECE), BF)
        special = [vm(2, 16, width, PIECE), dma]
    seq = away.shape[1] * QB
    scratch = special + [
        vm(tokens, width, dtype=F32),
        vm(tokens, width),
        vm(tokens, width),
        vm(width, tokens),
        vm(width, tokens),
        vm(2, VECTORS, width, dtype=F32),
        vm(tokens, 128, dtype=F32),
        vm(4, tokens, PIECE),
        vm(4, width, PIECE),
        vm(2, half, width),
        vm(3, tokens, half),
        vm(seq + 2 * HALO, half),
        vm(seq + 2 * HALO, half),
        vm(tokens, width),
        vm(2, tokens, width),
        dma((4,)), dma((4,)), dma((2,)), dma((3,)), dma, dma, dma, dma((4,)), dma((4,)),
    ]
    return pl.pallas_call(
        functools.partial(bwd_kernel, comm),
        out_shape=(dx, small, grads),
        in_specs=[any_spec()] * 7 + [vmem_spec()] + [any_spec()] * 4 + [vmem_spec()],
        out_specs=(any_spec(), vmem_spec(), any_spec()),
        scratch_shapes=scratch,
        compiler_params=pltpu.CompilerParams(
            collective_id=2, has_side_effects=True, vmem_limit_bytes=64 << 20
        ),
        name="backward",
    )(cot, acts, o_full, m_full, qkv, pp, stats, away, wqkv, wo, win, wout, par)


def results_kernel(shares, vectors, y, dx, y_out, dx_out, fq, fo, fi, fu, gain_out, bias_out, inner_out, land, stage, rows_in, lsem, fsem, csem):
    me = lax.axis_index("dp")
    rows, width = fo.shape
    half, ff = width // 2, fi.shape[1] // 2
    ffh = ff // 2
    arrivals = [pltpu.make_async_copy(v, rows_in.at[i], csem.at[i]) for i, v in enumerate((y, dx))]
    copies = [pltpu.make_async_copy(rows_in.at[i], v, csem.at[2 + i]) for i, v in enumerate((y_out, dx_out))]
    loads = [pltpu.make_async_copy(shares.at[n], land.at[n], lsem.at[n]) for n in range(16)]
    for c in arrivals + loads:
        c.start()
    for i in range(2):
        arrivals[i].wait()
        copies[i].start()

    def place(n, k):
        if n < 4:
            return fu.at[n * rows : (n + 1) * rows, k * half : (k + 1) * half]
        if n < 12:
            jj, g, i = (n - 4) // 4, (n - 4) // 2 % 2, n % 2
            start = g * ff + k * ffh + (2 * jj + i) * PIECE
            return fi.at[:, start : start + PIECE]
        if n == 12:
            return fo.at[:, k * half : (k + 1) * half]
        start = (n - 13) * width + k * half
        return fq.at[:, start : start + half]

    stores = []
    for n in range(16):
        loads[n].wait()
        for k in range(2):
            total = land[n, k, 0].astype(F32) + land[n, k, 1].astype(F32)
            if n % EARLY != 1:
                total = total + (land[n, k, 2].astype(F32) + land[n, k, 3].astype(F32))
            stage[n, k] = total
            stores.append(pltpu.make_async_copy(stage.at[n, k], place(n, k), fsem.at[n, k]))
            stores[-1].start()
    turned = pltpu.roll(vectors[0:8, :], (width - me * rows) % width, axis=1)
    gain_out[...] = turned[0:2, 0:rows]
    for j in range(6):
        bias_out[j] = turned[2 + j : 3 + j, 0:rows]
    line = vectors[pl.ds(8 + me // 2, 1), :]
    inner_out[...] = jnp.where(me % 2 == 0, line[:, :half], line[:, half:])
    for c in stores + copies:
        c.wait()


def run_results(shares, vectors, y, dx, ff):
    _, _, _, rows, half = shares.shape
    width = 2 * half
    dma = pltpu.SemaphoreType.DMA

    def out(*shape):
        return jax.ShapeDtypeStruct(shape, F32)

    return pl.pallas_call(
        results_kernel,
        out_shape=(
            jax.ShapeDtypeStruct(y.shape, BF), jax.ShapeDtypeStruct(dx.shape, BF),
            out(rows, 3 * width), out(rows, width), out(rows, 2 * ff), out(ff // 16, width),
            out(2, rows), out(6, 1, rows), out(1, 2 * ff // 16),
        ),
        in_specs=[any_spec(), vmem_spec(), any_spec(), any_spec()],
        out_specs=tuple([any_spec()] * 6 + [vmem_spec()] * 3),
        scratch_shapes=[
            vm(*shares.shape), vm(16, 2, rows, half, dtype=F32), vm(2, *y.shape), dma((16,)), dma((16, 2)), dma((4,)),
        ],
        compiler_params=pltpu.CompilerParams(vmem_limit_bytes=60 << 20),
        name="results",
    )(shares, vectors, y, dx)


def assemble(halves, width, ff):
    def columns(v):
        return jnp.concatenate(v, axis=1)

    gu = columns([h[:4].reshape(ff, PIECE) for h in halves])
    inner = [
        columns([h[4 + 4 * jj + 2 * k + i] for jj in range(2) for i in range(2)]) for k in range(2) for h in halves
    ]
    gi = columns(inner)
    go = columns([h[12] for h in halves])
    gq = columns([h[13 + j] for j in range(3) for h in halves])
    return gq, go, gi, gu


def shards(comm, hidden, segs, w_qkv, w_o, w_in, w_out, gains, biases, b_in, cot):
    w_qkv, w_o, w_in, w_out, gains = (v[0] for v in (w_qkv, w_o, w_in, w_out, gains))
    biases = jnp.transpose(biases, (1, 0, 2))
    micro, _, seq, width = hidden.shape
    ff = w_out.shape[0]
    tokens = micro * seq
    y, acts, o_full, m_full, qkv, pp, stats, wqkv2, wo2, win2, wout2, par2, away = run_forward(
        hidden.reshape(micro, seq, width), segs, w_qkv, w_o, w_in, w_out, gains, biases, b_in
    )
    dx, small, grads = run_backward(
        comm, cot.reshape(tokens, width), acts.reshape(2, 4, tokens, width), o_full.reshape(2, tokens, width),
        m_full.reshape(2, tokens, ff), qkv.reshape(2, 3, tokens, width // 2), pp.reshape(2, 2, tokens, ff // 2),
        stats.reshape(2, tokens, 128), away, wqkv2, wo2, win2, wout2, par2,
    )
    if comm:
        y, dx, gq, go, gi, gu, gain, bias, inner = run_results(grads, small, y.reshape(tokens, width), dx, ff)
        return (
            y.reshape(1, *hidden.shape), dx.reshape(1, *hidden.shape), gq[None], go[None], gi[None], gu[None],
            gain[None], jnp.transpose(bias, (1, 0, 2)), inner,
        )
    owners, me = lax.axis_size("dp"), lax.axis_index("dp")
    first = lax.axis_index("section") == 0
    swap = [(0, 1), (1, 0)]

    def pick(v):
        own = jnp.where(first, v[1], v[0])
        return own, lax.ppermute(jnp.where(first, v[0], v[1]), "section", swap)

    own, other = pick(grads)
    halves = [jnp.where(first, own, other), jnp.where(first, other, own)]

    def share(v):
        parts = v.reshape(owners, v.shape[0] // owners, v.shape[1])
        got = lax.all_to_all(parts, "dp", split_axis=0, concat_axis=0, tiled=True)
        return jnp.sum(got.astype(F32), axis=0)

    gq, go, gi, gu = (share(v) for v in assemble(halves, width, ff))
    own, other = pick(small)
    small = lax.psum(own + other, "dp")
    part = width // owners
    mine = lax.dynamic_slice_in_dim(small[:8], me * part, part, axis=1)
    inner = lax.dynamic_slice_in_dim(small[8:].reshape(1, 2 * ff), me * (2 * ff // owners), 2 * ff // owners, axis=1)
    return (
        y.reshape(1, *hidden.shape), dx.reshape(1, *hidden.shape), gq[None], go[None], gi[None], gu[None],
        mine[None, :2], mine[None, 2:], inner,
    )


def solution(mesh):
    rows = P(None, "dp", None, None)
    layer = P("section", None, None)
    comm = mesh.shape["dp"] == 16
    return jax.shard_map(
        functools.partial(shards, comm),
        mesh=mesh,
        in_specs=(rows, P(None, "dp", None)) + (layer,) * 6 + (P("section", None), rows),
        out_specs=(
            P("section", None, "dp", None, None),
            P("section", None, "dp", None, None),
            P("section", "dp", None),
            P("section", "dp", None),
            P("section", "dp", None),
            P("section", "dp", None),
            P("section", None, "dp"),
            P("section", None, "dp"),
            P("section", "dp"),
        ),
        check_vma=False,
    )
```

```python
import functools
import math

import jax
import jax.numpy as jnp
from jax import lax
from jax.experimental import pallas as pl
from jax.experimental.pallas import tpu as pltpu
from jax.sharding import PartitionSpec as P

HEADS = 12
HEAD = 64
GROUP = 2
LANES = GROUP * HEAD
QB = 128
HALO = 64
KW = QB + 2 * HALO
EPS = 1e-05
MASKED = -1.0e30
TILE = 256
UNITS = 256
PIECE = 384
BF = jnp.bfloat16
F32 = jnp.float32
MESH = pl.DeviceIdType.MESH
NT = (((1,), (1,)), ((), ()))
TN = (((0,), (0,)), ((), ()))
H_, NA_, NB_, X_ = range(4)
M_, P1_, P2_ = range(3)
GAIN0, GAIN1, BIAS_Q, BIAS_V, BIAS_O, BIAS_A, BIAS_F, BIAS_B, BIAS_IN = range(9)
VECTORS = 16
FEED = 512
AHEAD1, AHEAD2 = 3, 3
EARLY = 3
RSTD_A, RSTD_B = HEADS, HEADS + 1


def slope_list(head_count):
    base = 2 ** int(math.floor(math.log2(head_count)))
    leading = [2.0 ** (-8.0 * (k + 1) / base) for k in range(base)]
    trailing = [2.0 ** (-4.0 * (2 * k + 1) / base) for k in range(head_count - base)]
    return leading + trailing


def dot(a, b):
    return jnp.dot(a, b, preferred_element_type=F32)


def dot_nt(a, b):
    return lax.dot_general(a, b, NT, preferred_element_type=F32)


def dot_tn(a, b):
    return lax.dot_general(a, b, TN, preferred_element_type=F32)


def normalize(v):
    c = v - jnp.mean(v, axis=-1, keepdims=True)
    rstd = lax.rsqrt(jnp.mean(c * c, axis=-1, keepdims=True) + EPS)
    return c * rstd, rstd


def stack_heads(v):
    head = lax.broadcasted_iota(jnp.int32, v.shape, 1) // HEAD
    zero = jnp.zeros_like(v)
    return jnp.concatenate([jnp.where(head == h, v, zero) for h in range(GROUP)], axis=0)


def merge_heads(r):
    rows = r.shape[0] // GROUP
    head = lax.broadcasted_iota(jnp.int32, (rows, r.shape[1]), 1) // HEAD
    out = r[:rows]
    for h in range(1, GROUP):
        out = jnp.where(head == h, r[h * rows : (h + 1) * rows], out)
    return out


def fill_away(away, segs):
    micro, _, seq = segs.shape
    r = lax.broadcasted_iota(jnp.int32, (QB, KW), 0)
    c = lax.broadcasted_iota(jnp.int32, (QB, KW), 1)
    apart = -jnp.abs(r + HALO - c).astype(F32)
    outside = jnp.full((QB, 128), -1.0, F32)
    for m in range(micro):
        seg = jnp.broadcast_to(segs[m].astype(F32), (QB, seq))
        keys = pltpu.roll(jnp.concatenate([outside, seg, outside], axis=1), seq + 256 - HALO, axis=1)
        for i in range(seq // QB):
            own = seg[:, i * QB : (i + 1) * QB].T
            own = jnp.concatenate([own, own], axis=1)
            same = own == keys[:, i * QB : i * QB + KW]
            away[m, i] = jnp.where(same, apart, MASKED).astype(BF)


def slope_of(sec, g, h):
    table = slope_list(HEADS)
    return jnp.where(sec == 0, table[g * GROUP + h], table[HEADS // 2 + g * GROUP + h]).astype(F32)


def tile_rows(t):
    return pl.ds(pl.multiple_of(t * TILE, TILE), TILE)


def lanes_at(start, count):
    return pl.ds(pl.multiple_of(start, 128), count)


def fwd_kernel(
    hid, segs, wqkv_h, wo_h, win_h, wout_h, gains_in, biases_in, bin_in,
    y_out, acts_out, o_out, m_out, qkv_out, p_out, stats_out,
    wqkv_out, wo_out, win_out, wout_out, par_out, away_out,
    wqkv, wo, win, wout, par, bin_, xy, qkvs, os_, hs, big, psend, precv, acc, kpad, vpad, held, away, stats,
    lsem, rsend, rrecv, wsave, hsem, ysem, asem, qsem, osem, osend, orecv, bsem, msend, mrecv, tsem, ssend, srecv,
    parsem, awaysem,
):
    dp = lax.axis_index("dp")
    sec = lax.axis_index("section")
    _, micro, seq, width = xy.shape
    half, ffh, ff = wo.shape[1], wout.shape[1], wout_h.shape[0]
    sib = (1 - sec, dp)

    parts = []
    for j in range(3):
        parts.append((wqkv_h, wqkv, lambda c, j=j: (slice(None), lanes_at(j * width + c * half, half)),
                      (slice(None), slice(j * half, (j + 1) * half))))
    parts.append((wo_h, wo, lambda c: (pl.ds(pl.multiple_of(c * half, 128), half), slice(None)), (slice(None), slice(None))))
    for j in range(2):
        parts.append((win_h, win, lambda c, j=j: (slice(None), lanes_at(j * ff + c * ffh, ffh)),
                      (slice(None), slice(j * ffh, (j + 1) * ffh))))
    parts.append((wout_h, wout, lambda c: (pl.ds(pl.multiple_of(c * ffh, 128), ffh), slice(None)), (slice(None), slice(None))))

    def own_part(i):
        src, dst, pick, place = parts[i]
        return pltpu.make_async_copy(src.at[pick(sec)], dst.at[(sec, *place)], lsem.at[i])

    def other_part(i):
        src, dst, pick, place = parts[i]
        return pltpu.make_async_remote_copy(
            src_ref=src.at[pick(1 - sec)], dst_ref=dst.at[(sec, *place)],
            send_sem=rsend.at[i], recv_sem=rrecv.at[i], device_id=sib, device_id_type=MESH,
        )

    def other_vectors():
        return [
            pltpu.make_async_remote_copy(
                src_ref=v.at[sec], dst_ref=v.at[sec], send_sem=rsend.at[7 + i], recv_sem=rrecv.at[7 + i],
                device_id=sib, device_id_type=MESH,
            )
            for i, v in enumerate((par, bin_))
        ]

    def x_load(m):
        return pltpu.make_async_copy(hid.at[m], xy.at[0, m], hsem.at[m])

    for m in range(micro):
        x_load(m).start()
    for i in range(7):
        own_part(i).start()
    par[sec, 0:2] = gains_in[...]
    for j in range(6):
        par[sec, 2 + j : 3 + j] = biases_in[j]
    bin_[sec] = bin_in[...]
    barrier = pltpu.get_barrier_semaphore()
    pl.semaphore_signal(barrier, inc=1, device_id=sib, device_id_type=MESH)
    pl.semaphore_wait(barrier, 1)
    for c in other_vectors():
        c.start()
    for i in range(7):
        other_part(i).start()
    fill_away(away, segs)
    away_save = pltpu.make_async_copy(away, away_out, awaysem)
    away_save.start()
    for pad in (kpad, vpad):
        pad[0:HALO, :] = jnp.zeros((HALO, half), BF)
        pad[HALO + seq :, :] = jnp.zeros((HALO, half), BF)
    for m in range(micro):
        x_load(m).wait()

    def need(l, which):
        @pl.when(l == sec)
        def _():
            for i in which:
                own_part(i).wait()

        @pl.when(l != sec)
        def _():
            for i in which:
                other_part(i).wait_recv()

    def save(kind, l, m):
        src = xy.at[l, m] if kind == X_ else hs.at[kind, m]
        return pltpu.make_async_copy(src, acts_out.at[l, kind, m], asem.at[kind, l, m])

    def save_qkv(kind, l, m):
        return pltpu.make_async_copy(qkvs.at[m, kind], qkv_out.at[l, kind, m], qsem.at[kind, l, m])

    def save_o(l, m):
        return pltpu.make_async_copy(os_.at[m], o_out.at[l, m, :, lanes_at(sec * half, half)], osem.at[l, m])

    def share_o(l, m):
        return pltpu.make_async_remote_copy(
            src_ref=os_.at[m], dst_ref=o_out.at[l, m, :, lanes_at(sec * half, half)],
            send_sem=osend.at[l, m], recv_sem=orecv.at[l, m], device_id=sib, device_id_type=MESH,
        )

    def save_big(kind, l, m):
        if kind == M_:
            dst = m_out.at[l, m, :, lanes_at(sec * ffh, ffh)]
        else:
            dst = p_out.at[l, kind - 1, m]
        return pltpu.make_async_copy(big.at[m, kind], dst, bsem.at[kind, l, m])

    def share_m(l, m):
        return pltpu.make_async_remote_copy(
            src_ref=big.at[m, M_], dst_ref=m_out.at[l, m, :, lanes_at(sec * ffh, ffh)],
            send_sem=msend.at[l, m], recv_sem=mrecv.at[l, m], device_id=sib, device_id_type=MESH,
        )

    def save_stats(l, m):
        return pltpu.make_async_copy(stats.at[l, m], stats_out.at[l, m], tsem.at[l, m])

    def save_y(m):
        return pltpu.make_async_copy(xy.at[sec + 1, m], y_out.at[m], ysem.at[m])

    def partial(phase, l, m):
        return pltpu.make_async_remote_copy(
            src_ref=psend.at[phase, m], dst_ref=precv.at[phase, l, m],
            send_sem=ssend.at[phase, l, m], recv_sem=srecv.at[phase, l, m], device_id=sib, device_id_type=MESH,
        )

    def weight_saves(l):
        pairs = ((wqkv, wqkv_out), (wo, wo_out), (win, win_out), (wout, wout_out))
        return [pltpu.make_async_copy(s.at[l], d.at[l], wsave.at[i, l]) for i, (s, d) in enumerate(pairs)]

    par_save = pltpu.make_async_copy(par, par_out, parsem)

    def attend(l, m):
        @pl.when(m == 0)
        def _():
            need(l, (0, 1, 2))

            @pl.when(l != sec)
            def _():
                for c in other_vectors():
                    c.wait_recv()

        @pl.when(l > 0)
        def _():
            for kind in range(3):
                save_qkv(kind, l - 1, m).wait()
            save_o(l - 1, m).wait()
            share_o(l - 1, m).wait_send()
            partial(0, l - 1, m).wait_send()

        save(X_, l, m).start()
        bias_q = par[l, BIAS_Q : BIAS_Q + 1, lanes_at(sec * half, half)]
        bias_v = par[l, BIAS_V : BIAS_V + 1, lanes_at(sec * half, half)]

        r = dot(xy[l, m], wqkv[l])
        q = (r[:, :half] + bias_q).astype(BF)
        k = r[:, half : 2 * half].astype(BF)
        v = (r[:, 2 * half :] + bias_v).astype(BF)
        for j, w in enumerate((q, k, v)):
            qkvs[m, j] = w
        kpad[HALO : HALO + seq, :] = k
        vpad[HALO : HALO + seq, :] = v
        for kind in range(3):
            save_qkv(kind, l, m).start()

        lane = lax.broadcasted_iota(jnp.int32, (QB, 128), 1)
        for g in range(half // LANES):
            cols = slice(g * LANES, (g + 1) * LANES)
            for i in range(seq // QB):
                rows = slice(i * QB, (i + 1) * QB)
                far = away[m, i].astype(F32)
                qs = stack_heads(qkvs[m, 0, rows, cols] * BF(HEAD**-0.5))
                s = dot_nt(qs, kpad[i * QB : i * QB + KW, cols])
                probs = []
                kept = stats[l, m, rows, :]
                for h in range(GROUP):
                    sh = s[h * QB : (h + 1) * QB] + slope_of(sec, g, h) * far
                    top = jnp.max(sh, axis=-1, keepdims=True)
                    e = jnp.exp(sh - top)
                    total = jnp.sum(e, axis=-1, keepdims=True)
                    probs.append((e * (1.0 / total)).astype(BF))
                    kept = jnp.where(lane == g * GROUP + h, top + jnp.log(total), kept)
                stats[l, m, rows, :] = kept
                held[:, i * KW : (i + 1) * KW] = jnp.concatenate(probs, axis=0)
            for i in range(seq // QB):
                rows = slice(i * QB, (i + 1) * QB)
                r = dot(held[:, i * KW : (i + 1) * KW], vpad[i * QB : i * QB + KW, cols])
                os_[m, rows, cols] = merge_heads(r).astype(BF)

        save_o(l, m).start()
        share_o(l, m).start()

        @pl.when(m == 0)
        def _():
            need(l, (3,))

        psend[0, m] = dot(os_[m], wo[l]).astype(BF)
        partial(0, l, m).start()

    def feed(l, m):
        @pl.when(m == 0)
        def _():
            need(l, (4, 5, 6))
            for c in weight_saves(l):
                c.start()

        @pl.when(l > 0)
        def _():
            save(H_, l - 1, m).wait()
            save(NA_, l - 1, m).wait()
            for kind in range(3):
                save_big(kind, l - 1, m).wait()
            share_m(l - 1, m).wait_send()
            partial(1, l - 1, m).wait_send()

        partial(0, l, m).wait_recv()
        lane = lax.broadcasted_iota(jnp.int32, (TILE, 128), 1)

        def norm(t, carry):
            rows = tile_rows(t)
            a = xy[l, m, rows, :].astype(F32) + (
                psend[0, m, rows, :].astype(F32) + precv[0, l, m, rows, :].astype(F32) + par[l, BIAS_O : BIAS_O + 1, :]
            )
            n, rstd = normalize(a)
            hs[NA_, m, rows, :] = n.astype(BF)
            hs[H_, m, rows, :] = (n * par[l, GAIN0 : GAIN0 + 1, :] + par[l, BIAS_A : BIAS_A + 1, :]).astype(BF)
            stats[l, m, rows, :] = jnp.where(lane == RSTD_A, rstd, stats[l, m, rows, :])
            return carry

        lax.fori_loop(0, seq // TILE, norm, 0)
        save(H_, l, m).start()
        save(NA_, l, m).start()
        h = hs[H_, m]
        for c in range(ffh // FEED):
            cols = slice(c * FEED, (c + 1) * FEED)
            unit = sec * ffh + c * FEED
            gate = dot(h, win[l, :, cols]) + bin_[l, :, lanes_at(unit, FEED)]
            up = dot(h, win[l, :, ffh + c * FEED : ffh + (c + 1) * FEED]) + bin_[l, :, lanes_at(ff + unit, FEED)]
            cdf = 0.5 + 0.5 * lax.erf(gate * (0.5**0.5))
            act = gate * cdf
            slope = cdf + gate * (jnp.exp(gate * gate * -0.5) * (2.0 * math.pi) ** -0.5)
            mixed = (act * up).astype(BF)
            big[m, M_, :, cols] = mixed
            big[m, P1_, :, cols] = act.astype(BF)
            big[m, P2_, :, cols] = (up * slope).astype(BF)
            down = dot(mixed, wout[l, cols, :])
            acc[...] = down if c == 0 else acc[...] + down

        psend[1, m] = acc[...].astype(BF)
        partial(1, l, m).start()
        for kind in range(3):
            save_big(kind, l, m).start()
        share_m(l, m).start()

    def finish(l, m):
        @pl.when(l > 0)
        def _():
            save(NB_, l - 1, m).wait()

        partial(1, l, m).wait_recv()
        lane = lax.broadcasted_iota(jnp.int32, (TILE, 128), 1)

        def norm(t, carry):
            rows = tile_rows(t)
            b = hs[H_, m, rows, :].astype(F32) + (
                psend[1, m, rows, :].astype(F32) + precv[1, l, m, rows, :].astype(F32) + par[l, BIAS_F : BIAS_F + 1, :]
            )
            n, rstd = normalize(b)
            hs[NB_, m, rows, :] = n.astype(BF)
            xy[l + 1, m, rows, :] = (n * par[l, GAIN1 : GAIN1 + 1, :] + par[l, BIAS_B : BIAS_B + 1, :]).astype(BF)
            stats[l, m, rows, :] = jnp.where(lane == RSTD_B, rstd, stats[l, m, rows, :])
            return carry

        lax.fori_loop(0, seq // TILE, norm, 0)
        save(NB_, l, m).start()
        save_stats(l, m).start()

        @pl.when(l == sec)
        def _():
            save_y(m).start()

    def layer(l, carry):
        def first(m, carry):
            @pl.when(l > 0)
            def _():
                finish(l - 1, m)

            attend(l, m)
            return carry

        lax.fori_loop(0, micro, first, 0)

        def second(m, carry):
            feed(l, m)
            return carry

        lax.fori_loop(0, micro, second, 0)
        return carry

    lax.fori_loop(0, 2, layer, 0)
    par_save.start()

    def last(m, carry):
        finish(1, m)
        return carry

    lax.fori_loop(0, micro, last, 0)

    def drain(m, carry):
        for kind in range(3):
            save_qkv(kind, 1, m).wait()
            save_big(kind, 1, m).wait()
        for kind in (H_, NA_, NB_):
            save(kind, 1, m).wait()
        save_o(1, m).wait()
        share_o(1, m).wait_send()
        share_m(1, m).wait_send()
        for phase in range(2):
            partial(phase, 1, m).wait_send()
        for l in range(2):
            save(X_, l, m).wait()
            save_stats(l, m).wait()
            share_o(l, m).wait_recv()
            share_m(l, m).wait_recv()
        save_y(m).wait()
        return carry

    lax.fori_loop(0, micro, drain, 0)
    for l in range(2):
        for c in weight_saves(l):
            c.wait()
    for i in range(7):
        other_part(i).wait_send()
    for c in other_vectors():
        c.wait_send()
    par_save.wait()
    away_save.wait()


def any_spec():
    return pl.BlockSpec(memory_space=pl.ANY)


def vmem_spec():
    return pl.BlockSpec(memory_space=pltpu.VMEM)


def smem_spec():
    return pl.BlockSpec(memory_space=pltpu.SMEM)


def vm(*shape, dtype=BF):
    return pltpu.VMEM(shape, dtype)


def run_forward(hid, segs, w_qkv, w_o, w_in, w_out, gains, biases, b_in):
    micro, seq, width = hid.shape
    ff = w_out.shape[0]
    half, ffh = width // 2, ff // 2
    dma = pltpu.SemaphoreType.DMA

    def out(*shape, dtype=BF):
        return jax.ShapeDtypeStruct(shape, dtype)

    shapes = (
        out(micro, seq, width),
        out(2, 4, micro, seq, width),
        out(2, micro, seq, width),
        out(2, micro, seq, ff),
        out(2, 3, micro, seq, half),
        out(2, 2, micro, seq, ffh),
        out(2, micro, seq, 128, dtype=F32),
        out(2, width, 3 * half),
        out(2, half, width),
        out(2, width, 2 * ffh),
        out(2, ffh, width),
        out(2, 8, width, dtype=F32),
        out(micro, seq // QB, QB, KW),
    )
    return pl.pallas_call(
        fwd_kernel,
        out_shape=shapes,
        in_specs=[any_spec(), vmem_spec()] + [any_spec()] * 4 + [vmem_spec()] * 3,
        out_specs=tuple([any_spec()] * len(shapes)),
        scratch_shapes=[
            vm(2, width, 3 * half),
            vm(2, half, width),
            vm(2, width, 2 * ffh),
            vm(2, ffh, width),
            vm(2, 8, width, dtype=F32),
            vm(2, 1, 2 * ff, dtype=F32),
            vm(3, micro, seq, width),
            vm(micro, 3, seq, half),
            vm(micro, seq, half),
            vm(3, micro, seq, width),
            vm(micro, 3, seq, ffh),
            vm(2, micro, seq, width),
            vm(2, 2, micro, seq, width),
            vm(seq, width, dtype=F32),
            vm(seq + 2 * HALO, half),
            vm(seq + 2 * HALO, half),
            vm(GROUP * QB, seq // QB * KW),
            vm(micro, seq // QB, QB, KW),
            vm(2, micro, seq, 128, dtype=F32),
            dma((7,)), dma((9,)), dma((9,)), dma((4, 2)), dma((micro,)), dma((micro,)), dma((4, 2, micro)),
            dma((3, 2, micro)), dma((2, micro)), dma((2, micro)), dma((2, micro)), dma((3, 2, micro)),
            dma((2, micro)), dma((2, micro)), dma((2, micro)), dma((2, 2, micro)), dma((2, 2, micro)), dma, dma,
        ],
        compiler_params=pltpu.CompilerParams(
            collective_id=1, has_side_effects=True, vmem_limit_bytes=62 << 20
        ),
        name="forward",
    )(hid, segs, w_qkv, w_o, w_in, w_out, gains, biases, b_in)


def column_total(v):
    return jnp.sum(v.astype(F32), axis=0, keepdims=True)


def bwd_kernel(
    comm, cot, acts, o_full, m_full, qkv, pp, stats_h, away, wqkv, wo, win, wout, par, *refs
):
    if comm:
        (dx_out, small_out, shares, *rest) = refs
        (buf, l1, l2, lz, v1, v2, v3, v4, s1, r1, s2, r2, sz, rz, s3, r3, ksem, vs, vr, *rest) = rest
    else:
        (dx_out, small_out, grads_out, *rest) = refs
        (buf, gsem, *rest) = rest
    (acc, df, dy, tr, mt, small, stats, pool, wpool, wslot, gbuf, kpad, vpad, psend, precv,
     poolsem, wsem, usem, nsem, ssem, ysem, xsem, esend, erecv) = rest
    dp = lax.axis_index("dp")
    sec = lax.axis_index("section")
    sib = (1 - sec, dp)
    tokens, width = df.shape
    rows_n, seq = away.shape[0], away.shape[1] * QB
    ff = m_full.shape[2]
    half, ffh = width // 2, ff // 2
    ntile = tokens // TILE
    own = lanes_at(sec * half, half)

    if comm:
        bx, by, bz = dp % 2, (dp // 2) % 2, dp // 4
        xp = dp + 1 - 2 * bx
        yp = dp + 2 - 4 * by
        zp = [dp] + [((bz + d) % 4) * 4 + dp % 4 for d in range(1, 4)]
        near = xp * (1 - sec) + yp * sec
        far = yp * (1 - sec) + xp * sec
        b1 = bx * (1 - sec) + by * sec
        b2 = by * (1 - sec) + bx * sec
        greet = [(sec, xp), (sec, yp)] + [(sec, z) for z in zp[1:]] + [(1 - sec, z) for z in zp[1:] + [xp, yp]]
    else:
        greet = []

    def pool_load(slot, count, src, first):
        return pltpu.make_async_copy(src.at[:, lanes_at(first, count)], pool.at[slot, :, 0:count], poolsem.at[slot])

    def weight_load(slot, count, src, first):
        return pltpu.make_async_copy(src.at[:, lanes_at(first, count)], wpool.at[slot, :, 0:count], wsem.at[slot])

    def rows_load(slot, count, src, first):
        return pltpu.make_async_copy(
            src.at[pl.ds(pl.multiple_of(first, 128), count), :], wslot.at[slot, 0:count], usem.at[slot]
        )

    def norm_load(l, kind, j, slot):
        return pltpu.make_async_copy(acts.at[l, kind, :, j * half : (j + 1) * half], gbuf.at[slot], nsem.at[slot])

    def stats_load(l):
        return pltpu.make_async_copy(stats_h.at[l], stats, ssem)

    def m_loads(l, i, odd):
        return [
            pltpu.make_async_copy(
                m_full.at[l, :, lanes_at((2 * i + j) * PIECE, PIECE)],
                gbuf.at[j] if odd else pool.at[2 + j],
                nsem.at[j] if odd else poolsem.at[2 + j],
            )
            for j in range(2)
        ]

    def h_loads(l):
        return [pool_load(j, half, acts.at[l, H_], j * half) for j in range(2)]

    def chunk_loads(l, slot, c):
        first = c * UNITS
        return [
            weight_load(2 * slot, UNITS, win.at[l], first),
            weight_load(2 * slot + 1, UNITS, win.at[l], ffh + first),
            rows_load(slot, UNITS, wout.at[l], first),
            pool_load(2 * slot, UNITS, pp.at[l, 0], first),
            pool_load(2 * slot + 1, UNITS, pp.at[l, 1], first),
        ]

    def exchange(e):
        return pltpu.make_async_remote_copy(
            src_ref=psend, dst_ref=precv.at[e % 2], send_sem=esend.at[e], recv_sem=erecv.at[e],
            device_id=sib, device_id_type=MESH,
        )

    x_store = pltpu.make_async_copy(dy, dx_out, xsem)
    cot_load = pltpu.make_async_copy(cot, dy, ysem)
    cot_load.start()

    def first_loads(l):
        stats_load(l).start()
        for load in m_loads(l, 0, False) + h_loads(l):
            load.start()

    for j in range(2):
        norm_load(1, NB_, j, j).start()
    first_loads(1)
    barrier = pltpu.get_barrier_semaphore()
    for peer in [sib] + greet:
        pl.semaphore_signal(barrier, inc=1, device_id=peer, device_id_type=MESH)
    pl.semaphore_wait(barrier, 1 + len(greet))

    def put(t, n, lane, value):
        lanes = slice(lane, lane + value.shape[1])
        if not comm:
            buf[t, n, :, lanes] = value
            return
        share = value.shape[0] // 16
        for o in range(16):
            x, y, z = o % 2, (o // 2) % 2, o // 4
            f = x * (1 - sec) + y * sec
            s = y * (1 - sec) + x * sec
            buf[t, n, f, s, z, :, lanes] = value[o * share : (o + 1) * share]

    if comm:

        def remote(src, dst, ss, rs, to):
            return pltpu.make_async_remote_copy(
                src_ref=src, dst_ref=dst, send_sem=ss, recv_sem=rs, device_id=to, device_id_type=MESH
            )

        def stage1(t, n):
            return remote(buf.at[t, n, 1 - b1], l1.at[t, n], s1.at[t, n], r1.at[t, n], (sec, near))

        def stage2(t, n):
            return remote(buf.at[t, n, b1, 1 - b2], l2.at[t, n], s2.at[t, n], r2.at[t, n], (sec, far))

        def early(n):
            return n % EARLY == 1

        def stagez(t, n, d):
            dst = l2.at[t, n, pl.ds(2 * (d - 1), 2)] if d < 3 else lz.at[t, n // EARLY]
            return remote(
                buf.at[t, n, b1, :, (bz + d) % 4], dst, sz.at[t, n // EARLY, d - 1], rz.at[t, n // EARLY, d - 1], (sec, zp[d])
            )

        def stage3(t, n, d):
            return remote(
                buf.at[t, n, b1, b2, (bz + d) % 4], shares.at[n, sec, d], s3.at[t, n, d], r3.at[n, sec, d], (1 - t, zp[d])
            )

        def stage3_far(t, n):
            return remote(
                buf.at[t, n, b1, 1 - b2, bz], shares.at[n, sec, 1], s3.at[t, n, 1], r3.at[n, sec, 1], (1 - t, far)
            )

        def keep(t, n):
            return pltpu.make_async_copy(buf.at[t, n, b1, b2, bz], shares.at[n, sec, 0], ksem.at[n])

        def landed(n, k, d):
            return remote(shares.at[n, k, d], shares.at[n, k, d], s3.at[0, n, d], r3.at[n, k, d], (1 - sec, dp))

        def join(t, n, second):
            for z in range(4):
                at = (t, n, b1, second, z)
                buf[at] = (buf[at].astype(F32) + l1[t, n, second, z].astype(F32)).astype(BF)

        def after1(t, n):
            stage1(t, n).wait()
            join(t, n, 1 - b2)

            @pl.when(early(n))
            def _():
                join(t, n, b2)
                for d in (1, 2, 3):
                    stagez(t, n, d).start()

            @pl.when(~early(n))
            def _():
                stage2(t, n).start()
                join(t, n, b2)

        def own_share(t, n):
            @pl.when(sec != 1 - t)
            def _():
                stage3(t, n, 0).start()

            @pl.when(sec == 1 - t)
            def _():
                keep(t, n).start()

        def after2(t, n):
            @pl.when(early(n))
            def _():
                for d in (1, 2, 3):
                    stagez(t, n, d).wait()
                for order in (0, 1):
                    second = (1 - b2) if order == 0 else b2
                    at = (t, n, b1, second, bz)
                    total = buf[at].astype(F32) + l2[t, n, second].astype(F32)
                    total = total + (l2[t, n, 2 + second].astype(F32) + lz[t, n // EARLY, second].astype(F32))
                    buf[at] = total.astype(BF)
                    if order == 0:
                        stage3_far(t, n).start()
                own_share(t, n)

            @pl.when(~early(n))
            def _():
                stage2(t, n).wait()
                for z in range(4):
                    at = (t, n, b1, b2, z)
                    buf[at] = (buf[at].astype(F32) + l2[t, n, z].astype(F32)).astype(BF)
                for d in (1, 2, 3):
                    stage3(t, n, d).start()
                own_share(t, n)

        def sent3(t, n):
            @pl.when(early(n))
            def _():
                stage3_far(t, n).wait_send()

            @pl.when(~early(n))
            def _():
                for d in (1, 2, 3):
                    stage3(t, n, d).wait_send()

            @pl.when(sec != 1 - t)
            def _():
                stage3(t, n, 0).wait_send()

        def arrived(t, n):
            for k in range(2):
                landed(n, k, 1).wait_recv()

                @pl.when(~early(n))
                def _():
                    for d in (2, 3):
                        landed(n, k, d).wait_recv()

                @pl.when(sec != k)
                def _():
                    landed(n, k, 0).wait_recv()

            keep(t, n).wait()

        def span(lo, hi, fn):
            def one(n, carry):
                fn(n)
                return carry

            lax.fori_loop(lo, hi, one, 0)

        def step(i, fresh=True):
            if fresh:
                stage1(i // 16, i % 16).start()
            for back, fn in ((AHEAD1, after1), (AHEAD1 + AHEAD2, after2)):
                j = i - back

                @pl.when((j >= 0) & (j < 32))
                def _():
                    fn(j // 16, j % 16)

    small[...] = jnp.zeros_like(small)
    for pad in (kpad, vpad):
        pad[0:HALO, :] = jnp.zeros((HALO, half), BF)
        pad[HALO + seq :, :] = jnp.zeros((HALO, half), BF)
    cot_load.wait()

    def layer(t, carry):
        l = 1 - t

        def transpose_pool(slots):
            for j, slot in enumerate(slots):
                tr[j * half : (j + 1) * half, :] = pool[slot].T

        stats_load(l).wait()
        for j in range(2):
            norm_load(l, NB_, j, j).wait()

        def norm_back(slots, counted, dv, rows, rstd_lane, gain, gain_sum, offset_sum, round_sum):
            n = jnp.concatenate([gbuf[j, rows, :] for j in slots], axis=1).astype(F32)
            rstd = stats[rows, rstd_lane : rstd_lane + 1]
            dn = dv * par[l, gain : gain + 1, :]
            d = rstd * (
                dn - jnp.mean(dn, axis=-1, keepdims=True) - n * jnp.mean(dn * n, axis=-1, keepdims=True)
            )
            low = d.astype(BF)
            df[rows, :] = low

            @pl.when(counted)
            def _():
                small[t, gain_sum : gain_sum + 1, :] += column_total(dv * n)
                small[t, offset_sum : offset_sum + 1, :] += column_total(dv)
                small[t, round_sum : round_sum + 1, :] += column_total(low)

        def out_norm(i, carry):
            rows = tile_rows(i)
            norm_back((0, 1), i // (ntile // 2) == sec, dy[rows, :].astype(F32), rows, RSTD_B, GAIN1, GAIN1, BIAS_B, BIAS_F)
            acc[rows, :] = jnp.zeros((TILE, width), F32)
            return carry

        lax.fori_loop(0, ntile, out_norm, 0)

        for load in m_loads(l, 1, True):
            load.start()
        for load in h_loads(l):
            load.wait()
        transpose_pool((0, 1))
        for load in chunk_loads(l, 0, 0):
            load.start()

        def out_grad(ii, carry):
            for odd in range(2):
                i = 2 * ii + odd
                for load in m_loads(l, i, odd):
                    load.wait()
                for j in range(2):
                    mt[j * PIECE : (j + 1) * PIECE, :] = (gbuf[j] if odd else pool[2 + j]).T

                @pl.when(i + 2 < ff // width)
                def _():
                    for load in m_loads(l, i + 2, odd):
                        load.start()

                g = dot(mt[...], df[:, own]).astype(BF)
                if comm:
                    for o in range(4):
                        x, y = o % 2, o // 2
                        f = x * (1 - sec) + y * sec
                        s = y * (1 - sec) + x * sec
                        for q in range(4):
                            buf[t, q, f, s, i] = g[o * 192 + q * 48 : o * 192 + (q + 1) * 48]
                else:
                    buf[t, i] = g
            return carry

        lax.fori_loop(0, ff // width // 2, out_grad, 0)
        if comm:
            step(16 * t)
            step(16 * t + 1)

        o_loads = [pool_load(j, half, o_full.at[l], j * half) for j in range(2)]
        wo_load = rows_load(0, half, wo.at[l], 0)
        head_weights = [weight_load(j, half, wqkv.at[l], j * half) for j in range(3)]
        late_loads = [norm_load(l, NA_, 0, 2)] + o_loads + [wo_load] + head_weights[:2]

        def feed(jj, carry):
            for part in range(3):
                c = 3 * jj + part
                slot = c % 2
                for load in chunk_loads(l, slot, c):
                    load.wait()

                @pl.when(c + 1 < ffh // UNITS)
                def _():
                    for load in chunk_loads(l, 1 - slot, c + 1):
                        load.start()

                @pl.when(c + 1 == ffh // UNITS)
                def _():
                    for load in late_loads:
                        load.start()

                dm = dot_nt(df[...], wslot[slot, 0:UNITS])
                gbuf[0, :, 0:UNITS] = (dm * pool[2 * slot + 1, :, 0:UNITS].astype(F32)).astype(BF)
                gbuf[1, :, 0:UNITS] = (dm * pool[2 * slot, :, 0:UNITS].astype(F32)).astype(BF)
                acc[...] += dot_nt(gbuf[0, :, 0:UNITS], wpool[2 * slot, :, 0:UNITS]) + dot_nt(
                    gbuf[1, :, 0:UNITS], wpool[2 * slot + 1, :, 0:UNITS]
                )

                @pl.when(c == ffh // UNITS - 1)
                def _():
                    @pl.when(t > 0)
                    def _():
                        exchange(1).wait_send()

                    psend[...] = acc[...].astype(BF)
                    exchange(2 * t).start()

                unit = sec * ffh + c * UNITS
                spot = lanes_at(unit % width, UNITS)
                for k in range(2):
                    small[t, pl.ds(BIAS_IN + k * (ff // width) + unit // width, 1), spot] = column_total(
                        gbuf[k, :, 0:UNITS]
                    )
                    g = dot(tr[...], gbuf[k, :, 0:UNITS]).astype(BF)
                    n = 4 + 4 * jj + 2 * k
                    if part == 0:
                        put(t, n, 0, g)
                    elif part == 1:
                        put(t, n, 256, g[:, :128])
                        put(t, n + 1, 0, g[:, 128:])
                    else:
                        put(t, n + 1, 128, g)
                if comm:
                    step(16 * t + 2 + c)
            return carry

        lax.fori_loop(0, ffh // (3 * UNITS), feed, 0)
        norm_load(l, NA_, 1, 0).start()
        head_weights[2].start()

        for load in o_loads:
            load.wait()
        transpose_pool((0, 1))
        head_rows = [pool_load(j, half, qkv.at[l, j], 0) for j in range(3)]
        for load in head_rows:
            load.start()
        pool_load(3, half, acts.at[l, X_], 0).start()
        norm_load(l, NA_, 0, 2).wait()
        norm_load(l, NA_, 1, 0).wait()
        exchange(2 * t).wait_recv()

        def attn_norm(i, carry):
            rows = tile_rows(i)
            dh = df[rows, :].astype(F32) + (psend[rows, :].astype(F32) + precv[0, rows, :].astype(F32))
            norm_back((2, 0), i // (ntile // 2) == sec, dh, rows, RSTD_A, GAIN0, GAIN0, BIAS_A, BIAS_O)
            return carry

        lax.fori_loop(0, ntile, attn_norm, 0)

        wo_load.wait()

        @pl.when((t == 1) & (sec == 1))
        def _():
            x_store.wait()

        dy[:, 0:half] = dot_nt(df[...], wslot[0]).astype(BF)
        put(t, 12, 0, dot(tr[...], df[:, own]).astype(BF))
        if comm:
            step(16 * t + 8)
            step(16 * t + 9)

        for load in head_rows:
            load.wait()

        def row(r, carry):
            base = pl.multiple_of(r * seq, seq)
            kpad[HALO : HALO + seq, :] = pool[1, pl.ds(base, seq), :]
            vpad[HALO : HALO + seq, :] = pool[2, pl.ds(base, seq), :]
            lane = lax.broadcasted_iota(jnp.int32, (QB, 128), 1)

            for g in range(half // LANES):
                cols = slice(g * LANES, (g + 1) * LANES)

                def operands(i):
                    rows = pl.ds(pl.multiple_of(base + i * QB, QB), QB)
                    window = slice(i * QB, i * QB + KW)
                    qs = stack_heads(pool[0, rows, cols] * BF(HEAD**-0.5))
                    return rows, kpad[window, cols], qs, stack_heads(dy[rows, cols])

                for i in range(seq // QB):
                    rows, kw, qs, os = operands(i)
                    far = away[r, i].astype(F32)
                    s = dot_nt(qs, kw)
                    d = dot_nt(os, vpad[i * QB : i * QB + KW, cols])
                    kept = stats[rows, :]
                    for h in range(GROUP):
                        part = slice(h * QB, (h + 1) * QB)
                        lse = jnp.sum(jnp.where(lane == g * GROUP + h, kept, 0.0), axis=-1, keepdims=True)
                        p = jnp.exp(s[part] + slope_of(sec, g, h) * far - lse)
                        pd = p * d[part]
                        mt[part, i * KW : (i + 1) * KW] = (pd - p * jnp.sum(pd, axis=-1, keepdims=True)).astype(BF)
                        mt[GROUP * QB + h * QB : GROUP * QB + (h + 1) * QB, i * KW : (i + 1) * KW] = p.astype(BF)
                for i in range(seq // QB):
                    rows, kw, qs, os = operands(i)
                    ds = mt[0 : GROUP * QB, i * KW : (i + 1) * KW]
                    ps = mt[GROUP * QB : 2 * GROUP * QB, i * KW : (i + 1) * KW]
                    gbuf[0, rows, cols] = (merge_heads(dot(ds, kw)) * HEAD**-0.5).astype(BF)
                    dk, dv = dot_tn(ds, qs), dot_tn(ps, os)
                    if i == 0:
                        at, skip = pl.ds(base, HALO), HALO
                    else:
                        at, skip = pl.ds(pl.multiple_of(base + i * QB - HALO, HALO), QB), 0
                        dk = jnp.concatenate([dk[:QB] + left_k, dk[QB:]], axis=0)
                        dv = jnp.concatenate([dv[:QB] + left_v, dv[QB:]], axis=0)
                    gbuf[1, at, cols] = dk[skip:QB].astype(BF)
                    gbuf[2, at, cols] = dv[skip:QB].astype(BF)
                    left_k, left_v = dk[QB:], dv[QB:]
                at = pl.ds(pl.multiple_of(base + seq - HALO, HALO), HALO)
                gbuf[1, at, cols] = left_k[:HALO].astype(BF)
                gbuf[2, at, cols] = left_v[:HALO].astype(BF)
            if comm:
                step(16 * t + 10 + r)
            return carry

        lax.fori_loop(0, rows_n, row, 0)
        pool_load(0, half, acts.at[l, X_], half).start()
        for load in head_weights:
            load.wait()
        exchange(2 * t).wait_send()

        total = dot_nt(gbuf[0], wpool[0])
        for j in (1, 2):
            total += dot_nt(gbuf[j], wpool[j])
        psend[...] = total.astype(BF)
        exchange(2 * t + 1).start()
        small[t, BIAS_Q : BIAS_Q + 1, own] = column_total(gbuf[0])
        small[t, BIAS_V : BIAS_V + 1, own] = column_total(gbuf[2])
        pool_load(3, half, acts.at[l, X_], 0).wait()
        pool_load(0, half, acts.at[l, X_], half).wait()
        transpose_pool((3, 0))

        @pl.when(t == 0)
        def _():
            first_loads(0)

        if comm:
            step(16 * t + 12)
        for j in range(3):
            put(t, 13 + j, 0, dot(tr[...], gbuf[j]).astype(BF))
            if j < 2:

                @pl.when(t == 0)
                def _():
                    norm_load(0, NB_, j, j).start()

            if comm and j == 0:
                step(16 * t + 13)
        exchange(2 * t + 1).wait_recv()

        def result(i, carry):
            rows = tile_rows(i)
            dx = df[rows, :].astype(F32) + (psend[rows, :].astype(F32) + precv[1, rows, :].astype(F32))
            dy[rows, :] = dx.astype(BF)
            return carry

        lax.fori_loop(0, ntile, result, 0)

        @pl.when(sec == l)
        def _():
            x_store.start()

        if comm:
            step(16 * t + 14)
            step(16 * t + 15)
        return carry

    lax.fori_loop(0, 2, layer, 0)
    exchange(3).wait_send()

    @pl.when(sec == 0)
    def _():
        x_store.wait()

    if comm:
        mine = 1 - sec

        def vectors(stage):
            if stage == 0:
                return [remote(small.at[sec], v1, vs.at[0], vr.at[0], sib)]
            if stage == 1:
                return [remote(v1, v2, vs.at[1], vr.at[1], (sec, xp))]
            if stage == 2:
                return [remote(v2, v3, vs.at[2], vr.at[2], (sec, yp))]
            return [remote(v3, v4.at[d - 1], vs.at[2 + d], vr.at[2 + d], (sec, zp[d])) for d in (1, 2, 3)]

        def go(stage):
            for c in vectors(stage):
                c.start()

        def done(stage):
            for c in vectors(stage):
                c.wait()

        def rest(lo, hi):
            span(lo, hi, lambda i: step(i, False))

        def combine(stage, there, here):
            done(stage)
            there[...] += here
            go(stage + 1)

        last = 32 + AHEAD1 + AHEAD2
        go(0)
        rest(32, 34)
        combine(0, v1, small[mine])
        rest(34, 36)
        combine(1, v2, v1[...])
        rest(36, last)
        combine(2, v3, v2[...])
        for t in range(2):
            span(0, 16, lambda n, t=t: sent3(t, n))
        span(0, 16, lambda n: arrived(mine, n))
        done(3)
        small_out[...] = v3[...] + v4[0] + v4[1] + v4[2]
    else:
        store = pltpu.make_async_copy(buf, grads_out, gsem)
        store.start()
        small_out[...] = small[...]
        store.wait()


def run_backward(comm, cot, acts, o_full, m_full, qkv, pp, stats, away, wqkv, wo, win, wout, par):
    tokens, width = cot.shape
    ff = m_full.shape[2]
    half = width // 2
    dma = pltpu.SemaphoreType.DMA
    dx = jax.ShapeDtypeStruct((tokens, width), BF)
    if comm:
        r = width // 16
        small = jax.ShapeDtypeStruct((VECTORS, width), F32)
        grads = jax.ShapeDtypeStruct((16, 2, 4, r, PIECE), BF)
        special = [
            vm(2, 16, 2, 2, 4, r, PIECE),
            vm(2, 16, 2, 4, r, PIECE),
            vm(2, 16, 4, r, PIECE),
            vm(2, 5, 2, r, PIECE),
            vm(VECTORS, width, dtype=F32),
            vm(VECTORS, width, dtype=F32),
            vm(VECTORS, width, dtype=F32),
            vm(3, VECTORS, width, dtype=F32),
            dma((2, 16)), dma((2, 16)), dma((2, 16)), dma((2, 16)), dma((2, 5, 3)), dma((2, 5, 3)),
            dma((2, 16, 4)), dma((16, 2, 4)), dma((16,)),
            dma((6,)), dma((6,)),
        ]
    else:
        small = jax.ShapeDtypeStruct((2, VECTORS, width), F32)
        grads = jax.ShapeDtypeStruct((2, 16, width, PIECE), BF)
        special = [vm(2, 16, width, PIECE), dma]
    seq = away.shape[1] * QB
    scratch = special + [
        vm(tokens, width, dtype=F32),
        vm(tokens, width),
        vm(tokens, width),
        vm(width, tokens),
        vm(width, tokens),
        vm(2, VECTORS, width, dtype=F32),
        vm(tokens, 128, dtype=F32),
        vm(4, tokens, PIECE),
        vm(4, width, PIECE),
        vm(2, half, width),
        vm(3, tokens, half),
        vm(seq + 2 * HALO, half),
        vm(seq + 2 * HALO, half),
        vm(tokens, width),
        vm(2, tokens, width),
        dma((4,)), dma((4,)), dma((2,)), dma((3,)), dma, dma, dma, dma((4,)), dma((4,)),
    ]
    return pl.pallas_call(
        functools.partial(bwd_kernel, comm),
        out_shape=(dx, small, grads),
        in_specs=[any_spec()] * 7 + [vmem_spec()] + [any_spec()] * 4 + [vmem_spec()],
        out_specs=(any_spec(), vmem_spec(), any_spec()),
        scratch_shapes=scratch,
        compiler_params=pltpu.CompilerParams(
            collective_id=2, has_side_effects=True, vmem_limit_bytes=64 << 20
        ),
        name="backward",
    )(cot, acts, o_full, m_full, qkv, pp, stats, away, wqkv, wo, win, wout, par)


def results_kernel(shares, vectors, fq, fo, fi, fu, gain_out, bias_out, inner_out, land, stage, lsem, fsem):
    me = lax.axis_index("dp")
    rows, width = fo.shape
    half, ff = width // 2, fi.shape[1] // 2
    ffh = ff // 2
    loads = []
    for n in range(16):
        used = 2 if n % EARLY == 1 else 4
        loads.append(
            pltpu.make_async_copy(shares.at[n, :, 0:used], land.at[n, :, 0:used], lsem.at[n])
        )
    for c in loads:
        c.start()

    def place(n, k):
        if n < 4:
            return fu.at[n * rows : (n + 1) * rows, k * half : (k + 1) * half]
        if n < 12:
            jj, g, i = (n - 4) // 4, (n - 4) // 2 % 2, n % 2
            start = g * ff + k * ffh + (2 * jj + i) * PIECE
            return fi.at[:, start : start + PIECE]
        if n == 12:
            return fo.at[:, k * half : (k + 1) * half]
        start = (n - 13) * width + k * half
        return fq.at[:, start : start + half]

    stores = []
    for n in range(16):
        loads[n].wait()
        for k in range(2):
            total = land[n, k, 0].astype(F32) + land[n, k, 1].astype(F32)
            if n % EARLY != 1:
                total = total + (land[n, k, 2].astype(F32) + land[n, k, 3].astype(F32))
            stage[n, k] = total
            stores.append(pltpu.make_async_copy(stage.at[n, k], place(n, k), fsem.at[n, k]))
            stores[-1].start()
    turned = pltpu.roll(vectors[0:8, :], (width - me * rows) % width, axis=1)
    gain_out[...] = turned[0:2, 0:rows]
    for j in range(6):
        bias_out[j] = turned[2 + j : 3 + j, 0:rows]
    line = vectors[pl.ds(8 + me // 2, 1), :]
    inner_out[...] = jnp.where(me % 2 == 0, line[:, :half], line[:, half:])
    for c in stores:
        c.wait()


def run_results(shares, vectors, ff):
    _, _, _, rows, half = shares.shape
    width = 2 * half
    dma = pltpu.SemaphoreType.DMA

    def out(*shape):
        return jax.ShapeDtypeStruct(shape, F32)

    return pl.pallas_call(
        results_kernel,
        out_shape=(
            out(rows, 3 * width), out(rows, width), out(rows, 2 * ff), out(ff // 16, width),
            out(2, rows), out(6, 1, rows), out(1, 2 * ff // 16),
        ),
        in_specs=[any_spec(), vmem_spec()],
        out_specs=tuple([any_spec()] * 4 + [vmem_spec()] * 3),
        scratch_shapes=[
            vm(*shares.shape), vm(16, 2, rows, half, dtype=F32), dma((16,)), dma((16, 2)),
        ],
        compiler_params=pltpu.CompilerParams(vmem_limit_bytes=60 << 20),
        name="results",
    )(shares, vectors)


def assemble(halves, width, ff):
    def columns(v):
        return jnp.concatenate(v, axis=1)

    gu = columns([h[:4].reshape(ff, PIECE) for h in halves])
    inner = [
        columns([h[4 + 4 * jj + 2 * k + i] for jj in range(2) for i in range(2)]) for k in range(2) for h in halves
    ]
    gi = columns(inner)
    go = columns([h[12] for h in halves])
    gq = columns([h[13 + j] for j in range(3) for h in halves])
    return gq, go, gi, gu


def shards(comm, hidden, segs, w_qkv, w_o, w_in, w_out, gains, biases, b_in, cot):
    w_qkv, w_o, w_in, w_out, gains = (v[0] for v in (w_qkv, w_o, w_in, w_out, gains))
    biases = jnp.transpose(biases, (1, 0, 2))
    micro, _, seq, width = hidden.shape
    ff = w_out.shape[0]
    tokens = micro * seq
    y, acts, o_full, m_full, qkv, pp, stats, wqkv2, wo2, win2, wout2, par2, away = run_forward(
        hidden.reshape(micro, seq, width), segs, w_qkv, w_o, w_in, w_out, gains, biases, b_in
    )
    dx, small, grads = run_backward(
        comm, cot.reshape(tokens, width), acts.reshape(2, 4, tokens, width), o_full.reshape(2, tokens, width),
        m_full.reshape(2, tokens, ff), qkv.reshape(2, 3, tokens, width // 2), pp.reshape(2, 2, tokens, ff // 2),
        stats.reshape(2, tokens, 128), away, wqkv2, wo2, win2, wout2, par2,
    )
    if comm:
        gq, go, gi, gu, gain, bias, inner = run_results(grads, small, ff)
        return (
            y.reshape(1, *hidden.shape), dx.reshape(1, *hidden.shape), gq[None], go[None], gi[None], gu[None],
            gain[None], jnp.transpose(bias, (1, 0, 2)), inner,
        )
    owners, me = lax.axis_size("dp"), lax.axis_index("dp")
    first = lax.axis_index("section") == 0
    swap = [(0, 1), (1, 0)]

    def pick(v):
        own = jnp.where(first, v[1], v[0])
        return own, lax.ppermute(jnp.where(first, v[0], v[1]), "section", swap)

    own, other = pick(grads)
    halves = [jnp.where(first, own, other), jnp.where(first, other, own)]

    def share(v):
        parts = v.reshape(owners, v.shape[0] // owners, v.shape[1])
        got = lax.all_to_all(parts, "dp", split_axis=0, concat_axis=0, tiled=True)
        return jnp.sum(got.astype(F32), axis=0)

    gq, go, gi, gu = (share(v) for v in assemble(halves, width, ff))
    own, other = pick(small)
    small = lax.psum(own + other, "dp")
    part = width // owners
    mine = lax.dynamic_slice_in_dim(small[:8], me * part, part, axis=1)
    inner = lax.dynamic_slice_in_dim(small[8:].reshape(1, 2 * ff), me * (2 * ff // owners), 2 * ff // owners, axis=1)
    return (
        y.reshape(1, *hidden.shape), dx.reshape(1, *hidden.shape), gq[None], go[None], gi[None], gu[None],
        mine[None, :2], mine[None, 2:], inner,
    )


def solution(mesh):
    rows = P(None, "dp", None, None)
    layer = P("section", None, None)
    comm = mesh.shape["dp"] == 16
    return jax.shard_map(
        functools.partial(shards, comm),
        mesh=mesh,
        in_specs=(rows, P(None, "dp", None)) + (layer,) * 6 + (P("section", None), rows),
        out_specs=(
            P("section", None, "dp", None, None),
            P("section", None, "dp", None, None),
            P("section", "dp", None),
            P("section", "dp", None),
            P("section", "dp", None),
            P("section", "dp", None),
            P("section", None, "dp"),
            P("section", None, "dp"),
            P("section", "dp"),
        ),
        check_vma=False,
    )
```

```python
import functools
import math

import jax
import jax.numpy as jnp
from jax import lax
from jax.experimental import pallas as pl
from jax.experimental.pallas import tpu as pltpu
from jax.sharding import PartitionSpec as P

HEADS = 12
HEAD = 64
GROUP = 2
LANES = GROUP * HEAD
QB = 128
HALO = 64
KW = QB + 2 * HALO
EPS = 1e-05
MASKED = -1.0e30
TILE = 256
UNITS = 256
PIECE = 384
BF = jnp.bfloat16
F32 = jnp.float32
MESH = pl.DeviceIdType.MESH
NT = (((1,), (1,)), ((), ()))
TN = (((0,), (0,)), ((), ()))
H_, NA_, NB_, X_ = range(4)
M_, P1_, P2_ = range(3)
GAIN0, GAIN1, BIAS_Q, BIAS_V, BIAS_O, BIAS_A, BIAS_F, BIAS_B, BIAS_IN = range(9)
VECTORS = 16
FEED = 512
AHEAD1, AHEAD2 = 3, 3
EARLY = 3
RSTD_A, RSTD_B = HEADS, HEADS + 1


def slope_list(head_count):
    base = 2 ** int(math.floor(math.log2(head_count)))
    leading = [2.0 ** (-8.0 * (k + 1) / base) for k in range(base)]
    trailing = [2.0 ** (-4.0 * (2 * k + 1) / base) for k in range(head_count - base)]
    return leading + trailing


def dot(a, b):
    return jnp.dot(a, b, preferred_element_type=F32)


def dot_nt(a, b):
    return lax.dot_general(a, b, NT, preferred_element_type=F32)


def dot_tn(a, b):
    return lax.dot_general(a, b, TN, preferred_element_type=F32)


def normalize(v):
    c = v - jnp.mean(v, axis=-1, keepdims=True)
    rstd = lax.rsqrt(jnp.mean(c * c, axis=-1, keepdims=True) + EPS)
    return c * rstd, rstd


def stack_heads(v):
    head = lax.broadcasted_iota(jnp.int32, v.shape, 1) // HEAD
    zero = jnp.zeros_like(v)
    return jnp.concatenate([jnp.where(head == h, v, zero) for h in range(GROUP)], axis=0)


def merge_heads(r):
    rows = r.shape[0] // GROUP
    head = lax.broadcasted_iota(jnp.int32, (rows, r.shape[1]), 1) // HEAD
    out = r[:rows]
    for h in range(1, GROUP):
        out = jnp.where(head == h, r[h * rows : (h + 1) * rows], out)
    return out


def fill_away(away, segs):
    micro, _, seq = segs.shape
    r = lax.broadcasted_iota(jnp.int32, (QB, KW), 0)
    c = lax.broadcasted_iota(jnp.int32, (QB, KW), 1)
    apart = -jnp.abs(r + HALO - c).astype(F32)
    outside = jnp.full((QB, 128), -1.0, F32)
    for m in range(micro):
        seg = jnp.broadcast_to(segs[m].astype(F32), (QB, seq))
        keys = pltpu.roll(jnp.concatenate([outside, seg, outside], axis=1), seq + 256 - HALO, axis=1)
        for i in range(seq // QB):
            own = seg[:, i * QB : (i + 1) * QB].T
            own = jnp.concatenate([own, own], axis=1)
            same = own == keys[:, i * QB : i * QB + KW]
            away[m, i] = jnp.where(same, apart, MASKED).astype(BF)


def slope_of(sec, g, h):
    table = slope_list(HEADS)
    return jnp.where(sec == 0, table[g * GROUP + h], table[HEADS // 2 + g * GROUP + h]).astype(F32)


def tile_rows(t):
    return pl.ds(pl.multiple_of(t * TILE, TILE), TILE)


def lanes_at(start, count):
    return pl.ds(pl.multiple_of(start, 128), count)


def fwd_kernel(
    hid, segs, wqkv_h, wo_h, win_h, wout_h, gains_in, biases_in, bin_in,
    y_out, acts_out, o_out, m_out, qkv_out, p_out, stats_out,
    wqkv_out, wo_out, win_out, wout_out, par_out, away_out,
    wqkv, wo, win, wout, par, bin_, xy, qkvs, os_, hs, big, psend, precv, acc, kpad, vpad, held, away, stats,
    lsem, rsend, rrecv, wsave, hsem, ysem, asem, qsem, osem, osend, orecv, bsem, msend, mrecv, tsem, ssend, srecv,
    parsem, awaysem,
):
    dp = lax.axis_index("dp")
    sec = lax.axis_index("section")
    _, micro, seq, width = xy.shape
    half, ffh, ff = wo.shape[1], wout.shape[1], wout_h.shape[0]
    sib = (1 - sec, dp)

    parts = []
    for j in range(3):
        parts.append((wqkv_h, wqkv, lambda c, j=j: (slice(None), lanes_at(j * width + c * half, half)),
                      (slice(None), slice(j * half, (j + 1) * half))))
    parts.append((wo_h, wo, lambda c: (pl.ds(pl.multiple_of(c * half, 128), half), slice(None)), (slice(None), slice(None))))
    for q in range(ffh // FEED):
        for j in range(2):
            parts.append((win_h, win, lambda c, j=j, q=q: (slice(None), lanes_at(j * ff + c * ffh + q * FEED, FEED)),
                          (slice(None), slice(j * ffh + q * FEED, j * ffh + (q + 1) * FEED))))
        parts.append((wout_h, wout, lambda c, q=q: (pl.ds(pl.multiple_of(c * ffh + q * FEED, 128), FEED), slice(None)),
                      (slice(q * FEED, (q + 1) * FEED), slice(None))))

    def own_part(i):
        src, dst, pick, place = parts[i]
        return pltpu.make_async_copy(src.at[pick(sec)], dst.at[(sec, *place)], lsem.at[i])

    def other_part(i):
        src, dst, pick, place = parts[i]
        return pltpu.make_async_remote_copy(
            src_ref=src.at[pick(1 - sec)], dst_ref=dst.at[(sec, *place)],
            send_sem=rsend.at[i], recv_sem=rrecv.at[i], device_id=sib, device_id_type=MESH,
        )

    def other_vectors():
        return [
            pltpu.make_async_remote_copy(
                src_ref=v.at[sec], dst_ref=v.at[sec], send_sem=rsend.at[len(parts) + i], recv_sem=rrecv.at[len(parts) + i],
                device_id=sib, device_id_type=MESH,
            )
            for i, v in enumerate((par, bin_))
        ]

    def x_load(m):
        return pltpu.make_async_copy(hid.at[m], xy.at[0, m], hsem.at[m])

    for m in range(micro):
        x_load(m).start()
    for i in range(3):
        own_part(i).start()
    par[sec, 0:2] = gains_in[...]
    for j in range(6):
        par[sec, 2 + j : 3 + j] = biases_in[j]
    bin_[sec] = bin_in[...]
    barrier = pltpu.get_barrier_semaphore()
    pl.semaphore_signal(barrier, inc=1, device_id=sib, device_id_type=MESH)
    pl.semaphore_wait(barrier, 1)
    for c in other_vectors():
        c.start()
    for i in range(3):
        other_part(i).start()
    for i in range(3, len(parts)):
        own_part(i).start()
    fill_away(away, segs)
    away_save = pltpu.make_async_copy(away, away_out, awaysem)
    away_save.start()
    for pad in (kpad, vpad):
        pad[0:HALO, :] = jnp.zeros((HALO, half), BF)
        pad[HALO + seq :, :] = jnp.zeros((HALO, half), BF)
    for m in range(micro):
        x_load(m).wait()

    def send_weights(when, lo, hi):
        @pl.when(when)
        def _():
            for i in range(lo, hi):
                other_part(i).start()

    def need(l, which):
        @pl.when(l == sec)
        def _():
            for i in which:
                own_part(i).wait()

        @pl.when(l != sec)
        def _():
            for i in which:
                other_part(i).wait_recv()

    def save(kind, l, m):
        src = xy.at[l, m] if kind == X_ else hs.at[kind, m]
        return pltpu.make_async_copy(src, acts_out.at[l, kind, m], asem.at[kind, l, m])

    def save_qkv(kind, l, m):
        return pltpu.make_async_copy(qkvs.at[m, kind], qkv_out.at[l, kind, m], qsem.at[kind, l, m])

    def save_o(l, m):
        return pltpu.make_async_copy(os_.at[m], o_out.at[l, m, :, lanes_at(sec * half, half)], osem.at[l, m])

    def share_o(l, m):
        return pltpu.make_async_remote_copy(
            src_ref=os_.at[m], dst_ref=o_out.at[l, m, :, lanes_at(sec * half, half)],
            send_sem=osend.at[l, m], recv_sem=orecv.at[l, m], device_id=sib, device_id_type=MESH,
        )

    def save_big(kind, l, m):
        if kind == M_:
            dst = m_out.at[l, m, :, lanes_at(sec * ffh, ffh)]
        else:
            dst = p_out.at[l, kind - 1, m]
        return pltpu.make_async_copy(big.at[m, kind], dst, bsem.at[kind, l, m])

    def share_m(l, m):
        return pltpu.make_async_remote_copy(
            src_ref=big.at[m, M_], dst_ref=m_out.at[l, m, :, lanes_at(sec * ffh, ffh)],
            send_sem=msend.at[l, m], recv_sem=mrecv.at[l, m], device_id=sib, device_id_type=MESH,
        )

    def save_stats(l, m):
        return pltpu.make_async_copy(stats.at[l, m], stats_out.at[l, m], tsem.at[l, m])

    def save_y(m):
        return pltpu.make_async_copy(xy.at[sec + 1, m], y_out.at[m], ysem.at[m])

    def partial(phase, l, m):
        return pltpu.make_async_remote_copy(
            src_ref=psend.at[phase, m], dst_ref=precv.at[phase, l, m],
            send_sem=ssend.at[phase, l, m], recv_sem=srecv.at[phase, l, m], device_id=sib, device_id_type=MESH,
        )

    def weight_saves(l):
        pairs = ((wqkv, wqkv_out), (wo, wo_out), (win, win_out), (wout, wout_out))
        return [pltpu.make_async_copy(s.at[l], d.at[l], wsave.at[i, l]) for i, (s, d) in enumerate(pairs)]

    par_save = pltpu.make_async_copy(par, par_out, parsem)

    def attend(l, m):
        @pl.when(m == 0)
        def _():
            need(l, (0, 1, 2))

            @pl.when(l != sec)
            def _():
                for c in other_vectors():
                    c.wait_recv()

        @pl.when(l > 0)
        def _():
            for kind in range(3):
                save_qkv(kind, l - 1, m).wait()
            save_o(l - 1, m).wait()
            share_o(l - 1, m).wait_send()
            partial(0, l - 1, m).wait_send()

        save(X_, l, m).start()
        bias_q = par[l, BIAS_Q : BIAS_Q + 1, lanes_at(sec * half, half)]
        bias_v = par[l, BIAS_V : BIAS_V + 1, lanes_at(sec * half, half)]

        r = dot(xy[l, m], wqkv[l])
        q = (r[:, :half] + bias_q).astype(BF)
        k = r[:, half : 2 * half].astype(BF)
        v = (r[:, 2 * half :] + bias_v).astype(BF)
        for j, w in enumerate((q, k, v)):
            qkvs[m, j] = w
        kpad[HALO : HALO + seq, :] = k
        vpad[HALO : HALO + seq, :] = v
        for kind in range(3):
            save_qkv(kind, l, m).start()
        send_weights((l == 0) & (m == 0), 3, 7)

        lane = lax.broadcasted_iota(jnp.int32, (QB, 128), 1)
        for g in range(half // LANES):
            cols = slice(g * LANES, (g + 1) * LANES)
            for i in range(seq // QB):
                rows = slice(i * QB, (i + 1) * QB)
                far = away[m, i].astype(F32)
                qs = stack_heads(qkvs[m, 0, rows, cols] * BF(HEAD**-0.5))
                s = dot_nt(qs, kpad[i * QB : i * QB + KW, cols])
                probs = []
                kept = stats[l, m, rows, :]
                for h in range(GROUP):
                    sh = s[h * QB : (h + 1) * QB] + slope_of(sec, g, h) * far
                    top = jnp.max(sh, axis=-1, keepdims=True)
                    e = jnp.exp(sh - top)
                    total = jnp.sum(e, axis=-1, keepdims=True)
                    probs.append((e * (1.0 / total)).astype(BF))
                    kept = jnp.where(lane == g * GROUP + h, top + jnp.log(total), kept)
                stats[l, m, rows, :] = kept
                held[:, i * KW : (i + 1) * KW] = jnp.concatenate(probs, axis=0)
            for i in range(seq // QB):
                rows = slice(i * QB, (i + 1) * QB)
                r = dot(held[:, i * KW : (i + 1) * KW], vpad[i * QB : i * QB + KW, cols])
                os_[m, rows, cols] = merge_heads(r).astype(BF)

        save_o(l, m).start()
        share_o(l, m).start()

        @pl.when(m == 0)
        def _():
            need(l, (3,))

        psend[0, m] = dot(os_[m], wo[l]).astype(BF)
        send_weights((l == 0) & (m == 0), 7, len(parts))
        partial(0, l, m).start()

    def feed(l, m):
        @pl.when(l > 0)
        def _():
            save(H_, l - 1, m).wait()
            save(NA_, l - 1, m).wait()
            for kind in range(3):
                save_big(kind, l - 1, m).wait()
            share_m(l - 1, m).wait_send()
            partial(1, l - 1, m).wait_send()

        partial(0, l, m).wait_recv()
        lane = lax.broadcasted_iota(jnp.int32, (TILE, 128), 1)

        def norm(t, carry):
            rows = tile_rows(t)
            a = xy[l, m, rows, :].astype(F32) + (
                psend[0, m, rows, :].astype(F32) + precv[0, l, m, rows, :].astype(F32) + par[l, BIAS_O : BIAS_O + 1, :]
            )
            n, rstd = normalize(a)
            hs[NA_, m, rows, :] = n.astype(BF)
            hs[H_, m, rows, :] = (n * par[l, GAIN0 : GAIN0 + 1, :] + par[l, BIAS_A : BIAS_A + 1, :]).astype(BF)
            stats[l, m, rows, :] = jnp.where(lane == RSTD_A, rstd, stats[l, m, rows, :])
            return carry

        lax.fori_loop(0, seq // TILE, norm, 0)
        save(H_, l, m).start()
        save(NA_, l, m).start()
        def chunks(waiting):
            h = hs[H_, m]
            for c in range(ffh // FEED):
                cols = slice(c * FEED, (c + 1) * FEED)
                unit = sec * ffh + c * FEED

                if waiting:
                    need(l, (4 + 3 * c, 5 + 3 * c, 6 + 3 * c))
                gate = dot(h, win[l, :, cols]) + bin_[l, :, lanes_at(unit, FEED)]
                up = dot(h, win[l, :, ffh + c * FEED : ffh + (c + 1) * FEED]) + bin_[l, :, lanes_at(ff + unit, FEED)]
                cdf = 0.5 + 0.5 * lax.erf(gate * (0.5**0.5))
                act = gate * cdf
                slope = cdf + gate * (jnp.exp(gate * gate * -0.5) * (2.0 * math.pi) ** -0.5)
                mixed = (act * up).astype(BF)
                big[m, M_, :, cols] = mixed
                big[m, P1_, :, cols] = act.astype(BF)
                big[m, P2_, :, cols] = (up * slope).astype(BF)
                down = dot(mixed, wout[l, cols, :])
                acc[...] = down if c == 0 else acc[...] + down

        @pl.when((l == 0) & (m == 0))
        def _():
            chunks(True)

        @pl.when((l > 0) & (m == 0))
        def _():
            need(l, range(4, len(parts)))

        @pl.when((l > 0) | (m > 0))
        def _():
            chunks(False)

        @pl.when(m == 0)
        def _():
            for c in weight_saves(l):
                c.start()

        psend[1, m] = acc[...].astype(BF)
        partial(1, l, m).start()
        for kind in range(3):
            save_big(kind, l, m).start()
        share_m(l, m).start()

    def finish(l, m):
        @pl.when(l > 0)
        def _():
            save(NB_, l - 1, m).wait()

        partial(1, l, m).wait_recv()
        lane = lax.broadcasted_iota(jnp.int32, (TILE, 128), 1)

        def norm(t, carry):
            rows = tile_rows(t)
            b = hs[H_, m, rows, :].astype(F32) + (
                psend[1, m, rows, :].astype(F32) + precv[1, l, m, rows, :].astype(F32) + par[l, BIAS_F : BIAS_F + 1, :]
            )
            n, rstd = normalize(b)
            hs[NB_, m, rows, :] = n.astype(BF)
            xy[l + 1, m, rows, :] = (n * par[l, GAIN1 : GAIN1 + 1, :] + par[l, BIAS_B : BIAS_B + 1, :]).astype(BF)
            stats[l, m, rows, :] = jnp.where(lane == RSTD_B, rstd, stats[l, m, rows, :])
            return carry

        lax.fori_loop(0, seq // TILE, norm, 0)
        save(NB_, l, m).start()
        save_stats(l, m).start()

        @pl.when(l == sec)
        def _():
            save_y(m).start()

    def layer(l, carry):
        def first(m, carry):
            @pl.when(l > 0)
            def _():
                finish(l - 1, m)

            attend(l, m)
            return carry

        lax.fori_loop(0, micro, first, 0)

        def second(m, carry):
            feed(l, m)
            return carry

        lax.fori_loop(0, micro, second, 0)
        return carry

    lax.fori_loop(0, 2, layer, 0)
    par_save.start()

    def last(m, carry):
        finish(1, m)
        return carry

    lax.fori_loop(0, micro, last, 0)

    def drain(m, carry):
        for kind in range(3):
            save_qkv(kind, 1, m).wait()
            save_big(kind, 1, m).wait()
        for kind in (H_, NA_, NB_):
            save(kind, 1, m).wait()
        save_o(1, m).wait()
        share_o(1, m).wait_send()
        share_m(1, m).wait_send()
        for phase in range(2):
            partial(phase, 1, m).wait_send()
        for l in range(2):
            save(X_, l, m).wait()
            save_stats(l, m).wait()
            share_o(l, m).wait_recv()
            share_m(l, m).wait_recv()
        save_y(m).wait()
        return carry

    lax.fori_loop(0, micro, drain, 0)
    for l in range(2):
        for c in weight_saves(l):
            c.wait()
    for i in range(len(parts)):
        other_part(i).wait_send()
    for c in other_vectors():
        c.wait_send()
    par_save.wait()
    away_save.wait()


def any_spec():
    return pl.BlockSpec(memory_space=pl.ANY)


def vmem_spec():
    return pl.BlockSpec(memory_space=pltpu.VMEM)


def smem_spec():
    return pl.BlockSpec(memory_space=pltpu.SMEM)


def vm(*shape, dtype=BF):
    return pltpu.VMEM(shape, dtype)


def run_forward(hid, segs, w_qkv, w_o, w_in, w_out, gains, biases, b_in):
    micro, seq, width = hid.shape
    ff = w_out.shape[0]
    half, ffh = width // 2, ff // 2
    dma = pltpu.SemaphoreType.DMA

    def out(*shape, dtype=BF):
        return jax.ShapeDtypeStruct(shape, dtype)

    shapes = (
        out(micro, seq, width),
        out(2, 4, micro, seq, width),
        out(2, micro, seq, width),
        out(2, micro, seq, ff),
        out(2, 3, micro, seq, half),
        out(2, 2, micro, seq, ffh),
        out(2, micro, seq, 128, dtype=F32),
        out(2, width, 3 * half),
        out(2, half, width),
        out(2, width, 2 * ffh),
        out(2, ffh, width),
        out(2, 8, width, dtype=F32),
        out(micro, seq // QB, QB, KW),
    )
    return pl.pallas_call(
        fwd_kernel,
        out_shape=shapes,
        in_specs=[any_spec(), vmem_spec()] + [any_spec()] * 4 + [vmem_spec()] * 3,
        out_specs=tuple([any_spec()] * len(shapes)),
        scratch_shapes=[
            vm(2, width, 3 * half),
            vm(2, half, width),
            vm(2, width, 2 * ffh),
            vm(2, ffh, width),
            vm(2, 8, width, dtype=F32),
            vm(2, 1, 2 * ff, dtype=F32),
            vm(3, micro, seq, width),
            vm(micro, 3, seq, half),
            vm(micro, seq, half),
            vm(3, micro, seq, width),
            vm(micro, 3, seq, ffh),
            vm(2, micro, seq, width),
            vm(2, 2, micro, seq, width),
            vm(seq, width, dtype=F32),
            vm(seq + 2 * HALO, half),
            vm(seq + 2 * HALO, half),
            vm(GROUP * QB, seq // QB * KW),
            vm(micro, seq // QB, QB, KW),
            vm(2, micro, seq, 128, dtype=F32),
            dma((13,)), dma((15,)), dma((15,)), dma((4, 2)), dma((micro,)), dma((micro,)), dma((4, 2, micro)),
            dma((3, 2, micro)), dma((2, micro)), dma((2, micro)), dma((2, micro)), dma((3, 2, micro)),
            dma((2, micro)), dma((2, micro)), dma((2, micro)), dma((2, 2, micro)), dma((2, 2, micro)), dma, dma,
        ],
        compiler_params=pltpu.CompilerParams(
            collective_id=1, has_side_effects=True, vmem_limit_bytes=62 << 20
        ),
        name="forward",
    )(hid, segs, w_qkv, w_o, w_in, w_out, gains, biases, b_in)


def column_total(v):
    return jnp.sum(v.astype(F32), axis=0, keepdims=True)


def bwd_kernel(
    comm, cot, acts, o_full, m_full, qkv, pp, stats_h, away, wqkv, wo, win, wout, par, *refs
):
    if comm:
        (dx_out, small_out, shares, *rest) = refs
        (buf, l1, l2, lz, v1, v2, v3, v4, s1, r1, s2, r2, sz, rz, s3, r3, ksem, vs, vr, *rest) = rest
    else:
        (dx_out, small_out, grads_out, *rest) = refs
        (buf, gsem, *rest) = rest
    (acc, df, dy, tr, mt, small, stats, pool, wpool, wslot, gbuf, kpad, vpad, psend, precv,
     poolsem, wsem, usem, nsem, ssem, ysem, xsem, esend, erecv) = rest
    dp = lax.axis_index("dp")
    sec = lax.axis_index("section")
    sib = (1 - sec, dp)
    tokens, width = df.shape
    rows_n, seq = away.shape[0], away.shape[1] * QB
    ff = m_full.shape[2]
    half, ffh = width // 2, ff // 2
    ntile = tokens // TILE
    own = lanes_at(sec * half, half)

    if comm:
        bx, by, bz = dp % 2, (dp // 2) % 2, dp // 4
        xp = dp + 1 - 2 * bx
        yp = dp + 2 - 4 * by
        zp = [dp] + [((bz + d) % 4) * 4 + dp % 4 for d in range(1, 4)]
        near = xp * (1 - sec) + yp * sec
        far = yp * (1 - sec) + xp * sec
        b1 = bx * (1 - sec) + by * sec
        b2 = by * (1 - sec) + bx * sec
        greet = [(sec, xp), (sec, yp)] + [(sec, z) for z in zp[1:]] + [(1 - sec, z) for z in zp[1:] + [xp, yp]]
    else:
        greet = []

    def pool_load(slot, count, src, first):
        return pltpu.make_async_copy(src.at[:, lanes_at(first, count)], pool.at[slot, :, 0:count], poolsem.at[slot])

    def weight_load(slot, count, src, first):
        return pltpu.make_async_copy(src.at[:, lanes_at(first, count)], wpool.at[slot, :, 0:count], wsem.at[slot])

    def rows_load(slot, count, src, first):
        return pltpu.make_async_copy(
            src.at[pl.ds(pl.multiple_of(first, 128), count), :], wslot.at[slot, 0:count], usem.at[slot]
        )

    def norm_load(l, kind, j, slot):
        return pltpu.make_async_copy(acts.at[l, kind, :, j * half : (j + 1) * half], gbuf.at[slot], nsem.at[slot])

    def stats_load(l):
        return pltpu.make_async_copy(stats_h.at[l], stats, ssem)

    def m_loads(l, i, odd):
        return [
            pltpu.make_async_copy(
                m_full.at[l, :, lanes_at((2 * i + j) * PIECE, PIECE)],
                gbuf.at[j] if odd else pool.at[2 + j],
                nsem.at[j] if odd else poolsem.at[2 + j],
            )
            for j in range(2)
        ]

    def h_loads(l):
        return [pool_load(j, half, acts.at[l, H_], j * half) for j in range(2)]

    def chunk_loads(l, slot, c):
        first = c * UNITS
        return [
            weight_load(2 * slot, UNITS, win.at[l], first),
            weight_load(2 * slot + 1, UNITS, win.at[l], ffh + first),
            rows_load(slot, UNITS, wout.at[l], first),
            pool_load(2 * slot, UNITS, pp.at[l, 0], first),
            pool_load(2 * slot + 1, UNITS, pp.at[l, 1], first),
        ]

    def exchange(e):
        return pltpu.make_async_remote_copy(
            src_ref=psend, dst_ref=precv.at[e % 2], send_sem=esend.at[e], recv_sem=erecv.at[e],
            device_id=sib, device_id_type=MESH,
        )

    x_store = pltpu.make_async_copy(dy, dx_out, xsem)
    cot_load = pltpu.make_async_copy(cot, dy, ysem)
    cot_load.start()

    def first_loads(l):
        stats_load(l).start()
        for load in m_loads(l, 0, False) + h_loads(l):
            load.start()

    for j in range(2):
        norm_load(1, NB_, j, j).start()
    first_loads(1)
    barrier = pltpu.get_barrier_semaphore()
    for peer in [sib] + greet:
        pl.semaphore_signal(barrier, inc=1, device_id=peer, device_id_type=MESH)
    pl.semaphore_wait(barrier, 1 + len(greet))

    def put(t, n, lane, value):
        lanes = slice(lane, lane + value.shape[1])
        if not comm:
            buf[t, n, :, lanes] = value
            return
        share = value.shape[0] // 16
        for o in range(16):
            x, y, z = o % 2, (o // 2) % 2, o // 4
            f = x * (1 - sec) + y * sec
            s = y * (1 - sec) + x * sec
            buf[t, n, f, s, z, :, lanes] = value[o * share : (o + 1) * share]

    if comm:

        def remote(src, dst, ss, rs, to):
            return pltpu.make_async_remote_copy(
                src_ref=src, dst_ref=dst, send_sem=ss, recv_sem=rs, device_id=to, device_id_type=MESH
            )

        def stage1(t, n):
            return remote(buf.at[t, n, 1 - b1], l1.at[t, n], s1.at[t, n], r1.at[t, n], (sec, near))

        def stage2(t, n):
            return remote(buf.at[t, n, b1, 1 - b2], l2.at[t, n], s2.at[t, n], r2.at[t, n], (sec, far))

        def early(n):
            return n % EARLY == 1

        def stagez(t, n, d):
            dst = l2.at[t, n, pl.ds(2 * (d - 1), 2)] if d < 3 else lz.at[t, n // EARLY]
            return remote(
                buf.at[t, n, b1, :, (bz + d) % 4], dst, sz.at[t, n // EARLY, d - 1], rz.at[t, n // EARLY, d - 1], (sec, zp[d])
            )

        def stage3(t, n, d):
            return remote(
                buf.at[t, n, b1, b2, (bz + d) % 4], shares.at[n, sec, d], s3.at[t, n, d], r3.at[n, sec, d], (1 - t, zp[d])
            )

        def stage3_far(t, n):
            return remote(
                buf.at[t, n, b1, 1 - b2, bz], shares.at[n, sec, 1], s3.at[t, n, 1], r3.at[n, sec, 1], (1 - t, far)
            )

        def keep(t, n):
            return pltpu.make_async_copy(buf.at[t, n, b1, b2, bz], shares.at[n, sec, 0], ksem.at[n])

        def landed(n, k, d):
            return remote(shares.at[n, k, d], shares.at[n, k, d], s3.at[0, n, d], r3.at[n, k, d], (1 - sec, dp))

        def join(t, n, second):
            for z in range(4):
                at = (t, n, b1, second, z)
                buf[at] = (buf[at].astype(F32) + l1[t, n, second, z].astype(F32)).astype(BF)

        def after1(t, n):
            stage1(t, n).wait()
            join(t, n, 1 - b2)

            @pl.when(early(n))
            def _():
                join(t, n, b2)
                for d in (1, 2, 3):
                    stagez(t, n, d).start()

            @pl.when(~early(n))
            def _():
                stage2(t, n).start()
                join(t, n, b2)

        def own_share(t, n):
            @pl.when(sec != 1 - t)
            def _():
                stage3(t, n, 0).start()

            @pl.when(sec == 1 - t)
            def _():
                keep(t, n).start()

        def after2(t, n):
            @pl.when(early(n))
            def _():
                for d in (1, 2, 3):
                    stagez(t, n, d).wait()
                for order in (0, 1):
                    second = (1 - b2) if order == 0 else b2
                    at = (t, n, b1, second, bz)
                    total = buf[at].astype(F32) + l2[t, n, second].astype(F32)
                    total = total + (l2[t, n, 2 + second].astype(F32) + lz[t, n // EARLY, second].astype(F32))
                    buf[at] = total.astype(BF)
                    if order == 0:
                        stage3_far(t, n).start()
                own_share(t, n)

            @pl.when(~early(n))
            def _():
                stage2(t, n).wait()
                for z in range(4):
                    at = (t, n, b1, b2, z)
                    buf[at] = (buf[at].astype(F32) + l2[t, n, z].astype(F32)).astype(BF)
                for d in (1, 2, 3):
                    stage3(t, n, d).start()
                own_share(t, n)

        def sent3(t, n):
            @pl.when(early(n))
            def _():
                stage3_far(t, n).wait_send()

            @pl.when(~early(n))
            def _():
                for d in (1, 2, 3):
                    stage3(t, n, d).wait_send()

            @pl.when(sec != 1 - t)
            def _():
                stage3(t, n, 0).wait_send()

        def arrived(t, n):
            for k in range(2):
                landed(n, k, 1).wait_recv()

                @pl.when(~early(n))
                def _():
                    for d in (2, 3):
                        landed(n, k, d).wait_recv()

                @pl.when(sec != k)
                def _():
                    landed(n, k, 0).wait_recv()

            keep(t, n).wait()

        def span(lo, hi, fn):
            def one(n, carry):
                fn(n)
                return carry

            lax.fori_loop(lo, hi, one, 0)

        def step(i, fresh=True):
            if fresh:
                stage1(i // 16, i % 16).start()
            for back, fn in ((AHEAD1, after1), (AHEAD1 + AHEAD2, after2)):
                j = i - back

                @pl.when((j >= 0) & (j < 32))
                def _():
                    fn(j // 16, j % 16)

    small[...] = jnp.zeros_like(small)
    for pad in (kpad, vpad):
        pad[0:HALO, :] = jnp.zeros((HALO, half), BF)
        pad[HALO + seq :, :] = jnp.zeros((HALO, half), BF)
    cot_load.wait()

    def layer(t, carry):
        l = 1 - t

        def transpose_pool(slots):
            for j, slot in enumerate(slots):
                tr[j * half : (j + 1) * half, :] = pool[slot].T

        stats_load(l).wait()
        for j in range(2):
            norm_load(l, NB_, j, j).wait()

        def norm_back(slots, counted, dv, rows, rstd_lane, gain, gain_sum, offset_sum, round_sum):
            n = jnp.concatenate([gbuf[j, rows, :] for j in slots], axis=1).astype(F32)
            rstd = stats[rows, rstd_lane : rstd_lane + 1]
            dn = dv * par[l, gain : gain + 1, :]
            d = rstd * (
                dn - jnp.mean(dn, axis=-1, keepdims=True) - n * jnp.mean(dn * n, axis=-1, keepdims=True)
            )
            low = d.astype(BF)
            df[rows, :] = low

            @pl.when(counted)
            def _():
                small[t, gain_sum : gain_sum + 1, :] += column_total(dv * n)
                small[t, offset_sum : offset_sum + 1, :] += column_total(dv)
                small[t, round_sum : round_sum + 1, :] += column_total(low)

        def out_norm(i, carry):
            rows = tile_rows(i)
            norm_back((0, 1), i // (ntile // 2) == sec, dy[rows, :].astype(F32), rows, RSTD_B, GAIN1, GAIN1, BIAS_B, BIAS_F)
            acc[rows, :] = jnp.zeros((TILE, width), F32)
            return carry

        lax.fori_loop(0, ntile, out_norm, 0)

        for load in m_loads(l, 1, True):
            load.start()
        for load in h_loads(l):
            load.wait()
        transpose_pool((0, 1))
        for load in chunk_loads(l, 0, 0):
            load.start()

        def out_grad(ii, carry):
            for odd in range(2):
                i = 2 * ii + odd
                for load in m_loads(l, i, odd):
                    load.wait()
                for j in range(2):
                    mt[j * PIECE : (j + 1) * PIECE, :] = (gbuf[j] if odd else pool[2 + j]).T

                @pl.when(i + 2 < ff // width)
                def _():
                    for load in m_loads(l, i + 2, odd):
                        load.start()

                g = dot(mt[...], df[:, own]).astype(BF)
                if comm:
                    for o in range(4):
                        x, y = o % 2, o // 2
                        f = x * (1 - sec) + y * sec
                        s = y * (1 - sec) + x * sec
                        for q in range(4):
                            buf[t, q, f, s, i] = g[o * 192 + q * 48 : o * 192 + (q + 1) * 48]
                else:
                    buf[t, i] = g
            return carry

        lax.fori_loop(0, ff // width // 2, out_grad, 0)
        if comm:
            step(16 * t)
            step(16 * t + 1)

        o_loads = [pool_load(j, half, o_full.at[l], j * half) for j in range(2)]
        wo_load = rows_load(0, half, wo.at[l], 0)
        head_weights = [weight_load(j, half, wqkv.at[l], j * half) for j in range(3)]
        late_loads = [norm_load(l, NA_, 0, 2)] + o_loads + [wo_load] + head_weights[:2]

        def feed(jj, carry):
            for part in range(3):
                c = 3 * jj + part
                slot = c % 2
                for load in chunk_loads(l, slot, c):
                    load.wait()

                @pl.when(c + 1 < ffh // UNITS)
                def _():
                    for load in chunk_loads(l, 1 - slot, c + 1):
                        load.start()

                @pl.when(c + 1 == ffh // UNITS)
                def _():
                    for load in late_loads:
                        load.start()

                dm = dot_nt(df[...], wslot[slot, 0:UNITS])
                gbuf[0, :, 0:UNITS] = (dm * pool[2 * slot + 1, :, 0:UNITS].astype(F32)).astype(BF)
                gbuf[1, :, 0:UNITS] = (dm * pool[2 * slot, :, 0:UNITS].astype(F32)).astype(BF)
                acc[...] += dot_nt(gbuf[0, :, 0:UNITS], wpool[2 * slot, :, 0:UNITS]) + dot_nt(
                    gbuf[1, :, 0:UNITS], wpool[2 * slot + 1, :, 0:UNITS]
                )

                @pl.when(c == ffh // UNITS - 1)
                def _():
                    @pl.when(t > 0)
                    def _():
                        exchange(1).wait_send()

                    psend[...] = acc[...].astype(BF)
                    exchange(2 * t).start()

                unit = sec * ffh + c * UNITS
                spot = lanes_at(unit % width, UNITS)
                for k in range(2):
                    small[t, pl.ds(BIAS_IN + k * (ff // width) + unit // width, 1), spot] = column_total(
                        gbuf[k, :, 0:UNITS]
                    )
                    g = dot(tr[...], gbuf[k, :, 0:UNITS]).astype(BF)
                    n = 4 + 4 * jj + 2 * k
                    if part == 0:
                        put(t, n, 0, g)
                    elif part == 1:
                        put(t, n, 256, g[:, :128])
                        put(t, n + 1, 0, g[:, 128:])
                    else:
                        put(t, n + 1, 128, g)
                if comm:
                    step(16 * t + 2 + c)
            return carry

        lax.fori_loop(0, ffh // (3 * UNITS), feed, 0)
        norm_load(l, NA_, 1, 0).start()
        head_weights[2].start()

        for load in o_loads:
            load.wait()
        transpose_pool((0, 1))
        head_rows = [pool_load(j, half, qkv.at[l, j], 0) for j in range(3)]
        for load in head_rows:
            load.start()
        pool_load(3, half, acts.at[l, X_], 0).start()
        norm_load(l, NA_, 0, 2).wait()
        norm_load(l, NA_, 1, 0).wait()
        exchange(2 * t).wait_recv()

        def attn_norm(i, carry):
            rows = tile_rows(i)
            dh = df[rows, :].astype(F32) + (psend[rows, :].astype(F32) + precv[0, rows, :].astype(F32))
            norm_back((2, 0), i // (ntile // 2) == sec, dh, rows, RSTD_A, GAIN0, GAIN0, BIAS_A, BIAS_O)
            return carry

        lax.fori_loop(0, ntile, attn_norm, 0)

        wo_load.wait()

        @pl.when((t == 1) & (sec == 1))
        def _():
            x_store.wait()

        dy[:, 0:half] = dot_nt(df[...], wslot[0]).astype(BF)
        put(t, 12, 0, dot(tr[...], df[:, own]).astype(BF))
        if comm:
            step(16 * t + 8)
            step(16 * t + 9)

        for load in head_rows:
            load.wait()

        def row(r, carry):
            base = pl.multiple_of(r * seq, seq)
            kpad[HALO : HALO + seq, :] = pool[1, pl.ds(base, seq), :]
            vpad[HALO : HALO + seq, :] = pool[2, pl.ds(base, seq), :]
            lane = lax.broadcasted_iota(jnp.int32, (QB, 128), 1)

            for g in range(half // LANES):
                cols = slice(g * LANES, (g + 1) * LANES)

                def operands(i):
                    rows = pl.ds(pl.multiple_of(base + i * QB, QB), QB)
                    window = slice(i * QB, i * QB + KW)
                    qs = stack_heads(pool[0, rows, cols] * BF(HEAD**-0.5))
                    return rows, kpad[window, cols], qs, stack_heads(dy[rows, cols])

                for i in range(seq // QB):
                    rows, kw, qs, os = operands(i)
                    far = away[r, i].astype(F32)
                    s = dot_nt(qs, kw)
                    d = dot_nt(os, vpad[i * QB : i * QB + KW, cols])
                    kept = stats[rows, :]
                    for h in range(GROUP):
                        part = slice(h * QB, (h + 1) * QB)
                        lse = jnp.sum(jnp.where(lane == g * GROUP + h, kept, 0.0), axis=-1, keepdims=True)
                        p = jnp.exp(s[part] + slope_of(sec, g, h) * far - lse)
                        pd = p * d[part]
                        mt[part, i * KW : (i + 1) * KW] = (pd - p * jnp.sum(pd, axis=-1, keepdims=True)).astype(BF)
                        mt[GROUP * QB + h * QB : GROUP * QB + (h + 1) * QB, i * KW : (i + 1) * KW] = p.astype(BF)
                for i in range(seq // QB):
                    rows, kw, qs, os = operands(i)
                    ds = mt[0 : GROUP * QB, i * KW : (i + 1) * KW]
                    ps = mt[GROUP * QB : 2 * GROUP * QB, i * KW : (i + 1) * KW]
                    gbuf[0, rows, cols] = (merge_heads(dot(ds, kw)) * HEAD**-0.5).astype(BF)
                    dk, dv = dot_tn(ds, qs), dot_tn(ps, os)
                    if i == 0:
                        at, skip = pl.ds(base, HALO), HALO
                    else:
                        at, skip = pl.ds(pl.multiple_of(base + i * QB - HALO, HALO), QB), 0
                        dk = jnp.concatenate([dk[:QB] + left_k, dk[QB:]], axis=0)
                        dv = jnp.concatenate([dv[:QB] + left_v, dv[QB:]], axis=0)
                    gbuf[1, at, cols] = dk[skip:QB].astype(BF)
                    gbuf[2, at, cols] = dv[skip:QB].astype(BF)
                    left_k, left_v = dk[QB:], dv[QB:]
                at = pl.ds(pl.multiple_of(base + seq - HALO, HALO), HALO)
                gbuf[1, at, cols] = left_k[:HALO].astype(BF)
                gbuf[2, at, cols] = left_v[:HALO].astype(BF)
            if comm:
                step(16 * t + 10 + r)
            return carry

        lax.fori_loop(0, rows_n, row, 0)
        pool_load(0, half, acts.at[l, X_], half).start()
        for load in head_weights:
            load.wait()
        exchange(2 * t).wait_send()

        total = dot_nt(gbuf[0], wpool[0])
        for j in (1, 2):
            total += dot_nt(gbuf[j], wpool[j])
        psend[...] = total.astype(BF)
        exchange(2 * t + 1).start()
        small[t, BIAS_Q : BIAS_Q + 1, own] = column_total(gbuf[0])
        small[t, BIAS_V : BIAS_V + 1, own] = column_total(gbuf[2])
        pool_load(3, half, acts.at[l, X_], 0).wait()
        pool_load(0, half, acts.at[l, X_], half).wait()
        transpose_pool((3, 0))

        @pl.when(t == 0)
        def _():
            first_loads(0)

        if comm:
            step(16 * t + 12)
        for j in range(3):
            put(t, 13 + j, 0, dot(tr[...], gbuf[j]).astype(BF))
            if j < 2:

                @pl.when(t == 0)
                def _():
                    norm_load(0, NB_, j, j).start()

            if comm and j == 0:
                step(16 * t + 13)
        exchange(2 * t + 1).wait_recv()

        def result(i, carry):
            rows = tile_rows(i)
            dx = df[rows, :].astype(F32) + (psend[rows, :].astype(F32) + precv[1, rows, :].astype(F32))
            dy[rows, :] = dx.astype(BF)
            return carry

        lax.fori_loop(0, ntile, result, 0)

        @pl.when(sec == l)
        def _():
            x_store.start()

        if comm:
            step(16 * t + 14)
            step(16 * t + 15)
        return carry

    lax.fori_loop(0, 2, layer, 0)
    exchange(3).wait_send()

    @pl.when(sec == 0)
    def _():
        x_store.wait()

    if comm:
        mine = 1 - sec

        def vectors(stage):
            if stage == 0:
                return [remote(small.at[sec], v1, vs.at[0], vr.at[0], sib)]
            if stage == 1:
                return [remote(v1, v2, vs.at[1], vr.at[1], (sec, xp))]
            if stage == 2:
                return [remote(v2, v3, vs.at[2], vr.at[2], (sec, yp))]
            return [remote(v3, v4.at[d - 1], vs.at[2 + d], vr.at[2 + d], (sec, zp[d])) for d in (1, 2, 3)]

        def go(stage):
            for c in vectors(stage):
                c.start()

        def done(stage):
            for c in vectors(stage):
                c.wait()

        def rest(lo, hi):
            span(lo, hi, lambda i: step(i, False))

        def combine(stage, there, here):
            done(stage)
            there[...] += here
            go(stage + 1)

        last = 32 + AHEAD1 + AHEAD2
        go(0)
        rest(32, 34)
        combine(0, v1, small[mine])
        rest(34, 36)
        combine(1, v2, v1[...])
        rest(36, last)
        combine(2, v3, v2[...])
        for t in range(2):
            span(0, 16, lambda n, t=t: sent3(t, n))
        span(0, 16, lambda n: arrived(mine, n))
        done(3)
        small_out[...] = v3[...] + v4[0] + v4[1] + v4[2]
    else:
        store = pltpu.make_async_copy(buf, grads_out, gsem)
        store.start()
        small_out[...] = small[...]
        store.wait()


def run_backward(comm, cot, acts, o_full, m_full, qkv, pp, stats, away, wqkv, wo, win, wout, par):
    tokens, width = cot.shape
    ff = m_full.shape[2]
    half = width // 2
    dma = pltpu.SemaphoreType.DMA
    dx = jax.ShapeDtypeStruct((tokens, width), BF)
    if comm:
        r = width // 16
        small = jax.ShapeDtypeStruct((VECTORS, width), F32)
        grads = jax.ShapeDtypeStruct((16, 2, 4, r, PIECE), BF)
        special = [
            vm(2, 16, 2, 2, 4, r, PIECE),
            vm(2, 16, 2, 4, r, PIECE),
            vm(2, 16, 4, r, PIECE),
            vm(2, 5, 2, r, PIECE),
            vm(VECTORS, width, dtype=F32),
            vm(VECTORS, width, dtype=F32),
            vm(VECTORS, width, dtype=F32),
            vm(3, VECTORS, width, dtype=F32),
            dma((2, 16)), dma((2, 16)), dma((2, 16)), dma((2, 16)), dma((2, 5, 3)), dma((2, 5, 3)),
            dma((2, 16, 4)), dma((16, 2, 4)), dma((16,)),
            dma((6,)), dma((6,)),
        ]
    else:
        small = jax.ShapeDtypeStruct((2, VECTORS, width), F32)
        grads = jax.ShapeDtypeStruct((2, 16, width, PIECE), BF)
        special = [vm(2, 16, width, PIECE), dma]
    seq = away.shape[1] * QB
    scratch = special + [
        vm(tokens, width, dtype=F32),
        vm(tokens, width),
        vm(tokens, width),
        vm(width, tokens),
        vm(width, tokens),
        vm(2, VECTORS, width, dtype=F32),
        vm(tokens, 128, dtype=F32),
        vm(4, tokens, PIECE),
        vm(4, width, PIECE),
        vm(2, half, width),
        vm(3, tokens, half),
        vm(seq + 2 * HALO, half),
        vm(seq + 2 * HALO, half),
        vm(tokens, width),
        vm(2, tokens, width),
        dma((4,)), dma((4,)), dma((2,)), dma((3,)), dma, dma, dma, dma((4,)), dma((4,)),
    ]
    return pl.pallas_call(
        functools.partial(bwd_kernel, comm),
        out_shape=(dx, small, grads),
        in_specs=[any_spec()] * 7 + [vmem_spec()] + [any_spec()] * 4 + [vmem_spec()],
        out_specs=(any_spec(), vmem_spec(), any_spec()),
        scratch_shapes=scratch,
        compiler_params=pltpu.CompilerParams(
            collective_id=2, has_side_effects=True, vmem_limit_bytes=64 << 20
        ),
        name="backward",
    )(cot, acts, o_full, m_full, qkv, pp, stats, away, wqkv, wo, win, wout, par)


def results_kernel(shares, vectors, fq, fo, fi, fu, gain_out, bias_out, inner_out, land, stage, lsem, fsem):
    me = lax.axis_index("dp")
    rows, width = fo.shape
    half, ff = width // 2, fi.shape[1] // 2
    ffh = ff // 2
    loads = []
    for n in range(16):
        used = 2 if n % EARLY == 1 else 4
        loads.append(
            pltpu.make_async_copy(shares.at[n, :, 0:used], land.at[n, :, 0:used], lsem.at[n])
        )
    for c in loads:
        c.start()

    def place(n, k):
        if n < 4:
            return fu.at[n * rows : (n + 1) * rows, k * half : (k + 1) * half]
        if n < 12:
            jj, g, i = (n - 4) // 4, (n - 4) // 2 % 2, n % 2
            start = g * ff + k * ffh + (2 * jj + i) * PIECE
            return fi.at[:, start : start + PIECE]
        if n == 12:
            return fo.at[:, k * half : (k + 1) * half]
        start = (n - 13) * width + k * half
        return fq.at[:, start : start + half]

    stores = []
    for n in range(16):
        loads[n].wait()
        for k in range(2):
            total = land[n, k, 0].astype(F32) + land[n, k, 1].astype(F32)
            if n % EARLY != 1:
                total = total + (land[n, k, 2].astype(F32) + land[n, k, 3].astype(F32))
            stage[n, k] = total
            stores.append(pltpu.make_async_copy(stage.at[n, k], place(n, k), fsem.at[n, k]))
            stores[-1].start()
    turned = pltpu.roll(vectors[0:8, :], (width - me * rows) % width, axis=1)
    gain_out[...] = turned[0:2, 0:rows]
    for j in range(6):
        bias_out[j] = turned[2 + j : 3 + j, 0:rows]
    line = vectors[pl.ds(8 + me // 2, 1), :]
    inner_out[...] = jnp.where(me % 2 == 0, line[:, :half], line[:, half:])
    for c in stores:
        c.wait()


def run_results(shares, vectors, ff):
    _, _, _, rows, half = shares.shape
    width = 2 * half
    dma = pltpu.SemaphoreType.DMA

    def out(*shape):
        return jax.ShapeDtypeStruct(shape, F32)

    return pl.pallas_call(
        results_kernel,
        out_shape=(
            out(rows, 3 * width), out(rows, width), out(rows, 2 * ff), out(ff // 16, width),
            out(2, rows), out(6, 1, rows), out(1, 2 * ff // 16),
        ),
        in_specs=[any_spec(), vmem_spec()],
        out_specs=tuple([any_spec()] * 4 + [vmem_spec()] * 3),
        scratch_shapes=[
            vm(*shares.shape), vm(16, 2, rows, half, dtype=F32), dma((16,)), dma((16, 2)),
        ],
        compiler_params=pltpu.CompilerParams(vmem_limit_bytes=60 << 20),
        name="results",
    )(shares, vectors)


def assemble(halves, width, ff):
    def columns(v):
        return jnp.concatenate(v, axis=1)

    gu = columns([h[:4].reshape(ff, PIECE) for h in halves])
    inner = [
        columns([h[4 + 4 * jj + 2 * k + i] for jj in range(2) for i in range(2)]) for k in range(2) for h in halves
    ]
    gi = columns(inner)
    go = columns([h[12] for h in halves])
    gq = columns([h[13 + j] for j in range(3) for h in halves])
    return gq, go, gi, gu


def shards(comm, hidden, segs, w_qkv, w_o, w_in, w_out, gains, biases, b_in, cot):
    w_qkv, w_o, w_in, w_out, gains = (v[0] for v in (w_qkv, w_o, w_in, w_out, gains))
    biases = jnp.transpose(biases, (1, 0, 2))
    micro, _, seq, width = hidden.shape
    ff = w_out.shape[0]
    tokens = micro * seq
    y, acts, o_full, m_full, qkv, pp, stats, wqkv2, wo2, win2, wout2, par2, away = run_forward(
        hidden.reshape(micro, seq, width), segs, w_qkv, w_o, w_in, w_out, gains, biases, b_in
    )
    dx, small, grads = run_backward(
        comm, cot.reshape(tokens, width), acts.reshape(2, 4, tokens, width), o_full.reshape(2, tokens, width),
        m_full.reshape(2, tokens, ff), qkv.reshape(2, 3, tokens, width // 2), pp.reshape(2, 2, tokens, ff // 2),
        stats.reshape(2, tokens, 128), away, wqkv2, wo2, win2, wout2, par2,
    )
    if comm:
        gq, go, gi, gu, gain, bias, inner = run_results(grads, small, ff)
        return (
            y.reshape(1, *hidden.shape), dx.reshape(1, *hidden.shape), gq[None], go[None], gi[None], gu[None],
            gain[None], jnp.transpose(bias, (1, 0, 2)), inner,
        )
    owners, me = lax.axis_size("dp"), lax.axis_index("dp")
    first = lax.axis_index("section") == 0
    swap = [(0, 1), (1, 0)]

    def pick(v):
        own = jnp.where(first, v[1], v[0])
        return own, lax.ppermute(jnp.where(first, v[0], v[1]), "section", swap)

    own, other = pick(grads)
    halves = [jnp.where(first, own, other), jnp.where(first, other, own)]

    def share(v):
        parts = v.reshape(owners, v.shape[0] // owners, v.shape[1])
        got = lax.all_to_all(parts, "dp", split_axis=0, concat_axis=0, tiled=True)
        return jnp.sum(got.astype(F32), axis=0)

    gq, go, gi, gu = (share(v) for v in assemble(halves, width, ff))
    own, other = pick(small)
    small = lax.psum(own + other, "dp")
    part = width // owners
    mine = lax.dynamic_slice_in_dim(small[:8], me * part, part, axis=1)
    inner = lax.dynamic_slice_in_dim(small[8:].reshape(1, 2 * ff), me * (2 * ff // owners), 2 * ff // owners, axis=1)
    return (
        y.reshape(1, *hidden.shape), dx.reshape(1, *hidden.shape), gq[None], go[None], gi[None], gu[None],
        mine[None, :2], mine[None, 2:], inner,
    )


def solution(mesh):
    rows = P(None, "dp", None, None)
    layer = P("section", None, None)
    comm = mesh.shape["dp"] == 16
    return jax.shard_map(
        functools.partial(shards, comm),
        mesh=mesh,
        in_specs=(rows, P(None, "dp", None)) + (layer,) * 6 + (P("section", None), rows),
        out_specs=(
            P("section", None, "dp", None, None),
            P("section", None, "dp", None, None),
            P("section", "dp", None),
            P("section", "dp", None),
            P("section", "dp", None),
            P("section", "dp", None),
            P("section", None, "dp"),
            P("section", None, "dp"),
            P("section", "dp"),
        ),
        check_vma=False,
    )
```

```python
import functools
import math

import jax
import jax.numpy as jnp
from jax import lax
from jax.experimental import pallas as pl
from jax.experimental.pallas import tpu as pltpu
from jax.sharding import PartitionSpec as P

HEADS = 12
HEAD = 64
GROUP = 2
LANES = GROUP * HEAD
QB = 128
HALO = 64
KW = QB + 2 * HALO
EPS = 1e-05
MASKED = -1.0e30
TILE = 256
UNITS = 256
PIECE = 384
BF = jnp.bfloat16
F32 = jnp.float32
MESH = pl.DeviceIdType.MESH
NT = (((1,), (1,)), ((), ()))
TN = (((0,), (0,)), ((), ()))
H_, NA_, NB_, X_ = range(4)
M_, P1_, P2_ = range(3)
GAIN0, GAIN1, BIAS_Q, BIAS_V, BIAS_O, BIAS_A, BIAS_F, BIAS_B, BIAS_IN = range(9)
VECTORS = 16
FEED = 512
AHEAD1, AHEAD2 = 3, 2
EARLY = 3
RSTD_A, RSTD_B = HEADS, HEADS + 1


def slope_list(head_count):
    base = 2 ** int(math.floor(math.log2(head_count)))
    leading = [2.0 ** (-8.0 * (k + 1) / base) for k in range(base)]
    trailing = [2.0 ** (-4.0 * (2 * k + 1) / base) for k in range(head_count - base)]
    return leading + trailing


def dot(a, b):
    return jnp.dot(a, b, preferred_element_type=F32)


def dot_nt(a, b):
    return lax.dot_general(a, b, NT, preferred_element_type=F32)


def dot_tn(a, b):
    return lax.dot_general(a, b, TN, preferred_element_type=F32)


def normalize(v):
    c = v - jnp.mean(v, axis=-1, keepdims=True)
    rstd = lax.rsqrt(jnp.mean(c * c, axis=-1, keepdims=True) + EPS)
    return c * rstd, rstd


def stack_heads(v):
    head = lax.broadcasted_iota(jnp.int32, v.shape, 1) // HEAD
    zero = jnp.zeros_like(v)
    return jnp.concatenate([jnp.where(head == h, v, zero) for h in range(GROUP)], axis=0)


def merge_heads(r):
    rows = r.shape[0] // GROUP
    head = lax.broadcasted_iota(jnp.int32, (rows, r.shape[1]), 1) // HEAD
    out = r[:rows]
    for h in range(1, GROUP):
        out = jnp.where(head == h, r[h * rows : (h + 1) * rows], out)
    return out


def fill_away(away, segs):
    micro, _, seq = segs.shape
    r = lax.broadcasted_iota(jnp.int32, (QB, KW), 0)
    c = lax.broadcasted_iota(jnp.int32, (QB, KW), 1)
    apart = -jnp.abs(r + HALO - c).astype(F32)
    outside = jnp.full((QB, 128), -1.0, F32)
    for m in range(micro):
        seg = jnp.broadcast_to(segs[m].astype(F32), (QB, seq))
        keys = pltpu.roll(jnp.concatenate([outside, seg, outside], axis=1), seq + 256 - HALO, axis=1)
        for i in range(seq // QB):
            own = seg[:, i * QB : (i + 1) * QB].T
            own = jnp.concatenate([own, own], axis=1)
            same = own == keys[:, i * QB : i * QB + KW]
            away[m, i] = jnp.where(same, apart, MASKED).astype(BF)


def slope_of(sec, g, h):
    table = slope_list(HEADS)
    return jnp.where(sec == 0, table[g * GROUP + h], table[HEADS // 2 + g * GROUP + h]).astype(F32)


def tile_rows(t):
    return pl.ds(pl.multiple_of(t * TILE, TILE), TILE)


def lanes_at(start, count):
    return pl.ds(pl.multiple_of(start, 128), count)


def fwd_kernel(
    hid, segs, wqkv_h, wo_h, win_h, wout_h, gains_in, biases_in, bin_in,
    y_out, acts_out, o_out, m_out, qkv_out, p_out, stats_out,
    wqkv_out, wo_out, win_out, wout_out, par_out, away_out,
    wqkv, wo, win, wout, par, bin_, xy, qkvs, os_, hs, big, psend, precv, acc, kpad, vpad, held, away, stats,
    lsem, rsend, rrecv, wsave, hsem, ysem, asem, qsem, osem, osend, orecv, bsem, msend, mrecv, tsem, ssend, srecv,
    parsem, awaysem,
):
    dp = lax.axis_index("dp")
    sec = lax.axis_index("section")
    _, micro, seq, width = xy.shape
    half, ffh, ff = wo.shape[1], wout.shape[1], wout_h.shape[0]
    sib = (1 - sec, dp)

    parts = []
    for j in range(3):
        parts.append((wqkv_h, wqkv, lambda c, j=j: (slice(None), lanes_at(j * width + c * half, half)),
                      (slice(None), slice(j * half, (j + 1) * half))))
    parts.append((wo_h, wo, lambda c: (pl.ds(pl.multiple_of(c * half, 128), half), slice(None)), (slice(None), slice(None))))
    for j in range(2):
        parts.append((win_h, win, lambda c, j=j: (slice(None), lanes_at(j * ff + c * ffh, ffh)),
                      (slice(None), slice(j * ffh, (j + 1) * ffh))))
    parts.append((wout_h, wout, lambda c: (pl.ds(pl.multiple_of(c * ffh, 128), ffh), slice(None)), (slice(None), slice(None))))

    def own_part(i):
        src, dst, pick, place = parts[i]
        return pltpu.make_async_copy(src.at[pick(sec)], dst.at[(sec, *place)], lsem.at[i])

    def other_part(i):
        src, dst, pick, place = parts[i]
        return pltpu.make_async_remote_copy(
            src_ref=src.at[pick(1 - sec)], dst_ref=dst.at[(sec, *place)],
            send_sem=rsend.at[i], recv_sem=rrecv.at[i], device_id=sib, device_id_type=MESH,
        )

    def other_vectors():
        return [
            pltpu.make_async_remote_copy(
                src_ref=v.at[sec], dst_ref=v.at[sec], send_sem=rsend.at[7 + i], recv_sem=rrecv.at[7 + i],
                device_id=sib, device_id_type=MESH,
            )
            for i, v in enumerate((par, bin_))
        ]

    def x_load(m):
        return pltpu.make_async_copy(hid.at[m], xy.at[0, m], hsem.at[m])

    for m in range(micro):
        x_load(m).start()
    for i in range(7):
        own_part(i).start()
    par[sec, 0:2] = gains_in[...]
    for j in range(6):
        par[sec, 2 + j : 3 + j] = biases_in[j]
    bin_[sec] = bin_in[...]
    barrier = pltpu.get_barrier_semaphore()
    pl.semaphore_signal(barrier, inc=1, device_id=sib, device_id_type=MESH)
    pl.semaphore_wait(barrier, 1)
    for c in other_vectors():
        c.start()
    for i in range(7):
        other_part(i).start()
    fill_away(away, segs)
    away_save = pltpu.make_async_copy(away, away_out, awaysem)
    away_save.start()
    for pad in (kpad, vpad):
        pad[0:HALO, :] = jnp.zeros((HALO, half), BF)
        pad[HALO + seq :, :] = jnp.zeros((HALO, half), BF)
    for m in range(micro):
        x_load(m).wait()

    def need(l, which):
        @pl.when(l == sec)
        def _():
            for i in which:
                own_part(i).wait()

        @pl.when(l != sec)
        def _():
            for i in which:
                other_part(i).wait_recv()

    def save(kind, l, m):
        src = xy.at[l, m] if kind == X_ else hs.at[kind, m]
        return pltpu.make_async_copy(src, acts_out.at[l, kind, m], asem.at[kind, l, m])

    def save_qkv(kind, l, m):
        return pltpu.make_async_copy(qkvs.at[m, kind], qkv_out.at[l, kind, m], qsem.at[kind, l, m])

    def save_o(l, m):
        return pltpu.make_async_copy(os_.at[m], o_out.at[l, m, :, lanes_at(sec * half, half)], osem.at[l, m])

    def share_o(l, m):
        return pltpu.make_async_remote_copy(
            src_ref=os_.at[m], dst_ref=o_out.at[l, m, :, lanes_at(sec * half, half)],
            send_sem=osend.at[l, m], recv_sem=orecv.at[l, m], device_id=sib, device_id_type=MESH,
        )

    def save_big(kind, l, m):
        if kind == M_:
            dst = m_out.at[l, m, :, lanes_at(sec * ffh, ffh)]
        else:
            dst = p_out.at[l, kind - 1, m]
        return pltpu.make_async_copy(big.at[m, kind], dst, bsem.at[kind, l, m])

    def share_m(l, m):
        return pltpu.make_async_remote_copy(
            src_ref=big.at[m, M_], dst_ref=m_out.at[l, m, :, lanes_at(sec * ffh, ffh)],
            send_sem=msend.at[l, m], recv_sem=mrecv.at[l, m], device_id=sib, device_id_type=MESH,
        )

    def save_stats(l, m):
        return pltpu.make_async_copy(stats.at[l, m], stats_out.at[l, m], tsem.at[l, m])

    def save_y(m):
        return pltpu.make_async_copy(xy.at[sec + 1, m], y_out.at[m], ysem.at[m])

    def partial(phase, l, m):
        return pltpu.make_async_remote_copy(
            src_ref=psend.at[phase, m], dst_ref=precv.at[phase, l, m],
            send_sem=ssend.at[phase, l, m], recv_sem=srecv.at[phase, l, m], device_id=sib, device_id_type=MESH,
        )

    def weight_saves(l):
        pairs = ((wqkv, wqkv_out), (wo, wo_out), (win, win_out), (wout, wout_out))
        return [pltpu.make_async_copy(s.at[l], d.at[l], wsave.at[i, l]) for i, (s, d) in enumerate(pairs)]

    par_save = pltpu.make_async_copy(par, par_out, parsem)

    def attend(l, m):
        @pl.when(m == 0)
        def _():
            need(l, (0, 1, 2))

            @pl.when(l != sec)
            def _():
                for c in other_vectors():
                    c.wait_recv()

        @pl.when(l > 0)
        def _():
            for kind in range(3):
                save_qkv(kind, l - 1, m).wait()
            save_o(l - 1, m).wait()
            share_o(l - 1, m).wait_send()
            partial(0, l - 1, m).wait_send()

        save(X_, l, m).start()
        bias_q = par[l, BIAS_Q : BIAS_Q + 1, lanes_at(sec * half, half)]
        bias_v = par[l, BIAS_V : BIAS_V + 1, lanes_at(sec * half, half)]

        r = dot(xy[l, m], wqkv[l])
        q = (r[:, :half] + bias_q).astype(BF)
        k = r[:, half : 2 * half].astype(BF)
        v = (r[:, 2 * half :] + bias_v).astype(BF)
        for j, w in enumerate((q, k, v)):
            qkvs[m, j] = w
        kpad[HALO : HALO + seq, :] = k
        vpad[HALO : HALO + seq, :] = v
        for kind in range(3):
            save_qkv(kind, l, m).start()

        lane = lax.broadcasted_iota(jnp.int32, (QB, 128), 1)
        for g in range(half // LANES):
            cols = slice(g * LANES, (g + 1) * LANES)
            for i in range(seq // QB):
                rows = slice(i * QB, (i + 1) * QB)
                far = away[m, i].astype(F32)
                qs = stack_heads(qkvs[m, 0, rows, cols] * BF(HEAD**-0.5))
                s = dot_nt(qs, kpad[i * QB : i * QB + KW, cols])
                probs = []
                kept = stats[l, m, rows, :]
                for h in range(GROUP):
                    sh = s[h * QB : (h + 1) * QB] + slope_of(sec, g, h) * far
                    top = jnp.max(sh, axis=-1, keepdims=True)
                    e = jnp.exp(sh - top)
                    total = jnp.sum(e, axis=-1, keepdims=True)
                    probs.append((e * (1.0 / total)).astype(BF))
                    kept = jnp.where(lane == g * GROUP + h, top + jnp.log(total), kept)
                stats[l, m, rows, :] = kept
                held[:, i * KW : (i + 1) * KW] = jnp.concatenate(probs, axis=0)
            for i in range(seq // QB):
                rows = slice(i * QB, (i + 1) * QB)
                r = dot(held[:, i * KW : (i + 1) * KW], vpad[i * QB : i * QB + KW, cols])
                os_[m, rows, cols] = merge_heads(r).astype(BF)

        save_o(l, m).start()
        share_o(l, m).start()

        @pl.when(m == 0)
        def _():
            need(l, (3,))

        psend[0, m] = dot(os_[m], wo[l]).astype(BF)
        partial(0, l, m).start()

    def feed(l, m):
        @pl.when(m == 0)
        def _():
            need(l, (4, 5, 6))
            for c in weight_saves(l):
                c.start()

        @pl.when(l > 0)
        def _():
            save(H_, l - 1, m).wait()
            save(NA_, l - 1, m).wait()
            for kind in range(3):
                save_big(kind, l - 1, m).wait()
            share_m(l - 1, m).wait_send()
            partial(1, l - 1, m).wait_send()

        partial(0, l, m).wait_recv()
        lane = lax.broadcasted_iota(jnp.int32, (TILE, 128), 1)

        def norm(t, carry):
            rows = tile_rows(t)
            a = xy[l, m, rows, :].astype(F32) + (
                psend[0, m, rows, :].astype(F32) + precv[0, l, m, rows, :].astype(F32) + par[l, BIAS_O : BIAS_O + 1, :]
            )
            n, rstd = normalize(a)
            hs[NA_, m, rows, :] = n.astype(BF)
            hs[H_, m, rows, :] = (n * par[l, GAIN0 : GAIN0 + 1, :] + par[l, BIAS_A : BIAS_A + 1, :]).astype(BF)
            stats[l, m, rows, :] = jnp.where(lane == RSTD_A, rstd, stats[l, m, rows, :])
            return carry

        lax.fori_loop(0, seq // TILE, norm, 0)
        save(H_, l, m).start()
        save(NA_, l, m).start()
        h = hs[H_, m]
        for c in range(ffh // FEED):
            cols = slice(c * FEED, (c + 1) * FEED)
            unit = sec * ffh + c * FEED
            gate = dot(h, win[l, :, cols]) + bin_[l, :, lanes_at(unit, FEED)]
            up = dot(h, win[l, :, ffh + c * FEED : ffh + (c + 1) * FEED]) + bin_[l, :, lanes_at(ff + unit, FEED)]
            cdf = 0.5 + 0.5 * lax.erf(gate * (0.5**0.5))
            act = gate * cdf
            slope = cdf + gate * (jnp.exp(gate * gate * -0.5) * (2.0 * math.pi) ** -0.5)
            mixed = (act * up).astype(BF)
            big[m, M_, :, cols] = mixed
            big[m, P1_, :, cols] = act.astype(BF)
            big[m, P2_, :, cols] = (up * slope).astype(BF)
            down = dot(mixed, wout[l, cols, :])
            acc[...] = down if c == 0 else acc[...] + down

        psend[1, m] = acc[...].astype(BF)
        partial(1, l, m).start()
        for kind in range(3):
            save_big(kind, l, m).start()
        share_m(l, m).start()

    def finish(l, m):
        @pl.when(l > 0)
        def _():
            save(NB_, l - 1, m).wait()

        partial(1, l, m).wait_recv()
        lane = lax.broadcasted_iota(jnp.int32, (TILE, 128), 1)

        def norm(t, carry):
            rows = tile_rows(t)
            b = hs[H_, m, rows, :].astype(F32) + (
                psend[1, m, rows, :].astype(F32) + precv[1, l, m, rows, :].astype(F32) + par[l, BIAS_F : BIAS_F + 1, :]
            )
            n, rstd = normalize(b)
            hs[NB_, m, rows, :] = n.astype(BF)
            xy[l + 1, m, rows, :] = (n * par[l, GAIN1 : GAIN1 + 1, :] + par[l, BIAS_B : BIAS_B + 1, :]).astype(BF)
            stats[l, m, rows, :] = jnp.where(lane == RSTD_B, rstd, stats[l, m, rows, :])
            return carry

        lax.fori_loop(0, seq // TILE, norm, 0)
        save(NB_, l, m).start()
        save_stats(l, m).start()

        @pl.when(l == sec)
        def _():
            save_y(m).start()

    def layer(l, carry):
        def first(m, carry):
            @pl.when(l > 0)
            def _():
                finish(l - 1, m)

            attend(l, m)
            return carry

        lax.fori_loop(0, micro, first, 0)

        def second(m, carry):
            feed(l, m)
            return carry

        lax.fori_loop(0, micro, second, 0)
        return carry

    lax.fori_loop(0, 2, layer, 0)
    par_save.start()

    def last(m, carry):
        finish(1, m)
        return carry

    lax.fori_loop(0, micro, last, 0)

    def drain(m, carry):
        for kind in range(3):
            save_qkv(kind, 1, m).wait()
            save_big(kind, 1, m).wait()
        for kind in (H_, NA_, NB_):
            save(kind, 1, m).wait()
        save_o(1, m).wait()
        share_o(1, m).wait_send()
        share_m(1, m).wait_send()
        for phase in range(2):
            partial(phase, 1, m).wait_send()
        for l in range(2):
            save(X_, l, m).wait()
            save_stats(l, m).wait()
            share_o(l, m).wait_recv()
            share_m(l, m).wait_recv()
        save_y(m).wait()
        return carry

    lax.fori_loop(0, micro, drain, 0)
    for l in range(2):
        for c in weight_saves(l):
            c.wait()
    for i in range(7):
        other_part(i).wait_send()
    for c in other_vectors():
        c.wait_send()
    par_save.wait()
    away_save.wait()


def any_spec():
    return pl.BlockSpec(memory_space=pl.ANY)


def vmem_spec():
    return pl.BlockSpec(memory_space=pltpu.VMEM)


def smem_spec():
    return pl.BlockSpec(memory_space=pltpu.SMEM)


def vm(*shape, dtype=BF):
    return pltpu.VMEM(shape, dtype)


def run_forward(hid, segs, w_qkv, w_o, w_in, w_out, gains, biases, b_in):
    micro, seq, width = hid.shape
    ff = w_out.shape[0]
    half, ffh = width // 2, ff // 2
    dma = pltpu.SemaphoreType.DMA

    def out(*shape, dtype=BF):
        return jax.ShapeDtypeStruct(shape, dtype)

    shapes = (
        out(micro, seq, width),
        out(2, 4, micro, seq, width),
        out(2, micro, seq, width),
        out(2, micro, seq, ff),
        out(2, 3, micro, seq, half),
        out(2, 2, micro, seq, ffh),
        out(2, micro, seq, 128, dtype=F32),
        out(2, width, 3 * half),
        out(2, half, width),
        out(2, width, 2 * ffh),
        out(2, ffh, width),
        out(2, 8, width, dtype=F32),
        out(micro, seq // QB, QB, KW),
    )
    return pl.pallas_call(
        fwd_kernel,
        out_shape=shapes,
        in_specs=[any_spec(), vmem_spec()] + [any_spec()] * 4 + [vmem_spec()] * 3,
        out_specs=tuple([any_spec()] * len(shapes)),
        scratch_shapes=[
            vm(2, width, 3 * half),
            vm(2, half, width),
            vm(2, width, 2 * ffh),
            vm(2, ffh, width),
            vm(2, 8, width, dtype=F32),
            vm(2, 1, 2 * ff, dtype=F32),
            vm(3, micro, seq, width),
            vm(micro, 3, seq, half),
            vm(micro, seq, half),
            vm(3, micro, seq, width),
            vm(micro, 3, seq, ffh),
            vm(2, micro, seq, width),
            vm(2, 2, micro, seq, width),
            vm(seq, width, dtype=F32),
            vm(seq + 2 * HALO, half),
            vm(seq + 2 * HALO, half),
            vm(GROUP * QB, seq // QB * KW),
            vm(micro, seq // QB, QB, KW),
            vm(2, micro, seq, 128, dtype=F32),
            dma((7,)), dma((9,)), dma((9,)), dma((4, 2)), dma((micro,)), dma((micro,)), dma((4, 2, micro)),
            dma((3, 2, micro)), dma((2, micro)), dma((2, micro)), dma((2, micro)), dma((3, 2, micro)),
            dma((2, micro)), dma((2, micro)), dma((2, micro)), dma((2, 2, micro)), dma((2, 2, micro)), dma, dma,
        ],
        compiler_params=pltpu.CompilerParams(
            collective_id=1, has_side_effects=True, vmem_limit_bytes=62 << 20
        ),
        name="forward",
    )(hid, segs, w_qkv, w_o, w_in, w_out, gains, biases, b_in)


def column_total(v):
    return jnp.sum(v.astype(F32), axis=0, keepdims=True)


def bwd_kernel(
    comm, cot, acts, o_full, m_full, qkv, pp, stats_h, away, wqkv, wo, win, wout, par, *refs
):
    if comm:
        (dx_out, small_out, shares, *rest) = refs
        (buf, l1, l2, lz, v1, v2, v3, v4, s1, r1, s2, r2, sz, rz, s3, r3, ksem, vs, vr, *rest) = rest
    else:
        (dx_out, small_out, grads_out, *rest) = refs
        (buf, gsem, *rest) = rest
    (acc, df, dy, tr, mt, small, stats, pool, wpool, wslot, gbuf, kpad, vpad, psend, precv,
     poolsem, wsem, usem, nsem, ssem, ysem, xsem, esend, erecv) = rest
    dp = lax.axis_index("dp")
    sec = lax.axis_index("section")
    sib = (1 - sec, dp)
    tokens, width = df.shape
    rows_n, seq = away.shape[0], away.shape[1] * QB
    ff = m_full.shape[2]
    half, ffh = width // 2, ff // 2
    ntile = tokens // TILE
    own = lanes_at(sec * half, half)

    if comm:
        bx, by, bz = dp % 2, (dp // 2) % 2, dp // 4
        xp = dp + 1 - 2 * bx
        yp = dp + 2 - 4 * by
        zp = [dp] + [((bz + d) % 4) * 4 + dp % 4 for d in range(1, 4)]
        near = xp * (1 - sec) + yp * sec
        far = yp * (1 - sec) + xp * sec
        b1 = bx * (1 - sec) + by * sec
        b2 = by * (1 - sec) + bx * sec
        greet = [(sec, xp), (sec, yp)] + [(sec, z) for z in zp[1:]] + [(1 - sec, z) for z in zp[1:] + [xp, yp]]
    else:
        greet = []

    def pool_load(slot, count, src, first):
        return pltpu.make_async_copy(src.at[:, lanes_at(first, count)], pool.at[slot, :, 0:count], poolsem.at[slot])

    def weight_load(slot, count, src, first):
        return pltpu.make_async_copy(src.at[:, lanes_at(first, count)], wpool.at[slot, :, 0:count], wsem.at[slot])

    def rows_load(slot, count, src, first):
        return pltpu.make_async_copy(
            src.at[pl.ds(pl.multiple_of(first, 128), count), :], wslot.at[slot, 0:count], usem.at[slot]
        )

    def norm_load(l, kind, j, slot):
        return pltpu.make_async_copy(acts.at[l, kind, :, j * half : (j + 1) * half], gbuf.at[slot], nsem.at[slot])

    def stats_load(l):
        return pltpu.make_async_copy(stats_h.at[l], stats, ssem)

    def m_loads(l, i, odd):
        return [
            pltpu.make_async_copy(
                m_full.at[l, :, lanes_at((2 * i + j) * PIECE, PIECE)],
                gbuf.at[j] if odd else pool.at[2 + j],
                nsem.at[j] if odd else poolsem.at[2 + j],
            )
            for j in range(2)
        ]

    def h_loads(l):
        return [pool_load(j, half, acts.at[l, H_], j * half) for j in range(2)]

    def chunk_loads(l, slot, c):
        first = c * UNITS
        return [
            weight_load(2 * slot, UNITS, win.at[l], first),
            weight_load(2 * slot + 1, UNITS, win.at[l], ffh + first),
            rows_load(slot, UNITS, wout.at[l], first),
            pool_load(2 * slot, UNITS, pp.at[l, 0], first),
            pool_load(2 * slot + 1, UNITS, pp.at[l, 1], first),
        ]

    def exchange(e):
        return pltpu.make_async_remote_copy(
            src_ref=psend, dst_ref=precv.at[e % 2], send_sem=esend.at[e], recv_sem=erecv.at[e],
            device_id=sib, device_id_type=MESH,
        )

    x_store = pltpu.make_async_copy(dy, dx_out, xsem)
    cot_load = pltpu.make_async_copy(cot, dy, ysem)
    cot_load.start()

    def first_loads(l):
        stats_load(l).start()
        for load in m_loads(l, 0, False) + h_loads(l):
            load.start()

    for j in range(2):
        norm_load(1, NB_, j, j).start()
    first_loads(1)
    barrier = pltpu.get_barrier_semaphore()
    for peer in [sib] + greet:
        pl.semaphore_signal(barrier, inc=1, device_id=peer, device_id_type=MESH)
    pl.semaphore_wait(barrier, 1 + len(greet))

    def put(t, n, lane, value):
        lanes = slice(lane, lane + value.shape[1])
        if not comm:
            buf[t, n, :, lanes] = value
            return
        share = value.shape[0] // 16
        for o in range(16):
            x, y, z = o % 2, (o // 2) % 2, o // 4
            f = x * (1 - sec) + y * sec
            s = y * (1 - sec) + x * sec
            buf[t, n, f, s, z, :, lanes] = value[o * share : (o + 1) * share]

    if comm:

        def remote(src, dst, ss, rs, to):
            return pltpu.make_async_remote_copy(
                src_ref=src, dst_ref=dst, send_sem=ss, recv_sem=rs, device_id=to, device_id_type=MESH
            )

        def stage1(t, n):
            return remote(buf.at[t, n, 1 - b1], l1.at[t, n], s1.at[t, n], r1.at[t, n], (sec, near))

        def stage2(t, n):
            return remote(buf.at[t, n, b1, 1 - b2], l2.at[t, n], s2.at[t, n], r2.at[t, n], (sec, far))

        def early(n):
            return n % EARLY == 1

        def stagez(t, n, d):
            dst = l2.at[t, n, pl.ds(2 * (d - 1), 2)] if d < 3 else lz.at[t, n // EARLY]
            return remote(
                buf.at[t, n, b1, :, (bz + d) % 4], dst, sz.at[t, n // EARLY, d - 1], rz.at[t, n // EARLY, d - 1], (sec, zp[d])
            )

        def stage3(t, n, d):
            return remote(
                buf.at[t, n, b1, b2, (bz + d) % 4], shares.at[n, sec, d], s3.at[t, n, d], r3.at[n, sec, d], (1 - t, zp[d])
            )

        def stage3_far(t, n):
            return remote(
                buf.at[t, n, b1, 1 - b2, bz], shares.at[n, sec, 1], s3.at[t, n, 1], r3.at[n, sec, 1], (1 - t, far)
            )

        def keep(t, n):
            return pltpu.make_async_copy(buf.at[t, n, b1, b2, bz], shares.at[n, sec, 0], ksem.at[n])

        def landed(n, k, d):
            return remote(shares.at[n, k, d], shares.at[n, k, d], s3.at[0, n, d], r3.at[n, k, d], (1 - sec, dp))

        def join(t, n, second):
            for z in range(4):
                at = (t, n, b1, second, z)
                buf[at] = (buf[at].astype(F32) + l1[t, n, second, z].astype(F32)).astype(BF)

        def after1(t, n):
            stage1(t, n).wait()
            join(t, n, 1 - b2)

            @pl.when(early(n))
            def _():
                join(t, n, b2)
                for d in (1, 2, 3):
                    stagez(t, n, d).start()

            @pl.when(~early(n))
            def _():
                stage2(t, n).start()
                join(t, n, b2)

        def own_share(t, n):
            @pl.when(sec != 1 - t)
            def _():
                stage3(t, n, 0).start()

            @pl.when(sec == 1 - t)
            def _():
                keep(t, n).start()

        def after2(t, n):
            @pl.when(early(n))
            def _():
                for d in (1, 2, 3):
                    stagez(t, n, d).wait()
                for order in (0, 1):
                    second = (1 - b2) if order == 0 else b2
                    at = (t, n, b1, second, bz)
                    total = buf[at].astype(F32) + l2[t, n, second].astype(F32)
                    total = total + (l2[t, n, 2 + second].astype(F32) + lz[t, n // EARLY, second].astype(F32))
                    buf[at] = total.astype(BF)
                    if order == 0:
                        stage3_far(t, n).start()
                own_share(t, n)

            @pl.when(~early(n))
            def _():
                stage2(t, n).wait()
                for z in range(4):
                    at = (t, n, b1, b2, z)
                    buf[at] = (buf[at].astype(F32) + l2[t, n, z].astype(F32)).astype(BF)
                for d in (1, 2, 3):
                    stage3(t, n, d).start()
                own_share(t, n)

        def sent3(t, n):
            @pl.when(early(n))
            def _():
                stage3_far(t, n).wait_send()

            @pl.when(~early(n))
            def _():
                for d in (1, 2, 3):
                    stage3(t, n, d).wait_send()

            @pl.when(sec != 1 - t)
            def _():
                stage3(t, n, 0).wait_send()

        def arrived(t, n):
            for k in range(2):
                landed(n, k, 1).wait_recv()

                @pl.when(~early(n))
                def _():
                    for d in (2, 3):
                        landed(n, k, d).wait_recv()

                @pl.when(sec != k)
                def _():
                    landed(n, k, 0).wait_recv()

            keep(t, n).wait()

        def span(lo, hi, fn):
            def one(n, carry):
                fn(n)
                return carry

            lax.fori_loop(lo, hi, one, 0)

        def step(i, fresh=True):
            if fresh:
                stage1(i // 16, i % 16).start()
            for back, fn in ((AHEAD1, after1), (AHEAD1 + AHEAD2, after2)):
                j = i - back

                @pl.when((j >= 0) & (j < 32))
                def _():
                    fn(j // 16, j % 16)

    small[...] = jnp.zeros_like(small)
    for pad in (kpad, vpad):
        pad[0:HALO, :] = jnp.zeros((HALO, half), BF)
        pad[HALO + seq :, :] = jnp.zeros((HALO, half), BF)
    cot_load.wait()

    def layer(t, carry):
        l = 1 - t

        def transpose_pool(slots):
            for j, slot in enumerate(slots):
                tr[j * half : (j + 1) * half, :] = pool[slot].T

        stats_load(l).wait()
        for j in range(2):
            norm_load(l, NB_, j, j).wait()

        def norm_back(slots, counted, dv, rows, rstd_lane, gain, gain_sum, offset_sum, round_sum):
            n = jnp.concatenate([gbuf[j, rows, :] for j in slots], axis=1).astype(F32)
            rstd = stats[rows, rstd_lane : rstd_lane + 1]
            dn = dv * par[l, gain : gain + 1, :]
            d = rstd * (
                dn - jnp.mean(dn, axis=-1, keepdims=True) - n * jnp.mean(dn * n, axis=-1, keepdims=True)
            )
            low = d.astype(BF)
            df[rows, :] = low

            @pl.when(counted)
            def _():
                small[t, gain_sum : gain_sum + 1, :] += column_total(dv * n)
                small[t, offset_sum : offset_sum + 1, :] += column_total(dv)
                small[t, round_sum : round_sum + 1, :] += column_total(low)

        def out_norm(i, carry):
            rows = tile_rows(i)
            norm_back((0, 1), i // (ntile // 2) == sec, dy[rows, :].astype(F32), rows, RSTD_B, GAIN1, GAIN1, BIAS_B, BIAS_F)
            acc[rows, :] = jnp.zeros((TILE, width), F32)
            return carry

        lax.fori_loop(0, ntile, out_norm, 0)

        for load in m_loads(l, 1, True):
            load.start()
        for load in h_loads(l):
            load.wait()
        transpose_pool((0, 1))
        for load in chunk_loads(l, 0, 0):
            load.start()

        def out_grad(ii, carry):
            for odd in range(2):
                i = 2 * ii + odd
                for load in m_loads(l, i, odd):
                    load.wait()
                for j in range(2):
                    mt[j * PIECE : (j + 1) * PIECE, :] = (gbuf[j] if odd else pool[2 + j]).T

                @pl.when(i + 2 < ff // width)
                def _():
                    for load in m_loads(l, i + 2, odd):
                        load.start()

                g = dot(mt[...], df[:, own]).astype(BF)
                if comm:
                    for o in range(4):
                        x, y = o % 2, o // 2
                        f = x * (1 - sec) + y * sec
                        s = y * (1 - sec) + x * sec
                        for q in range(4):
                            buf[t, q, f, s, i] = g[o * 192 + q * 48 : o * 192 + (q + 1) * 48]
                else:
                    buf[t, i] = g
            return carry

        lax.fori_loop(0, ff // width // 2, out_grad, 0)
        if comm:
            step(16 * t)
            step(16 * t + 1)

        o_loads = [pool_load(j, half, o_full.at[l], j * half) for j in range(2)]
        wo_load = rows_load(0, half, wo.at[l], 0)
        head_weights = [weight_load(j, half, wqkv.at[l], j * half) for j in range(3)]
        late_loads = [norm_load(l, NA_, 0, 2)] + o_loads + [wo_load] + head_weights[:2]

        def feed(jj, carry):
            for part in range(3):
                c = 3 * jj + part
                slot = c % 2
                for load in chunk_loads(l, slot, c):
                    load.wait()

                @pl.when(c + 1 < ffh // UNITS)
                def _():
                    for load in chunk_loads(l, 1 - slot, c + 1):
                        load.start()

                @pl.when(c + 1 == ffh // UNITS)
                def _():
                    for load in late_loads:
                        load.start()

                dm = dot_nt(df[...], wslot[slot, 0:UNITS])
                gbuf[0, :, 0:UNITS] = (dm * pool[2 * slot + 1, :, 0:UNITS].astype(F32)).astype(BF)
                gbuf[1, :, 0:UNITS] = (dm * pool[2 * slot, :, 0:UNITS].astype(F32)).astype(BF)
                acc[...] += dot_nt(gbuf[0, :, 0:UNITS], wpool[2 * slot, :, 0:UNITS]) + dot_nt(
                    gbuf[1, :, 0:UNITS], wpool[2 * slot + 1, :, 0:UNITS]
                )

                @pl.when(c == ffh // UNITS - 1)
                def _():
                    @pl.when(t > 0)
                    def _():
                        exchange(1).wait_send()

                    psend[...] = acc[...].astype(BF)
                    exchange(2 * t).start()

                unit = sec * ffh + c * UNITS
                spot = lanes_at(unit % width, UNITS)
                for k in range(2):
                    small[t, pl.ds(BIAS_IN + k * (ff // width) + unit // width, 1), spot] = column_total(
                        gbuf[k, :, 0:UNITS]
                    )
                    g = dot(tr[...], gbuf[k, :, 0:UNITS]).astype(BF)
                    n = 4 + 4 * jj + 2 * k
                    if part == 0:
                        put(t, n, 0, g)
                    elif part == 1:
                        put(t, n, 256, g[:, :128])
                        put(t, n + 1, 0, g[:, 128:])
                    else:
                        put(t, n + 1, 128, g)
                if comm:
                    step(16 * t + 2 + c)
            return carry

        lax.fori_loop(0, ffh // (3 * UNITS), feed, 0)
        norm_load(l, NA_, 1, 0).start()
        head_weights[2].start()

        for load in o_loads:
            load.wait()
        transpose_pool((0, 1))
        head_rows = [pool_load(j, half, qkv.at[l, j], 0) for j in range(3)]
        for load in head_rows:
            load.start()
        pool_load(3, half, acts.at[l, X_], 0).start()
        norm_load(l, NA_, 0, 2).wait()
        norm_load(l, NA_, 1, 0).wait()
        exchange(2 * t).wait_recv()

        def attn_norm(i, carry):
            rows = tile_rows(i)
            dh = df[rows, :].astype(F32) + (psend[rows, :].astype(F32) + precv[0, rows, :].astype(F32))
            norm_back((2, 0), i // (ntile // 2) == sec, dh, rows, RSTD_A, GAIN0, GAIN0, BIAS_A, BIAS_O)
            return carry

        lax.fori_loop(0, ntile, attn_norm, 0)

        wo_load.wait()

        @pl.when((t == 1) & (sec == 1))
        def _():
            x_store.wait()

        dy[:, 0:half] = dot_nt(df[...], wslot[0]).astype(BF)
        put(t, 12, 0, dot(tr[...], df[:, own]).astype(BF))
        if comm:
            step(16 * t + 8)
            step(16 * t + 9)

        for load in head_rows:
            load.wait()

        def row(r, carry):
            base = pl.multiple_of(r * seq, seq)
            kpad[HALO : HALO + seq, :] = pool[1, pl.ds(base, seq), :]
            vpad[HALO : HALO + seq, :] = pool[2, pl.ds(base, seq), :]
            lane = lax.broadcasted_iota(jnp.int32, (QB, 128), 1)

            for g in range(half // LANES):
                cols = slice(g * LANES, (g + 1) * LANES)

                def operands(i):
                    rows = pl.ds(pl.multiple_of(base + i * QB, QB), QB)
                    window = slice(i * QB, i * QB + KW)
                    qs = stack_heads(pool[0, rows, cols] * BF(HEAD**-0.5))
                    return rows, kpad[window, cols], qs, stack_heads(dy[rows, cols])

                for i in range(seq // QB):
                    rows, kw, qs, os = operands(i)
                    far = away[r, i].astype(F32)
                    s = dot_nt(qs, kw)
                    d = dot_nt(os, vpad[i * QB : i * QB + KW, cols])
                    kept = stats[rows, :]
                    for h in range(GROUP):
                        part = slice(h * QB, (h + 1) * QB)
                        lse = jnp.sum(jnp.where(lane == g * GROUP + h, kept, 0.0), axis=-1, keepdims=True)
                        p = jnp.exp(s[part] + slope_of(sec, g, h) * far - lse)
                        pd = p * d[part]
                        mt[part, i * KW : (i + 1) * KW] = (pd - p * jnp.sum(pd, axis=-1, keepdims=True)).astype(BF)
                        mt[GROUP * QB + h * QB : GROUP * QB + (h + 1) * QB, i * KW : (i + 1) * KW] = p.astype(BF)
                for i in range(seq // QB):
                    rows, kw, qs, os = operands(i)
                    ds = mt[0 : GROUP * QB, i * KW : (i + 1) * KW]
                    ps = mt[GROUP * QB : 2 * GROUP * QB, i * KW : (i + 1) * KW]
                    gbuf[0, rows, cols] = (merge_heads(dot(ds, kw)) * HEAD**-0.5).astype(BF)
                    dk, dv = dot_tn(ds, qs), dot_tn(ps, os)
                    if i == 0:
                        at, skip = pl.ds(base, HALO), HALO
                    else:
                        at, skip = pl.ds(pl.multiple_of(base + i * QB - HALO, HALO), QB), 0
                        dk = jnp.concatenate([dk[:QB] + left_k, dk[QB:]], axis=0)
                        dv = jnp.concatenate([dv[:QB] + left_v, dv[QB:]], axis=0)
                    gbuf[1, at, cols] = dk[skip:QB].astype(BF)
                    gbuf[2, at, cols] = dv[skip:QB].astype(BF)
                    left_k, left_v = dk[QB:], dv[QB:]
                at = pl.ds(pl.multiple_of(base + seq - HALO, HALO), HALO)
                gbuf[1, at, cols] = left_k[:HALO].astype(BF)
                gbuf[2, at, cols] = left_v[:HALO].astype(BF)
            if comm:
                step(16 * t + 10 + r)
            return carry

        lax.fori_loop(0, rows_n, row, 0)
        pool_load(0, half, acts.at[l, X_], half).start()
        for load in head_weights:
            load.wait()
        exchange(2 * t).wait_send()

        total = dot_nt(gbuf[0], wpool[0])
        for j in (1, 2):
            total += dot_nt(gbuf[j], wpool[j])
        psend[...] = total.astype(BF)
        exchange(2 * t + 1).start()
        small[t, BIAS_Q : BIAS_Q + 1, own] = column_total(gbuf[0])
        small[t, BIAS_V : BIAS_V + 1, own] = column_total(gbuf[2])
        pool_load(3, half, acts.at[l, X_], 0).wait()
        pool_load(0, half, acts.at[l, X_], half).wait()
        transpose_pool((3, 0))

        @pl.when(t == 0)
        def _():
            first_loads(0)

        if comm:
            step(16 * t + 12)
        for j in range(3):
            put(t, 13 + j, 0, dot(tr[...], gbuf[j]).astype(BF))
            if j < 2:

                @pl.when(t == 0)
                def _():
                    norm_load(0, NB_, j, j).start()

            if comm and j == 0:
                step(16 * t + 13)
        exchange(2 * t + 1).wait_recv()

        def result(i, carry):
            rows = tile_rows(i)
            dx = df[rows, :].astype(F32) + (psend[rows, :].astype(F32) + precv[1, rows, :].astype(F32))
            dy[rows, :] = dx.astype(BF)
            return carry

        lax.fori_loop(0, ntile, result, 0)

        @pl.when(sec == l)
        def _():
            x_store.start()

        if comm:
            step(16 * t + 14)
            step(16 * t + 15)
        return carry

    lax.fori_loop(0, 2, layer, 0)
    exchange(3).wait_send()

    @pl.when(sec == 0)
    def _():
        x_store.wait()

    if comm:
        mine = 1 - sec

        def vectors(stage):
            if stage == 0:
                return [remote(small.at[sec], v1, vs.at[0], vr.at[0], sib)]
            if stage == 1:
                return [remote(v1, v2, vs.at[1], vr.at[1], (sec, xp))]
            if stage == 2:
                return [remote(v2, v3, vs.at[2], vr.at[2], (sec, yp))]
            return [remote(v3, v4.at[d - 1], vs.at[2 + d], vr.at[2 + d], (sec, zp[d])) for d in (1, 2, 3)]

        def go(stage):
            for c in vectors(stage):
                c.start()

        def done(stage):
            for c in vectors(stage):
                c.wait()

        def rest(lo, hi):
            span(lo, hi, lambda i: step(i, False))

        def combine(stage, there, here):
            done(stage)
            there[...] += here
            go(stage + 1)

        last = 32 + AHEAD1 + AHEAD2
        go(0)
        rest(32, 34)
        combine(0, v1, small[mine])
        rest(34, 36)
        combine(1, v2, v1[...])
        rest(36, last)
        combine(2, v3, v2[...])
        for t in range(2):
            span(0, 16, lambda n, t=t: sent3(t, n))
        span(0, 16, lambda n: arrived(mine, n))
        done(3)
        small_out[...] = v3[...] + v4[0] + v4[1] + v4[2]
    else:
        store = pltpu.make_async_copy(buf, grads_out, gsem)
        store.start()
        small_out[...] = small[...]
        store.wait()


def run_backward(comm, cot, acts, o_full, m_full, qkv, pp, stats, away, wqkv, wo, win, wout, par):
    tokens, width = cot.shape
    ff = m_full.shape[2]
    half = width // 2
    dma = pltpu.SemaphoreType.DMA
    dx = jax.ShapeDtypeStruct((tokens, width), BF)
    if comm:
        r = width // 16
        small = jax.ShapeDtypeStruct((VECTORS, width), F32)
        grads = jax.ShapeDtypeStruct((16, 2, 4, r, PIECE), BF)
        special = [
            vm(2, 16, 2, 2, 4, r, PIECE),
            vm(2, 16, 2, 4, r, PIECE),
            vm(2, 16, 4, r, PIECE),
            vm(2, 5, 2, r, PIECE),
            vm(VECTORS, width, dtype=F32),
            vm(VECTORS, width, dtype=F32),
            vm(VECTORS, width, dtype=F32),
            vm(3, VECTORS, width, dtype=F32),
            dma((2, 16)), dma((2, 16)), dma((2, 16)), dma((2, 16)), dma((2, 5, 3)), dma((2, 5, 3)),
            dma((2, 16, 4)), dma((16, 2, 4)), dma((16,)),
            dma((6,)), dma((6,)),
        ]
    else:
        small = jax.ShapeDtypeStruct((2, VECTORS, width), F32)
        grads = jax.ShapeDtypeStruct((2, 16, width, PIECE), BF)
        special = [vm(2, 16, width, PIECE), dma]
    seq = away.shape[1] * QB
    scratch = special + [
        vm(tokens, width, dtype=F32),
        vm(tokens, width),
        vm(tokens, width),
        vm(width, tokens),
        vm(width, tokens),
        vm(2, VECTORS, width, dtype=F32),
        vm(tokens, 128, dtype=F32),
        vm(4, tokens, PIECE),
        vm(4, width, PIECE),
        vm(2, half, width),
        vm(3, tokens, half),
        vm(seq + 2 * HALO, half),
        vm(seq + 2 * HALO, half),
        vm(tokens, width),
        vm(2, tokens, width),
        dma((4,)), dma((4,)), dma((2,)), dma((3,)), dma, dma, dma, dma((4,)), dma((4,)),
    ]
    return pl.pallas_call(
        functools.partial(bwd_kernel, comm),
        out_shape=(dx, small, grads),
        in_specs=[any_spec()] * 7 + [vmem_spec()] + [any_spec()] * 4 + [vmem_spec()],
        out_specs=(any_spec(), vmem_spec(), any_spec()),
        scratch_shapes=scratch,
        compiler_params=pltpu.CompilerParams(
            collective_id=2, has_side_effects=True, vmem_limit_bytes=64 << 20
        ),
        name="backward",
    )(cot, acts, o_full, m_full, qkv, pp, stats, away, wqkv, wo, win, wout, par)


def results_kernel(shares, vectors, fq, fo, fi, fu, gain_out, bias_out, inner_out, land, stage, lsem, fsem):
    me = lax.axis_index("dp")
    rows, width = fo.shape
    half, ff = width // 2, fi.shape[1] // 2
    ffh = ff // 2
    loads = []
    for n in range(16):
        used = 2 if n % EARLY == 1 else 4
        loads.append(
            pltpu.make_async_copy(shares.at[n, :, 0:used], land.at[n, :, 0:used], lsem.at[n])
        )
    for c in loads:
        c.start()

    def place(n, k):
        if n < 4:
            return fu.at[n * rows : (n + 1) * rows, k * half : (k + 1) * half]
        if n < 12:
            jj, g, i = (n - 4) // 4, (n - 4) // 2 % 2, n % 2
            start = g * ff + k * ffh + (2 * jj + i) * PIECE
            return fi.at[:, start : start + PIECE]
        if n == 12:
            return fo.at[:, k * half : (k + 1) * half]
        start = (n - 13) * width + k * half
        return fq.at[:, start : start + half]

    stores = []
    for n in range(16):
        loads[n].wait()
        for k in range(2):
            total = land[n, k, 0].astype(F32) + land[n, k, 1].astype(F32)
            if n % EARLY != 1:
                total = total + (land[n, k, 2].astype(F32) + land[n, k, 3].astype(F32))
            stage[n, k] = total
            stores.append(pltpu.make_async_copy(stage.at[n, k], place(n, k), fsem.at[n, k]))
            stores[-1].start()
    turned = pltpu.roll(vectors[0:8, :], (width - me * rows) % width, axis=1)
    gain_out[...] = turned[0:2, 0:rows]
    for j in range(6):
        bias_out[j] = turned[2 + j : 3 + j, 0:rows]
    line = vectors[pl.ds(8 + me // 2, 1), :]
    inner_out[...] = jnp.where(me % 2 == 0, line[:, :half], line[:, half:])
    for c in stores:
        c.wait()


def run_results(shares, vectors, ff):
    _, _, _, rows, half = shares.shape
    width = 2 * half
    dma = pltpu.SemaphoreType.DMA

    def out(*shape):
        return jax.ShapeDtypeStruct(shape, F32)

    return pl.pallas_call(
        results_kernel,
        out_shape=(
            out(rows, 3 * width), out(rows, width), out(rows, 2 * ff), out(ff // 16, width),
            out(2, rows), out(6, 1, rows), out(1, 2 * ff // 16),
        ),
        in_specs=[any_spec(), vmem_spec()],
        out_specs=tuple([any_spec()] * 4 + [vmem_spec()] * 3),
        scratch_shapes=[
            vm(*shares.shape), vm(16, 2, rows, half, dtype=F32), dma((16,)), dma((16, 2)),
        ],
        compiler_params=pltpu.CompilerParams(vmem_limit_bytes=60 << 20),
        name="results",
    )(shares, vectors)


def assemble(halves, width, ff):
    def columns(v):
        return jnp.concatenate(v, axis=1)

    gu = columns([h[:4].reshape(ff, PIECE) for h in halves])
    inner = [
        columns([h[4 + 4 * jj + 2 * k + i] for jj in range(2) for i in range(2)]) for k in range(2) for h in halves
    ]
    gi = columns(inner)
    go = columns([h[12] for h in halves])
    gq = columns([h[13 + j] for j in range(3) for h in halves])
    return gq, go, gi, gu


def shards(comm, hidden, segs, w_qkv, w_o, w_in, w_out, gains, biases, b_in, cot):
    w_qkv, w_o, w_in, w_out, gains = (v[0] for v in (w_qkv, w_o, w_in, w_out, gains))
    biases = jnp.transpose(biases, (1, 0, 2))
    micro, _, seq, width = hidden.shape
    ff = w_out.shape[0]
    tokens = micro * seq
    y, acts, o_full, m_full, qkv, pp, stats, wqkv2, wo2, win2, wout2, par2, away = run_forward(
        hidden.reshape(micro, seq, width), segs, w_qkv, w_o, w_in, w_out, gains, biases, b_in
    )
    dx, small, grads = run_backward(
        comm, cot.reshape(tokens, width), acts.reshape(2, 4, tokens, width), o_full.reshape(2, tokens, width),
        m_full.reshape(2, tokens, ff), qkv.reshape(2, 3, tokens, width // 2), pp.reshape(2, 2, tokens, ff // 2),
        stats.reshape(2, tokens, 128), away, wqkv2, wo2, win2, wout2, par2,
    )
    if comm:
        gq, go, gi, gu, gain, bias, inner = run_results(grads, small, ff)
        return (
            y.reshape(1, *hidden.shape), dx.reshape(1, *hidden.shape), gq[None], go[None], gi[None], gu[None],
            gain[None], jnp.transpose(bias, (1, 0, 2)), inner,
        )
    owners, me = lax.axis_size("dp"), lax.axis_index("dp")
    first = lax.axis_index("section") == 0
    swap = [(0, 1), (1, 0)]

    def pick(v):
        own = jnp.where(first, v[1], v[0])
        return own, lax.ppermute(jnp.where(first, v[0], v[1]), "section", swap)

    own, other = pick(grads)
    halves = [jnp.where(first, own, other), jnp.where(first, other, own)]

    def share(v):
        parts = v.reshape(owners, v.shape[0] // owners, v.shape[1])
        got = lax.all_to_all(parts, "dp", split_axis=0, concat_axis=0, tiled=True)
        return jnp.sum(got.astype(F32), axis=0)

    gq, go, gi, gu = (share(v) for v in assemble(halves, width, ff))
    own, other = pick(small)
    small = lax.psum(own + other, "dp")
    part = width // owners
    mine = lax.dynamic_slice_in_dim(small[:8], me * part, part, axis=1)
    inner = lax.dynamic_slice_in_dim(small[8:].reshape(1, 2 * ff), me * (2 * ff // owners), 2 * ff // owners, axis=1)
    return (
        y.reshape(1, *hidden.shape), dx.reshape(1, *hidden.shape), gq[None], go[None], gi[None], gu[None],
        mine[None, :2], mine[None, 2:], inner,
    )


def solution(mesh):
    rows = P(None, "dp", None, None)
    layer = P("section", None, None)
    comm = mesh.shape["dp"] == 16
    return jax.shard_map(
        functools.partial(shards, comm),
        mesh=mesh,
        in_specs=(rows, P(None, "dp", None)) + (layer,) * 6 + (P("section", None), rows),
        out_specs=(
            P("section", None, "dp", None, None),
            P("section", None, "dp", None, None),
            P("section", "dp", None),
            P("section", "dp", None),
            P("section", "dp", None),
            P("section", "dp", None),
            P("section", None, "dp"),
            P("section", None, "dp"),
            P("section", "dp"),
        ),
        check_vma=False,
    )
```
